32 devices in a mesh: dp: 4 (over y, core), tensor: 8 (over z, x).
Axes of the slice: x: 2, y: 2, z: 4, core: 2. Of those that a mesh axis runs over, the one named last changes fastest.
Arguments:
- patches: bfloat16 [32, 256, 1152], P('dp'), may hold values from -6 to 6
- conditioning: bfloat16 [32, 1152], P('dp'), may hold values from -6 to 6
- keep_count: int32 [32], P('dp'), may hold values from 64 to 192, as said below
- keep_index: int32 [32, 192], P('dp'), may hold values from 0 to 255, as said below
- mod_weight: bfloat16 [1152, 6912], P(None, 'tensor'), may hold values from -0.1875 to 0.1875
- mod_bias: bfloat16 [6912], P('tensor'), may hold values from -3 to 3
- qkv_weight: bfloat16 [3, 1152, 1152], P(None, None, 'tensor'), may hold values from -0.1875 to 0.1875
- qv_bias: bfloat16 [2, 1152], P(None, 'tensor'), may hold values from -3 to 3
- out_weight: bfloat16 [1152, 1152], P('tensor'), may hold values from -1.25 to 1.25
- out_bias: bfloat16 [1152], replicated, may hold values from -2 to 2
- up_weight: bfloat16 [1152, 4608], P(None, 'tensor'), may hold values from -0.1875 to 0.1875
- up_bias: bfloat16 [4608], P('tensor'), may hold values from -3 to 3
- down_weight: bfloat16 [4608, 1152], P('tensor'), may hold values from -0.09375 to 0.09375
- down_bias: bfloat16 [1152], replicated, may hold values from -2 to 2
- out_cotangent: bfloat16 [32, 192, 1152], P('dp'), may hold values from -6 to 6
Outputs:
- block_out: bfloat16 [32, 192, 1152], P('dp')
- grad_patches: bfloat16 [32, 256, 1152], P('dp')
- grad_conditioning: bfloat16 [32, 1152], P('dp')
- mod_weight_grad: float32 [1152, 6912], P(None, 'tensor')
- mod_bias_grad: float32 [6912], P('tensor')
- qkv_weight_grad: float32 [3, 1152, 1152], P(None, None, 'tensor')
- qv_bias_grad: float32 [2, 1152], P(None, 'tensor')
- out_weight_grad: float32 [1152, 1152], P('tensor')
- out_bias_grad: float32 [1152], replicated
- up_weight_grad: float32 [1152, 4608], P(None, 'tensor')
- up_bias_grad: float32 [4608], P('tensor')
- down_weight_grad: float32 [4608, 1152], P('tensor')
- down_bias_grad: float32 [1152], replicated
The draws below stay inside these ranges and needn't reach their ends.
Inputs may be any that keep to these rules, and one draw needn't show every extreme that they name: `keep_count`: some image keeps 192 tokens and some keeps 64. A row of keep_index lists 192 different patch positions; the first keep_count of them are the image's kept tokens, the others are not read.
All inputs are finite; a program needn't handle non-finite values.
Results may differ from the reference program's by a relative error of at most 0.014.
The reference program's roundings to bfloat16 on the way count: a program that leaves them out, or rounds other values in their place, can miss the bound.
Values may be sent and summed in bfloat16 or wider, within the bound.
A program may use at most 192 MiB of HBM per device.

```python
import jax
import jax.numpy as jnp
from jax import lax

HEADS = 16
HD = 72
D = 1152
FF = 4608
MODS = 6912
PATCHES = 256
KEEP = 192
LEAST = 64
IMAGES = 32


def draw_keep_count(key, part):
    counts = jax.random.randint(key, (IMAGES,), LEAST, KEEP + 1)
    return counts.at[0].set(KEEP).at[IMAGES - 1].set(LEAST).astype(jnp.int32)


def draw_keep_index(key, part):
    subkeys = jax.random.split(jax.random.fold_in(key, 7), IMAGES)
    ranking = jax.vmap(lambda subkey: jax.random.permutation(subkey, PATCHES))(subkeys).astype(jnp.int32)
    ranking = ranking.at[0, PATCHES - 1].set(-2).at[0, 0].set(-1)
    ordering = jnp.argsort(ranking, axis=1, stable=True)
    return ordering[:, :KEEP].astype(jnp.int32)


def steps_of(own_key, dims, cuts, smallest, high):
    gain = 1.0
    for position, blocks in cuts:
        heights = jax.random.uniform(jax.random.fold_in(jax.random.fold_in(own_key, 6), position), (blocks,), jnp.float32, smallest / len(cuts), high / len(cuts))
        gain = gain * jnp.repeat(jnp.exp(heights), dims[position] // blocks).reshape((-1,) + (1,) * (len(dims) - 1 - position))
    return gain


def gaussian(stream_key, dims, spread, limit, pieces=(), kind=jnp.bfloat16):
    array = jax.random.normal(stream_key, dims, jnp.float32) * spread
    if len(pieces) > 0:
        array = steps_of(stream_key, dims, pieces, -0.22, 0.18) * array
    return jnp.clip(array, min=-limit, max=limit).astype(kind)


def setup_inputs(seed: int = 0) -> dict:
    seeds = jax.random.split(jax.random.key(seed), 16)
    patches = gaussian(seeds[0], (IMAGES, PATCHES, D), 1.0, 6.0, ((0, 4),))
    conditioning = gaussian(seeds[1], (IMAGES, D), 1.0, 6.0, ((0, 4),))
    keep_count = draw_keep_count(jax.random.fold_in(seeds[15], 71), 0)
    keep_index = draw_keep_index(jax.random.fold_in(seeds[15], 71), 0)
    mod_weight = gaussian(seeds[4], (D, MODS), D ** -0.5, 0.1875, ((1, 8),))
    mod_bias = gaussian(seeds[5], (MODS,), 0.5, 3.0, ((0, 8),))
    qkv_weight = gaussian(seeds[6], (3, D, D), D ** -0.5, 0.1875, ((2, 8),))
    qv_bias = gaussian(seeds[7], (2, D), 0.5, 3.0, ((1, 8),))
    out_weight = gaussian(seeds[8], (D, D), (max(D // 48, 1)) ** -0.5, 1.25, ((0, 8),))
    out_bias = gaussian(seeds[9], (D,), 0.3, 2.0)
    up_weight = gaussian(seeds[10], (D, FF), D ** -0.5, 0.1875, ((1, 8),))
    up_bias = gaussian(seeds[11], (FF,), 0.5, 3.0, ((0, 8),))
    down_weight = gaussian(seeds[12], (FF, D), FF ** -0.5, 0.09375, ((0, 8),))
    down_bias = gaussian(seeds[13], (D,), 0.3, 2.0)
    out_cotangent = gaussian(seeds[14], (IMAGES, KEEP, D), 1.0, 6.0, ((0, 4),))
    return dict(patches=patches, conditioning=conditioning, keep_count=keep_count, keep_index=keep_index, mod_weight=mod_weight, mod_bias=mod_bias, qkv_weight=qkv_weight, qv_bias=qv_bias, out_weight=out_weight, out_bias=out_bias, up_weight=up_weight, up_bias=up_bias, down_weight=down_weight, down_bias=down_bias, out_cotangent=out_cotangent)


@jax.custom_vjp
def low(v):
    return lax.optimization_barrier(v.astype(jnp.bfloat16)).astype(jnp.float32)

@jax.custom_vjp
def low_back(v):
    return v

def low_keep(v):
    return (low(v), None)

def low_pass(kept, grad):
    return (grad,)

def back_keep(v):
    return (v, None)

def back_low(kept, grad):
    return (low(grad),)
low.defvjp(low_keep, low_pass)
low_back.defvjp(back_keep, back_low)

def layer_norm(inputs):
    centred = inputs - lax.optimization_barrier(jnp.mean(inputs, axis=-1, keepdims=True))
    return centred * lax.rsqrt(lax.optimization_barrier(jnp.mean(centred * centred, axis=-1, keepdims=True)) + 1e-06)

def matmul(left, right):
    return jnp.dot(left, right, precision=lax.Precision.HIGHEST)

def attend_one(members):
    queries, key_rows, value_rows, live_keys = members
    scores = low_back(jnp.einsum('qhd,khd->hqk', queries, key_rows, precision=lax.Precision.HIGHEST) * HD ** (-0.5))
    scores = jnp.where(live_keys[None, None, :] > 0, scores, -1e+30)
    row_top = lax.optimization_barrier(jnp.max(scores, axis=-1, keepdims=True))
    exp_scores = jnp.exp(scores - row_top)
    weights = exp_scores / lax.optimization_barrier(jnp.sum(exp_scores, axis=-1, keepdims=True))
    return jnp.einsum('hqk,khd->qhd', low(weights), value_rows, precision=lax.Precision.HIGHEST)

def forward(patches, conditioning, mod_weight, mod_bias, qkv_weight, qv_bias, out_weight, out_bias, up_weight, up_bias, down_weight, down_bias, keep_count, keep_index):
    live_rows = (jnp.arange(KEEP, dtype=jnp.int32)[None, :] < keep_count[:, None]).astype(jnp.float32)
    tokens = jnp.take_along_axis(patches, keep_index[:, :, None], axis=1) * live_rows[:, :, None]
    modulation = low(matmul(low(jax.nn.silu(conditioning)), mod_weight) + mod_bias)
    blocks = [modulation[:, None, member * D:(member + 1) * D] for member in range(6)]
    shift_one, scale_one, gate_one, shift_two, scale_two, gate_two = blocks
    normed_one = low(layer_norm(tokens) * (1.0 + scale_one) + shift_one).reshape(IMAGES * KEEP, D)
    queries = low(low_back(matmul(normed_one, qkv_weight[0]) + qv_bias[0])).reshape(IMAGES, KEEP, HEADS, HD)
    key_rows = low(low_back(matmul(normed_one, qkv_weight[1]))).reshape(IMAGES, KEEP, HEADS, HD)
    value_rows = low(low_back(matmul(normed_one, qkv_weight[2]) + qv_bias[1])).reshape(IMAGES, KEEP, HEADS, HD)
    attended = lax.map(jax.checkpoint(attend_one), (queries, key_rows, value_rows, live_rows))
    attended = low(low_back(attended.reshape(IMAGES * KEEP, D)))
    branch = low_back(matmul(attended, out_weight) + out_bias).reshape(IMAGES, KEEP, D)
    middle = tokens + gate_one * branch
    normed_two = low(layer_norm(middle) * (1.0 + scale_two) + shift_two).reshape(IMAGES * KEEP, D)
    pre_act = low_back(matmul(normed_two, up_weight) + up_bias)
    hidden = low(jax.nn.gelu(pre_act, approximate=True))
    mlp_out = low_back(matmul(hidden, down_weight) + down_bias).reshape(IMAGES, KEEP, D)
    return (middle + gate_two * mlp_out) * live_rows[:, :, None]

def reference(patches, conditioning, keep_count, keep_index, mod_weight, mod_bias, qkv_weight, qv_bias, out_weight, out_bias, up_weight, up_bias, down_weight, down_bias, out_cotangent):
    floats = (patches, conditioning, mod_weight, mod_bias, qkv_weight, qv_bias, out_weight, out_bias, up_weight, up_bias, down_weight, down_bias)
    floats = tuple((member.astype(jnp.float32) for member in floats))

    def closed(*inputs):
        return forward(*inputs, keep_count, keep_index)
    block_out, pull = jax.vjp(closed, *floats)
    grads = pull(out_cotangent.astype(jnp.float32))
    return (block_out.astype(jnp.bfloat16), grads[0].astype(jnp.bfloat16), grads[1].astype(jnp.bfloat16), grads[2], grads[3], grads[4], grads[5], grads[6], grads[7], grads[8], grads[9], grads[10], grads[11])
```

```python
import functools

import jax
import jax.numpy as jnp
from jax import lax
from jax.experimental import pallas as pl
from jax.experimental.pallas import tpu as pltpu
from jax.sharding import PartitionSpec as P

HD = 72
MESH = pl.DeviceIdType.MESH
F32 = jnp.float32
LOW = jnp.bfloat16
DMA = pltpu.SemaphoreType.DMA
VM = pl.BlockSpec(memory_space=pltpu.VMEM)
SM = pl.BlockSpec(memory_space=pltpu.SMEM)
HB = pl.BlockSpec(memory_space=pl.ANY)
PAIR = 2
GELU_ROOT = 0.7978845608028654
GELU_CUBE = 0.044715


def remote(source, target, send_sem, recv_sem, device):
    return pltpu.make_async_remote_copy(
        src_ref=source,
        dst_ref=target,
        send_sem=send_sem,
        recv_sem=recv_sem,
        device_id={"tensor": device},
        device_id_type=MESH,
    )


def place(depth):
    me = lax.axis_index("tensor")
    return me, me // PAIR, me % PAIR


def meet(peers):
    barrier = pltpu.get_barrier_semaphore()
    for peer in peers:
        pl.semaphore_signal(barrier, inc=1, device_id={"tensor": peer}, device_id_type=MESH)
    pl.semaphore_wait(barrier, len(peers))


def column_peers(depth):
    me, up, side = place(depth)
    return [((up + step) % depth) * PAIR + side for step in range(1, depth)]


def dot(left, right):
    return jnp.dot(left, right, preferred_element_type=F32)


def dot_nt(left, right):
    return lax.dot_general(left, right, (((1,), (1,)), ((), ())), preferred_element_type=F32)


def dot_tn(left, right):
    return lax.dot_general(left, right, (((0,), (0,)), ((), ())), preferred_element_type=F32)


def norm_parts(rows):
    width = rows.shape[-1]
    centred = rows - jnp.sum(rows, axis=-1, keepdims=True) * (1.0 / width)
    spread = lax.rsqrt(jnp.sum(centred * centred, axis=-1, keepdims=True) * (1.0 / width) + 1e-06)
    return centred * spread, spread


def norm_back(norm, spread, grad):
    width = norm.shape[-1]
    mean_grad = jnp.sum(grad, axis=-1, keepdims=True) * (1.0 / width)
    mean_both = jnp.sum(grad * norm, axis=-1, keepdims=True) * (1.0 / width)
    return (grad - mean_grad - norm * mean_both) * spread


class Gather:
    def __init__(self, buffer, share, depth, pieces, send, recv):
        self.buffer, self.share, self.depth, self.pieces = buffer, share, depth, pieces
        self.send, self.recv = send, recv
        self.me, self.up, self.side = place(depth)

    def piece(self, index, part):
        rows = self.share // self.pieces
        return self.buffer.at[pl.ds(pl.multiple_of(index * self.share + part * rows, rows), rows), :]

    def copy(self, way, step, part):
        source = self.up - (step - 1) * (1 - 2 * way)
        target = self.up + 1 - 2 * way
        view = self.piece(source, part)
        return remote(
            view,
            view,
            self.send.at[way, step, part],
            self.recv.at[way, step, part],
            target * PAIR + self.side,
        )

    def may_send(self, way, step):
        if way == 0:
            return (self.up + 1 < self.depth) & (self.up >= step - 1)
        return (self.up >= 1) & (self.up + step - 1 < self.depth)

    def open(self):
        for part in range(self.pieces):
            for way in range(2):

                @pl.when(self.may_send(way, 1))
                def _():
                    self.copy(way, 1, part).start()

    def arrival(self, turn):
        below = self.up
        above = self.depth - 1 - self.up
        both = jnp.minimum(below, above)
        mixed = turn <= 2 * both
        way = jnp.where(mixed, (turn + 1) % 2, jnp.where(below > above, 0, 1))
        step = jnp.where(mixed, (turn + 1) // 2, turn - both)
        step = jnp.where(turn == 0, 0, step)
        return way, step, self.up - step * (1 - 2 * way)

    def take(self, turn):
        way, step, source = self.arrival(turn)
        ahead = jnp.where(way == 0, self.up + 1 < self.depth, self.up >= 1)

        @pl.when(turn > 0)
        def _():
            for part in range(self.pieces):
                view = self.piece(source, part)
                remote(
                    view,
                    view,
                    self.send.at[way, step, part],
                    self.recv.at[way, step, part],
                    self.me,
                ).wait_recv()

                @pl.when(ahead)
                def _():
                    self.copy(way, step + 1, part).start()

        return source

    def close(self):
        for way in range(2):
            for step in range(1, self.depth):

                @pl.when(self.may_send(way, step))
                def _():
                    for part in range(self.pieces):
                        self.copy(way, step, part).wait_send()


class Reduce:
    def __init__(self, terms, landing, share, depth, pieces, send, recv):
        self.terms, self.landing, self.share, self.depth, self.pieces = (
            terms,
            landing,
            share,
            depth,
            pieces,
        )
        self.send, self.recv = send, recv
        self.me, self.up, self.side = place(depth)
        self.rows = share // pieces

    def span(self, index, part):
        return pl.ds(pl.multiple_of(index * self.share + part * self.rows, self.rows), self.rows)

    def copy(self, way, owner, part):
        target = self.up + 1 - 2 * way
        slot = owner if way == 0 else jnp.where(owner == target, self.depth, owner)
        return remote(
            self.terms.at[self.span(owner, part), :],
            self.landing.at[self.span(slot, part), :],
            self.send.at[owner, part],
            self.recv.at[slot, part],
            target * PAIR + self.side,
        )

    def landed(self, slot, part):
        view = self.landing.at[self.span(slot, part), :]
        remote(view, view, self.send.at[0, part], self.recv.at[slot, part], self.me).wait_recv()

    def ready(self, owner):
        @pl.when((self.up == 0) & (owner > 0))
        def _():
            for part in range(self.pieces):
                self.copy(0, owner, part).start()

        @pl.when((self.up == self.depth - 1) & (owner < self.depth - 1))
        def _():
            for part in range(self.pieces):
                self.copy(1, owner, part).start()

    def add(self, target, target_start, term_start, starts):
        def body(index, carry):
            offset = index * 16
            value = self.terms[
                pl.ds(pl.multiple_of(term_start + offset, 16), 16), :
            ].astype(F32)
            for start in starts:
                value = value + self.landing[
                    pl.ds(pl.multiple_of(start + offset, 16), 16), :
                ].astype(F32)
            target[pl.ds(pl.multiple_of(target_start + offset, 16), 16), :] = value.astype(
                target.dtype
            )
            return carry

        lax.fori_loop(0, self.rows // 16, body, 0)

    def relay(self, owner, part):
        start = owner * self.share + part * self.rows

        def pass_on(way):
            self.landed(owner, part)
            self.add(self.terms, start, start, [start])
            self.copy(way, owner, part).start()

        @pl.when((owner > self.up) & (self.up > 0))
        def _():
            pass_on(0)

        @pl.when((owner < self.up) & (self.up < self.depth - 1))
        def _():
            pass_on(1)

    def finish(self, total):
        start = self.up * self.share
        end = self.depth * self.share
        for part in range(self.pieces):
            skip = part * self.rows

            @pl.when(self.up == 0)
            def _():
                self.landed(self.depth, part)
                self.add(total, skip, start + skip, [end + skip])

            @pl.when(self.up == self.depth - 1)
            def _():
                self.landed(self.up, part)
                self.add(total, skip, start + skip, [start + skip])

            @pl.when((self.up > 0) & (self.up < self.depth - 1))
            def _():
                self.landed(self.up, part)
                self.landed(self.depth, part)
                self.add(total, skip, start + skip, [start + skip, end + skip])

    def close(self):
        for owner in range(self.depth):

            @pl.when(self.up != owner)
            def _():
                for part in range(self.pieces):
                    remote(
                        self.terms.at[self.span(owner, part), :],
                        self.landing.at[self.span(owner, part), :],
                        self.send.at[owner, part],
                        self.recv.at[owner, part],
                        self.me,
                    ).wait_send()


def far_first(turn, group, count):
    low = group < count // 2
    own = jnp.where(low, count - 1 - group, group)
    moved = jnp.where(turn >= own, turn + 1, turn)
    other = jnp.where(low, count - 1 - moved, moved)
    return jnp.where(turn == count - 1, group, other)


def near_first(turn, up, depth):
    low = up < depth // 2
    ahead = jnp.where(turn < depth - 1 - up, up + 1 + turn, depth - 2 - turn)
    behind = jnp.where(turn < up, up - 1 - turn, turn + 1)
    return jnp.where(low, ahead, behind)


def modulation_kernel(devices, cond, weight, bias, gathered, silu_out, mine, send, recv):
    me = lax.axis_index("tensor")
    meet([(me + step) % devices for step in range(1, devices)])
    value = cond[...].astype(F32)
    silu = (value / (1.0 + jnp.exp(-value))).astype(LOW)
    silu_out[...] = silu
    local = (dot(silu, weight[...]) + bias[...].astype(F32)).astype(LOW)
    mine[...] = local
    gathered[me] = local
    copies = []
    for step in range(1, devices):
        copy = remote(
            mine, gathered.at[me], send.at[step], recv.at[step], (me + step) % devices
        )
        copy.start()
        copies.append(copy)
    for step in range(1, devices):
        source = (me + devices - step) % devices
        remote(mine, gathered.at[source], send.at[step], recv.at[step], me).wait_recv()
    for copy in copies:
        copy.wait_send()


def modulation(cond, weight, bias, devices):
    images, width = cond.shape
    columns = weight.shape[1]
    return pl.pallas_call(
        functools.partial(modulation_kernel, devices),
        out_shape=(
            jax.ShapeDtypeStruct((devices, images, columns), LOW),
            jax.ShapeDtypeStruct((images, width), LOW),
        ),
        in_specs=[VM] * 3,
        out_specs=(VM, VM),
        scratch_shapes=[pltpu.VMEM((images, columns), LOW), DMA((devices,)), DMA((devices,))],
        compiler_params=pltpu.CompilerParams(collective_id=0, has_side_effects=True),
        name="modulation",
    )(cond, weight, bias)


def head_mask(head, width):
    lane = lax.broadcasted_iota(jnp.int32, (1, width), 1)
    return (lane >= head * HD) & (lane < (head + 1) * HD)


def softmax_rows(queries, keys, key_live, scale):
    scores = dot_nt(queries, keys) * scale
    scores = jnp.where(key_live, scores, -1e30)
    top = jnp.max(scores, axis=-1, keepdims=True)
    raised = jnp.exp(scores - top)
    return raised / jnp.sum(raised, axis=-1, keepdims=True)


def attend_kernel(
    sizes,
    count,
    index,
    patches,
    mod,
    qkv_own,
    qkv_other,
    qv_own,
    qv_other,
    out_own,
    out_other,
    out_bias,
    normed_out,
    proj_out,
    attended_out,
    tokens_own,
    mid_out,
    branch_out,
    normed_two_out,
    patch_rows,
    tokens,
    terms,
    landing,
    total,
    patch_sem,
    send,
    recv,
):
    depth, images, kept, share, pieces = sizes
    me, up, side = place(depth)
    width = patches.shape[2]
    local = out_own.shape[0]
    scale = HD ** (-0.5)
    fold = depth // images
    first = side * images

    def fetch(image):
        return pltpu.make_async_copy(
            patches.at[first + image], patch_rows.at[image], patch_sem.at[image]
        )

    for turn in range(images):
        fetch(far_first(turn, up // fold, images)).start()
    meet(column_peers(depth))
    reduce = Reduce(terms, landing, share, depth, pieces, send, recv)

    def one(turn, carry):
        image = far_first(turn, up // fold, images)
        fetch(image).wait()
        rows = pl.ds(pl.multiple_of(image * kept, kept), kept)
        kept_count = count[first + image]
        spots = lax.broadcasted_iota(jnp.int32, (patches.shape[1], kept), 0)
        slots = lax.broadcasted_iota(jnp.int32, (patches.shape[1], kept), 1)
        pick = jnp.where((spots == index[first + image]) & (slots < kept_count), 1.0, 0.0)
        rows_float = dot_tn(pick.astype(LOW), patch_rows[image])
        tokens[rows, :] = rows_float.astype(LOW)
        norm, _ = norm_parts(rows_float)
        normed = (
            norm * (1.0 + mod[first + image, 1:2, :]) + mod[first + image, 0:1, :]
        ).astype(LOW)
        normed_out[rows, :] = normed
        key_live = lax.broadcasted_iota(jnp.int32, (1, kept), 1) < kept_count
        branch = None
        for shard, (qkv, qv, out) in enumerate(
            ((qkv_own, qv_own, out_own), (qkv_other, qv_other, out_other))
        ):
            queries = (dot(normed, qkv[0]) + qv[0:1, :].astype(F32)).astype(LOW)
            keys = dot(normed, qkv[1]).astype(LOW)
            values = (dot(normed, qkv[2]) + qv[1:2, :].astype(F32)).astype(LOW)
            proj_out[shard, 0, rows, :] = queries
            proj_out[shard, 1, rows, :] = keys
            proj_out[shard, 2, rows, :] = values
            attended = jnp.zeros((kept, local), F32)
            for head in range(local // HD):
                mask = head_mask(head, local)
                weights = softmax_rows(
                    jnp.where(mask, queries, 0.0).astype(LOW), keys, key_live, scale
                )
                attended = attended + dot(
                    weights.astype(LOW), jnp.where(mask, values, 0.0).astype(LOW)
                )
            attended = attended.astype(LOW)
            attended_out[shard, rows, :] = attended
            part = dot(attended, out[...])
            branch = part if branch is None else branch + part
        terms[rows, :] = branch.astype(LOW)
        for part in range(fold):
            reduce.ready(image * fold + part)
        return carry

    lax.fori_loop(0, images, one, 0)
    for turn in range(depth - 1):
        for part in range(pieces):
            reduce.relay(far_first(turn, up, depth), part)
    reduce.finish(total)
    image = first + (up * share) // kept
    own = tokens[pl.ds(pl.multiple_of(up * share, share), share), :]
    tokens_own[...] = own
    branch = total[...] + out_bias[...].astype(F32)
    branch_out[...] = branch
    mid = own.astype(F32) + mod[image, 2:3, :] * branch
    mid_out[...] = mid
    norm, _ = norm_parts(mid)
    normed_two_out[...] = (norm * (1.0 + mod[image, 4:5, :]) + mod[image, 3:4, :]).astype(LOW)
    reduce.close()


def attend(sizes, args):
    depth, images, kept, share, pieces = sizes
    width = args[2].shape[2]
    spots = args[2].shape[1]
    local = args[8].shape[0]
    rows = images * kept
    return pl.pallas_call(
        functools.partial(attend_kernel, sizes),
        out_shape=(
            jax.ShapeDtypeStruct((rows, width), LOW),
            jax.ShapeDtypeStruct((PAIR, 3, rows, local), LOW),
            jax.ShapeDtypeStruct((PAIR, rows, local), LOW),
            jax.ShapeDtypeStruct((share, width), LOW),
            jax.ShapeDtypeStruct((share, width), F32),
            jax.ShapeDtypeStruct((share, width), F32),
            jax.ShapeDtypeStruct((share, width), LOW),
        ),
        in_specs=[SM, VM, HB] + [VM] * 8,
        out_specs=(VM,) * 7,
        scratch_shapes=[
            pltpu.VMEM((images, spots, width), LOW),
            pltpu.VMEM((rows, width), LOW),
            pltpu.VMEM((rows, width), LOW),
            pltpu.VMEM((rows + share, width), LOW),
            pltpu.VMEM((share, width), F32),
            DMA((images,)),
            DMA((depth, pieces)),
            DMA((depth + 1, pieces)),
        ],
        compiler_params=pltpu.CompilerParams(
            collective_id=1, has_side_effects=True, vmem_limit_bytes=60 << 20
        ),
        name="attend",
    )(*args)


def feed_kernel(
    sizes,
    count,
    normed_own,
    cotangent,
    mod,
    up_own,
    up_other,
    up_bias_own,
    up_bias_other,
    down_own,
    down_other,
    down_bias,
    mid,
    branch,
    up_grad,
    down_grad,
    up_bias_grad,
    down_bias_grad,
    block_own,
    grad_mid_out,
    grad_branch_out,
    sums_out,
    normed,
    cot,
    hidden,
    grad_pre,
    grad_mlp,
    terms,
    landing,
    mlp_terms,
    mlp_landing,
    total,
    mlp_total,
    cot_sem,
    own_sem,
    gather_send,
    gather_recv,
    send,
    recv,
    mlp_send,
    mlp_recv,
):
    depth, images, kept, share, pieces = sizes
    me, up, side = place(depth)
    width = normed_own.shape[1]
    fold = depth // images
    first = side * images
    own_rows = pl.ds(pl.multiple_of(up * share, share), share)
    own_copy = pltpu.make_async_copy(normed_own, normed.at[own_rows, :], own_sem)
    own_copy.start()

    def fetch(image):
        return pltpu.make_async_copy(
            cotangent.at[first + image],
            cot.at[pl.ds(pl.multiple_of(image * kept, kept), kept), :],
            cot_sem.at[image],
        )

    for image in range(images):
        fetch(image).start()
    meet(column_peers(depth))
    own_copy.wait()
    gather = Gather(normed, share, depth, pieces, gather_send, gather_recv)
    reduce = Reduce(terms, landing, share, depth, pieces, send, recv)
    mlp_reduce = Reduce(mlp_terms, mlp_landing, share, depth, pieces, mlp_send, mlp_recv)
    gather.open()
    up_bias_grad[...] = jnp.zeros_like(up_bias_grad)
    down_bias_grad[...] = jnp.zeros_like(down_bias_grad)

    def one(image):
        fetch(image).wait()
        rows = pl.ds(pl.multiple_of(image * kept, kept), kept)
        live = lax.broadcasted_iota(jnp.int32, (kept, 1), 0) < count[first + image]
        grad = jnp.where(live, cot[rows, :].astype(F32), 0.0)
        grad = (mod[first + image, 5:6, :] * grad).astype(LOW)
        grad_mlp[rows, :] = grad
        down_bias_grad[...] += jnp.sum(grad.astype(F32), axis=0, keepdims=True)
        source = normed[rows, :]
        mlp = None
        back = None
        for shard, (weight_up, bias, weight_down) in enumerate(
            ((up_own, up_bias_own, down_own), (up_other, up_bias_other, down_other))
        ):
            pre = dot(source, weight_up[...]) + bias[...].astype(F32)
            square = pre * pre
            bent = jnp.tanh(GELU_ROOT * pre * (1.0 + GELU_CUBE * square))
            half = 0.5 * (1.0 + bent)
            low_hidden = (pre * half).astype(LOW)
            hidden[shard, rows, :] = low_hidden
            slope = half + 0.5 * pre * (1.0 - bent * bent) * (
                GELU_ROOT * (1.0 + 3.0 * GELU_CUBE * square)
            )
            low_grad = (slope * dot_nt(grad, weight_down[...])).astype(LOW)
            grad_pre[shard, rows, :] = low_grad
            up_bias_grad[shard : shard + 1, :] += jnp.sum(
                low_grad.astype(F32), axis=0, keepdims=True
            )
            mlp_part = dot(low_hidden, weight_down[...])
            back_part = dot_nt(low_grad, weight_up[...])
            mlp = mlp_part if mlp is None else mlp + mlp_part
            back = back_part if back is None else back + back_part
        terms[rows, :] = back.astype(LOW)
        mlp_terms[rows, :] = mlp.astype(LOW)
        for part in range(fold):
            reduce.ready(image * fold + part)

    if fold == 1:

        def turn_of(turn, carry):
            one(gather.take(turn))
            return carry

        lax.fori_loop(0, depth, turn_of, 0)
    else:

        def take_of(turn, carry):
            gather.take(turn)
            return carry

        def image_of(image, carry):
            one(image)
            return carry

        lax.fori_loop(0, depth, take_of, 0)
        lax.fori_loop(0, images, image_of, 0)
    for owner in range(depth):
        mlp_reduce.ready(owner)
    for turn in range(depth - 1):
        for part in range(pieces):
            reduce.relay(near_first(turn, up, depth), part)
    for shard in range(PAIR):

        def tile(step, carry):
            columns = pl.ds(pl.multiple_of(step * 128, 128), 128)
            up_grad[shard, columns, :] = dot_tn(
                normed[:, columns], grad_pre[shard]
            ).astype(LOW)
            down_grad[shard, :, columns] = dot_tn(hidden[shard], grad_mlp[:, columns]).astype(LOW)
            return carry

        lax.fori_loop(0, width // 128, tile, 0)
    reduce.finish(total)
    for turn in range(depth - 1):
        for part in range(pieces):
            mlp_reduce.relay(far_first(turn, up, depth), part)
    image = first + (up * share) // kept
    place_in = (up * share) % kept
    live = (
        lax.broadcasted_iota(jnp.int32, (share, 1), 0) + place_in < count[image]
    )
    grad_out = jnp.where(live, cot[own_rows, :].astype(F32), 0.0)
    norm, spread = norm_parts(mid[...])
    back = total[...]
    grad_mid = grad_out + norm_back(norm, spread, back * (1.0 + mod[image, 4:5, :]))
    grad_mid_out[...] = grad_mid
    grad_branch_out[...] = (mod[image, 2:3, :] * grad_mid).astype(LOW)
    sums_out[0:1, :] = jnp.sum(grad_mid * branch[...], axis=0, keepdims=True)
    sums_out[1:2, :] = jnp.sum(back, axis=0, keepdims=True)
    sums_out[2:3, :] = jnp.sum(back * norm, axis=0, keepdims=True)
    mlp_reduce.finish(mlp_total)
    mlp = mlp_total[...] + down_bias[...].astype(F32)
    sums_out[3:4, :] = jnp.sum(grad_out * mlp, axis=0, keepdims=True)
    block_own[...] = jnp.where(live, mid[...] + mod[image, 5:6, :] * mlp, 0.0).astype(LOW)
    gather.close()
    reduce.close()
    mlp_reduce.close()


def feed(sizes, args):
    depth, images, kept, share, pieces = sizes
    width = args[1].shape[1]
    units = args[4].shape[1]
    rows = images * kept
    shape = jax.ShapeDtypeStruct
    return pl.pallas_call(
        functools.partial(feed_kernel, sizes),
        out_shape=(
            shape((PAIR, width, units), LOW),
            shape((PAIR, units, width), LOW),
            shape((PAIR, units), F32),
            shape((1, width), F32),
            shape((share, width), LOW),
            shape((share, width), F32),
            shape((share, width), LOW),
            shape((4, width), F32),
        ),
        in_specs=[SM, VM, HB] + [VM] * 10,
        out_specs=(VM,) * 8,
        scratch_shapes=[
            pltpu.VMEM((rows, width), LOW),
            pltpu.VMEM((rows, width), LOW),
            pltpu.VMEM((PAIR, rows, units), LOW),
            pltpu.VMEM((PAIR, rows, units), LOW),
            pltpu.VMEM((rows, width), LOW),
            pltpu.VMEM((rows, width), LOW),
            pltpu.VMEM((rows + share, width), LOW),
            pltpu.VMEM((rows, width), LOW),
            pltpu.VMEM((rows + share, width), LOW),
            pltpu.VMEM((share, width), F32),
            pltpu.VMEM((share, width), F32),
            DMA((images,)),
            DMA,
            DMA((2, depth, pieces)),
            DMA((2, depth, pieces)),
            DMA((depth, pieces)),
            DMA((depth + 1, pieces)),
            DMA((depth, pieces)),
            DMA((depth + 1, pieces)),
        ],
        compiler_params=pltpu.CompilerParams(
            collective_id=2, has_side_effects=True, vmem_limit_bytes=60 << 20
        ),
        name="feed",
    )(*args)


def attend_back_kernel(
    sizes,
    count,
    grad_own,
    normed,
    proj,
    attended,
    qkv_own,
    qkv_other,
    out_own,
    out_other,
    mod,
    tokens_own,
    grad_mid,
    qkv_grad,
    out_grad,
    qv_grad,
    out_bias_grad,
    grad_tokens,
    sums_out,
    grads,
    grad_proj,
    terms,
    landing,
    total,
    own_sem,
    gather_send,
    gather_recv,
    send,
    recv,
):
    depth, images, kept, share, pieces = sizes
    me, up, side = place(depth)
    width = grad_own.shape[1]
    local = out_own.shape[0]
    scale = HD ** (-0.5)
    fold = depth // images
    first = side * images
    own_rows = pl.ds(pl.multiple_of(up * share, share), share)
    own_copy = pltpu.make_async_copy(grad_own, grads.at[own_rows, :], own_sem)
    own_copy.start()
    meet(column_peers(depth))
    own_copy.wait()
    gather = Gather(grads, share, depth, pieces, gather_send, gather_recv)
    reduce = Reduce(terms, landing, share, depth, pieces, send, recv)
    gather.open()
    qv_grad[...] = jnp.zeros_like(qv_grad)
    out_bias_grad[...] = jnp.zeros_like(out_bias_grad)

    def one(image):
        rows = pl.ds(pl.multiple_of(image * kept, kept), kept)
        key_live = lax.broadcasted_iota(jnp.int32, (1, kept), 1) < count[first + image]
        grad = grads[rows, :]
        out_bias_grad[...] += jnp.sum(grad.astype(F32), axis=0, keepdims=True)
        back = None
        for shard, (qkv, out) in enumerate(((qkv_own, out_own), (qkv_other, out_other))):
            grad_att = dot_nt(grad, out[...]).astype(LOW)
            queries = proj[shard, 0, rows, :]
            keys = proj[shard, 1, rows, :]
            values = proj[shard, 2, rows, :]
            grad_q = jnp.zeros((kept, local), F32)
            grad_k = jnp.zeros((kept, local), F32)
            grad_v = jnp.zeros((kept, local), F32)
            for head in range(local // HD):
                mask = head_mask(head, local)
                head_q = jnp.where(mask, queries, 0.0).astype(LOW)
                head_grad = jnp.where(mask, grad_att, 0.0).astype(LOW)
                weights = softmax_rows(head_q, keys, key_live, scale)
                grad_weights = dot_nt(head_grad, values)
                inner = jnp.sum(weights * grad_weights, axis=-1, keepdims=True)
                grad_scores = (weights * (grad_weights - inner)).astype(LOW)
                grad_v = grad_v + dot_tn(weights.astype(LOW), head_grad)
                grad_q = grad_q + dot(grad_scores, jnp.where(mask, keys, 0.0).astype(LOW))
                grad_k = grad_k + dot_tn(grad_scores, head_q)
            for member, value in enumerate((grad_q * scale, grad_k * scale, grad_v)):
                low = value.astype(LOW)
                grad_proj[shard, member, rows, :] = low
                part = dot_nt(low, qkv[member])
                back = part if back is None else back + part
                if member != 1:
                    row = 2 * shard + member // 2
                    qv_grad[row : row + 1, :] += jnp.sum(low.astype(F32), axis=0, keepdims=True)
        terms[rows, :] = back.astype(LOW)
        for part in range(fold):
            reduce.ready(image * fold + part)

    if fold == 1:

        def turn_of(turn, carry):
            one(gather.take(turn))
            return carry

        lax.fori_loop(0, depth, turn_of, 0)
    else:

        def take_of(turn, carry):
            gather.take(turn)
            return carry

        def image_of(image, carry):
            one(image)
            return carry

        lax.fori_loop(0, depth, take_of, 0)
        lax.fori_loop(0, images, image_of, 0)
    for turn in range(depth - 1):
        for part in range(pieces):
            reduce.relay(near_first(turn, up, depth), part)
    for shard in range(PAIR):

        def tile(step, carry):
            columns = pl.ds(pl.multiple_of(step * 128, 128), 128)
            source = normed[:, columns]
            for member in range(3):
                qkv_grad[shard, member, columns, :] = dot_tn(
                    source, grad_proj[shard, member]
                ).astype(LOW)
            out_grad[shard, :, columns] = dot_tn(attended[shard], grads[:, columns]).astype(LOW)
            return carry

        lax.fori_loop(0, width // 128, tile, 0)
    reduce.finish(total)
    image = first + (up * share) // kept
    live = (
        lax.broadcasted_iota(jnp.int32, (share, 1), 0) + (up * share) % kept < count[image]
    )
    norm, spread = norm_parts(tokens_own[...].astype(F32))
    back = total[...]
    grad = grad_mid[...] + norm_back(norm, spread, back * (1.0 + mod[image, 1:2, :]))
    grad_tokens[...] = jnp.where(live, grad, 0.0).astype(LOW)
    sums_out[0:1, :] = jnp.sum(back, axis=0, keepdims=True)
    sums_out[1:2, :] = jnp.sum(back * norm, axis=0, keepdims=True)
    gather.close()
    reduce.close()


def attend_back(sizes, args):
    depth, images, kept, share, pieces = sizes
    width = args[1].shape[1]
    local = args[7].shape[0]
    rows = images * kept
    shape = jax.ShapeDtypeStruct
    return pl.pallas_call(
        functools.partial(attend_back_kernel, sizes),
        out_shape=(
            shape((PAIR, 3, width, local), LOW),
            shape((PAIR, local, width), LOW),
            shape((2 * PAIR, local), F32),
            shape((1, width), F32),
            shape((share, width), LOW),
            shape((2, width), F32),
        ),
        in_specs=[SM] + [VM] * 11,
        out_specs=(VM,) * 6,
        scratch_shapes=[
            pltpu.VMEM((rows, width), LOW),
            pltpu.VMEM((PAIR, 3, rows, local), LOW),
            pltpu.VMEM((rows, width), LOW),
            pltpu.VMEM((rows + share, width), LOW),
            pltpu.VMEM((share, width), F32),
            DMA,
            DMA((2, depth, pieces)),
            DMA((2, depth, pieces)),
            DMA((depth, pieces)),
            DMA((depth + 1, pieces)),
        ],
        compiler_params=pltpu.CompilerParams(
            collective_id=3, has_side_effects=True, vmem_limit_bytes=60 << 20
        ),
        name="attend_back",
    )(*args)


def spread_kernel(sizes, own, whole, own_sem, send, recv, side_send, side_recv):
    depth, share, pieces = sizes
    me, up, side = place(depth)
    half = depth * share
    rows = share // pieces

    def column(index):
        return side * half + index * share

    own_copy = pltpu.make_async_copy(
        own, whole.at[pl.ds(pl.multiple_of(column(up), share), share), :], own_sem
    )
    own_copy.start()
    meet(column_peers(depth) + [up * PAIR + 1 - side])
    own_copy.wait()
    here = whole.at[pl.ds(pl.multiple_of(side * half, share), half), :]
    gather = Gather(here, share, depth, pieces, send, recv)

    def across(index, part):
        view = whole.at[pl.ds(pl.multiple_of(column(index) + part * rows, rows), rows), :]
        return remote(
            view,
            view,
            side_send.at[index, part],
            side_recv.at[index, part],
            up * PAIR + 1 - side,
        )

    gather.open()
    for part in range(pieces):
        across(up, part).start()
    for turn in range(1, depth):
        source = gather.take(turn)
        for part in range(pieces):
            across(source, part).start()
    gather.close()
    for index in range(depth):
        for part in range(pieces):
            start = (1 - side) * half + index * share + part * rows
            view = whole.at[pl.ds(pl.multiple_of(start, rows), rows), :]
            remote(
                view, view, side_send.at[index, part], side_recv.at[index, part], me
            ).wait_recv()
            across(index, part).wait_send()


def spread(own, sizes, ident):
    depth, share, pieces = sizes
    width = own.shape[1]
    return pl.pallas_call(
        functools.partial(spread_kernel, sizes),
        out_shape=jax.ShapeDtypeStruct((PAIR * depth * share, width), own.dtype),
        in_specs=[VM],
        out_specs=VM,
        scratch_shapes=[
            DMA,
            DMA((2, depth, pieces)),
            DMA((2, depth, pieces)),
            DMA((depth, pieces)),
            DMA((depth, pieces)),
        ],
        compiler_params=pltpu.CompilerParams(collective_id=ident, has_side_effects=True),
        name="spread",
    )(own)


def scatter_kernel(index, grads, out):
    spots, kept = out.shape[0], grads.shape[0]
    rows = lax.broadcasted_iota(jnp.int32, (spots, kept), 0)
    pick = jnp.where(rows == index[...], 1.0, 0.0).astype(LOW)
    out[...] = dot(pick, grads[...]).astype(LOW)


def scatter(index, grads, spots):
    images, kept, width = grads.shape
    return pl.pallas_call(
        scatter_kernel,
        out_shape=jax.ShapeDtypeStruct((images, spots, width), LOW),
        grid=(images,),
        in_specs=[
            pl.BlockSpec((None, 1, kept), lambda image: (image, 0, 0)),
            pl.BlockSpec((None, kept, width), lambda image: (image, 0, 0)),
        ],
        out_specs=pl.BlockSpec((None, spots, width), lambda image: (image, 0, 0)),
        name="scatter",
    )(index, grads)


def on_device(
    patches,
    conditioning,
    keep_count,
    keep_index,
    mod_weight,
    mod_bias,
    qkv_weight,
    qv_bias,
    out_weight,
    out_bias,
    up_weight,
    up_bias,
    down_weight,
    down_bias,
    out_cotangent,
):
    devices = lax.axis_size("tensor")
    depth = devices // PAIR
    all_images, kept = keep_index.shape
    width = patches.shape[2]
    images = all_images // PAIR
    share = images * kept // depth
    pieces = 4 if share % 64 == 0 else 2
    sizes = (depth, images, kept, share, pieces)
    me = lax.axis_index("tensor")
    swap = [(member, member ^ 1) for member in range(devices)]

    def other(value):
        return lax.ppermute(value, "tensor", swap)

    qkv_other, qv_other, out_other = other(qkv_weight), other(qv_bias), other(out_weight)
    up_other, down_other = other(up_weight), other(down_weight)
    up_bias_row = up_bias[None, :]
    up_bias_other = other(up_bias_row)
    gathered, silu_low = modulation(conditioning, mod_weight, mod_bias[None, :], devices)
    mod = (
        gathered.transpose(1, 0, 2).reshape(all_images, 6, width).astype(F32)
    )
    index = keep_index[:, None, :]
    normed_one, proj, attended, tokens_own, mid, branch, normed_two = attend(
        sizes,
        (
            keep_count,
            index,
            patches,
            mod,
            qkv_weight,
            qkv_other,
            qv_bias,
            qv_other,
            out_weight,
            out_other,
            out_bias[None, :],
        ),
    )
    (
        up_grad,
        down_grad,
        up_bias_grad,
        down_bias_grad,
        block_own,
        grad_mid,
        grad_branch,
        sums_two,
    ) = feed(
        sizes,
        (
            keep_count,
            normed_two,
            out_cotangent,
            mod,
            up_weight,
            up_other,
            up_bias_row,
            up_bias_other,
            down_weight,
            down_other,
            down_bias[None, :],
            mid,
            branch,
        ),
    )
    qkv_grad, out_grad, qv_grad, out_bias_grad, grad_tokens, sums_one = attend_back(
        sizes,
        (
            keep_count,
            grad_branch,
            normed_one,
            proj,
            attended,
            qkv_weight,
            qkv_other,
            out_weight,
            out_other,
            mod,
            tokens_own,
            grad_mid,
        ),
    )
    block_out = spread(block_own, (depth, share, pieces), 4).reshape(all_images, kept, width)
    token_grads = spread(grad_tokens, (depth, share, pieces), 5).reshape(all_images, kept, width)
    grad_patches = scatter(index, token_grads, patches.shape[1])

    own_mod = jnp.concatenate(
        [sums_one[0], sums_one[1], sums_two[0], sums_two[1], sums_two[2], sums_two[3]]
    )
    columns = mod_weight.shape[1]
    every_mod = lax.all_gather(own_mod, ("dp", "tensor"))
    mine = lax.dynamic_slice_in_dim(every_mod, me * columns, columns, 1)
    groups = lax.axis_size("dp")
    holder = jnp.arange(devices)
    image_of = (holder % PAIR) * images + (holder // PAIR) * share // kept
    chosen = (image_of[None, :] == jnp.arange(all_images)[:, None]).astype(F32)
    per_image = jnp.einsum(
        "id,gdm->gim",
        chosen,
        mine.reshape(groups, devices, columns),
        precision=lax.Precision.HIGHEST,
    )
    silu_all = lax.all_gather(silu_low, "dp").astype(F32)
    mod_weight_grad = jnp.einsum(
        "gid,gim->dm", silu_all, per_image, precision=lax.Precision.HIGHEST
    )
    mod_bias_grad = jnp.sum(per_image, axis=(0, 1))
    here = lax.dynamic_index_in_dim(per_image, lax.axis_index("dp"), 0, keepdims=False)
    silu_term = jnp.einsum(
        "bm,dm->bd", here, mod_weight.astype(F32), precision=lax.Precision.HIGHEST
    )
    cond_float = conditioning.astype(F32)
    grad_silu = lax.psum(silu_term, "tensor")
    silu_pull = jax.vjp(jax.nn.silu, cond_float)[1]
    grad_conditioning = silu_pull(grad_silu)[0].astype(LOW)

    def total(both):
        pair = both[0].astype(F32) + other(both[1]).astype(F32)
        return lax.psum(pair.astype(LOW), "dp").astype(F32)

    qv_pair = qv_grad.reshape(PAIR, 2, qv_grad.shape[1])
    whole_bias = jnp.concatenate([down_bias_grad, out_bias_grad])
    return (
        block_out,
        grad_patches,
        grad_conditioning,
        mod_weight_grad,
        mod_bias_grad,
        total(qkv_grad),
        total(qv_pair.astype(LOW)),
        total(out_grad),
        total(jnp.stack([out_bias_grad[0], out_bias_grad[0]]).astype(LOW)),
        total(up_grad),
        total(up_bias_grad.astype(LOW)),
        total(down_grad),
        total(jnp.stack([down_bias_grad[0], down_bias_grad[0]]).astype(LOW)),
    )


def solution(mesh):
    placed = (
        P("dp", None, None),
        P("dp", None),
        P("dp"),
        P("dp", None),
        P(None, "tensor"),
        P("tensor"),
        P(None, None, "tensor"),
        P(None, "tensor"),
        P("tensor", None),
        P(),
        P(None, "tensor"),
        P("tensor"),
        P("tensor", None),
        P(),
        P("dp", None, None),
    )
    return jax.shard_map(
        on_device,
        mesh=mesh,
        in_specs=placed,
        out_specs=(
            P("dp", None, None),
            P("dp", None, None),
            P("dp", None),
            P(None, "tensor"),
            P("tensor"),
            P(None, None, "tensor"),
            P(None, "tensor"),
            P("tensor", None),
            P(),
            P(None, "tensor"),
            P("tensor"),
            P("tensor", None),
            P(),
        ),
        check_vma=False,
    )
```

```python
import functools

import jax
import jax.numpy as jnp
from jax import lax
from jax.experimental import pallas as pl
from jax.experimental.pallas import tpu as pltpu
from jax.sharding import PartitionSpec as P

HD = 72
MESH = pl.DeviceIdType.MESH
F32 = jnp.float32
LOW = jnp.bfloat16
DMA = pltpu.SemaphoreType.DMA
VM = pl.BlockSpec(memory_space=pltpu.VMEM)
SM = pl.BlockSpec(memory_space=pltpu.SMEM)
HB = pl.BlockSpec(memory_space=pl.ANY)
PAIR = 2
GELU_ROOT = 0.7978845608028654
GELU_CUBE = 0.044715


def remote(source, target, send_sem, recv_sem, device, group=None):
    there = {"tensor": device} if group is None else {"dp": group, "tensor": device}
    return pltpu.make_async_remote_copy(
        src_ref=source,
        dst_ref=target,
        send_sem=send_sem,
        recv_sem=recv_sem,
        device_id=there,
        device_id_type=MESH,
    )


def place(depth):
    me = lax.axis_index("tensor")
    return me, me // PAIR, me % PAIR


def meet(peers):
    barrier = pltpu.get_barrier_semaphore()
    for group, peer in peers:
        pl.semaphore_signal(
            barrier, inc=1, device_id={"dp": group, "tensor": peer}, device_id_type=MESH
        )
    pl.semaphore_wait(barrier, len(peers))


def column_peers(depth):
    me, up, side = place(depth)
    group = lax.axis_index("dp")
    return [(group, ((up + step) % depth) * PAIR + side) for step in range(1, depth)]


def cube_peers(groups):
    me = lax.axis_index("tensor")
    group = lax.axis_index("dp")
    peers = [((group + step) % groups, me) for step in range(1, groups)]
    return peers + [((group + step) % groups, me + 1 - 2 * (me % PAIR)) for step in range(groups)]


def dot(left, right):
    return jnp.dot(left, right, preferred_element_type=F32)


def dot_nt(left, right):
    return lax.dot_general(left, right, (((1,), (1,)), ((), ())), preferred_element_type=F32)


def dot_tn(left, right):
    return lax.dot_general(left, right, (((0,), (0,)), ((), ())), preferred_element_type=F32)


def norm_parts(rows):
    width = rows.shape[-1]
    centred = rows - jnp.sum(rows, axis=-1, keepdims=True) * (1.0 / width)
    spread = lax.rsqrt(jnp.sum(centred * centred, axis=-1, keepdims=True) * (1.0 / width) + 1e-06)
    return centred * spread, spread


def norm_back(norm, spread, grad):
    width = norm.shape[-1]
    mean_grad = jnp.sum(grad, axis=-1, keepdims=True) * (1.0 / width)
    mean_both = jnp.sum(grad * norm, axis=-1, keepdims=True) * (1.0 / width)
    return (grad - mean_grad - norm * mean_both) * spread


class Gather:
    def __init__(self, buffer, share, depth, pieces, send, recv):
        self.buffer, self.share, self.depth, self.pieces = buffer, share, depth, pieces
        self.send, self.recv = send, recv
        self.me, self.up, self.side = place(depth)

    def piece(self, index, part):
        rows = self.share // self.pieces
        return self.buffer.at[pl.ds(pl.multiple_of(index * self.share + part * rows, rows), rows), :]

    def copy(self, way, step, part):
        source = self.up - (step - 1) * (1 - 2 * way)
        target = self.up + 1 - 2 * way
        view = self.piece(source, part)
        return remote(
            view,
            view,
            self.send.at[way, step, part],
            self.recv.at[way, step, part],
            target * PAIR + self.side,
        )

    def may_send(self, way, step):
        if way == 0:
            return (self.up + 1 < self.depth) & (self.up >= step - 1)
        return (self.up >= 1) & (self.up + step - 1 < self.depth)

    def open(self):
        for part in range(self.pieces):
            for way in range(2):

                @pl.when(self.may_send(way, 1))
                def _():
                    self.copy(way, 1, part).start()

    def arrival(self, turn):
        below = self.up
        above = self.depth - 1 - self.up
        both = jnp.minimum(below, above)
        mixed = turn <= 2 * both
        way = jnp.where(mixed, (turn + 1) % 2, jnp.where(below > above, 0, 1))
        step = jnp.where(mixed, (turn + 1) // 2, turn - both)
        step = jnp.where(turn == 0, 0, step)
        return way, step, self.up - step * (1 - 2 * way)

    def take(self, turn):
        way, step, source = self.arrival(turn)
        ahead = jnp.where(way == 0, self.up + 1 < self.depth, self.up >= 1)

        @pl.when(turn > 0)
        def _():
            for part in range(self.pieces):
                view = self.piece(source, part)
                remote(
                    view,
                    view,
                    self.send.at[way, step, part],
                    self.recv.at[way, step, part],
                    self.me,
                ).wait_recv()

                @pl.when(ahead)
                def _():
                    self.copy(way, step + 1, part).start()

        return source

    def close(self):
        for way in range(2):
            for step in range(1, self.depth):

                @pl.when(self.may_send(way, step))
                def _():
                    for part in range(self.pieces):
                        self.copy(way, step, part).wait_send()


class Reduce:
    def __init__(self, terms, landing, share, depth, pieces, send, recv):
        self.terms, self.landing, self.share, self.depth, self.pieces = (
            terms,
            landing,
            share,
            depth,
            pieces,
        )
        self.send, self.recv = send, recv
        self.me, self.up, self.side = place(depth)
        self.rows = share // pieces

    def span(self, index, part):
        return pl.ds(pl.multiple_of(index * self.share + part * self.rows, self.rows), self.rows)

    def copy(self, way, owner, part):
        target = self.up + 1 - 2 * way
        slot = owner if way == 0 else jnp.where(owner == target, self.depth, owner)
        return remote(
            self.terms.at[self.span(owner, part), :],
            self.landing.at[self.span(slot, part), :],
            self.send.at[owner, part],
            self.recv.at[slot, part],
            target * PAIR + self.side,
        )

    def landed(self, slot, part):
        view = self.landing.at[self.span(slot, part), :]
        remote(view, view, self.send.at[0, part], self.recv.at[slot, part], self.me).wait_recv()

    def ready(self, owner):
        @pl.when((self.up == 0) & (owner > 0))
        def _():
            for part in range(self.pieces):
                self.copy(0, owner, part).start()

        @pl.when((self.up == self.depth - 1) & (owner < self.depth - 1))
        def _():
            for part in range(self.pieces):
                self.copy(1, owner, part).start()

    def add(self, target, target_start, term_start, starts):
        def body(index, carry):
            offset = index * 16
            value = self.terms[
                pl.ds(pl.multiple_of(term_start + offset, 16), 16), :
            ].astype(F32)
            for start in starts:
                value = value + self.landing[
                    pl.ds(pl.multiple_of(start + offset, 16), 16), :
                ].astype(F32)
            target[pl.ds(pl.multiple_of(target_start + offset, 16), 16), :] = value.astype(
                target.dtype
            )
            return carry

        lax.fori_loop(0, self.rows // 16, body, 0)

    def relay(self, owner, part):
        start = owner * self.share + part * self.rows

        def pass_on(way):
            self.landed(owner, part)
            self.add(self.terms, start, start, [start])
            self.copy(way, owner, part).start()

        @pl.when((owner > self.up) & (self.up > 0))
        def _():
            pass_on(0)

        @pl.when((owner < self.up) & (self.up < self.depth - 1))
        def _():
            pass_on(1)

    def finish(self, total):
        start = self.up * self.share
        end = self.depth * self.share
        for part in range(self.pieces):
            skip = part * self.rows

            @pl.when(self.up == 0)
            def _():
                self.landed(self.depth, part)
                self.add(total, skip, start + skip, [end + skip])

            @pl.when(self.up == self.depth - 1)
            def _():
                self.landed(self.up, part)
                self.add(total, skip, start + skip, [start + skip])

            @pl.when((self.up > 0) & (self.up < self.depth - 1))
            def _():
                self.landed(self.up, part)
                self.landed(self.depth, part)
                self.add(total, skip, start + skip, [start + skip, end + skip])

    def close(self):
        for owner in range(self.depth):

            @pl.when(self.up != owner)
            def _():
                for part in range(self.pieces):
                    remote(
                        self.terms.at[self.span(owner, part), :],
                        self.landing.at[self.span(owner, part), :],
                        self.send.at[owner, part],
                        self.recv.at[owner, part],
                        self.me,
                    ).wait_send()


class Fold:
    def __init__(self, source, scratch, out, groups, split):
        self.source, self.out, self.groups, self.split = source, out, groups, split
        self.stage, self.near, self.side_land, self.far, self.low, self.send, self.recv = scratch
        self.me = lax.axis_index("tensor")
        self.group = lax.axis_index("dp")
        self.core = self.group % PAIR
        self.line = self.group // PAIR
        self.mate = self.group + 1 - 2 * self.core
        self.partner = self.me + 1 - 2 * (self.me % PAIR)
        self.lines = groups // PAIR
        self.rows = self.stage.shape[1]
        self.start = self.core * self.rows if split else 0

    @staticmethod
    def scratch(shape, groups, split):
        _, rows, width = shape
        half = rows // 2 if split else rows
        lines = groups // PAIR
        return [
            pltpu.VMEM((PAIR, half, width), LOW),
            pltpu.VMEM((PAIR, half, width), LOW),
            pltpu.VMEM((half, width), LOW),
            pltpu.VMEM((lines, half, width), LOW),
            pltpu.VMEM((rows, width), LOW),
            DMA((3 + lines,)),
            DMA((3 + lines,)),
        ]

    def each(self, body):
        step = 48 if self.rows % 48 == 0 else self.rows

        def run(index, carry):
            body(pl.multiple_of(index * step, step), step)
            return carry

        lax.fori_loop(0, self.rows // step, run, 0)

    def window(self, start, size):
        return pl.ds(pl.multiple_of(start, 16) if self.split else start, size)

    def near_copy(self):
        if self.split:
            away = self.window((1 - self.core) * self.rows, self.rows)
            source = self.source.at[:, away, :]
        else:
            source = self.source
        return remote(
            source, self.near, self.send.at[0], self.recv.at[0], self.me, self.mate
        )

    def side_copy(self):
        return remote(
            self.stage.at[1],
            self.side_land,
            self.send.at[1],
            self.recv.at[1],
            self.partner,
            self.group,
        )

    def far_copy(self, step):
        line = (self.line + step) % self.lines
        return remote(
            self.far.at[self.line],
            self.far.at[self.line],
            self.send.at[2 + step],
            self.recv.at[2 + step],
            self.me,
            line * PAIR + self.core,
        )

    def mate_copy(self, core):
        view = self.low.at[self.window(core * self.rows, self.rows), :]
        return remote(view, view, self.send.at[2], self.recv.at[2], self.me, self.mate)

    def one(self):
        self.near_copy().start()

    def two(self):
        self.near_copy().wait_recv()

        def add(at, size):
            for shard in range(PAIR):
                mine = self.source[shard, self.window(self.start + at, size), :].astype(F32)
                rows = self.window(at, size)
                self.stage[shard, rows, :] = (
                    mine + self.near[shard, rows, :].astype(F32)
                ).astype(LOW)

        self.each(add)
        self.side_copy().start()

    def three(self):
        self.side_copy().wait_recv()

        def add(at, size):
            rows = self.window(at, size)
            self.far[self.line, rows, :] = (
                self.stage[0, rows, :].astype(F32) + self.side_land[rows, :].astype(F32)
            ).astype(LOW)

        self.each(add)
        for step in range(1, self.lines):
            self.far_copy(step).start()

    def four(self):
        for step in range(1, self.lines):
            line = (self.line + self.lines - step) % self.lines
            view = self.far.at[line]
            remote(
                view, view, self.send.at[2 + step], self.recv.at[2 + step], self.me, self.mate
            ).wait_recv()

        def add(at, size):
            rows = self.window(at, size)
            value = self.far[0, rows, :].astype(F32)
            for line in range(1, self.lines):
                value = value + self.far[line, rows, :].astype(F32)
            low = value.astype(LOW)
            spot = self.window(self.start + at, size)
            self.low[spot, :] = low
            self.out[spot, :] = low.astype(F32)

        self.each(add)
        if self.split:
            self.mate_copy(self.core).start()

    def five(self):
        if self.split:
            self.mate_copy(1 - self.core).wait_recv()

            def put(at, size):
                spot = self.window((1 - self.core) * self.rows + at, size)
                self.out[spot, :] = self.low[spot, :].astype(F32)

            self.each(put)
            self.mate_copy(self.core).wait_send()
        self.near_copy().wait_send()
        self.side_copy().wait_send()
        for step in range(1, self.lines):
            self.far_copy(step).wait_send()


class Spread:
    def __init__(self, whole, share, depth, pieces, scratch):
        self.whole, self.share, self.depth, self.pieces = whole, share, depth, pieces
        send, recv, self.side_send, self.side_recv = scratch
        self.me, self.up, self.side = place(depth)
        self.half = depth * share
        here = whole.at[pl.ds(pl.multiple_of(self.side * self.half, share), self.half), :]
        self.gather = Gather(here, share, depth, pieces, send, recv)

    @staticmethod
    def scratch(depth, pieces):
        return [
            DMA((2, depth, pieces)),
            DMA((2, depth, pieces)),
            DMA((depth, pieces)),
            DMA((depth, pieces)),
        ]

    def view(self, side, index, part):
        rows = self.share // self.pieces
        start = side * self.half + index * self.share + part * rows
        return self.whole.at[pl.ds(pl.multiple_of(start, rows), rows), :]

    def own(self):
        start = self.side * self.half + self.up * self.share
        return self.whole.at[pl.ds(pl.multiple_of(start, self.share), self.share), :]

    def across(self, index, part):
        view = self.view(self.side, index, part)
        return remote(
            view,
            view,
            self.side_send.at[index, part],
            self.side_recv.at[index, part],
            self.me + 1 - 2 * self.side,
        )

    def open(self):
        self.gather.open()
        for part in range(self.pieces):
            self.across(self.up, part).start()

    def take(self, turn):
        source = self.gather.take(turn)
        for part in range(self.pieces):
            self.across(source, part).start()

    def crossed(self, index):
        for part in range(self.pieces):
            view = self.view(1 - self.side, index, part)
            remote(
                view, view, self.side_send.at[index, part], self.side_recv.at[index, part], self.me
            ).wait_recv()

    def close(self):
        self.gather.close()
        for index in range(self.depth):
            for part in range(self.pieces):
                self.across(index, part).wait_send()


def far_first(turn, group, count):
    low = group < count // 2
    own = jnp.where(low, count - 1 - group, group)
    moved = jnp.where(turn >= own, turn + 1, turn)
    other = jnp.where(low, count - 1 - moved, moved)
    return jnp.where(turn == count - 1, group, other)


def near_first(turn, up, depth):
    low = up < depth // 2
    ahead = jnp.where(turn < depth - 1 - up, up + 1 + turn, depth - 2 - turn)
    behind = jnp.where(turn < up, up - 1 - turn, turn + 1)
    return jnp.where(low, ahead, behind)


def head_mask(head, width):
    lane = lax.broadcasted_iota(jnp.int32, (1, width), 1)
    return (lane >= head * HD) & (lane < (head + 1) * HD)


def softmax_rows(queries, keys, key_live, scale):
    scores = dot_nt(queries, keys) * scale
    scores = jnp.where(key_live, scores, -1e30)
    top = jnp.max(scores, axis=-1, keepdims=True)
    raised = jnp.exp(scores - top)
    return raised / jnp.sum(raised, axis=-1, keepdims=True)


def attend_shard(normed, qkv, qv, proj_out, shard, rows, key_live, scale):
    local = qkv.shape[2]
    queries = (dot(normed, qkv[0]) + qv[0:1, :].astype(F32)).astype(LOW)
    keys = dot(normed, qkv[1]).astype(LOW)
    values = (dot(normed, qkv[2]) + qv[1:2, :].astype(F32)).astype(LOW)
    proj_out[shard, 0, rows, :] = queries
    proj_out[shard, 1, rows, :] = keys
    proj_out[shard, 2, rows, :] = values
    attended = jnp.zeros((normed.shape[0], local), F32)
    for head in range(local // HD):
        mask = head_mask(head, local)
        weights = softmax_rows(jnp.where(mask, queries, 0.0).astype(LOW), keys, key_live, scale)
        attended = attended + dot(weights.astype(LOW), jnp.where(mask, values, 0.0).astype(LOW))
    return attended.astype(LOW)


def attend_kernel(
    sizes,
    groups,
    count,
    index,
    patches,
    cond,
    mod_weight,
    mod_bias,
    qkv_own,
    qv_own,
    out_own,
    out_bias,
    up_own,
    down_own,
    up_bias_own,
    normed_out,
    proj_out,
    attended_out,
    tokens_own,
    mid_out,
    branch_out,
    normed_two_out,
    mod,
    silu_all,
    qkv_other,
    qv_other,
    out_other,
    up_other,
    down_other,
    up_bias_other,
    patch_rows,
    tokens,
    terms,
    landing,
    total,
    mod_mine,
    mod_gathered,
    patch_sem,
    send,
    recv,
    mod_send,
    mod_recv,
    silu_send,
    silu_recv,
    weight_send,
    weight_recv,
    mate_send,
    mate_recv,
):
    depth, images, kept, share, pieces = sizes
    devices = depth * PAIR
    me, up, side = place(depth)
    group = lax.axis_index("dp")
    core = group % PAIR
    mate = group + 1 - 2 * core
    partner = me + 1 - 2 * side
    width = patches.shape[2]
    scale = HD ** (-0.5)
    fold = depth // images
    first = side * images

    def fetch(image):
        return pltpu.make_async_copy(
            patches.at[first + image], patch_rows.at[image], patch_sem.at[image]
        )

    for turn in range(images):
        fetch(far_first(turn, up // fold, images)).start()
    meet(
        [(group, (me + step) % devices) for step in range(1, devices)]
        + [((group + step) % groups, me) for step in range(1, groups)]
    )
    value = cond[...].astype(F32)
    silu = (value / (1.0 + jnp.exp(-value))).astype(LOW)
    silu_all[group] = silu
    local_mod = (dot(silu, mod_weight[...]) + mod_bias[...].astype(F32)).astype(LOW)
    mod_mine[...] = local_mod
    mod_gathered[me] = local_mod
    mod_copies = [
        remote(
            mod_mine,
            mod_gathered.at[me],
            mod_send.at[step],
            mod_recv.at[step],
            (me + step) % devices,
        )
        for step in range(1, devices)
    ]
    silu_copies = [
        remote(
            silu_all.at[group],
            silu_all.at[group],
            silu_send.at[step],
            silu_recv.at[step],
            me,
            (group + step) % groups,
        )
        for step in range(1, groups)
    ]
    for copy in mod_copies + silu_copies:
        copy.start()

    def part_of(array, which):
        if len(array.shape) == 3:
            rows = array.shape[1] // 2
            return array.at[:, pl.ds(pl.multiple_of(which * rows, 16), rows), :]
        rows = array.shape[0] // 2
        return array.at[pl.ds(pl.multiple_of(which * rows, 16), rows), :]

    halved = [(qkv_own, qkv_other), (up_own, up_other), (down_own, down_other)]
    full = [(qv_own, qv_other), (out_own, out_other), (up_bias_own, up_bias_other)]

    def half_copy(which):
        source, target = halved[which]
        return remote(
            part_of(source, core),
            part_of(target, core),
            weight_send.at[which],
            weight_recv.at[which],
            partner,
        )

    def full_copy(which):
        source, target = full[which]
        return remote(
            source,
            target,
            weight_send.at[3 + which],
            weight_recv.at[3 + which],
            partner,
        )

    def mate_copy(which, half):
        view = part_of(halved[which][1], half)
        return remote(view, view, mate_send.at[which], mate_recv.at[which], me, mate)

    full_copy(0).start()
    half_copy(0).start()
    full_copy(1).start()
    full_copy(2).start()
    half_copy(1).start()
    half_copy(2).start()
    reduce = Reduce(terms, landing, share, depth, pieces, send, recv)

    def pick_rows(turn, carry):
        image = far_first(turn, up // fold, images)
        fetch(image).wait()
        rows = pl.ds(pl.multiple_of(image * kept, kept), kept)
        spots = lax.broadcasted_iota(jnp.int32, (patches.shape[1], kept), 0)
        slots = lax.broadcasted_iota(jnp.int32, (patches.shape[1], kept), 1)
        pick = jnp.where(
            (spots == index[first + image]) & (slots < count[first + image]), 1.0, 0.0
        )
        tokens[rows, :] = dot_tn(pick.astype(LOW), patch_rows[image]).astype(LOW)
        return carry

    lax.fori_loop(0, images, pick_rows, 0)
    for step in range(1, devices):
        source = (me + devices - step) % devices
        remote(
            mod_mine, mod_gathered.at[source], mod_send.at[step], mod_recv.at[step], me
        ).wait_recv()
    mod[...] = jnp.concatenate(
        [mod_gathered[device].astype(F32) for device in range(devices)], axis=-1
    )

    def block(image, member):
        return mod[pl.ds(first + image, 1), member * width : (member + 1) * width]

    def one(turn, carry):
        image = far_first(turn, up // fold, images)
        rows = pl.ds(pl.multiple_of(image * kept, kept), kept)

        @pl.when(turn == images - 1)
        def _():
            half_copy(0).wait_recv()
            mate_copy(0, core).start()

        norm, _ = norm_parts(tokens[rows, :].astype(F32))
        normed = (norm * (1.0 + block(image, 1)) + block(image, 0)).astype(LOW)
        normed_out[rows, :] = normed
        key_live = lax.broadcasted_iota(jnp.int32, (1, kept), 1) < count[first + image]
        attended_out[0, rows, :] = attend_shard(
            normed, qkv_own, qv_own, proj_out, 0, rows, key_live, scale
        )
        return carry

    def two(turn, carry):
        image = far_first(turn, up // fold, images)
        rows = pl.ds(pl.multiple_of(image * kept, kept), kept)
        key_live = lax.broadcasted_iota(jnp.int32, (1, kept), 1) < count[first + image]
        attended = attend_shard(
            normed_out[rows, :], qkv_other, qv_other, proj_out, 1, rows, key_live, scale
        )
        attended_out[1, rows, :] = attended
        branch = dot(attended_out[0, rows, :], out_own[...]) + dot(attended, out_other[...])
        terms[rows, :] = branch.astype(LOW)
        for part in range(fold):
            reduce.ready(image * fold + part)
        return carry

    lax.fori_loop(0, images, one, 0)
    full_copy(0).wait_recv()
    full_copy(1).wait_recv()
    mate_copy(0, 1 - core).wait_recv()
    lax.fori_loop(0, images, two, 0)
    for turn in range(depth - 1):
        for part in range(pieces):
            reduce.relay(far_first(turn, up, depth), part)
        if turn == 0:
            half_copy(1).wait_recv()
            mate_copy(1, core).start()
    half_copy(2).wait_recv()
    mate_copy(2, core).start()
    reduce.finish(total)
    image = (up * share) // kept
    own = tokens[pl.ds(pl.multiple_of(up * share, share), share), :]
    tokens_own[...] = own
    branch = total[...] + out_bias[...].astype(F32)
    branch_out[...] = branch
    mid = own.astype(F32) + block(image, 2) * branch
    mid_out[...] = mid
    norm, _ = norm_parts(mid)
    normed_two_out[...] = (norm * (1.0 + block(image, 4)) + block(image, 3)).astype(LOW)
    reduce.close()
    full_copy(2).wait_recv()
    mate_copy(1, 1 - core).wait_recv()
    mate_copy(2, 1 - core).wait_recv()
    for step in range(1, groups):
        source = (group + groups - step) % groups
        view = silu_all.at[source]
        remote(
            view, view, silu_send.at[step], silu_recv.at[step], me, mate
        ).wait_recv()
    for which in range(3):
        half_copy(which).wait_send()
        full_copy(which).wait_send()
        mate_copy(which, core).wait_send()
    for copy in mod_copies + silu_copies:
        copy.wait_send()


def attend(sizes, groups, args):
    depth, images, kept, share, pieces = sizes
    (count, index, patches, cond, mod_weight, mod_bias, qkv, qv, out, out_bias, up, down, up_bias) = args
    spots, width = patches.shape[1:]
    local = out.shape[0]
    rows = images * kept
    shape = jax.ShapeDtypeStruct
    devices = depth * PAIR
    return pl.pallas_call(
        functools.partial(attend_kernel, sizes, groups),
        out_shape=(
            shape((rows, width), LOW),
            shape((PAIR, 3, rows, local), LOW),
            shape((PAIR, rows, local), LOW),
            shape((share, width), LOW),
            shape((share, width), F32),
            shape((share, width), F32),
            shape((share, width), LOW),
            shape((cond.shape[0], devices * mod_weight.shape[1]), F32),
            shape((groups,) + cond.shape, LOW),
            shape(qkv.shape, LOW),
            shape(qv.shape, LOW),
            shape(out.shape, LOW),
            shape(up.shape, LOW),
            shape(down.shape, LOW),
            shape(up_bias.shape, LOW),
        ),
        in_specs=[SM, VM, HB] + [VM] * 10,
        out_specs=(VM,) * 15,
        scratch_shapes=[
            pltpu.VMEM((images, spots, width), LOW),
            pltpu.VMEM((rows, width), LOW),
            pltpu.VMEM((rows, width), LOW),
            pltpu.VMEM((rows + share, width), LOW),
            pltpu.VMEM((share, width), F32),
            pltpu.VMEM((cond.shape[0], mod_weight.shape[1]), LOW),
            pltpu.VMEM((devices, cond.shape[0], mod_weight.shape[1]), LOW),
            DMA((images,)),
            DMA((depth, pieces)),
            DMA((depth + 1, pieces)),
            DMA((devices,)),
            DMA((devices,)),
            DMA((groups,)),
            DMA((groups,)),
            DMA((6,)),
            DMA((6,)),
            DMA((3,)),
            DMA((3,)),
        ],
        compiler_params=pltpu.CompilerParams(
            collective_id=1, has_side_effects=True, vmem_limit_bytes=60 << 20
        ),
        name="attend",
    )(*args)


def feed_kernel(
    sizes,
    count,
    normed_own,
    cotangent,
    mod,
    up_own,
    up_other,
    up_bias_own,
    up_bias_other,
    down_own,
    down_other,
    down_bias,
    mid,
    branch,
    up_grad,
    down_grad,
    up_bias_grad,
    down_bias_grad,
    block_own,
    grad_mid_out,
    grad_branch_out,
    sums_out,
    normed,
    cot,
    hidden,
    grad_pre,
    grad_mlp,
    terms,
    landing,
    mlp_terms,
    mlp_landing,
    total,
    mlp_total,
    up_sums,
    down_sums,
    cot_sem,
    own_sem,
    gather_send,
    gather_recv,
    send,
    recv,
    mlp_send,
    mlp_recv,
):
    depth, images, kept, share, pieces = sizes
    me, up, side = place(depth)
    width = normed_own.shape[1]
    fold = depth // images
    first = side * images
    own_rows = pl.ds(pl.multiple_of(up * share, share), share)
    own_copy = pltpu.make_async_copy(normed_own, normed.at[own_rows, :], own_sem)
    own_copy.start()

    def fetch(image):
        return pltpu.make_async_copy(
            cotangent.at[first + image],
            cot.at[pl.ds(pl.multiple_of(image * kept, kept), kept), :],
            cot_sem.at[image],
        )

    for image in range(images):
        fetch(image).start()
    meet(column_peers(depth))
    own_copy.wait()
    gather = Gather(normed, share, depth, pieces, gather_send, gather_recv)
    reduce = Reduce(terms, landing, share, depth, pieces, send, recv)
    mlp_reduce = Reduce(mlp_terms, mlp_landing, share, depth, pieces, mlp_send, mlp_recv)
    gather.open()

    def block(image, member):
        return mod[pl.ds(image, 1), member * width : (member + 1) * width]

    def one(image):
        fetch(image).wait()
        rows = pl.ds(pl.multiple_of(image * kept, kept), kept)
        live = lax.broadcasted_iota(jnp.int32, (kept, 1), 0) < count[first + image]
        grad = jnp.where(live, cot[rows, :].astype(F32), 0.0)
        grad = (block(first + image, 5) * grad).astype(LOW)
        grad_mlp[rows, :] = grad
        down_sums[image] = jnp.sum(grad.astype(F32), axis=0, keepdims=True)
        source = normed[rows, :]
        mlp = None
        back = None
        for shard, (weight_up, bias, weight_down) in enumerate(
            ((up_own, up_bias_own, down_own), (up_other, up_bias_other, down_other))
        ):
            pre = dot(source, weight_up[...]) + bias[...].astype(F32)
            square = pre * pre
            bent = jnp.tanh(GELU_ROOT * pre * (1.0 + GELU_CUBE * square))
            half = 0.5 * (1.0 + bent)
            low_hidden = (pre * half).astype(LOW)
            hidden[shard, rows, :] = low_hidden
            slope = half + 0.5 * pre * (1.0 - bent * bent) * (
                GELU_ROOT * (1.0 + 3.0 * GELU_CUBE * square)
            )
            low_grad = (slope * dot_nt(grad, weight_down[...])).astype(LOW)
            grad_pre[shard, rows, :] = low_grad
            up_sums[shard, image] = jnp.sum(low_grad.astype(F32), axis=0, keepdims=True)
            mlp_part = dot(low_hidden, weight_down[...])
            back_part = dot_nt(low_grad, weight_up[...])
            mlp = mlp_part if mlp is None else mlp + mlp_part
            back = back_part if back is None else back + back_part
        terms[rows, :] = back.astype(LOW)
        mlp_terms[rows, :] = mlp.astype(LOW)
        for part in range(fold):
            reduce.ready(image * fold + part)

    if fold == 1:

        def turn_of(turn, carry):
            one(gather.take(turn))
            return carry

        lax.fori_loop(0, depth, turn_of, 0)
    else:

        def take_of(turn, carry):
            gather.take(turn)
            return carry

        def image_of(image, carry):
            one(image)
            return carry

        lax.fori_loop(0, depth, take_of, 0)
        lax.fori_loop(0, images, image_of, 0)
    for owner in range(depth):
        mlp_reduce.ready(owner)
    for turn in range(depth - 1):
        for part in range(pieces):
            reduce.relay(near_first(turn, up, depth), part)
    for shard in range(PAIR):

        def tile(step, carry):
            columns = pl.ds(pl.multiple_of(step * 128, 128), 128)
            up_grad[shard, columns, :] = dot_tn(
                normed[:, columns], grad_pre[shard]
            ).astype(LOW)
            down_grad[shard, :, columns] = dot_tn(hidden[shard], grad_mlp[:, columns]).astype(LOW)
            return carry

        lax.fori_loop(0, width // 128, tile, 0)
    reduce.finish(total)
    for turn in range(depth - 1):
        for part in range(pieces):
            mlp_reduce.relay(far_first(turn, up, depth), part)
    for shard in range(PAIR):
        up_bias_grad[shard : shard + 1, :] = sum(up_sums[shard, image] for image in range(images))
    down_bias_grad[...] = sum(down_sums[image] for image in range(images))
    image = first + (up * share) // kept
    place_in = (up * share) % kept
    live = (
        lax.broadcasted_iota(jnp.int32, (share, 1), 0) + place_in < count[image]
    )
    grad_out = jnp.where(live, cot[own_rows, :].astype(F32), 0.0)
    norm, spread = norm_parts(mid[...])
    back = total[...]
    grad_mid = grad_out + norm_back(norm, spread, back * (1.0 + block(image, 4)))
    grad_mid_out[...] = grad_mid
    grad_branch_out[...] = (block(image, 2) * grad_mid).astype(LOW)
    sums_out[0:1, :] = jnp.sum(grad_mid * branch[...], axis=0, keepdims=True)
    sums_out[1:2, :] = jnp.sum(back, axis=0, keepdims=True)
    sums_out[2:3, :] = jnp.sum(back * norm, axis=0, keepdims=True)
    mlp_reduce.finish(mlp_total)
    mlp = mlp_total[...] + down_bias[...].astype(F32)
    sums_out[3:4, :] = jnp.sum(grad_out * mlp, axis=0, keepdims=True)
    block_own[...] = jnp.where(live, mid[...] + block(image, 5) * mlp, 0.0).astype(LOW)
    gather.close()
    reduce.close()
    mlp_reduce.close()


def feed(sizes, args):
    depth, images, kept, share, pieces = sizes
    width = args[1].shape[1]
    units = args[4].shape[1]
    rows = images * kept
    shape = jax.ShapeDtypeStruct
    return pl.pallas_call(
        functools.partial(feed_kernel, sizes),
        out_shape=(
            shape((PAIR, width, units), LOW),
            shape((PAIR, units, width), LOW),
            shape((PAIR, units), F32),
            shape((1, width), F32),
            shape((share, width), LOW),
            shape((share, width), F32),
            shape((share, width), LOW),
            shape((4, width), F32),
        ),
        in_specs=[SM, VM, HB] + [VM] * 10,
        out_specs=(VM,) * 8,
        scratch_shapes=[
            pltpu.VMEM((rows, width), LOW),
            pltpu.VMEM((rows, width), LOW),
            pltpu.VMEM((PAIR, rows, units), LOW),
            pltpu.VMEM((PAIR, rows, units), LOW),
            pltpu.VMEM((rows, width), LOW),
            pltpu.VMEM((rows, width), LOW),
            pltpu.VMEM((rows + share, width), LOW),
            pltpu.VMEM((rows, width), LOW),
            pltpu.VMEM((rows + share, width), LOW),
            pltpu.VMEM((share, width), F32),
            pltpu.VMEM((share, width), F32),
            pltpu.VMEM((PAIR, images, 1, units), F32),
            pltpu.VMEM((images, 1, width), F32),
            DMA((images,)),
            DMA,
            DMA((2, depth, pieces)),
            DMA((2, depth, pieces)),
            DMA((depth, pieces)),
            DMA((depth + 1, pieces)),
            DMA((depth, pieces)),
            DMA((depth + 1, pieces)),
        ],
        compiler_params=pltpu.CompilerParams(
            collective_id=2, has_side_effects=True, vmem_limit_bytes=60 << 20
        ),
        name="feed",
    )(*args)


def attend_back_kernel(
    sizes,
    groups,
    count,
    grad_own,
    normed,
    proj,
    attended,
    qkv_own,
    qkv_other,
    out_own,
    out_other,
    mod,
    tokens_own,
    grad_mid,
    block_own,
    up_grad,
    down_grad,
    qkv_grad,
    out_grad,
    qv_grad,
    out_bias_grad,
    grad_tokens,
    sums_out,
    block_out,
    up_total,
    down_total,
    grads,
    grad_proj,
    terms,
    landing,
    total,
    qv_sums,
    out_sums,
    own_sem,
    gather_send,
    gather_recv,
    send,
    recv,
    *rest,
):
    depth, images, kept, share, pieces = sizes
    me, up, side = place(depth)
    width = grad_own.shape[1]
    local = out_own.shape[0]
    scale = HD ** (-0.5)
    fold = depth // images
    first = side * images
    up_fold = Fold(up_grad, rest[:7], up_total, groups, True)
    down_fold = Fold(down_grad, rest[7:14], down_total, groups, True)
    spread = Spread(block_out, share, depth, pieces, rest[14:18])
    own_rows = pl.ds(pl.multiple_of(up * share, share), share)
    own_copy = pltpu.make_async_copy(grad_own, grads.at[own_rows, :], own_sem.at[0])
    own_copy.start()
    block_copy = pltpu.make_async_copy(block_own, spread.own(), own_sem.at[1])
    block_copy.start()
    meet(column_peers(depth) + cube_peers(groups))
    own_copy.wait()
    gather = Gather(grads, share, depth, pieces, gather_send, gather_recv)
    reduce = Reduce(terms, landing, share, depth, pieces, send, recv)
    gather.open()
    up_fold.one()
    down_fold.one()
    block_copy.wait()

    def one(image):
        rows = pl.ds(pl.multiple_of(image * kept, kept), kept)
        key_live = lax.broadcasted_iota(jnp.int32, (1, kept), 1) < count[first + image]
        grad = grads[rows, :]
        out_sums[image] = jnp.sum(grad.astype(F32), axis=0, keepdims=True)
        back = None
        for shard, (qkv, out) in enumerate(((qkv_own, out_own), (qkv_other, out_other))):
            grad_att = dot_nt(grad, out[...]).astype(LOW)
            queries = proj[shard, 0, rows, :]
            keys = proj[shard, 1, rows, :]
            values = proj[shard, 2, rows, :]
            grad_q = jnp.zeros((kept, local), F32)
            grad_k = jnp.zeros((kept, local), F32)
            grad_v = jnp.zeros((kept, local), F32)
            for head in range(local // HD):
                mask = head_mask(head, local)
                head_q = jnp.where(mask, queries, 0.0).astype(LOW)
                head_grad = jnp.where(mask, grad_att, 0.0).astype(LOW)
                weights = softmax_rows(head_q, keys, key_live, scale)
                grad_weights = dot_nt(head_grad, values)
                inner = jnp.sum(weights * grad_weights, axis=-1, keepdims=True)
                grad_scores = (weights * (grad_weights - inner)).astype(LOW)
                grad_v = grad_v + dot_tn(weights.astype(LOW), head_grad)
                grad_q = grad_q + dot(grad_scores, jnp.where(mask, keys, 0.0).astype(LOW))
                grad_k = grad_k + dot_tn(grad_scores, head_q)
            for member, value in enumerate((grad_q * scale, grad_k * scale, grad_v)):
                low = value.astype(LOW)
                grad_proj[shard, member, rows, :] = low
                part = dot_nt(low, qkv[member])
                back = part if back is None else back + part
                if member != 1:
                    row = 2 * shard + member // 2
                    qv_sums[row, image] = jnp.sum(low.astype(F32), axis=0, keepdims=True)
        terms[rows, :] = back.astype(LOW)
        for part in range(fold):
            reduce.ready(image * fold + part)

    if fold == 1:

        def turn_of(turn, carry):
            one(gather.take(turn))

            @pl.when(turn == 0)
            def _():
                up_fold.two()
                down_fold.two()
                spread.open()

            @pl.when(turn == 2)
            def _():
                up_fold.three()

            @pl.when(turn >= 2)
            def _():
                spread.take(turn - 1)

            return carry

        lax.fori_loop(0, depth, turn_of, 0)
    else:

        def take_of(turn, carry):
            gather.take(turn)
            return carry

        def image_of(image, carry):
            one(image)
            return carry

        def spread_of(turn, carry):
            spread.take(turn)
            return carry

        lax.fori_loop(0, depth, take_of, 0)
        up_fold.two()
        down_fold.two()
        spread.open()
        lax.fori_loop(0, images, image_of, 0)
        up_fold.three()
        lax.fori_loop(1, depth - 1, spread_of, 0)
    down_fold.three()
    for turn in range(depth - 1):
        for part in range(pieces):
            reduce.relay(near_first(turn, up, depth), part)
    spread.take(depth - 1)
    up_fold.four()
    for shard in range(PAIR):

        def tile(step, carry):
            columns = pl.ds(pl.multiple_of(step * 128, 128), 128)
            source = normed[:, columns]
            for member in range(3):
                start = member * width + step * 128
                qkv_grad[shard, pl.ds(pl.multiple_of(start, 128), 128), :] = dot_tn(
                    source, grad_proj[shard, member]
                ).astype(LOW)
            out_grad[shard, :, columns] = dot_tn(attended[shard], grads[:, columns]).astype(LOW)
            return carry

        lax.fori_loop(0, width // 128, tile, 0)
    down_fold.four()
    reduce.finish(total)
    for row in range(2 * PAIR):
        qv_grad[row : row + 1, :] = sum(qv_sums[row, image] for image in range(images))
    out_bias_grad[...] = sum(out_sums[image] for image in range(images))
    image = first + (up * share) // kept
    live = (
        lax.broadcasted_iota(jnp.int32, (share, 1), 0) + (up * share) % kept < count[image]
    )
    norm, spread_rows = norm_parts(tokens_own[...].astype(F32))
    back = total[...]
    scale_one = mod[pl.ds(image, 1), width : 2 * width]
    grad = grad_mid[...] + norm_back(norm, spread_rows, back * (1.0 + scale_one))
    grad_tokens[...] = jnp.where(live, grad, 0.0).astype(LOW)
    sums_out[0:1, :] = jnp.sum(back, axis=0, keepdims=True)
    sums_out[1:2, :] = jnp.sum(back * norm, axis=0, keepdims=True)
    up_fold.five()
    down_fold.five()
    for index in range(depth):
        spread.crossed(index)
    spread.close()
    gather.close()
    reduce.close()


def attend_back(sizes, groups, args):
    depth, images, kept, share, pieces = sizes
    width = args[1].shape[1]
    local = args[7].shape[0]
    up_grad, down_grad = args[-2:]
    rows = images * kept
    shape = jax.ShapeDtypeStruct
    return pl.pallas_call(
        functools.partial(attend_back_kernel, sizes, groups),
        out_shape=(
            shape((PAIR, 3 * width, local), LOW),
            shape((PAIR, local, width), LOW),
            shape((2 * PAIR, local), F32),
            shape((1, width), F32),
            shape((share, width), LOW),
            shape((2, width), F32),
            shape((PAIR * rows, width), LOW),
            shape(up_grad.shape[1:], F32),
            shape(down_grad.shape[1:], F32),
        ),
        in_specs=[SM] + [VM] * 14,
        out_specs=(VM,) * 9,
        scratch_shapes=[
            pltpu.VMEM((rows, width), LOW),
            pltpu.VMEM((PAIR, 3, rows, local), LOW),
            pltpu.VMEM((rows, width), LOW),
            pltpu.VMEM((rows + share, width), LOW),
            pltpu.VMEM((share, width), F32),
            pltpu.VMEM((2 * PAIR, images, 1, local), F32),
            pltpu.VMEM((images, 1, width), F32),
            DMA((2,)),
            DMA((2, depth, pieces)),
            DMA((2, depth, pieces)),
            DMA((depth, pieces)),
            DMA((depth + 1, pieces)),
        ]
        + Fold.scratch(up_grad.shape, groups, True)
        + Fold.scratch(down_grad.shape, groups, True)
        + Spread.scratch(depth, pieces),
        compiler_params=pltpu.CompilerParams(
            collective_id=3, has_side_effects=True, vmem_limit_bytes=62 << 20
        ),
        name="attend_back",
    )(*args)


def split_low(value):
    high = value.astype(LOW)
    rest = value - high.astype(F32)
    low = rest.astype(LOW)
    return high, low, (rest - low.astype(F32)).astype(LOW)


def close_kernel(
    sizes,
    groups,
    index,
    grad_tokens,
    sums,
    biases,
    qkv_grad,
    out_grad,
    silu_all,
    mod_weight,
    cond,
    grad_patches,
    qkv_total,
    out_total,
    bias_total,
    mod_weight_grad,
    mod_bias_grad,
    grad_cond,
    whole,
    sum_row,
    sum_land,
    bias_land,
    cond_land,
    own_sem,
    sum_send,
    sum_recv,
    bias_send,
    bias_recv,
    cond_send,
    cond_recv,
    *rest,
):
    depth, images, kept, share, pieces = sizes
    devices = depth * PAIR
    everyone = devices * groups
    me, up, side = place(depth)
    group = lax.axis_index("dp")
    flat = group * devices + me
    width = grad_tokens.shape[1]
    columns = mod_weight.shape[1]
    span = sum_land.shape[2]
    spread = Spread(whole, share, depth, pieces, rest[:4])
    qkv_fold = Fold(qkv_grad, rest[4:11], qkv_total, groups, True)
    out_fold = Fold(out_grad, rest[11:18], out_total, groups, False)
    own_copy = pltpu.make_async_copy(grad_tokens, spread.own(), own_sem)
    own_copy.start()
    barrier = pltpu.get_barrier_semaphore()

    def greet(step, carry):
        there = (flat + step) % everyone
        pl.semaphore_signal(
            barrier,
            inc=1,
            device_id={"dp": there // devices, "tensor": there % devices},
            device_id_type=MESH,
        )
        return carry

    lax.fori_loop(1, everyone, greet, 0)
    pl.semaphore_wait(barrier, everyone - 1)
    own_copy.wait()
    spread.open()
    qkv_fold.one()
    out_fold.one()

    def aligned(device):
        return pl.multiple_of((device * columns) // 128 * 128, 128)

    for member in range(6):
        sum_row[:, member * width : (member + 1) * width] = sums[member : member + 1, :]
    sum_row[:, 6 * width :] = jnp.zeros((1, sum_row.shape[1] - 6 * width), F32)

    def sum_copy(step):
        there = (flat + step) % everyone
        device = there % devices
        return remote(
            sum_row.at[:, pl.ds(aligned(device), span)],
            sum_land.at[flat],
            sum_send.at[step],
            sum_recv.at[step],
            device,
            there // devices,
        )

    def send_sum(step, carry):
        sum_copy(step).start()
        return carry

    lax.fori_loop(1, everyone, send_sum, 0)
    sum_land[flat] = sum_row[:, pl.ds(aligned(me), span)]
    slot = side * groups + group
    bias_land[slot] = biases[...]
    partner = me + 1 - 2 * side

    def bias_copy(step):
        crossed = step // groups
        there = (group + step) % groups
        device = jnp.where(crossed == 1, partner, me)
        return remote(
            biases, bias_land.at[slot], bias_send.at[step], bias_recv.at[step], device, there
        )

    for step in range(1, PAIR * groups):
        bias_copy(step).start()
    qkv_fold.two()
    out_fold.two()

    def wait_sum(step, carry):
        source = (flat + everyone - step) % everyone
        view = sum_land.at[source]
        remote(view, view, sum_send.at[step], sum_recv.at[step], me).wait_recv()
        return carry

    lax.fori_loop(1, everyone, wait_sum, 0)
    offset = (me * columns) % 128
    grads = jnp.concatenate([sum_land[device] for device in range(everyone)], axis=0)
    grads = pltpu.roll(grads, lax.rem(span - offset, span), 1)[:, :columns]
    mod_bias_grad[...] = jnp.sum(grads, axis=0, keepdims=True)
    total_images = images * PAIR

    def image_of(device):
        return (device % PAIR) * images + (device // PAIR) * share // kept

    source = lax.broadcasted_iota(jnp.int32, (everyone, groups * total_images), 0)
    target = lax.broadcasted_iota(jnp.int32, (everyone, groups * total_images), 1)
    row_image = source // devices * total_images + image_of(source % devices)
    chosen = jnp.where(row_image == target, 1.0, 0.0).astype(LOW)
    silu_rows = dot(
        chosen,
        jnp.concatenate([silu_all[member].astype(F32) for member in range(groups)], axis=0).astype(
            LOW
        ),
    ).astype(LOW)
    parts = split_low(grads)
    spread.take(1)
    mod_weight_grad[...] = (
        dot_tn(silu_rows, parts[0]) + dot_tn(silu_rows, parts[1]) + dot_tn(silu_rows, parts[2])
    )
    source = lax.broadcasted_iota(jnp.int32, (total_images, everyone), 1)
    target = lax.broadcasted_iota(jnp.int32, (total_images, everyone), 0)
    chosen = jnp.where(
        (source // devices == group) & (image_of(source % devices) == target), 1.0, 0.0
    ).astype(LOW)
    mine = dot(chosen, parts[0]) + dot(chosen, parts[1]) + dot(chosen, parts[2])
    parts = split_low(mine)
    term = (
        dot_nt(parts[0], mod_weight[...])
        + dot_nt(parts[1], mod_weight[...])
        + dot_nt(parts[2], mod_weight[...])
    )
    cond_land[me] = term

    def cond_copy(step):
        return remote(
            cond_land.at[me],
            cond_land.at[me],
            cond_send.at[step],
            cond_recv.at[step],
            (me + step) % devices,
        )

    for step in range(1, devices):
        cond_copy(step).start()
    qkv_fold.three()
    out_fold.three()
    for turn in range(2, depth):
        spread.take(turn)
    for step in range(1, PAIR * groups):
        crossed = step // groups
        source_group = (group + groups - step % groups) % groups
        source_side = jnp.where(crossed == 1, 1 - side, side)
        view = bias_land.at[source_side * groups + source_group]
        remote(view, view, bias_send.at[step], bias_recv.at[step], me).wait_recv()
    rows = biases.shape[0]
    result = jnp.zeros((rows, width), F32)
    swapped = lax.broadcasted_iota(jnp.int32, (rows, 1), 0) < 6
    for member in range(PAIR * groups):
        value = bias_land[member]
        turned = jnp.concatenate([value[3:6, :], value[0:3, :], value[6:, :]], axis=0)
        same = side == member // groups
        result = result + jnp.where(same, value, turned)
    bias_total[...] = result
    for step in range(1, devices):
        source = (me + devices - step) % devices
        view = cond_land.at[source]
        remote(view, view, cond_send.at[step], cond_recv.at[step], me).wait_recv()
    back = cond_land[0]
    for device in range(1, devices):
        back = back + cond_land[device]
    value = cond[...].astype(F32)
    gate = 1.0 / (1.0 + jnp.exp(-value))
    grad_cond[...] = (back * (gate + value * gate * (1.0 - gate))).astype(LOW)
    qkv_fold.four()
    out_fold.four()

    def place_image(image):
        rows = pl.ds(pl.multiple_of(image * kept, kept), kept)
        spots = lax.broadcasted_iota(jnp.int32, (grad_patches.shape[1], kept), 0)
        pick = jnp.where(spots == index[image], 1.0, 0.0).astype(LOW)
        grad_patches[image] = dot(pick, whole[rows, :]).astype(LOW)

    def own_side(image, carry):
        place_image(side * images + image)
        return carry

    def other_side(image, carry):
        for part in range(depth // images):
            spread.crossed(image * (depth // images) + part)
        place_image((1 - side) * images + image)
        return carry

    lax.fori_loop(0, images, own_side, 0)
    lax.fori_loop(0, images, other_side, 0)
    qkv_fold.five()
    out_fold.five()
    spread.close()

    def done_sum(step, carry):
        sum_copy(step).wait_send()
        return carry

    lax.fori_loop(1, everyone, done_sum, 0)
    for step in range(1, PAIR * groups):
        bias_copy(step).wait_send()
    for step in range(1, devices):
        cond_copy(step).wait_send()


def close(sizes, groups, args):
    depth, images, kept, share, pieces = sizes
    index, grad_tokens, sums, biases, qkv_grad, out_grad, silu_all, mod_weight, cond, spots = args
    devices = depth * PAIR
    width = grad_tokens.shape[1]
    columns = mod_weight.shape[1]
    span = max(-(-((device * columns) % 128 + columns) // 128) * 128 for device in range(devices))
    long = max((device * columns) // 128 * 128 + span for device in range(devices))
    long = max(long, 6 * width + 128)
    shape = jax.ShapeDtypeStruct
    rows = PAIR * images * kept
    everyone = devices * groups
    return pl.pallas_call(
        functools.partial(close_kernel, sizes, groups),
        out_shape=(
            shape((PAIR * images, spots, width), LOW),
            shape(qkv_grad.shape[1:], F32),
            shape(out_grad.shape[1:], F32),
            shape(biases.shape, F32),
            shape(mod_weight.shape, F32),
            shape((1, columns), F32),
            shape(cond.shape, LOW),
        ),
        in_specs=[VM] * 9,
        out_specs=(VM,) * 7,
        scratch_shapes=[
            pltpu.VMEM((rows, width), LOW),
            pltpu.VMEM((1, long), F32),
            pltpu.VMEM((everyone, 1, span), F32),
            pltpu.VMEM((PAIR * groups,) + biases.shape, F32),
            pltpu.VMEM((devices,) + cond.shape, F32),
            DMA,
            DMA((everyone,)),
            DMA((everyone,)),
            DMA((PAIR * groups,)),
            DMA((PAIR * groups,)),
            DMA((devices,)),
            DMA((devices,)),
        ]
        + Spread.scratch(depth, pieces)
        + Fold.scratch(qkv_grad.shape, groups, True)
        + Fold.scratch(out_grad.shape, groups, False),
        compiler_params=pltpu.CompilerParams(
            collective_id=4, has_side_effects=True, vmem_limit_bytes=62 << 20
        ),
        name="close",
    )(*args[:-1])


def on_device(
    patches,
    conditioning,
    keep_count,
    keep_index,
    mod_weight,
    mod_bias,
    qkv_weight,
    qv_bias,
    out_weight,
    out_bias,
    up_weight,
    up_bias,
    down_weight,
    down_bias,
    out_cotangent,
):
    devices = lax.axis_size("tensor")
    depth = devices // PAIR
    all_images, kept = keep_index.shape
    width = patches.shape[2]
    images = all_images // PAIR
    share = images * kept // depth
    pieces = 4 if share % 64 == 0 else 2
    sizes = (depth, images, kept, share, pieces)
    groups = lax.axis_size("dp")
    index = keep_index[:, None, :]
    qkv_local, units = qkv_weight.shape[2], up_weight.shape[1]
    up_bias_row = up_bias[None, :]
    (
        normed_one,
        proj,
        attended,
        tokens_own,
        mid,
        branch,
        normed_two,
        mod,
        silu_all,
        qkv_other,
        qv_other,
        out_other,
        up_other,
        down_other,
        up_bias_other,
    ) = attend(
        sizes,
        groups,
        (
            keep_count,
            index,
            patches,
            conditioning,
            mod_weight,
            mod_bias[None, :],
            qkv_weight,
            qv_bias,
            out_weight,
            out_bias[None, :],
            up_weight,
            down_weight,
            up_bias_row,
        ),
    )
    (
        up_grad,
        down_grad,
        up_bias_grad,
        down_bias_grad,
        block_own,
        grad_mid,
        grad_branch,
        sums_two,
    ) = feed(
        sizes,
        (
            keep_count,
            normed_two,
            out_cotangent,
            mod,
            up_weight,
            up_other,
            up_bias_row,
            up_bias_other,
            down_weight,
            down_other,
            down_bias[None, :],
            mid,
            branch,
        ),
    )
    (
        qkv_grad,
        out_grad,
        qv_grad,
        out_bias_grad,
        grad_tokens,
        sums_one,
        block_out,
        up_total,
        down_total,
    ) = attend_back(
        sizes,
        groups,
        (
            keep_count,
            grad_branch,
            normed_one,
            proj,
            attended,
            qkv_weight,
            qkv_other,
            out_weight,
            out_other,
            mod,
            tokens_own,
            grad_mid,
            block_own,
            up_grad,
            down_grad,
        ),
    )

    def row(value):
        return jnp.pad(value, ((0, 0), (0, width - value.shape[1])))

    biases = jnp.concatenate(
        [
            row(up_bias_grad[0:1]),
            row(qv_grad[0:2]),
            row(up_bias_grad[1:2]),
            row(qv_grad[2:4]),
            down_bias_grad,
            out_bias_grad,
        ]
    )
    sums = jnp.concatenate([sums_one, sums_two])
    (
        grad_patches,
        qkv_total,
        out_total,
        bias_total,
        mod_weight_grad,
        mod_bias_grad,
        grad_conditioning,
    ) = close(
        sizes,
        groups,
        (
            index,
            grad_tokens,
            sums,
            biases,
            qkv_grad,
            out_grad,
            silu_all,
            mod_weight,
            conditioning,
            patches.shape[1],
        ),
    )
    return (
        block_out.reshape(all_images, kept, width),
        grad_patches,
        grad_conditioning,
        mod_weight_grad,
        mod_bias_grad[0],
        qkv_total.reshape(qkv_weight.shape),
        bias_total[1:3, :qkv_local],
        out_total,
        bias_total[7],
        up_total,
        bias_total[0, :units],
        down_total,
        bias_total[6],
    )


def solution(mesh):
    placed = (
        P("dp", None, None),
        P("dp", None),
        P("dp"),
        P("dp", None),
        P(None, "tensor"),
        P("tensor"),
        P(None, None, "tensor"),
        P(None, "tensor"),
        P("tensor", None),
        P(),
        P(None, "tensor"),
        P("tensor"),
        P("tensor", None),
        P(),
        P("dp", None, None),
    )
    return jax.shard_map(
        on_device,
        mesh=mesh,
        in_specs=placed,
        out_specs=(
            P("dp", None, None),
            P("dp", None, None),
            P("dp", None),
            P(None, "tensor"),
            P("tensor"),
            P(None, None, "tensor"),
            P(None, "tensor"),
            P("tensor", None),
            P(),
            P(None, "tensor"),
            P("tensor"),
            P("tensor", None),
            P(),
        ),
        check_vma=False,
    )
```

```python
import functools

import jax
import jax.numpy as jnp
from jax import lax
from jax.experimental import pallas as pl
from jax.experimental.pallas import tpu as pltpu
from jax.sharding import PartitionSpec as P

HD = 72
MESH = pl.DeviceIdType.MESH
F32 = jnp.float32
LOW = jnp.bfloat16
DMA = pltpu.SemaphoreType.DMA
VM = pl.BlockSpec(memory_space=pltpu.VMEM)
SM = pl.BlockSpec(memory_space=pltpu.SMEM)
HB = pl.BlockSpec(memory_space=pl.ANY)
PAIR = 2
GELU_ROOT = 0.7978845608028654
GELU_CUBE = 0.044715


def remote(source, target, send_sem, recv_sem, device, group=None):
    there = {"tensor": device} if group is None else {"dp": group, "tensor": device}
    return pltpu.make_async_remote_copy(
        src_ref=source,
        dst_ref=target,
        send_sem=send_sem,
        recv_sem=recv_sem,
        device_id=there,
        device_id_type=MESH,
    )


def place(depth):
    me = lax.axis_index("tensor")
    return me, me % depth, me // depth


def bits_of(depth):
    return depth.bit_length() - 1


def toward(spot, bit):
    return (1 - 2 * ((spot // (1 << bit)) % 2)) * (1 << bit)


def across(spot, offset, depth):
    result = spot
    for bit in range(bits_of(depth)):
        result = result + ((offset // (1 << bit)) % 2) * toward(spot, bit)
    return result


def offset_between(left, right, depth):
    result = 0
    for bit in range(bits_of(depth)):
        size = 1 << bit
        result = result + ((left // size + right // size) % 2) * size
    return result


def meet(peers):
    barrier = pltpu.get_barrier_semaphore()
    for group, peer in peers:
        pl.semaphore_signal(
            barrier, inc=1, device_id={"dp": group, "tensor": peer}, device_id_type=MESH
        )
    pl.semaphore_wait(barrier, len(peers))


def column_peers(depth):
    me, spot, side = place(depth)
    group = lax.axis_index("dp")
    return [(group, me + toward(spot, bit)) for bit in range(bits_of(depth))]


def cube_peers(depth, groups):
    me, spot, side = place(depth)
    group = lax.axis_index("dp")
    other = me + depth * (1 - 2 * side)
    peers = [((group + step) % groups, me) for step in range(1, groups)]
    return peers + [((group + step) % groups, other) for step in range(groups)]


def dot(left, right):
    return jnp.dot(left, right, preferred_element_type=F32)


def dot_nt(left, right):
    return lax.dot_general(left, right, (((1,), (1,)), ((), ())), preferred_element_type=F32)


def dot_tn(left, right):
    return lax.dot_general(left, right, (((0,), (0,)), ((), ())), preferred_element_type=F32)


def norm_parts(rows):
    width = rows.shape[-1]
    centred = rows - jnp.sum(rows, axis=-1, keepdims=True) * (1.0 / width)
    spread = lax.rsqrt(jnp.sum(centred * centred, axis=-1, keepdims=True) * (1.0 / width) + 1e-06)
    return centred * spread, spread


def norm_back(norm, spread, grad):
    width = norm.shape[-1]
    mean_grad = jnp.sum(grad, axis=-1, keepdims=True) * (1.0 / width)
    mean_both = jnp.sum(grad * norm, axis=-1, keepdims=True) * (1.0 / width)
    return (grad - mean_grad - norm * mean_both) * spread


class Line:
    def __init__(self, buffer, share, depth, pieces, send, recv):
        self.buffer, self.share, self.depth, self.pieces = buffer, share, depth, pieces
        self.send, self.recv = send, recv
        self.me = lax.axis_index("tensor")
        self.up, self.side = self.me // PAIR, self.me % PAIR

    def piece(self, index, part):
        rows = self.share // self.pieces
        start = (index * PAIR + self.side) * self.share + part * rows
        return self.buffer.at[pl.ds(pl.multiple_of(start, rows), rows), :]

    def copy(self, way, step, part):
        source = self.up - (step - 1) * (1 - 2 * way)
        target = self.up + 1 - 2 * way
        view = self.piece(source, part)
        return remote(
            view,
            view,
            self.send.at[way, step, part],
            self.recv.at[way, step, part],
            target * PAIR + self.side,
        )

    def may_send(self, way, step):
        if way == 0:
            return (self.up + 1 < self.depth) & (self.up >= step - 1)
        return (self.up >= 1) & (self.up + step - 1 < self.depth)

    def open(self):
        for part in range(self.pieces):
            for way in range(2):

                @pl.when(self.may_send(way, 1))
                def _():
                    self.copy(way, 1, part).start()

    def arrival(self, turn):
        below = self.up
        above = self.depth - 1 - self.up
        both = jnp.minimum(below, above)
        mixed = turn <= 2 * both
        way = jnp.where(mixed, (turn + 1) % 2, jnp.where(below > above, 0, 1))
        step = jnp.where(mixed, (turn + 1) // 2, turn - both)
        return way, step, self.up - step * (1 - 2 * way)

    def take(self, turn, then):
        way, step, source = self.arrival(turn)
        ahead = jnp.where(way == 0, self.up + 1 < self.depth, self.up >= 1)
        for part in range(self.pieces):
            view = self.piece(source, part)
            remote(
                view, view, self.send.at[way, step, part], self.recv.at[way, step, part], self.me
            ).wait_recv()

            @pl.when(ahead)
            def _():
                self.copy(way, step + 1, part).start()

            then(source, part)

    def close(self):
        for way in range(2):
            for step in range(1, self.depth):

                @pl.when(self.may_send(way, step))
                def _():
                    for part in range(self.pieces):
                        self.copy(way, step, part).wait_send()


class Cube:
    def __init__(self, share, depth, pieces):
        self.share, self.depth, self.pieces = share, depth, pieces
        self.me, self.spot, self.side = place(depth)
        self.bits = bits_of(depth)
        self.rows = share // pieces

    def order(self, part):
        ways = list(range(self.bits))
        return ways if part % 2 else ways[::-1]

    def span(self, index, part):
        return pl.ds(pl.multiple_of(index * self.share + part * self.rows, self.rows), self.rows)

    def neighbour(self, bit):
        return self.me + toward(self.spot, bit)


class Gather(Cube):
    def __init__(self, buffer, share, depth, pieces, send, recv):
        super().__init__(share, depth, pieces)
        self.buffer, self.send, self.recv = buffer, send, recv

    def last(self, offset, part):
        order = self.order(part)
        return max(
            (stage for stage in range(self.bits) if offset >> order[stage] & 1), default=-1
        )

    def copy(self, offset, stage, part):
        bit = self.order(part)[stage]
        view = self.buffer.at[self.span(across(self.spot, offset, self.depth), part), :]
        return remote(
            view,
            view,
            self.send.at[offset, stage, part],
            self.recv.at[offset ^ (1 << bit), part],
            self.neighbour(bit),
        )

    def landed(self, offset, part):
        view = self.buffer.at[self.span(across(self.spot, offset, self.depth), part), :]
        remote(
            view, view, self.send.at[0, 0, part], self.recv.at[offset, part], self.me
        ).wait_recv()

    def sends(self, offset):
        return [
            (stage, part)
            for part in range(self.pieces)
            for stage in range(self.last(offset, part) + 1, self.bits)
        ]

    def open(self):
        for stage, part in self.sends(0):
            self.copy(0, stage, part).start()

    def relay(self):
        for offset in sorted(range(1, self.depth), key=lambda value: bin(value).count("1")):
            for part in range(self.pieces):
                first = self.last(offset, part) + 1
                if first < self.bits:
                    self.landed(offset, part)
                    for stage in range(first, self.bits):
                        self.copy(offset, stage, part).start()

    def take(self, offset):
        for member in range(1, self.depth):

            @pl.when(offset == member)
            def _():
                for part in range(self.pieces):
                    if self.last(member, part) + 1 == self.bits:
                        self.landed(member, part)

    def close(self):
        for offset in range(self.depth):
            for stage, part in self.sends(offset):
                self.copy(offset, stage, part).wait_send()

    @staticmethod
    def scratch(depth, pieces):
        return [DMA((depth, bits_of(depth), pieces)), DMA((depth, pieces))]


class Reduce(Cube):
    def __init__(self, terms, landing, share, depth, pieces, send, recv):
        super().__init__(share, depth, pieces)
        self.terms, self.landing, self.send, self.recv = terms, landing, send, recv

    def slot(self, stage, offset, part):
        order = self.order(part)
        found = [
            (level, member)
            for level in range(self.bits)
            for member in range(self.depth)
            if not any(member >> order[below] & 1 for below in range(level + 1))
        ]
        return found.index((stage, offset))

    def first(self, offset, part):
        order = self.order(part)
        return min(stage for stage in range(self.bits) if offset >> order[stage] & 1)

    def copy(self, offset, part):
        stage = self.first(offset, part)
        bit = self.order(part)[stage]
        slot = self.slot(stage, offset ^ (1 << bit), part)
        return remote(
            self.terms.at[self.span(across(self.spot, offset, self.depth), part), :],
            self.landing.at[self.span(slot, part), :],
            self.send.at[offset, part],
            self.recv.at[slot, part],
            self.neighbour(bit),
        )

    def landed(self, slot, part):
        view = self.landing.at[self.span(slot, part), :]
        remote(view, view, self.send.at[0, part], self.recv.at[slot, part], self.me).wait_recv()

    def ready(self, offset):
        for member in range(1, self.depth):

            @pl.when(offset == member)
            def _():
                for part in range(self.pieces):
                    if self.first(member, part) == 0:
                        self.copy(member, part).start()

    def ready_share(self, index):
        self.ready(offset_between(index, self.spot, self.depth))

    def add(self, target, target_start, term_start, slots, part):
        def body(index, carry):
            offset = index * 16
            value = self.terms[pl.ds(pl.multiple_of(term_start + offset, 16), 16), :].astype(F32)
            for slot in slots:
                start = slot * self.share + part * self.rows
                value = value + self.landing[
                    pl.ds(pl.multiple_of(start + offset, 16), 16), :
                ].astype(F32)
            target[pl.ds(pl.multiple_of(target_start + offset, 16), 16), :] = value.astype(
                target.dtype
            )
            return carry

        lax.fori_loop(0, self.rows // 16, body, 0)

    def relay(self):
        for level in range(1, self.bits):
            for part in range(self.pieces):
                for offset in range(1, self.depth):
                    if self.first(offset, part) == level:
                        slots = [self.slot(below, offset, part) for below in range(level)]
                        for slot in slots:
                            self.landed(slot, part)
                        start = (
                            across(self.spot, offset, self.depth) * self.share + part * self.rows
                        )
                        self.add(self.terms, start, start, slots, part)
                        self.copy(offset, part).start()

    def finish(self, total):
        for part in range(self.pieces):
            slots = [self.slot(stage, 0, part) for stage in range(self.bits)]
            for slot in slots:
                self.landed(slot, part)
            skip = part * self.rows
            self.add(total, skip, self.spot * self.share + skip, slots, part)

    def close(self):
        for offset in range(1, self.depth):
            for part in range(self.pieces):
                self.copy(offset, part).wait_send()

    @staticmethod
    def scratch(depth, pieces):
        return [DMA((depth, pieces)), DMA((depth - 1, pieces))]


class Fold:
    def __init__(self, source, scratch, out, depth, groups, split):
        self.source, self.out, self.groups, self.split = source, out, groups, split
        self.stage, self.near, self.side_land, self.far, self.low, self.send, self.recv = scratch
        self.me = lax.axis_index("tensor")
        self.group = lax.axis_index("dp")
        self.core = self.group % PAIR
        self.line = self.group // PAIR
        self.mate = self.group + 1 - 2 * self.core
        self.partner = self.me + depth * (1 - 2 * (self.me // depth))
        self.lines = groups // PAIR
        self.rows = self.stage.shape[1]
        self.start = self.core * self.rows if split else 0

    @staticmethod
    def scratch(shape, groups, split):
        _, rows, width = shape
        half = rows // 2 if split else rows
        lines = groups // PAIR
        return [
            pltpu.VMEM((PAIR, half, width), LOW),
            pltpu.VMEM((PAIR, half, width), LOW),
            pltpu.VMEM((half, width), LOW),
            pltpu.VMEM((lines, half, width), LOW),
            pltpu.VMEM((rows, width), LOW),
            DMA((3 + lines,)),
            DMA((3 + lines,)),
        ]

    def each(self, body):
        step = 48 if self.rows % 48 == 0 else self.rows

        def run(index, carry):
            body(pl.multiple_of(index * step, step), step)
            return carry

        lax.fori_loop(0, self.rows // step, run, 0)

    def window(self, start, size):
        return pl.ds(pl.multiple_of(start, 16) if self.split else start, size)

    def near_copy(self):
        if self.split:
            away = self.window((1 - self.core) * self.rows, self.rows)
            source = self.source.at[:, away, :]
        else:
            source = self.source
        return remote(
            source, self.near, self.send.at[0], self.recv.at[0], self.me, self.mate
        )

    def side_copy(self):
        return remote(
            self.stage.at[1],
            self.side_land,
            self.send.at[1],
            self.recv.at[1],
            self.partner,
            self.group,
        )

    def far_copy(self, step):
        line = (self.line + step) % self.lines
        return remote(
            self.far.at[self.line],
            self.far.at[self.line],
            self.send.at[2 + step],
            self.recv.at[2 + step],
            self.me,
            line * PAIR + self.core,
        )

    def mate_copy(self, core):
        view = self.low.at[self.window(core * self.rows, self.rows), :]
        return remote(view, view, self.send.at[2], self.recv.at[2], self.me, self.mate)

    def one(self):
        self.near_copy().start()

    def two(self):
        self.near_copy().wait_recv()

        def add(at, size):
            for shard in range(PAIR):
                mine = self.source[shard, self.window(self.start + at, size), :].astype(F32)
                rows = self.window(at, size)
                self.stage[shard, rows, :] = (
                    mine + self.near[shard, rows, :].astype(F32)
                ).astype(LOW)

        self.each(add)
        self.side_copy().start()

    def three(self):
        self.side_copy().wait_recv()

        def add(at, size):
            rows = self.window(at, size)
            self.far[self.line, rows, :] = (
                self.stage[0, rows, :].astype(F32) + self.side_land[rows, :].astype(F32)
            ).astype(LOW)

        self.each(add)
        for step in range(1, self.lines):
            self.far_copy(step).start()

    def four(self):
        for step in range(1, self.lines):
            line = (self.line + self.lines - step) % self.lines
            view = self.far.at[line]
            remote(
                view, view, self.send.at[2 + step], self.recv.at[2 + step], self.me, self.mate
            ).wait_recv()

        def add(at, size):
            rows = self.window(at, size)
            value = self.far[0, rows, :].astype(F32)
            for line in range(1, self.lines):
                value = value + self.far[line, rows, :].astype(F32)
            low = value.astype(LOW)
            spot = self.window(self.start + at, size)
            self.low[spot, :] = low
            self.out[spot, :] = low.astype(F32)

        self.each(add)
        if self.split:
            self.mate_copy(self.core).start()

    def five(self):
        if self.split:
            self.mate_copy(1 - self.core).wait_recv()

            def put(at, size):
                spot = self.window((1 - self.core) * self.rows + at, size)
                self.out[spot, :] = self.low[spot, :].astype(F32)

            self.each(put)
            self.mate_copy(self.core).wait_send()
        self.near_copy().wait_send()
        self.side_copy().wait_send()
        for step in range(1, self.lines):
            self.far_copy(step).wait_send()


class Spread:
    def __init__(self, whole, share, depth, pieces, scratch):
        self.whole, self.share, self.depth, self.pieces = whole, share, depth, pieces
        send, recv, self.side_send, self.side_recv = scratch
        self.line = Line(whole, share, depth, pieces, send, recv)
        self.me, self.up, self.side = self.line.me, self.line.up, self.line.side

    @staticmethod
    def scratch(depth, pieces):
        return [
            DMA((2, depth, pieces)),
            DMA((2, depth, pieces)),
            DMA((depth, pieces)),
            DMA((depth, pieces)),
        ]

    def peers(self):
        group = lax.axis_index("dp")
        line = [
            (group, (self.up + step) % self.depth * PAIR + self.side)
            for step in range(1, self.depth)
        ]
        return line + [(group, self.me + 1 - 2 * self.side)]

    def peers_beyond(self, depth):
        me, spot, side = place(depth)
        group = lax.axis_index("dp")
        return [
            (group, (self.up + step) % self.depth * PAIR + self.side)
            for step in range(1, self.depth)
        ]

    def view(self, side, index, part):
        rows = self.share // self.pieces
        start = (index * PAIR + side) * self.share + part * rows
        return self.whole.at[pl.ds(pl.multiple_of(start, rows), rows), :]

    def own(self):
        return self.whole.at[pl.ds(pl.multiple_of(self.me * self.share, self.share), self.share), :]

    def across(self, index, part):
        view = self.view(self.side, index, part)
        return remote(
            view,
            view,
            self.side_send.at[index, part],
            self.side_recv.at[index, part],
            self.me + 1 - 2 * self.side,
        )

    def open(self):
        self.line.open()
        for part in range(self.pieces):
            self.across(self.up, part).start()

    def take(self, turn):
        self.line.take(turn, lambda source, part: self.across(source, part).start())

    def crossed(self, index):
        for part in range(self.pieces):
            view = self.view(1 - self.side, index, part)
            remote(
                view, view, self.side_send.at[index, part], self.side_recv.at[index, part], self.me
            ).wait_recv()

    def close(self):
        self.line.close()
        for index in range(self.depth):
            for part in range(self.pieces):
                self.across(index, part).wait_send()


class Share:
    def __init__(self, source, target, sems, depth, groups):
        self.source, self.target = source, target
        self.send, self.recv, self.near_send, self.near_recv = sems
        self.me, _, side = place(depth)
        self.group = lax.axis_index("dp")
        self.partner = self.me + depth * (1 - 2 * side)
        rows = source.shape[-2]
        self.parts = groups if rows % (groups * 16) == 0 else PAIR if rows % (PAIR * 16) == 0 else 1
        self.rows = rows // self.parts
        self.mine = self.group % self.parts

    def view(self, array, part):
        rows = pl.ds(pl.multiple_of(part * self.rows, 16) if self.parts > 1 else 0, self.rows)
        return array.at[:, rows, :] if len(array.shape) == 3 else array.at[rows, :]

    def copy(self):
        return remote(
            self.view(self.source, self.mine),
            self.view(self.target, self.mine),
            self.send,
            self.recv,
            self.partner,
        )

    def mate(self, step):
        base = self.group - self.mine
        return base + (self.mine + step) % self.parts

    def hand(self, step):
        view = self.view(self.target, self.mine)
        return remote(
            view, view, self.near_send.at[step], self.near_recv.at[step], self.me, self.mate(step)
        )

    def start(self):
        self.copy().start()

    def pass_on(self):
        self.copy().wait_recv()
        for step in range(1, self.parts):
            self.hand(step).start()

    def wait(self):
        for step in range(1, self.parts):
            part = (self.mine + self.parts - step) % self.parts
            view = self.view(self.target, part)
            remote(
                view, view, self.near_send.at[step], self.near_recv.at[step], self.me, self.group
            ).wait_recv()

    def close(self):
        self.copy().wait_send()
        for step in range(1, self.parts):
            self.hand(step).wait_send()


def head_mask(head, width):
    lane = lax.broadcasted_iota(jnp.int32, (1, width), 1)
    return (lane >= head * HD) & (lane < (head + 1) * HD)


def softmax_rows(queries, keys, key_live, scale):
    scores = dot_nt(queries, keys) * scale
    scores = jnp.where(key_live, scores, -1e30)
    top = jnp.max(scores, axis=-1, keepdims=True)
    raised = jnp.exp(scores - top)
    return raised / jnp.sum(raised, axis=-1, keepdims=True)


def attend_shard(normed, qkv, qv, proj_out, shard, rows, key_live, scale):
    local = qkv.shape[2]
    queries = (dot(normed, qkv[0]) + qv[0:1, :].astype(F32)).astype(LOW)
    keys = dot(normed, qkv[1]).astype(LOW)
    values = (dot(normed, qkv[2]) + qv[1:2, :].astype(F32)).astype(LOW)
    proj_out[shard, 0, rows, :] = queries
    proj_out[shard, 1, rows, :] = keys
    proj_out[shard, 2, rows, :] = values
    attended = jnp.zeros((normed.shape[0], local), F32)
    for head in range(local // HD):
        mask = head_mask(head, local)
        weights = softmax_rows(jnp.where(mask, queries, 0.0).astype(LOW), keys, key_live, scale)
        attended = attended + dot(weights.astype(LOW), jnp.where(mask, values, 0.0).astype(LOW))
    return attended.astype(LOW)


def attend_kernel(
    sizes,
    groups,
    count,
    index,
    patches,
    cond,
    mod_weight,
    mod_bias,
    qkv_own,
    qv_own,
    out_own,
    out_bias,
    up_own,
    down_own,
    up_bias_own,
    normed_out,
    proj_out,
    attended_out,
    tokens_own,
    mid_out,
    branch_out,
    normed_two_out,
    mod,
    silu_all,
    qkv_other,
    qv_other,
    out_other,
    up_other,
    down_other,
    up_bias_other,
    patch_rows,
    tokens,
    terms,
    landing,
    total,
    mod_mine,
    mod_gathered,
    patch_sem,
    send,
    recv,
    mod_send,
    mod_recv,
    silu_send,
    silu_recv,
    weight_send,
    weight_recv,
    near_send,
    near_recv,
):
    depth, images, kept, share, pieces = sizes
    devices = depth * PAIR
    me, up, side = place(depth)
    group = lax.axis_index("dp")
    width = patches.shape[2]
    scale = HD ** (-0.5)
    fold = depth // images
    first = side * images

    def fetch(image):
        return pltpu.make_async_copy(
            patches.at[first + image], patch_rows.at[image], patch_sem.at[image]
        )

    def image_at(turn):
        return across(up // fold, images - 1 - turn, images)

    for turn in range(images):
        fetch(image_at(turn)).start()
    meet(
        [(group, (me + step) % devices) for step in range(1, devices)]
        + [((group + step) % groups, me) for step in range(1, groups)]
    )
    value = cond[...].astype(F32)
    silu = (value / (1.0 + jnp.exp(-value))).astype(LOW)
    silu_all[group] = silu
    local_mod = (dot(silu, mod_weight[...]) + mod_bias[...].astype(F32)).astype(LOW)
    mod_mine[...] = local_mod
    mod_gathered[me] = local_mod
    mod_copies = [
        remote(
            mod_mine,
            mod_gathered.at[me],
            mod_send.at[step],
            mod_recv.at[step],
            (me + step) % devices,
        )
        for step in range(1, devices)
    ]
    silu_copies = [
        remote(
            silu_all.at[group],
            silu_all.at[group],
            silu_send.at[step],
            silu_recv.at[step],
            me,
            (group + step) % groups,
        )
        for step in range(1, groups)
    ]
    for copy in mod_copies + silu_copies:
        copy.start()

    shares = [
        Share(
            source,
            target,
            (
                weight_send.at[which],
                weight_recv.at[which],
                near_send.at[which],
                near_recv.at[which],
            ),
            depth,
            groups,
        )
        for which, (source, target) in enumerate(
            (
                (qv_own, qv_other),
                (qkv_own, qkv_other),
                (out_own, out_other),
                (up_bias_own, up_bias_other),
                (up_own, up_other),
                (down_own, down_other),
            )
        )
    ]
    for member in shares:
        member.start()
    reduce = Reduce(terms, landing, share, depth, pieces, send, recv)

    def pick_rows(turn, carry):
        image = image_at(turn)
        fetch(image).wait()
        rows = pl.ds(pl.multiple_of(image * kept, kept), kept)
        spots = lax.broadcasted_iota(jnp.int32, (patches.shape[1], kept), 0)
        slots = lax.broadcasted_iota(jnp.int32, (patches.shape[1], kept), 1)
        pick = jnp.where(
            (spots == index[first + image]) & (slots < count[first + image]), 1.0, 0.0
        )
        tokens[rows, :] = dot_tn(pick.astype(LOW), patch_rows[image]).astype(LOW)
        return carry

    lax.fori_loop(0, images, pick_rows, 0)
    for step in range(1, devices):
        source = (me + devices - step) % devices
        remote(
            mod_mine, mod_gathered.at[source], mod_send.at[step], mod_recv.at[step], me
        ).wait_recv()
    mod[...] = jnp.concatenate(
        [mod_gathered[device].astype(F32) for device in range(devices)], axis=-1
    )

    def block(image, member):
        return mod[pl.ds(first + image, 1), member * width : (member + 1) * width]

    def one(turn, carry):
        image = image_at(turn)
        rows = pl.ds(pl.multiple_of(image * kept, kept), kept)

        @pl.when(turn == images - 1)
        def _():
            shares[0].pass_on()
            shares[1].pass_on()

        norm, _ = norm_parts(tokens[rows, :].astype(F32))
        normed = (norm * (1.0 + block(image, 1)) + block(image, 0)).astype(LOW)
        normed_out[rows, :] = normed
        key_live = lax.broadcasted_iota(jnp.int32, (1, kept), 1) < count[first + image]
        attended_out[0, rows, :] = attend_shard(
            normed, qkv_own, qv_own, proj_out, 0, rows, key_live, scale
        )
        return carry

    def two(turn, carry):
        image = image_at(turn)
        rows = pl.ds(pl.multiple_of(image * kept, kept), kept)
        key_live = lax.broadcasted_iota(jnp.int32, (1, kept), 1) < count[first + image]
        attended = attend_shard(
            normed_out[rows, :], qkv_other, qv_other, proj_out, 1, rows, key_live, scale
        )
        attended_out[1, rows, :] = attended
        branch = dot(attended_out[0, rows, :], out_own[...]) + dot(attended, out_other[...])
        terms[rows, :] = branch.astype(LOW)
        for part in range(fold):
            reduce.ready_share(image * fold + part)
        return carry

    lax.fori_loop(0, images, one, 0)
    shares[2].pass_on()
    for member in shares[:3]:
        member.wait()
    lax.fori_loop(0, images, two, 0)
    shares[3].pass_on()
    shares[4].pass_on()
    reduce.relay()
    shares[5].pass_on()
    reduce.finish(total)
    image = (up * share) // kept
    own = tokens[pl.ds(pl.multiple_of(up * share, share), share), :]
    tokens_own[...] = own
    branch = total[...] + out_bias[...].astype(F32)
    branch_out[...] = branch
    mid = own.astype(F32) + block(image, 2) * branch
    mid_out[...] = mid
    norm, _ = norm_parts(mid)
    normed_two_out[...] = (norm * (1.0 + block(image, 4)) + block(image, 3)).astype(LOW)
    reduce.close()
    for member in shares[3:]:
        member.wait()
    for step in range(1, groups):
        source = (group + groups - step) % groups
        view = silu_all.at[source]
        remote(
            view, view, silu_send.at[step], silu_recv.at[step], me, group
        ).wait_recv()
    for member in shares:
        member.close()
    for copy in mod_copies + silu_copies:
        copy.wait_send()


def attend(sizes, groups, args):
    depth, images, kept, share, pieces = sizes
    (count, index, patches, cond, mod_weight, mod_bias, qkv, qv, out, out_bias, up, down, up_bias) = args
    spots, width = patches.shape[1:]
    local = out.shape[0]
    rows = images * kept
    shape = jax.ShapeDtypeStruct
    devices = depth * PAIR
    return pl.pallas_call(
        functools.partial(attend_kernel, sizes, groups),
        out_shape=(
            shape((rows, width), LOW),
            shape((PAIR, 3, rows, local), LOW),
            shape((PAIR, rows, local), LOW),
            shape((share, width), LOW),
            shape((share, width), F32),
            shape((share, width), F32),
            shape((share, width), LOW),
            shape((cond.shape[0], devices * mod_weight.shape[1]), F32),
            shape((groups,) + cond.shape, LOW),
            shape(qkv.shape, LOW),
            shape(qv.shape, LOW),
            shape(out.shape, LOW),
            shape(up.shape, LOW),
            shape(down.shape, LOW),
            shape(up_bias.shape, LOW),
        ),
        in_specs=[SM, VM, HB] + [VM] * 10,
        out_specs=(VM,) * 15,
        scratch_shapes=[
            pltpu.VMEM((images, spots, width), LOW),
            pltpu.VMEM((rows, width), LOW),
            pltpu.VMEM((rows, width), LOW),
            pltpu.VMEM((rows - share, width), LOW),
            pltpu.VMEM((share, width), F32),
            pltpu.VMEM((cond.shape[0], mod_weight.shape[1]), LOW),
            pltpu.VMEM((devices, cond.shape[0], mod_weight.shape[1]), LOW),
            DMA((images,)),
        ]
        + Reduce.scratch(depth, pieces)
        + [
            DMA((devices,)),
            DMA((devices,)),
            DMA((groups,)),
            DMA((groups,)),
            DMA((6,)),
            DMA((6,)),
            DMA((6, groups)),
            DMA((6, groups)),
        ],
        compiler_params=pltpu.CompilerParams(
            collective_id=1, has_side_effects=True, vmem_limit_bytes=60 << 20
        ),
        name="attend",
    )(*args)


def feed_kernel(
    sizes,
    count,
    normed_own,
    cotangent,
    mod,
    up_own,
    up_other,
    up_bias_own,
    up_bias_other,
    down_own,
    down_other,
    down_bias,
    mid,
    branch,
    up_grad,
    down_grad,
    up_bias_grad,
    down_bias_grad,
    block_own,
    grad_mid_out,
    grad_branch_out,
    sums_out,
    normed,
    cot,
    hidden,
    grad_pre,
    grad_mlp,
    terms,
    landing,
    mlp_terms,
    mlp_landing,
    total,
    mlp_total,
    up_sums,
    down_sums,
    cot_sem,
    own_sem,
    gather_send,
    gather_recv,
    send,
    recv,
    mlp_send,
    mlp_recv,
):
    depth, images, kept, share, pieces = sizes
    me, up, side = place(depth)
    width = normed_own.shape[1]
    fold = depth // images
    first = side * images
    own_rows = pl.ds(pl.multiple_of(up * share, share), share)
    own_copy = pltpu.make_async_copy(normed_own, normed.at[own_rows, :], own_sem)
    own_copy.start()

    def fetch(image):
        return pltpu.make_async_copy(
            cotangent.at[first + image],
            cot.at[pl.ds(pl.multiple_of(image * kept, kept), kept), :],
            cot_sem.at[image],
        )

    for image in range(images):
        fetch(image).start()
    meet(column_peers(depth))
    own_copy.wait()
    gather = Gather(normed, share, depth, pieces, gather_send, gather_recv)
    reduce = Reduce(terms, landing, share, depth, pieces, send, recv)
    mlp_reduce = Reduce(mlp_terms, mlp_landing, share, depth, pieces, mlp_send, mlp_recv)
    gather.open()

    def block(image, member):
        return mod[pl.ds(image, 1), member * width : (member + 1) * width]

    def one(image):
        fetch(image).wait()
        rows = pl.ds(pl.multiple_of(image * kept, kept), kept)
        live = lax.broadcasted_iota(jnp.int32, (kept, 1), 0) < count[first + image]
        grad = jnp.where(live, cot[rows, :].astype(F32), 0.0)
        grad = (block(first + image, 5) * grad).astype(LOW)
        grad_mlp[rows, :] = grad
        down_sums[image] = jnp.sum(grad.astype(F32), axis=0, keepdims=True)
        source = normed[rows, :]
        mlp = None
        back = None
        for shard, (weight_up, bias, weight_down) in enumerate(
            ((up_own, up_bias_own, down_own), (up_other, up_bias_other, down_other))
        ):
            pre = dot(source, weight_up[...]) + bias[...].astype(F32)
            square = pre * pre
            bent = jnp.tanh(GELU_ROOT * pre * (1.0 + GELU_CUBE * square))
            half = 0.5 * (1.0 + bent)
            low_hidden = (pre * half).astype(LOW)
            hidden[shard, rows, :] = low_hidden
            slope = half + 0.5 * pre * (1.0 - bent * bent) * (
                GELU_ROOT * (1.0 + 3.0 * GELU_CUBE * square)
            )
            low_grad = (slope * dot_nt(grad, weight_down[...])).astype(LOW)
            grad_pre[shard, rows, :] = low_grad
            up_sums[shard, image] = jnp.sum(low_grad.astype(F32), axis=0, keepdims=True)
            mlp_part = dot(low_hidden, weight_down[...])
            back_part = dot_nt(low_grad, weight_up[...])
            mlp = mlp_part if mlp is None else mlp + mlp_part
            back = back_part if back is None else back + back_part
        terms[rows, :] = back.astype(LOW)
        mlp_terms[rows, :] = mlp.astype(LOW)
        for part in range(fold):
            reduce.ready_share(image * fold + part)

    if fold == 1:

        def turn_of(turn, carry):
            @pl.when(turn == 1)
            def _():
                gather.relay()

            offset = turn + (turn // 2) * (1 - 2 * (turn % 2))
            gather.take(offset)
            one(across(up, offset, depth))
            return carry

        lax.fori_loop(0, depth, turn_of, 0)
    else:

        def image_of(image, carry):
            one(image)
            return carry

        gather.relay()
        for offset in range(1, depth):
            gather.take(offset)
        lax.fori_loop(0, images, image_of, 0)
    for offset in range(1, depth):
        mlp_reduce.ready(depth - offset)
    reduce.relay()
    for shard in range(PAIR):

        def tile(step, carry):
            columns = pl.ds(pl.multiple_of(step * 128, 128), 128)
            up_grad[shard, columns, :] = dot_tn(
                normed[:, columns], grad_pre[shard]
            ).astype(LOW)
            down_grad[shard, :, columns] = dot_tn(hidden[shard], grad_mlp[:, columns]).astype(LOW)
            return carry

        lax.fori_loop(0, width // 128, tile, 0)
    mlp_reduce.relay()
    reduce.finish(total)
    for shard in range(PAIR):
        up_bias_grad[shard : shard + 1, :] = sum(up_sums[shard, image] for image in range(images))
    down_bias_grad[...] = sum(down_sums[image] for image in range(images))
    image = first + (up * share) // kept
    place_in = (up * share) % kept
    live = (
        lax.broadcasted_iota(jnp.int32, (share, 1), 0) + place_in < count[image]
    )
    grad_out = jnp.where(live, cot[own_rows, :].astype(F32), 0.0)
    norm, spread = norm_parts(mid[...])
    back = total[...]
    grad_mid = grad_out + norm_back(norm, spread, back * (1.0 + block(image, 4)))
    grad_mid_out[...] = grad_mid
    grad_branch_out[...] = (block(image, 2) * grad_mid).astype(LOW)
    sums_out[0:1, :] = jnp.sum(grad_mid * branch[...], axis=0, keepdims=True)
    sums_out[1:2, :] = jnp.sum(back, axis=0, keepdims=True)
    sums_out[2:3, :] = jnp.sum(back * norm, axis=0, keepdims=True)
    mlp_reduce.finish(mlp_total)
    mlp = mlp_total[...] + down_bias[...].astype(F32)
    sums_out[3:4, :] = jnp.sum(grad_out * mlp, axis=0, keepdims=True)
    block_own[...] = jnp.where(live, mid[...] + block(image, 5) * mlp, 0.0).astype(LOW)
    gather.close()
    reduce.close()
    mlp_reduce.close()


def feed(sizes, args):
    depth, images, kept, share, pieces = sizes
    width = args[1].shape[1]
    units = args[4].shape[1]
    rows = images * kept
    shape = jax.ShapeDtypeStruct
    return pl.pallas_call(
        functools.partial(feed_kernel, sizes),
        out_shape=(
            shape((PAIR, width, units), LOW),
            shape((PAIR, units, width), LOW),
            shape((PAIR, units), F32),
            shape((1, width), F32),
            shape((share, width), LOW),
            shape((share, width), F32),
            shape((share, width), LOW),
            shape((4, width), F32),
        ),
        in_specs=[SM, VM, HB] + [VM] * 10,
        out_specs=(VM,) * 8,
        scratch_shapes=[
            pltpu.VMEM((rows, width), LOW),
            pltpu.VMEM((rows, width), LOW),
            pltpu.VMEM((PAIR, rows, units), LOW),
            pltpu.VMEM((PAIR, rows, units), LOW),
            pltpu.VMEM((rows, width), LOW),
            pltpu.VMEM((rows, width), LOW),
            pltpu.VMEM((rows - share, width), LOW),
            pltpu.VMEM((rows, width), LOW),
            pltpu.VMEM((rows - share, width), LOW),
            pltpu.VMEM((share, width), F32),
            pltpu.VMEM((share, width), F32),
            pltpu.VMEM((PAIR, images, 1, units), F32),
            pltpu.VMEM((images, 1, width), F32),
            DMA((images,)),
            DMA,
        ]
        + Gather.scratch(depth, pieces)
        + Reduce.scratch(depth, pieces)
        + Reduce.scratch(depth, pieces),
        compiler_params=pltpu.CompilerParams(
            collective_id=2, has_side_effects=True, vmem_limit_bytes=60 << 20
        ),
        name="feed",
    )(*args)


def attend_back_kernel(
    sizes,
    groups,
    count,
    grad_own,
    normed,
    proj,
    attended,
    qkv_own,
    qkv_other,
    out_own,
    out_other,
    mod,
    tokens_own,
    grad_mid,
    block_own,
    up_grad,
    down_grad,
    qkv_grad,
    out_grad,
    qv_grad,
    out_bias_grad,
    grad_tokens,
    sums_out,
    block_out,
    up_total,
    down_total,
    grads,
    grad_proj,
    terms,
    landing,
    total,
    qv_sums,
    out_sums,
    own_sem,
    gather_send,
    gather_recv,
    send,
    recv,
    *rest,
):
    depth, images, kept, share, pieces = sizes
    me, up, side = place(depth)
    width = grad_own.shape[1]
    local = out_own.shape[0]
    scale = HD ** (-0.5)
    fold = depth // images
    first = side * images
    up_fold = Fold(up_grad, rest[:7], up_total, depth, groups, True)
    down_fold = Fold(down_grad, rest[7:14], down_total, depth, groups, True)
    spread = Spread(block_out, share, depth, pieces, rest[14:18])
    own_rows = pl.ds(pl.multiple_of(up * share, share), share)
    own_copy = pltpu.make_async_copy(grad_own, grads.at[own_rows, :], own_sem.at[0])
    own_copy.start()
    block_copy = pltpu.make_async_copy(block_own, spread.own(), own_sem.at[1])
    block_copy.start()
    meet(column_peers(depth) + cube_peers(depth, groups) + spread.peers_beyond(depth))
    own_copy.wait()
    gather = Gather(grads, share, depth, pieces, gather_send, gather_recv)
    reduce = Reduce(terms, landing, share, depth, pieces, send, recv)
    gather.open()
    up_fold.one()
    down_fold.one()
    block_copy.wait()

    def one(image):
        rows = pl.ds(pl.multiple_of(image * kept, kept), kept)
        key_live = lax.broadcasted_iota(jnp.int32, (1, kept), 1) < count[first + image]
        grad = grads[rows, :]
        out_sums[image] = jnp.sum(grad.astype(F32), axis=0, keepdims=True)
        back = None
        for shard, (qkv, out) in enumerate(((qkv_own, out_own), (qkv_other, out_other))):
            grad_att = dot_nt(grad, out[...]).astype(LOW)
            queries = proj[shard, 0, rows, :]
            keys = proj[shard, 1, rows, :]
            values = proj[shard, 2, rows, :]
            grad_q = jnp.zeros((kept, local), F32)
            grad_k = jnp.zeros((kept, local), F32)
            grad_v = jnp.zeros((kept, local), F32)
            for head in range(local // HD):
                mask = head_mask(head, local)
                head_q = jnp.where(mask, queries, 0.0).astype(LOW)
                head_grad = jnp.where(mask, grad_att, 0.0).astype(LOW)
                weights = softmax_rows(head_q, keys, key_live, scale)
                grad_weights = dot_nt(head_grad, values)
                inner = jnp.sum(weights * grad_weights, axis=-1, keepdims=True)
                grad_scores = (weights * (grad_weights - inner)).astype(LOW)
                grad_v = grad_v + dot_tn(weights.astype(LOW), head_grad)
                grad_q = grad_q + dot(grad_scores, jnp.where(mask, keys, 0.0).astype(LOW))
                grad_k = grad_k + dot_tn(grad_scores, head_q)
            for member, value in enumerate((grad_q * scale, grad_k * scale, grad_v)):
                low = value.astype(LOW)
                grad_proj[shard, member, rows, :] = low
                part = dot_nt(low, qkv[member])
                back = part if back is None else back + part
                if member != 1:
                    row = 2 * shard + member // 2
                    qv_sums[row, image] = jnp.sum(low.astype(F32), axis=0, keepdims=True)
        terms[rows, :] = back.astype(LOW)
        for part in range(fold):
            reduce.ready_share(image * fold + part)

    if fold == 1:

        def turn_of(turn, carry):
            @pl.when(turn == 1)
            def _():
                gather.relay()

            offset = turn + (turn // 2) * (1 - 2 * (turn % 2))
            gather.take(offset)
            one(across(up, offset, depth))

            @pl.when(turn == 0)
            def _():
                up_fold.two()
                down_fold.two()

            @pl.when(turn == 1)
            def _():
                spread.open()

            @pl.when(turn == 2)
            def _():
                up_fold.three()

            return carry

        lax.fori_loop(0, depth, turn_of, 0)
    else:

        def image_of(image, carry):
            one(image)
            return carry

        gather.relay()
        for offset in range(1, depth):
            gather.take(offset)
        up_fold.two()
        down_fold.two()
        spread.open()
        lax.fori_loop(0, images, image_of, 0)
        up_fold.three()

    def spread_of(turn, carry):
        spread.take(turn)
        return carry

    reduce.relay()
    lax.fori_loop(1, depth - 1, spread_of, 0)
    down_fold.three()
    spread.take(depth - 1)
    up_fold.four()
    for shard in range(PAIR):

        def tile(step, carry):
            columns = pl.ds(pl.multiple_of(step * 128, 128), 128)
            source = normed[:, columns]
            for member in range(3):
                start = member * width + step * 128
                qkv_grad[shard, pl.ds(pl.multiple_of(start, 128), 128), :] = dot_tn(
                    source, grad_proj[shard, member]
                ).astype(LOW)
            out_grad[shard, :, columns] = dot_tn(attended[shard], grads[:, columns]).astype(LOW)
            return carry

        lax.fori_loop(0, width // 128, tile, 0)
    down_fold.four()
    reduce.finish(total)
    for row in range(2 * PAIR):
        qv_grad[row : row + 1, :] = sum(qv_sums[row, image] for image in range(images))
    out_bias_grad[...] = sum(out_sums[image] for image in range(images))
    image = first + (up * share) // kept
    live = (
        lax.broadcasted_iota(jnp.int32, (share, 1), 0) + (up * share) % kept < count[image]
    )
    norm, spread_rows = norm_parts(tokens_own[...].astype(F32))
    back = total[...]
    scale_one = mod[pl.ds(image, 1), width : 2 * width]
    grad = grad_mid[...] + norm_back(norm, spread_rows, back * (1.0 + scale_one))
    grad_tokens[...] = jnp.where(live, grad, 0.0).astype(LOW)
    sums_out[0:1, :] = jnp.sum(back, axis=0, keepdims=True)
    sums_out[1:2, :] = jnp.sum(back * norm, axis=0, keepdims=True)
    up_fold.five()
    down_fold.five()
    for index in range(depth):
        spread.crossed(index)
    spread.close()
    gather.close()
    reduce.close()


def attend_back(sizes, groups, args):
    depth, images, kept, share, pieces = sizes
    width = args[1].shape[1]
    local = args[7].shape[0]
    up_grad, down_grad = args[-2:]
    rows = images * kept
    shape = jax.ShapeDtypeStruct
    return pl.pallas_call(
        functools.partial(attend_back_kernel, sizes, groups),
        out_shape=(
            shape((PAIR, 3 * width, local), LOW),
            shape((PAIR, local, width), LOW),
            shape((2 * PAIR, local), F32),
            shape((1, width), F32),
            shape((share, width), LOW),
            shape((2, width), F32),
            shape((PAIR * rows, width), LOW),
            shape(up_grad.shape[1:], F32),
            shape(down_grad.shape[1:], F32),
        ),
        in_specs=[SM] + [VM] * 14,
        out_specs=(VM,) * 9,
        scratch_shapes=[
            pltpu.VMEM((rows, width), LOW),
            pltpu.VMEM((PAIR, 3, rows, local), LOW),
            pltpu.VMEM((rows, width), LOW),
            pltpu.VMEM((rows - share, width), LOW),
            pltpu.VMEM((share, width), F32),
            pltpu.VMEM((2 * PAIR, images, 1, local), F32),
            pltpu.VMEM((images, 1, width), F32),
            DMA((2,)),
        ]
        + Gather.scratch(depth, pieces)
        + Reduce.scratch(depth, pieces)
        + Fold.scratch(up_grad.shape, groups, True)
        + Fold.scratch(down_grad.shape, groups, True)
        + Spread.scratch(depth, pieces),
        compiler_params=pltpu.CompilerParams(
            collective_id=3, has_side_effects=True, vmem_limit_bytes=62 << 20
        ),
        name="attend_back",
    )(*args)


def split_low(value):
    high = value.astype(LOW)
    rest = value - high.astype(F32)
    low = rest.astype(LOW)
    return high, low, (rest - low.astype(F32)).astype(LOW)


def close_kernel(
    sizes,
    groups,
    index,
    grad_tokens,
    sums,
    biases,
    qkv_grad,
    out_grad,
    silu_all,
    mod_weight,
    cond,
    grad_patches,
    qkv_total,
    out_total,
    bias_total,
    mod_weight_grad,
    mod_bias_grad,
    grad_cond,
    whole,
    sum_row,
    sum_land,
    bias_land,
    cond_land,
    own_sem,
    sum_send,
    sum_recv,
    bias_send,
    bias_recv,
    cond_send,
    cond_recv,
    *rest,
):
    depth, images, kept, share, pieces = sizes
    devices = depth * PAIR
    everyone = devices * groups
    me, up, side = place(depth)
    group = lax.axis_index("dp")
    flat = group * devices + me
    width = grad_tokens.shape[1]
    columns = mod_weight.shape[1]
    span = sum_land.shape[2]
    spread = Spread(whole, share, depth, pieces, rest[:4])
    qkv_fold = Fold(qkv_grad, rest[4:11], qkv_total, depth, groups, True)
    out_fold = Fold(out_grad, rest[11:18], out_total, depth, groups, False)
    own_copy = pltpu.make_async_copy(grad_tokens, spread.own(), own_sem)
    own_copy.start()
    barrier = pltpu.get_barrier_semaphore()

    def greet(step, carry):
        there = (flat + step) % everyone
        pl.semaphore_signal(
            barrier,
            inc=1,
            device_id={"dp": there // devices, "tensor": there % devices},
            device_id_type=MESH,
        )
        return carry

    lax.fori_loop(1, everyone, greet, 0)
    pl.semaphore_wait(barrier, everyone - 1)
    own_copy.wait()
    spread.open()
    qkv_fold.one()
    out_fold.one()

    def aligned(device):
        return pl.multiple_of((device * columns) // 128 * 128, 128)

    for member in range(6):
        sum_row[:, member * width : (member + 1) * width] = sums[member : member + 1, :]
    sum_row[:, 6 * width :] = jnp.zeros((1, sum_row.shape[1] - 6 * width), F32)

    def sum_copy(step):
        there = (flat + step) % everyone
        device = there % devices
        return remote(
            sum_row.at[:, pl.ds(aligned(device), span)],
            sum_land.at[flat],
            sum_send.at[step],
            sum_recv.at[step],
            device,
            there // devices,
        )

    def send_sum(step, carry):
        sum_copy(step).start()
        return carry

    lax.fori_loop(1, everyone, send_sum, 0)
    sum_land[flat] = sum_row[:, pl.ds(aligned(me), span)]
    slot = side * groups + group
    bias_land[slot] = biases[...]
    partner = me + depth * (1 - 2 * side)

    def bias_copy(step):
        crossed = step // groups
        there = (group + step) % groups
        device = jnp.where(crossed == 1, partner, me)
        return remote(
            biases, bias_land.at[slot], bias_send.at[step], bias_recv.at[step], device, there
        )

    for step in range(1, PAIR * groups):
        bias_copy(step).start()
    qkv_fold.two()
    out_fold.two()

    def wait_sum(step, carry):
        source = (flat + everyone - step) % everyone
        view = sum_land.at[source]
        remote(view, view, sum_send.at[step], sum_recv.at[step], me).wait_recv()
        return carry

    lax.fori_loop(1, everyone, wait_sum, 0)
    offset = (me * columns) % 128
    grads = jnp.concatenate([sum_land[device] for device in range(everyone)], axis=0)
    grads = pltpu.roll(grads, lax.rem(span - offset, span), 1)[:, :columns]
    mod_bias_grad[...] = jnp.sum(grads, axis=0, keepdims=True)
    total_images = images * PAIR

    def image_of(device):
        return device * share // kept

    source = lax.broadcasted_iota(jnp.int32, (everyone, groups * total_images), 0)
    target = lax.broadcasted_iota(jnp.int32, (everyone, groups * total_images), 1)
    row_image = source // devices * total_images + image_of(source % devices)
    chosen = jnp.where(row_image == target, 1.0, 0.0).astype(LOW)
    silu_rows = dot(
        chosen,
        jnp.concatenate([silu_all[member].astype(F32) for member in range(groups)], axis=0).astype(
            LOW
        ),
    ).astype(LOW)
    parts = split_low(grads)
    spread.take(1)
    mod_weight_grad[...] = (
        dot_tn(silu_rows, parts[0]) + dot_tn(silu_rows, parts[1]) + dot_tn(silu_rows, parts[2])
    )
    source = lax.broadcasted_iota(jnp.int32, (total_images, everyone), 1)
    target = lax.broadcasted_iota(jnp.int32, (total_images, everyone), 0)
    chosen = jnp.where(
        (source // devices == group) & (image_of(source % devices) == target), 1.0, 0.0
    ).astype(LOW)
    mine = dot(chosen, parts[0]) + dot(chosen, parts[1]) + dot(chosen, parts[2])
    parts = split_low(mine)
    term = (
        dot_nt(parts[0], mod_weight[...])
        + dot_nt(parts[1], mod_weight[...])
        + dot_nt(parts[2], mod_weight[...])
    )
    cond_land[me] = term

    def cond_copy(step):
        return remote(
            cond_land.at[me],
            cond_land.at[me],
            cond_send.at[step],
            cond_recv.at[step],
            (me + step) % devices,
        )

    for step in range(1, devices):
        cond_copy(step).start()
    qkv_fold.three()
    out_fold.three()
    for turn in range(2, depth):
        spread.take(turn)
    for step in range(1, PAIR * groups):
        crossed = step // groups
        source_group = (group + groups - step % groups) % groups
        source_side = jnp.where(crossed == 1, 1 - side, side)
        view = bias_land.at[source_side * groups + source_group]
        remote(view, view, bias_send.at[step], bias_recv.at[step], me).wait_recv()
    rows = biases.shape[0]
    result = jnp.zeros((rows, width), F32)
    for member in range(PAIR * groups):
        value = bias_land[member]
        turned = jnp.concatenate([value[3:6, :], value[0:3, :], value[6:, :]], axis=0)
        same = side == member // groups
        result = result + jnp.where(same, value, turned)
    bias_total[...] = result
    for step in range(1, devices):
        source = (me + devices - step) % devices
        view = cond_land.at[source]
        remote(view, view, cond_send.at[step], cond_recv.at[step], me).wait_recv()
    back = cond_land[0]
    for device in range(1, devices):
        back = back + cond_land[device]
    value = cond[...].astype(F32)
    gate = 1.0 / (1.0 + jnp.exp(-value))
    grad_cond[...] = (back * (gate + value * gate * (1.0 - gate))).astype(LOW)
    qkv_fold.four()
    out_fold.four()

    def place_image(image):
        rows = pl.ds(pl.multiple_of(image * kept, kept), kept)
        spots = lax.broadcasted_iota(jnp.int32, (grad_patches.shape[1], kept), 0)
        pick = jnp.where(spots == index[image], 1.0, 0.0).astype(LOW)
        grad_patches[image] = dot(pick, whole[rows, :]).astype(LOW)

    for index_of in range(depth):
        spread.crossed(index_of)

    def put(image, carry):
        place_image(image)
        return carry

    lax.fori_loop(0, PAIR * images, put, 0)
    qkv_fold.five()
    out_fold.five()
    spread.close()

    def done_sum(step, carry):
        sum_copy(step).wait_send()
        return carry

    lax.fori_loop(1, everyone, done_sum, 0)
    for step in range(1, PAIR * groups):
        bias_copy(step).wait_send()
    for step in range(1, devices):
        cond_copy(step).wait_send()


def close(sizes, groups, args):
    depth, images, kept, share, pieces = sizes
    index, grad_tokens, sums, biases, qkv_grad, out_grad, silu_all, mod_weight, cond, spots = args
    devices = depth * PAIR
    width = grad_tokens.shape[1]
    columns = mod_weight.shape[1]
    span = max(-(-((device * columns) % 128 + columns) // 128) * 128 for device in range(devices))
    long = max((device * columns) // 128 * 128 + span for device in range(devices))
    long = max(long, 6 * width + 128)
    shape = jax.ShapeDtypeStruct
    rows = PAIR * images * kept
    everyone = devices * groups
    return pl.pallas_call(
        functools.partial(close_kernel, sizes, groups),
        out_shape=(
            shape((PAIR * images, spots, width), LOW),
            shape(qkv_grad.shape[1:], F32),
            shape(out_grad.shape[1:], F32),
            shape(biases.shape, F32),
            shape(mod_weight.shape, F32),
            shape((1, columns), F32),
            shape(cond.shape, LOW),
        ),
        in_specs=[VM] * 9,
        out_specs=(VM,) * 7,
        scratch_shapes=[
            pltpu.VMEM((rows, width), LOW),
            pltpu.VMEM((1, long), F32),
            pltpu.VMEM((everyone, 1, span), F32),
            pltpu.VMEM((PAIR * groups,) + biases.shape, F32),
            pltpu.VMEM((devices,) + cond.shape, F32),
            DMA,
            DMA((everyone,)),
            DMA((everyone,)),
            DMA((PAIR * groups,)),
            DMA((PAIR * groups,)),
            DMA((devices,)),
            DMA((devices,)),
        ]
        + Spread.scratch(depth, pieces)
        + Fold.scratch(qkv_grad.shape, groups, True)
        + Fold.scratch(out_grad.shape, groups, False),
        compiler_params=pltpu.CompilerParams(
            collective_id=4, has_side_effects=True, vmem_limit_bytes=62 << 20
        ),
        name="close",
    )(*args[:-1])


def on_device(
    patches,
    conditioning,
    keep_count,
    keep_index,
    mod_weight,
    mod_bias,
    qkv_weight,
    qv_bias,
    out_weight,
    out_bias,
    up_weight,
    up_bias,
    down_weight,
    down_bias,
    out_cotangent,
):
    devices = lax.axis_size("tensor")
    depth = devices // PAIR
    all_images, kept = keep_index.shape
    width = patches.shape[2]
    images = all_images // PAIR
    share = images * kept // depth
    pieces = 4 if share % 64 == 0 else 2
    sizes = (depth, images, kept, share, pieces)
    groups = lax.axis_size("dp")
    index = keep_index[:, None, :]
    qkv_local, units = qkv_weight.shape[2], up_weight.shape[1]
    up_bias_row = up_bias[None, :]
    (
        normed_one,
        proj,
        attended,
        tokens_own,
        mid,
        branch,
        normed_two,
        mod,
        silu_all,
        qkv_other,
        qv_other,
        out_other,
        up_other,
        down_other,
        up_bias_other,
    ) = attend(
        sizes,
        groups,
        (
            keep_count,
            index,
            patches,
            conditioning,
            mod_weight,
            mod_bias[None, :],
            qkv_weight,
            qv_bias,
            out_weight,
            out_bias[None, :],
            up_weight,
            down_weight,
            up_bias_row,
        ),
    )
    (
        up_grad,
        down_grad,
        up_bias_grad,
        down_bias_grad,
        block_own,
        grad_mid,
        grad_branch,
        sums_two,
    ) = feed(
        sizes,
        (
            keep_count,
            normed_two,
            out_cotangent,
            mod,
            up_weight,
            up_other,
            up_bias_row,
            up_bias_other,
            down_weight,
            down_other,
            down_bias[None, :],
            mid,
            branch,
        ),
    )
    (
        qkv_grad,
        out_grad,
        qv_grad,
        out_bias_grad,
        grad_tokens,
        sums_one,
        block_out,
        up_total,
        down_total,
    ) = attend_back(
        sizes,
        groups,
        (
            keep_count,
            grad_branch,
            normed_one,
            proj,
            attended,
            qkv_weight,
            qkv_other,
            out_weight,
            out_other,
            mod,
            tokens_own,
            grad_mid,
            block_own,
            up_grad,
            down_grad,
        ),
    )

    def row(value):
        return jnp.pad(value, ((0, 0), (0, width - value.shape[1])))

    biases = jnp.concatenate(
        [
            row(up_bias_grad[0:1]),
            row(qv_grad[0:2]),
            row(up_bias_grad[1:2]),
            row(qv_grad[2:4]),
            down_bias_grad,
            out_bias_grad,
        ]
    )
    sums = jnp.concatenate([sums_one, sums_two])
    (
        grad_patches,
        qkv_total,
        out_total,
        bias_total,
        mod_weight_grad,
        mod_bias_grad,
        grad_conditioning,
    ) = close(
        sizes,
        groups,
        (
            index,
            grad_tokens,
            sums,
            biases,
            qkv_grad,
            out_grad,
            silu_all,
            mod_weight,
            conditioning,
            patches.shape[1],
        ),
    )
    return (
        block_out.reshape(all_images, kept, width),
        grad_patches,
        grad_conditioning,
        mod_weight_grad,
        mod_bias_grad[0],
        qkv_total.reshape(qkv_weight.shape),
        bias_total[1:3, :qkv_local],
        out_total,
        bias_total[7],
        up_total,
        bias_total[0, :units],
        down_total,
        bias_total[6],
    )


def solution(mesh):
    placed = (
        P("dp", None, None),
        P("dp", None),
        P("dp"),
        P("dp", None),
        P(None, "tensor"),
        P("tensor"),
        P(None, None, "tensor"),
        P(None, "tensor"),
        P("tensor", None),
        P(),
        P(None, "tensor"),
        P("tensor"),
        P("tensor", None),
        P(),
        P("dp", None, None),
    )
    return jax.shard_map(
        on_device,
        mesh=mesh,
        in_specs=placed,
        out_specs=(
            P("dp", None, None),
            P("dp", None, None),
            P("dp", None),
            P(None, "tensor"),
            P("tensor"),
            P(None, None, "tensor"),
            P(None, "tensor"),
            P("tensor", None),
            P(),
            P(None, "tensor"),
            P("tensor"),
            P("tensor", None),
            P(),
        ),
        check_vma=False,
    )
```

```python
import functools

import jax
import jax.numpy as jnp
from jax import lax
from jax.experimental import pallas as pl
from jax.experimental.pallas import tpu as pltpu
from jax.sharding import PartitionSpec as P

HD = 72
MESH = pl.DeviceIdType.MESH
F32 = jnp.float32
LOW = jnp.bfloat16
DMA = pltpu.SemaphoreType.DMA
VM = pl.BlockSpec(memory_space=pltpu.VMEM)
SM = pl.BlockSpec(memory_space=pltpu.SMEM)
HB = pl.BlockSpec(memory_space=pl.ANY)
PAIR = 2
GELU_ROOT = 0.7978845608028654
GELU_CUBE = 0.044715


def remote(source, target, send_sem, recv_sem, device, group=None):
    there = {"tensor": device} if group is None else {"dp": group, "tensor": device}
    return pltpu.make_async_remote_copy(
        src_ref=source,
        dst_ref=target,
        send_sem=send_sem,
        recv_sem=recv_sem,
        device_id=there,
        device_id_type=MESH,
    )


def place(depth):
    me = lax.axis_index("tensor")
    return me, me % depth, me // depth


def bits_of(depth):
    return depth.bit_length() - 1


def toward(spot, bit):
    return (1 - 2 * ((spot // (1 << bit)) % 2)) * (1 << bit)


def across(spot, offset, depth):
    result = spot
    for bit in range(bits_of(depth)):
        result = result + ((offset // (1 << bit)) % 2) * toward(spot, bit)
    return result


def offset_between(left, right, depth):
    result = 0
    for bit in range(bits_of(depth)):
        size = 1 << bit
        result = result + ((left // size + right // size) % 2) * size
    return result


def meet(peers):
    barrier = pltpu.get_barrier_semaphore()
    for group, peer in peers:
        pl.semaphore_signal(
            barrier, inc=1, device_id={"dp": group, "tensor": peer}, device_id_type=MESH
        )
    pl.semaphore_wait(barrier, len(peers))


def column_peers(depth):
    me, spot, side = place(depth)
    group = lax.axis_index("dp")
    return [(group, me + toward(spot, bit)) for bit in range(bits_of(depth))]


def cube_peers(depth, groups):
    me, spot, side = place(depth)
    group = lax.axis_index("dp")
    other = me + depth * (1 - 2 * side)
    peers = [((group + step) % groups, me) for step in range(1, groups)]
    return peers + [((group + step) % groups, other) for step in range(groups)]


def padded(rows, groups):
    return -(-rows // (16 * groups)) * 16 * groups


def lanes(columns):
    return -(-columns // 128) * 128


def row_spots(width, units, local, mods):
    spots = {}
    start = 0
    for name, size in (
        ("out", width),
        ("down", width),
        ("up", units),
        ("query", local),
        ("value", local),
        ("mod", mods),
    ):
        spots[name] = start
        start += lanes(size)
    return spots, start


def tile_of(width):
    return 384 if width % 384 == 0 else 128


def dot(left, right):
    return jnp.dot(left, right, preferred_element_type=F32)


def dot_nt(left, right):
    return lax.dot_general(left, right, (((1,), (1,)), ((), ())), preferred_element_type=F32)


def dot_tn(left, right):
    return lax.dot_general(left, right, (((0,), (0,)), ((), ())), preferred_element_type=F32)


def norm_parts(rows):
    width = rows.shape[-1]
    centred = rows - jnp.sum(rows, axis=-1, keepdims=True) * (1.0 / width)
    spread = lax.rsqrt(jnp.sum(centred * centred, axis=-1, keepdims=True) * (1.0 / width) + 1e-06)
    return centred * spread, spread


def norm_back(norm, spread, grad):
    width = norm.shape[-1]
    mean_grad = jnp.sum(grad, axis=-1, keepdims=True) * (1.0 / width)
    mean_both = jnp.sum(grad * norm, axis=-1, keepdims=True) * (1.0 / width)
    return (grad - mean_grad - norm * mean_both) * spread


class Line:
    def __init__(self, buffer, share, depth, pieces, send, recv):
        self.buffer, self.share, self.depth, self.pieces = buffer, share, depth, pieces
        self.send, self.recv = send, recv
        self.me = lax.axis_index("tensor")
        self.up, self.side = self.me // PAIR, self.me % PAIR

    def piece(self, index, part):
        rows = self.share // self.pieces
        start = (index * PAIR + self.side) * self.share + part * rows
        return self.buffer.at[pl.ds(pl.multiple_of(start, rows), rows), :]

    def copy(self, way, step, part):
        source = self.up - (step - 1) * (1 - 2 * way)
        target = self.up + 1 - 2 * way
        view = self.piece(source, part)
        return remote(
            view,
            view,
            self.send.at[way, step, part],
            self.recv.at[way, step, part],
            target * PAIR + self.side,
        )

    def may_send(self, way, step):
        if way == 0:
            return (self.up + 1 < self.depth) & (self.up >= step - 1)
        return (self.up >= 1) & (self.up + step - 1 < self.depth)

    def open(self):
        for part in range(self.pieces):
            for way in range(2):

                @pl.when(self.may_send(way, 1))
                def _():
                    self.copy(way, 1, part).start()

    def arrival(self, turn):
        below = self.up
        above = self.depth - 1 - self.up
        both = jnp.minimum(below, above)
        mixed = turn <= 2 * both
        way = jnp.where(mixed, (turn + 1) % 2, jnp.where(below > above, 0, 1))
        step = jnp.where(mixed, (turn + 1) // 2, turn - both)
        return way, step, self.up - step * (1 - 2 * way)

    def take(self, turn, then):
        way, step, source = self.arrival(turn)
        ahead = jnp.where(way == 0, self.up + 1 < self.depth, self.up >= 1)
        for part in range(self.pieces):
            view = self.piece(source, part)
            remote(
                view, view, self.send.at[way, step, part], self.recv.at[way, step, part], self.me
            ).wait_recv()

            @pl.when(ahead)
            def _():
                self.copy(way, step + 1, part).start()

            then(source, part)

    def close(self):
        for way in range(2):
            for step in range(1, self.depth):

                @pl.when(self.may_send(way, step))
                def _():
                    for part in range(self.pieces):
                        self.copy(way, step, part).wait_send()


class Cube:
    def __init__(self, share, depth, pieces):
        self.share, self.depth, self.pieces = share, depth, pieces
        self.me, self.spot, self.side = place(depth)
        self.bits = bits_of(depth)
        self.rows = share // pieces

    def order(self, part):
        ways = list(range(self.bits))
        return ways if part % 2 else ways[::-1]

    def span(self, index, part):
        return pl.ds(pl.multiple_of(index * self.share + part * self.rows, self.rows), self.rows)

    def neighbour(self, bit):
        return self.me + toward(self.spot, bit)


class Gather(Cube):
    def __init__(self, buffer, share, depth, pieces, send, recv):
        super().__init__(share, depth, pieces)
        self.buffer, self.send, self.recv = buffer, send, recv

    def last(self, offset, part):
        order = self.order(part)
        return max(
            (stage for stage in range(self.bits) if offset >> order[stage] & 1), default=-1
        )

    def copy(self, offset, stage, part):
        bit = self.order(part)[stage]
        view = self.buffer.at[self.span(across(self.spot, offset, self.depth), part), :]
        return remote(
            view,
            view,
            self.send.at[offset, stage, part],
            self.recv.at[offset ^ (1 << bit), part],
            self.neighbour(bit),
        )

    def landed(self, offset, part):
        view = self.buffer.at[self.span(across(self.spot, offset, self.depth), part), :]
        remote(
            view, view, self.send.at[0, 0, part], self.recv.at[offset, part], self.me
        ).wait_recv()

    def sends(self, offset):
        return [
            (stage, part)
            for part in range(self.pieces)
            for stage in range(self.last(offset, part) + 1, self.bits)
        ]

    def open(self):
        for stage, part in self.sends(0):
            self.copy(0, stage, part).start()

    def relay(self):
        for offset in sorted(range(1, self.depth), key=lambda value: bin(value).count("1")):
            for part in range(self.pieces):
                first = self.last(offset, part) + 1
                if first < self.bits:
                    self.landed(offset, part)
                    for stage in range(first, self.bits):
                        self.copy(offset, stage, part).start()

    def take(self, offset):
        for member in range(1, self.depth):

            @pl.when(offset == member)
            def _():
                for part in range(self.pieces):
                    if self.last(member, part) + 1 == self.bits:
                        self.landed(member, part)

    def close(self):
        for offset in range(self.depth):
            for stage, part in self.sends(offset):
                self.copy(offset, stage, part).wait_send()

    @staticmethod
    def scratch(depth, pieces):
        return [DMA((depth, bits_of(depth), pieces)), DMA((depth, pieces))]


class Reduce(Cube):
    def __init__(self, terms, landing, share, depth, pieces, send, recv):
        super().__init__(share, depth, pieces)
        self.terms, self.landing, self.send, self.recv = terms, landing, send, recv

    def slot(self, stage, offset, part):
        order = self.order(part)
        found = [
            (level, member)
            for level in range(self.bits)
            for member in range(self.depth)
            if not any(member >> order[below] & 1 for below in range(level + 1))
        ]
        return found.index((stage, offset))

    def first(self, offset, part):
        order = self.order(part)
        return min(stage for stage in range(self.bits) if offset >> order[stage] & 1)

    def copy(self, offset, part):
        stage = self.first(offset, part)
        bit = self.order(part)[stage]
        slot = self.slot(stage, offset ^ (1 << bit), part)
        return remote(
            self.terms.at[self.span(across(self.spot, offset, self.depth), part), :],
            self.landing.at[self.span(slot, part), :],
            self.send.at[offset, part],
            self.recv.at[slot, part],
            self.neighbour(bit),
        )

    def landed(self, slot, part):
        view = self.landing.at[self.span(slot, part), :]
        remote(view, view, self.send.at[0, part], self.recv.at[slot, part], self.me).wait_recv()

    def ready(self, offset):
        for member in range(1, self.depth):

            @pl.when(offset == member)
            def _():
                for part in range(self.pieces):
                    if self.first(member, part) == 0:
                        self.copy(member, part).start()

    def ready_share(self, index):
        self.ready(offset_between(index, self.spot, self.depth))

    def add(self, target, target_start, term_start, slots, part):
        def body(index, carry):
            offset = index * 16
            value = self.terms[pl.ds(pl.multiple_of(term_start + offset, 16), 16), :].astype(F32)
            for slot in slots:
                start = slot * self.share + part * self.rows
                value = value + self.landing[
                    pl.ds(pl.multiple_of(start + offset, 16), 16), :
                ].astype(F32)
            target[pl.ds(pl.multiple_of(target_start + offset, 16), 16), :] = value.astype(
                target.dtype
            )
            return carry

        lax.fori_loop(0, self.rows // 16, body, 0)

    def relay(self):
        for level in range(1, self.bits):
            for part in range(self.pieces):
                for offset in range(1, self.depth):
                    if self.first(offset, part) == level:
                        slots = [self.slot(below, offset, part) for below in range(level)]
                        for slot in slots:
                            self.landed(slot, part)
                        start = (
                            across(self.spot, offset, self.depth) * self.share + part * self.rows
                        )
                        self.add(self.terms, start, start, slots, part)
                        self.copy(offset, part).start()

    def finish(self, total):
        for part in range(self.pieces):
            slots = [self.slot(stage, 0, part) for stage in range(self.bits)]
            for slot in slots:
                self.landed(slot, part)
            skip = part * self.rows
            self.add(total, skip, self.spot * self.share + skip, slots, part)

    def close(self):
        for offset in range(1, self.depth):
            for part in range(self.pieces):
                self.copy(offset, part).wait_send()

    @staticmethod
    def scratch(depth, pieces):
        return [DMA((depth, pieces)), DMA((depth - 1, pieces))]


class Fold:
    def __init__(self, source, scratch, out, depth, groups):
        self.source, self.out = source, out
        (
            self.stage,
            self.near,
            self.land,
            self.part,
            self.side_land,
            self.low,
            self.send,
            self.recv,
        ) = scratch
        self.me = lax.axis_index("tensor")
        self.group = lax.axis_index("dp")
        self.lines = groups // PAIR
        self.core = self.group % PAIR
        self.line = self.group // PAIR
        self.mate = self.group + 1 - 2 * self.core
        self.partner = self.me + depth * (1 - 2 * (self.me // depth))
        self.rows = self.part.shape[1]
        self.half = self.rows * self.lines

    @staticmethod
    def scratch(shape, groups):
        _, rows, width = shape
        lines = groups // PAIR
        part = rows // groups
        return [
            pltpu.VMEM((PAIR, part * lines, width), LOW),
            pltpu.VMEM((PAIR, part * lines, width), LOW),
            pltpu.VMEM((lines, PAIR, part, width), LOW),
            pltpu.VMEM((PAIR, part, width), LOW),
            pltpu.VMEM((part, width), LOW),
            pltpu.VMEM((rows, width), LOW),
            DMA((2 + 3 * lines,)),
            DMA((2 + 3 * lines,)),
        ]

    def each(self, rows, body):
        step = 48 if rows % 48 == 0 else 16 if rows % 16 == 0 else rows

        def run(index, carry):
            body(pl.multiple_of(index * step, step), step)
            return carry

        lax.fori_loop(0, rows // step, run, 0)

    def window(self, start, size):
        return pl.ds(pl.multiple_of(start, 16), size)

    def behind(self, step):
        return (self.line + self.lines - step) % self.lines

    def block(self, core, line):
        return self.low.at[self.window(core * self.half + line * self.rows, self.rows), :]

    def near_copy(self):
        return remote(
            self.source.at[:, self.window((1 - self.core) * self.half, self.half), :],
            self.near,
            self.send.at[0],
            self.recv.at[0],
            self.me,
            self.mate,
        )

    def cross_copy(self, step):
        line = (self.line + step) % self.lines
        return remote(
            self.stage.at[:, self.window(line * self.rows, self.rows), :],
            self.land.at[self.line],
            self.send.at[2 + step],
            self.recv.at[2 + step],
            self.me,
            line * PAIR + self.core,
        )

    def side_copy(self):
        return remote(
            self.part.at[1],
            self.side_land,
            self.send.at[1],
            self.recv.at[1],
            self.partner,
            self.group,
        )

    def line_copy(self, step):
        line = (self.line + step) % self.lines
        view = self.block(self.core, self.line)
        slot = 2 + self.lines + step
        return remote(
            view,
            view,
            self.send.at[slot],
            self.recv.at[slot],
            self.me,
            line * PAIR + self.core,
        )

    def mate_copy(self, core, line):
        view = self.block(core, line)
        slot = 2 + 2 * self.lines + line
        return remote(view, view, self.send.at[slot], self.recv.at[slot], self.me, self.mate)

    def one(self):
        self.near_copy().start()

    def two(self):
        self.near_copy().wait_recv()

        def add(at, size):
            rows = self.window(at, size)
            for shard in range(PAIR):
                mine = self.source[shard, self.window(self.core * self.half + at, size), :]
                self.stage[shard, rows, :] = (
                    mine.astype(F32) + self.near[shard, rows, :].astype(F32)
                ).astype(LOW)

        self.each(self.half, add)
        for step in range(1, self.lines):
            self.cross_copy(step).start()

    def three(self):
        for step in range(1, self.lines):
            view = self.land.at[self.behind(step)]
            remote(
                view, view, self.send.at[2 + step], self.recv.at[2 + step], self.me, self.mate
            ).wait_recv()

        def add(at, size):
            rows = self.window(at, size)
            for shard in range(PAIR):
                value = self.stage[
                    shard, self.window(self.line * self.rows + at, size), :
                ].astype(F32)
                for step in range(1, self.lines):
                    value = value + self.land[self.behind(step), shard, rows, :].astype(F32)
                self.part[shard, rows, :] = value.astype(LOW)

        self.each(self.rows, add)
        self.side_copy().start()

    def four(self):
        self.side_copy().wait_recv()

        def add(at, size):
            rows = self.window(at, size)
            value = self.part[0, rows, :].astype(F32) + self.side_land[rows, :].astype(F32)
            spot = self.window(self.core * self.half + self.line * self.rows + at, size)
            self.low[spot, :] = value.astype(LOW)

        self.each(self.rows, add)
        for step in range(1, self.lines):
            self.line_copy(step).start()
        self.mate_copy(self.core, self.line).start()

    def five(self):
        for step in range(1, self.lines):
            line = self.behind(step)
            view = self.block(self.core, line)
            slot = 2 + self.lines + step
            remote(
                view, view, self.send.at[slot], self.recv.at[slot], self.me, self.mate
            ).wait_recv()
            self.mate_copy(self.core, line).start()

    def six(self):
        for line in range(self.lines):
            self.mate_copy(1 - self.core, line).wait_recv()

        def put(at, size):
            rows = pl.ds(at, size)
            self.out[rows, :] = self.low[rows, :].astype(F32)

        self.each(self.out.shape[0], put)
        self.near_copy().wait_send()
        self.side_copy().wait_send()
        for step in range(1, self.lines):
            self.cross_copy(step).wait_send()
            self.line_copy(step).wait_send()
        for line in range(self.lines):
            self.mate_copy(self.core, line).wait_send()


class Spread:
    def __init__(self, whole, share, depth, pieces, scratch):
        self.whole, self.share, self.depth, self.pieces = whole, share, depth, pieces
        send, recv, self.side_send, self.side_recv = scratch
        self.line = Line(whole, share, depth, pieces, send, recv)
        self.me, self.up, self.side = self.line.me, self.line.up, self.line.side

    @staticmethod
    def scratch(depth, pieces):
        return [
            DMA((2, depth, pieces)),
            DMA((2, depth, pieces)),
            DMA((depth, pieces)),
            DMA((depth, pieces)),
        ]

    def peers(self):
        group = lax.axis_index("dp")
        line = [
            (group, (self.up + step) % self.depth * PAIR + self.side)
            for step in range(1, self.depth)
        ]
        return line + [(group, self.me + 1 - 2 * self.side)]

    def peers_beyond(self, depth):
        me, spot, side = place(depth)
        group = lax.axis_index("dp")
        return [
            (group, (self.up + step) % self.depth * PAIR + self.side)
            for step in range(1, self.depth)
        ]

    def view(self, side, index, part):
        rows = self.share // self.pieces
        start = (index * PAIR + side) * self.share + part * rows
        return self.whole.at[pl.ds(pl.multiple_of(start, rows), rows), :]

    def own(self):
        return self.whole.at[pl.ds(pl.multiple_of(self.me * self.share, self.share), self.share), :]

    def across(self, index, part):
        view = self.view(self.side, index, part)
        return remote(
            view,
            view,
            self.side_send.at[index, part],
            self.side_recv.at[index, part],
            self.me + 1 - 2 * self.side,
        )

    def open(self):
        self.line.open()
        for part in range(self.pieces):
            self.across(self.up, part).start()

    def take(self, turn):
        self.line.take(turn, lambda source, part: self.across(source, part).start())

    def crossed(self, index):
        for part in range(self.pieces):
            view = self.view(1 - self.side, index, part)
            remote(
                view, view, self.side_send.at[index, part], self.side_recv.at[index, part], self.me
            ).wait_recv()

    def close(self):
        self.line.close()
        for index in range(self.depth):
            for part in range(self.pieces):
                self.across(index, part).wait_send()


class Share:
    def __init__(self, source, target, send, recv, which, depth, groups):
        self.source, self.target = source, target
        self.send, self.recv, self.which = send, recv, which
        self.me, _, side = place(depth)
        self.group = lax.axis_index("dp")
        self.partner = self.me + depth * (1 - 2 * side)
        rows = source.shape[0]
        self.all_lines = groups // PAIR
        self.cores = PAIR if rows % (PAIR * 16) == 0 else 1
        self.lines = self.all_lines if rows % (groups * 16) == 0 else 1
        self.rows = rows // (self.cores * self.lines)
        self.core = self.group % PAIR
        self.line = self.group // PAIR
        self.my_core = self.core if self.cores > 1 else 0
        self.my_line = self.line if self.lines > 1 else 0

    @staticmethod
    def scratch(members, groups):
        lines = groups // PAIR
        return [DMA((members, 1 + 2 * lines)), DMA((members, 1 + 2 * lines))]

    def view(self, array, core, line):
        if self.cores == 1:
            return array
        start = (core * self.lines + line) * self.rows
        return array.at[pl.ds(pl.multiple_of(start, 16), self.rows), :]

    def behind(self, step):
        return (self.line + self.lines - step) % self.lines

    def copy(self):
        return remote(
            self.view(self.source, self.my_core, self.my_line),
            self.view(self.target, self.my_core, self.my_line),
            self.send.at[self.which, 0],
            self.recv.at[self.which, 0],
            self.partner,
        )

    def hand(self, step):
        view = self.view(self.target, self.my_core, self.my_line)
        return remote(
            view,
            view,
            self.send.at[self.which, step],
            self.recv.at[self.which, step],
            self.me,
            (self.line + step) % self.lines * PAIR + self.core,
        )

    def mate(self, core, line):
        view = self.view(self.target, core, line)
        slot = self.all_lines + line
        return remote(
            view,
            view,
            self.send.at[self.which, slot],
            self.recv.at[self.which, slot],
            self.me,
            self.group + 1 - 2 * self.core,
        )

    def start(self):
        self.copy().start()

    def pass_on(self):
        self.copy().wait_recv()
        for step in range(1, self.lines):
            self.hand(step).start()
        if self.cores > 1:
            self.mate(self.core, self.my_line).start()

    def relay(self):
        for step in range(1, self.lines):
            line = self.behind(step)
            view = self.view(self.target, self.core, line)
            remote(
                view,
                view,
                self.send.at[self.which, step],
                self.recv.at[self.which, step],
                self.me,
                self.group,
            ).wait_recv()
            self.mate(self.core, line).start()

    def wait(self):
        if self.cores > 1:
            for line in range(self.lines):
                self.mate(1 - self.core, line).wait_recv()

    def close(self):
        self.copy().wait_send()
        for step in range(1, self.lines):
            self.hand(step).wait_send()
        if self.cores > 1:
            for line in range(self.lines):
                self.mate(self.core, line).wait_send()


def head_mask(head, width):
    lane = lax.broadcasted_iota(jnp.int32, (1, width), 1)
    return (lane >= head * HD) & (lane < (head + 1) * HD)


def softmax_rows(queries, keys, key_live, scale):
    scores = dot_nt(queries, keys) * scale
    scores = jnp.where(key_live, scores, -1e30)
    top = jnp.max(scores, axis=-1, keepdims=True)
    raised = jnp.exp(scores - top)
    return raised / jnp.sum(raised, axis=-1, keepdims=True)


def attend_shard(normed, heads, row, spots, proj_out, shard, rows, key_live, scale):
    local = heads.shape[0] // 4
    query_bias = row[:, spots["query"] : spots["query"] + local]
    value_bias = row[:, spots["value"] : spots["value"] + local]
    queries = (dot_nt(normed, heads[0:local, :]) + query_bias).astype(LOW)
    keys = dot_nt(normed, heads[local : 2 * local, :]).astype(LOW)
    values = (dot_nt(normed, heads[2 * local : 3 * local, :]) + value_bias).astype(LOW)
    proj_out[shard, 0, rows, :] = queries
    proj_out[shard, 1, rows, :] = keys
    proj_out[shard, 2, rows, :] = values
    attended = jnp.zeros((normed.shape[0], local), F32)
    for head in range(local // HD):
        mask = head_mask(head, local)
        weights = softmax_rows(jnp.where(mask, queries, 0.0).astype(LOW), keys, key_live, scale)
        attended = attended + dot(weights.astype(LOW), jnp.where(mask, values, 0.0).astype(LOW))
    return attended.astype(LOW)


def attend_kernel(
    sizes,
    groups,
    count,
    index,
    patches,
    cond,
    mod_weight,
    heads_own,
    up_own,
    down_own,
    row_own,
    normed_out,
    proj_out,
    attended_out,
    tokens_own,
    mid_out,
    branch_out,
    normed_two_out,
    mod,
    silu_all,
    heads_other,
    up_other,
    down_other,
    row_other,
    patch_rows,
    tokens,
    terms,
    landing,
    total,
    mod_mine,
    mod_gathered,
    patch_sem,
    send,
    recv,
    mod_send,
    mod_recv,
    silu_send,
    silu_recv,
    weight_send,
    weight_recv,
):
    depth, images, kept, share, pieces = sizes
    devices = depth * PAIR
    me, up, side = place(depth)
    group = lax.axis_index("dp")
    width = patches.shape[2]
    local = heads_own.shape[0] // 4
    mods = mod_weight.shape[0]
    spots, _ = row_spots(width, up_own.shape[0], local, mods)
    scale = HD ** (-0.5)
    fold = depth // images
    first = side * images

    def fetch(image):
        return pltpu.make_async_copy(
            patches.at[first + image], patch_rows.at[image], patch_sem.at[image]
        )

    def image_at(turn):
        return across(up // fold, images - 1 - turn, images)

    for turn in range(images):
        fetch(image_at(turn)).start()
    meet(
        [(group, (me + step) % devices) for step in range(1, devices)]
        + [((group + step) % groups, me) for step in range(1, groups)]
    )
    value = cond[...].astype(F32)
    silu = (value / (1.0 + jnp.exp(-value))).astype(LOW)
    silu_all[group] = silu
    local_mod = (
        dot_nt(silu, mod_weight[...]) + row_own[:, spots["mod"] : spots["mod"] + mods]
    ).astype(LOW)
    mod_mine[...] = local_mod
    mod_gathered[me] = local_mod
    mod_copies = [
        remote(
            mod_mine,
            mod_gathered.at[me],
            mod_send.at[step],
            mod_recv.at[step],
            (me + step) % devices,
        )
        for step in range(1, devices)
    ]
    silu_copies = [
        remote(
            silu_all.at[group],
            silu_all.at[group],
            silu_send.at[step],
            silu_recv.at[step],
            me,
            (group + step) % groups,
        )
        for step in range(1, groups)
    ]
    for copy in mod_copies + silu_copies:
        copy.start()

    shares = [
        Share(source, target, weight_send, weight_recv, which, depth, groups)
        for which, (source, target) in enumerate(
            (
                (row_own, row_other),
                (heads_own, heads_other),
                (up_own, up_other),
                (down_own, down_other),
            )
        )
    ]
    for member in shares:
        member.start()
    reduce = Reduce(terms, landing, share, depth, pieces, send, recv)

    def pick_rows(turn, carry):
        image = image_at(turn)
        fetch(image).wait()
        rows = pl.ds(pl.multiple_of(image * kept, kept), kept)
        positions = lax.broadcasted_iota(jnp.int32, (patches.shape[1], kept), 0)
        slots = lax.broadcasted_iota(jnp.int32, (patches.shape[1], kept), 1)
        listed = index[pl.ds(first + image, 1), :]
        pick = jnp.where((positions == listed) & (slots < count[first + image]), 1.0, 0.0)
        tokens[rows, :] = dot_tn(pick.astype(LOW), patch_rows[image]).astype(LOW)
        return carry

    lax.fori_loop(0, images, pick_rows, 0)
    for step in range(1, devices):
        source = (me + devices - step) % devices
        remote(
            mod_mine, mod_gathered.at[source], mod_send.at[step], mod_recv.at[step], me
        ).wait_recv()
    mod[...] = jnp.concatenate(
        [mod_gathered[device].astype(F32) for device in range(devices)], axis=-1
    )

    def block(image, member):
        return mod[pl.ds(first + image, 1), member * width : (member + 1) * width]

    def one(turn, carry):
        image = image_at(turn)
        rows = pl.ds(pl.multiple_of(image * kept, kept), kept)

        @pl.when(turn == images - 2)
        def _():
            shares[0].pass_on()
            shares[1].pass_on()

        @pl.when(turn == images - 1)
        def _():
            shares[1].relay()

        norm, _ = norm_parts(tokens[rows, :].astype(F32))
        normed = (norm * (1.0 + block(image, 1)) + block(image, 0)).astype(LOW)
        normed_out[rows, :] = normed
        key_live = lax.broadcasted_iota(jnp.int32, (1, kept), 1) < count[first + image]
        attended_out[0, rows, :] = attend_shard(
            normed, heads_own, row_own, spots, proj_out, 0, rows, key_live, scale
        )
        return carry

    def two(turn, carry):
        image = image_at(turn)
        rows = pl.ds(pl.multiple_of(image * kept, kept), kept)
        key_live = lax.broadcasted_iota(jnp.int32, (1, kept), 1) < count[first + image]
        attended = attend_shard(
            normed_out[rows, :], heads_other, row_other, spots, proj_out, 1, rows, key_live, scale
        )
        attended_out[1, rows, :] = attended
        branch = dot(attended_out[0, rows, :], heads_own[3 * local :, :]) + dot(
            attended, heads_other[3 * local :, :]
        )
        terms[rows, :] = branch.astype(LOW)
        for part in range(fold):
            reduce.ready_share(image * fold + part)
        return carry

    lax.fori_loop(0, images, one, 0)
    shares[1].wait()
    lax.fori_loop(0, images, two, 0)
    shares[2].pass_on()
    reduce.relay()
    shares[2].relay()
    shares[3].pass_on()
    reduce.finish(total)
    image = (up * share) // kept
    own = tokens[pl.ds(pl.multiple_of(up * share, share), share), :]
    tokens_own[...] = own
    branch = total[...] + row_own[:, spots["out"] : spots["out"] + width]
    branch_out[...] = branch
    mid = own.astype(F32) + block(image, 2) * branch
    mid_out[...] = mid
    norm, _ = norm_parts(mid)
    normed_two_out[...] = (norm * (1.0 + block(image, 4)) + block(image, 3)).astype(LOW)
    shares[3].relay()
    reduce.close()
    for member in shares[2:]:
        member.wait()
    for step in range(1, groups):
        source = (group + groups - step) % groups
        view = silu_all.at[source]
        remote(
            view, view, silu_send.at[step], silu_recv.at[step], me, group
        ).wait_recv()
    for member in shares:
        member.close()
    for copy in mod_copies + silu_copies:
        copy.wait_send()


def attend(sizes, groups, args):
    depth, images, kept, share, pieces = sizes
    count, index, patches, cond, mod_weight, heads, up, down, row = args
    spots, width = patches.shape[1:]
    local = heads.shape[0] // 4
    mods = mod_weight.shape[0]
    rows = images * kept
    shape = jax.ShapeDtypeStruct
    devices = depth * PAIR
    return pl.pallas_call(
        functools.partial(attend_kernel, sizes, groups),
        out_shape=(
            shape((rows, width), LOW),
            shape((PAIR, 3, rows, local), LOW),
            shape((PAIR, rows, local), LOW),
            shape((share, width), LOW),
            shape((share, width), F32),
            shape((share, width), F32),
            shape((share, width), LOW),
            shape((cond.shape[0], devices * mods), F32),
            shape((groups,) + cond.shape, LOW),
            shape(heads.shape, LOW),
            shape(up.shape, LOW),
            shape(down.shape, LOW),
            shape(row.shape, F32),
        ),
        in_specs=[SM, VM, HB] + [VM] * 6,
        out_specs=(VM,) * 13,
        scratch_shapes=[
            pltpu.VMEM((images, spots, width), LOW),
            pltpu.VMEM((rows, width), LOW),
            pltpu.VMEM((rows, width), LOW),
            pltpu.VMEM((rows - share, width), LOW),
            pltpu.VMEM((share, width), F32),
            pltpu.VMEM((cond.shape[0], mods), LOW),
            pltpu.VMEM((devices, cond.shape[0], mods), LOW),
            DMA((images,)),
        ]
        + Reduce.scratch(depth, pieces)
        + [
            DMA((devices,)),
            DMA((devices,)),
            DMA((groups,)),
            DMA((groups,)),
        ]
        + Share.scratch(4, groups),
        compiler_params=pltpu.CompilerParams(
            collective_id=1, has_side_effects=True, vmem_limit_bytes=60 << 20
        ),
        name="attend",
    )(*args)


def feed_kernel(
    sizes,
    count,
    normed_own,
    cotangent,
    mod,
    up_own,
    up_other,
    row_own,
    row_other,
    down_own,
    down_other,
    mid,
    branch,
    up_grad,
    down_grad,
    up_bias_grad,
    down_bias_grad,
    block_own,
    grad_mid_out,
    grad_branch_out,
    sums_out,
    normed,
    cot,
    hidden,
    grad_pre,
    grad_mlp,
    terms,
    landing,
    mlp_terms,
    mlp_landing,
    total,
    mlp_total,
    up_sums,
    down_sums,
    cot_sem,
    own_sem,
    gather_send,
    gather_recv,
    send,
    recv,
    mlp_send,
    mlp_recv,
):
    depth, images, kept, share, pieces = sizes
    me, up, side = place(depth)
    width = normed_own.shape[1]
    units = up_own.shape[0]
    spots, _ = row_spots(width, units, 1, 1)
    fold = depth // images
    first = side * images
    own_rows = pl.ds(pl.multiple_of(up * share, share), share)
    own_copy = pltpu.make_async_copy(normed_own, normed.at[own_rows, :], own_sem)
    own_copy.start()

    def fetch(image):
        return pltpu.make_async_copy(
            cotangent.at[first + image],
            cot.at[pl.ds(pl.multiple_of(image * kept, kept), kept), :],
            cot_sem.at[image],
        )

    for image in range(images):
        fetch(image).start()
    meet(column_peers(depth))
    own_copy.wait()
    gather = Gather(normed, share, depth, pieces, gather_send, gather_recv)
    reduce = Reduce(terms, landing, share, depth, pieces, send, recv)
    mlp_reduce = Reduce(mlp_terms, mlp_landing, share, depth, pieces, mlp_send, mlp_recv)
    gather.open()

    def block(image, member):
        return mod[pl.ds(image, 1), member * width : (member + 1) * width]

    def one(image):
        fetch(image).wait()
        rows = pl.ds(pl.multiple_of(image * kept, kept), kept)
        live = lax.broadcasted_iota(jnp.int32, (kept, 1), 0) < count[first + image]
        grad = jnp.where(live, cot[rows, :].astype(F32), 0.0)
        grad = (block(first + image, 5) * grad).astype(LOW)
        grad_mlp[rows, :] = grad
        down_sums[image] = jnp.sum(grad.astype(F32), axis=0, keepdims=True)
        source = normed[rows, :]
        mlp = None
        back = None
        for shard, (weight_up, row, weight_down) in enumerate(
            ((up_own, row_own, down_own), (up_other, row_other, down_other))
        ):
            bias = row[:, spots["up"] : spots["up"] + units]
            pre = dot_nt(source, weight_up[...]) + bias
            square = pre * pre
            bent = jnp.tanh(GELU_ROOT * pre * (1.0 + GELU_CUBE * square))
            half = 0.5 * (1.0 + bent)
            low_hidden = (pre * half).astype(LOW)
            hidden[shard, rows, :] = low_hidden
            slope = half + 0.5 * pre * (1.0 - bent * bent) * (
                GELU_ROOT * (1.0 + 3.0 * GELU_CUBE * square)
            )
            low_grad = (slope * dot_nt(grad, weight_down[...])).astype(LOW)
            grad_pre[shard, rows, :] = low_grad
            up_sums[shard, image] = jnp.sum(low_grad.astype(F32), axis=0, keepdims=True)
            mlp_part = dot(low_hidden, weight_down[...])
            back_part = dot(low_grad, weight_up[...])
            mlp = mlp_part if mlp is None else mlp + mlp_part
            back = back_part if back is None else back + back_part
        terms[rows, :] = back.astype(LOW)
        mlp_terms[rows, :] = mlp.astype(LOW)
        for part in range(fold):
            reduce.ready_share(image * fold + part)
            mlp_reduce.ready_share(image * fold + part)

    if fold == 1:

        def turn_of(turn, carry):
            @pl.when(turn == 1)
            def _():
                gather.relay()

            offset = turn + (turn // 2) * (1 - 2 * (turn % 2))
            gather.take(offset)
            one(across(up, offset, depth))
            return carry

        lax.fori_loop(0, depth, turn_of, 0)
    else:

        def image_of(image, carry):
            one(image)
            return carry

        gather.relay()
        for offset in range(1, depth):
            gather.take(offset)
        lax.fori_loop(0, images, image_of, 0)
    reduce.relay()
    mlp_reduce.relay()
    wide = tile_of(width)
    for shard in range(PAIR):

        def tile(step, carry):
            columns = pl.ds(pl.multiple_of(step * wide, 128), wide)
            up_grad[shard, 0:units, columns] = dot_tn(
                grad_pre[shard], normed[:, columns]
            ).astype(LOW)
            down_grad[shard, 0:units, columns] = dot_tn(
                hidden[shard], grad_mlp[:, columns]
            ).astype(LOW)
            return carry

        lax.fori_loop(0, width // wide, tile, 0)
        if units < up_grad.shape[1]:
            rest = jnp.zeros((up_grad.shape[1] - units, width), LOW)
            up_grad[shard, units:, :] = rest
            down_grad[shard, units:, :] = rest
    reduce.finish(total)
    for shard in range(PAIR):
        up_bias_grad[shard : shard + 1, :] = sum(up_sums[shard, image] for image in range(images))
    down_bias_grad[...] = sum(down_sums[image] for image in range(images))
    image = first + (up * share) // kept
    place_in = (up * share) % kept
    live = (
        lax.broadcasted_iota(jnp.int32, (share, 1), 0) + place_in < count[image]
    )
    grad_out = jnp.where(live, cot[own_rows, :].astype(F32), 0.0)
    norm, spread = norm_parts(mid[...])
    back = total[...]
    grad_mid = grad_out + norm_back(norm, spread, back * (1.0 + block(image, 4)))
    grad_mid_out[...] = grad_mid
    grad_branch_out[...] = (block(image, 2) * grad_mid).astype(LOW)
    sums_out[0:1, :] = jnp.sum(grad_mid * branch[...], axis=0, keepdims=True)
    sums_out[1:2, :] = jnp.sum(back, axis=0, keepdims=True)
    sums_out[2:3, :] = jnp.sum(back * norm, axis=0, keepdims=True)
    mlp_reduce.finish(mlp_total)
    mlp = mlp_total[...] + row_own[:, spots["down"] : spots["down"] + width]
    sums_out[3:4, :] = jnp.sum(grad_out * mlp, axis=0, keepdims=True)
    block_own[...] = jnp.where(live, mid[...] + block(image, 5) * mlp, 0.0).astype(LOW)
    gather.close()
    reduce.close()
    mlp_reduce.close()


def feed(sizes, groups, args):
    depth, images, kept, share, pieces = sizes
    width = args[1].shape[1]
    units = args[4].shape[0]
    rows = images * kept
    shape = jax.ShapeDtypeStruct
    return pl.pallas_call(
        functools.partial(feed_kernel, sizes),
        out_shape=(
            shape((PAIR, padded(units, groups), width), LOW),
            shape((PAIR, padded(units, groups), width), LOW),
            shape((PAIR, units), F32),
            shape((1, width), F32),
            shape((share, width), LOW),
            shape((share, width), F32),
            shape((share, width), LOW),
            shape((4, width), F32),
        ),
        in_specs=[SM, VM, HB] + [VM] * 9,
        out_specs=(VM,) * 8,
        scratch_shapes=[
            pltpu.VMEM((rows, width), LOW),
            pltpu.VMEM((rows, width), LOW),
            pltpu.VMEM((PAIR, rows, units), LOW),
            pltpu.VMEM((PAIR, rows, units), LOW),
            pltpu.VMEM((rows, width), LOW),
            pltpu.VMEM((rows, width), LOW),
            pltpu.VMEM((rows - share, width), LOW),
            pltpu.VMEM((rows, width), LOW),
            pltpu.VMEM((rows - share, width), LOW),
            pltpu.VMEM((share, width), F32),
            pltpu.VMEM((share, width), F32),
            pltpu.VMEM((PAIR, images, 1, units), F32),
            pltpu.VMEM((images, 1, width), F32),
            DMA((images,)),
            DMA,
        ]
        + Gather.scratch(depth, pieces)
        + Reduce.scratch(depth, pieces)
        + Reduce.scratch(depth, pieces),
        compiler_params=pltpu.CompilerParams(
            collective_id=2, has_side_effects=True, vmem_limit_bytes=60 << 20
        ),
        name="feed",
    )(*args)


def attend_back_kernel(
    sizes,
    groups,
    count,
    grad_own,
    normed,
    proj,
    attended,
    heads_own,
    heads_other,
    mod,
    tokens_own,
    grad_mid,
    block_own,
    up_grad,
    down_grad,
    heads_grad,
    qv_grad,
    out_bias_grad,
    grad_tokens,
    sums_out,
    block_out,
    up_total,
    down_total,
    grads,
    grad_proj,
    terms,
    landing,
    total,
    qv_sums,
    out_sums,
    own_sem,
    gather_send,
    gather_recv,
    send,
    recv,
    *rest,
):
    depth, images, kept, share, pieces = sizes
    me, up, side = place(depth)
    width = grad_own.shape[1]
    local = heads_own.shape[0] // 4
    scale = HD ** (-0.5)
    fold = depth // images
    first = side * images
    up_fold = Fold(up_grad, rest[:8], up_total, depth, groups)
    down_fold = Fold(down_grad, rest[8:16], down_total, depth, groups)
    spread = Spread(block_out, share, depth, pieces, rest[16:20])
    own_rows = pl.ds(pl.multiple_of(up * share, share), share)
    own_copy = pltpu.make_async_copy(grad_own, grads.at[own_rows, :], own_sem.at[0])
    own_copy.start()
    block_copy = pltpu.make_async_copy(block_own, spread.own(), own_sem.at[1])
    block_copy.start()
    meet(column_peers(depth) + cube_peers(depth, groups) + spread.peers_beyond(depth))
    own_copy.wait()
    gather = Gather(grads, share, depth, pieces, gather_send, gather_recv)
    reduce = Reduce(terms, landing, share, depth, pieces, send, recv)
    gather.open()
    up_fold.one()
    down_fold.one()
    block_copy.wait()

    def one(image):
        rows = pl.ds(pl.multiple_of(image * kept, kept), kept)
        key_live = lax.broadcasted_iota(jnp.int32, (1, kept), 1) < count[first + image]
        grad = grads[rows, :]
        out_sums[image] = jnp.sum(grad.astype(F32), axis=0, keepdims=True)
        back = None
        for shard, heads in enumerate((heads_own, heads_other)):
            grad_att = dot_nt(grad, heads[3 * local :, :]).astype(LOW)
            queries = proj[shard, 0, rows, :]
            keys = proj[shard, 1, rows, :]
            values = proj[shard, 2, rows, :]
            grad_q = jnp.zeros((kept, local), F32)
            grad_k = jnp.zeros((kept, local), F32)
            grad_v = jnp.zeros((kept, local), F32)
            for head in range(local // HD):
                mask = head_mask(head, local)
                head_q = jnp.where(mask, queries, 0.0).astype(LOW)
                head_grad = jnp.where(mask, grad_att, 0.0).astype(LOW)
                weights = softmax_rows(head_q, keys, key_live, scale)
                grad_weights = dot_nt(head_grad, values)
                inner = jnp.sum(weights * grad_weights, axis=-1, keepdims=True)
                grad_scores = (weights * (grad_weights - inner)).astype(LOW)
                grad_v = grad_v + dot_tn(weights.astype(LOW), head_grad)
                grad_q = grad_q + dot(grad_scores, jnp.where(mask, keys, 0.0).astype(LOW))
                grad_k = grad_k + dot_tn(grad_scores, head_q)
            for member, value in enumerate((grad_q * scale, grad_k * scale, grad_v)):
                low = value.astype(LOW)
                grad_proj[shard, member, rows, :] = low
                part = dot(low, heads[member * local : (member + 1) * local, :])
                back = part if back is None else back + part
                if member != 1:
                    row = 2 * shard + member // 2
                    qv_sums[row, image] = jnp.sum(low.astype(F32), axis=0, keepdims=True)
        terms[rows, :] = back.astype(LOW)
        for part in range(fold):
            reduce.ready_share(image * fold + part)

    if fold == 1:

        def turn_of(turn, carry):
            @pl.when(turn == 1)
            def _():
                gather.relay()

            offset = turn + (turn // 2) * (1 - 2 * (turn % 2))
            gather.take(offset)
            one(across(up, offset, depth))

            @pl.when(turn == 0)
            def _():
                up_fold.two()
                down_fold.two()

            @pl.when(turn == 1)
            def _():
                spread.open()

            @pl.when(turn == 2)
            def _():
                up_fold.three()

            @pl.when(turn == 3)
            def _():
                down_fold.three()

            return carry

        lax.fori_loop(0, depth, turn_of, 0)
    else:

        def image_of(image, carry):
            one(image)
            return carry

        gather.relay()
        for offset in range(1, depth):
            gather.take(offset)
        up_fold.two()
        down_fold.two()
        spread.open()
        lax.fori_loop(0, images, image_of, 0)
        up_fold.three()
        down_fold.three()

    def spread_of(turn, carry):
        spread.take(turn)
        return carry

    reduce.relay()
    lax.fori_loop(1, depth - 1, spread_of, 0)
    up_fold.four()
    down_fold.four()
    wide = tile_of(width)
    for shard in range(PAIR):

        def tile(step, carry):
            columns = pl.ds(pl.multiple_of(step * wide, 128), wide)
            source = normed[:, columns]
            for member in range(3):
                heads_grad[shard, member * local : (member + 1) * local, columns] = dot_tn(
                    grad_proj[shard, member], source
                ).astype(LOW)
            heads_grad[shard, 3 * local : 4 * local, columns] = dot_tn(
                attended[shard], grads[:, columns]
            ).astype(LOW)
            return carry

        lax.fori_loop(0, width // wide, tile, 0)
        if 4 * local < heads_grad.shape[1]:
            heads_grad[shard, 4 * local :, :] = jnp.zeros(
                (heads_grad.shape[1] - 4 * local, width), LOW
            )
    up_fold.five()
    spread.take(depth - 1)
    down_fold.five()
    reduce.finish(total)
    for row in range(2 * PAIR):
        qv_grad[row : row + 1, :] = sum(qv_sums[row, image] for image in range(images))
    out_bias_grad[...] = sum(out_sums[image] for image in range(images))
    image = first + (up * share) // kept
    live = (
        lax.broadcasted_iota(jnp.int32, (share, 1), 0) + (up * share) % kept < count[image]
    )
    norm, spread_rows = norm_parts(tokens_own[...].astype(F32))
    back = total[...]
    scale_one = mod[pl.ds(image, 1), width : 2 * width]
    grad = grad_mid[...] + norm_back(norm, spread_rows, back * (1.0 + scale_one))
    grad_tokens[...] = jnp.where(live, grad, 0.0).astype(LOW)
    sums_out[0:1, :] = jnp.sum(back, axis=0, keepdims=True)
    sums_out[1:2, :] = jnp.sum(back * norm, axis=0, keepdims=True)
    up_fold.six()
    down_fold.six()
    for index in range(depth):
        spread.crossed(index)
    spread.close()
    gather.close()
    reduce.close()


def attend_back(sizes, groups, args):
    depth, images, kept, share, pieces = sizes
    width = args[1].shape[1]
    local = args[5].shape[0] // 4
    up_grad, down_grad, units = args[-3:]
    rows = images * kept
    shape = jax.ShapeDtypeStruct
    return pl.pallas_call(
        functools.partial(attend_back_kernel, sizes, groups),
        out_shape=(
            shape((PAIR, padded(4 * local, groups), width), LOW),
            shape((2 * PAIR, local), F32),
            shape((1, width), F32),
            shape((share, width), LOW),
            shape((2, width), F32),
            shape((PAIR * rows, width), LOW),
            shape((units, width), F32),
            shape((units, width), F32),
        ),
        in_specs=[SM] + [VM] * 12,
        out_specs=(VM,) * 8,
        scratch_shapes=[
            pltpu.VMEM((rows, width), LOW),
            pltpu.VMEM((PAIR, 3, rows, local), LOW),
            pltpu.VMEM((rows, width), LOW),
            pltpu.VMEM((rows - share, width), LOW),
            pltpu.VMEM((share, width), F32),
            pltpu.VMEM((2 * PAIR, images, 1, local), F32),
            pltpu.VMEM((images, 1, width), F32),
            DMA((2,)),
        ]
        + Gather.scratch(depth, pieces)
        + Reduce.scratch(depth, pieces)
        + Fold.scratch(up_grad.shape, groups)
        + Fold.scratch(down_grad.shape, groups)
        + Spread.scratch(depth, pieces),
        compiler_params=pltpu.CompilerParams(
            collective_id=3, has_side_effects=True, vmem_limit_bytes=62 << 20
        ),
        name="attend_back",
    )(*args[:-1])


def split_low(value):
    high = value.astype(LOW)
    rest = value - high.astype(F32)
    low = rest.astype(LOW)
    return high, low, (rest - low.astype(F32)).astype(LOW)


def close_kernel(
    sizes,
    groups,
    index,
    grad_tokens,
    sums_one,
    sums_two,
    up_bias_grad,
    qv_grad,
    down_bias_grad,
    out_bias_grad,
    heads_grad,
    silu_all,
    mod_weight,
    cond,
    grad_patches,
    heads_total,
    bias_total,
    mod_weight_grad,
    mod_bias_grad,
    grad_cond,
    whole,
    biases,
    sum_row,
    sum_land,
    bias_land,
    cond_land,
    own_sem,
    sum_send,
    sum_recv,
    bias_send,
    bias_recv,
    cond_send,
    cond_recv,
    *rest,
):
    depth, images, kept, share, pieces = sizes
    devices = depth * PAIR
    everyone = devices * groups
    me, _, side = place(depth)
    up = me // PAIR
    group = lax.axis_index("dp")
    flat = group * devices + me
    width = grad_tokens.shape[1]
    columns = mod_weight.shape[0]
    span = sum_land.shape[2]
    spread = Spread(whole, share, depth, pieces, rest[:4])
    fold = Fold(heads_grad, rest[4:12], heads_total, depth, groups)
    own_copy = pltpu.make_async_copy(grad_tokens, spread.own(), own_sem)
    own_copy.start()
    barrier = pltpu.get_barrier_semaphore()

    def greet(step, carry):
        there = (flat + step) % everyone
        pl.semaphore_signal(
            barrier,
            inc=1,
            device_id={"dp": there // devices, "tensor": there % devices},
            device_id_type=MESH,
        )
        return carry

    lax.fori_loop(1, everyone, greet, 0)
    pl.semaphore_wait(barrier, everyone - 1)
    own_copy.wait()
    fold.one()
    spread.open()

    def aligned(device):
        return pl.multiple_of((device * columns) // 128 * 128, 128)

    for member in range(6):
        part = sums_one[member : member + 1, :] if member < 2 else sums_two[member - 2 : member - 1, :]
        sum_row[:, member * width : (member + 1) * width] = part
    sum_row[:, 6 * width :] = jnp.zeros((1, sum_row.shape[1] - 6 * width), F32)

    def sum_copy(step):
        there = (flat + step) % everyone
        device = there % devices
        return remote(
            sum_row.at[:, pl.ds(aligned(device), span)],
            sum_land.at[flat],
            sum_send.at[step],
            sum_recv.at[step],
            device,
            there // devices,
        )

    def send_sum(step, carry):
        sum_copy(step).start()
        return carry

    lax.fori_loop(1, everyone, send_sum, 0)
    sum_land[flat] = sum_row[:, pl.ds(aligned(me), span)]
    units, local = up_bias_grad.shape[1], qv_grad.shape[1]
    biases[...] = jnp.zeros(biases.shape, F32)
    for shard in range(PAIR):
        biases[3 * shard : 3 * shard + 1, 0:units] = up_bias_grad[shard : shard + 1, :]
        biases[3 * shard + 1 : 3 * shard + 3, 0:local] = qv_grad[2 * shard : 2 * shard + 2, :]
    biases[6:7, :] = down_bias_grad[...]
    biases[7:8, :] = out_bias_grad[...]
    slot = side * groups + group
    bias_land[slot] = biases[...]
    partner = me + depth * (1 - 2 * side)

    def bias_copy(step):
        crossed = step // groups
        there = (group + step) % groups
        device = jnp.where(crossed == 1, partner, me)
        return remote(
            biases, bias_land.at[slot], bias_send.at[step], bias_recv.at[step], device, there
        )

    for step in range(1, PAIR * groups):
        bias_copy(step).start()
    fold.two()

    def wait_sum(step, carry):
        source = (flat + everyone - step) % everyone
        view = sum_land.at[source]
        remote(view, view, sum_send.at[step], sum_recv.at[step], me).wait_recv()
        return carry

    lax.fori_loop(1, everyone, wait_sum, 0)
    offset = (me * columns) % 128
    grads = jnp.concatenate([sum_land[device] for device in range(everyone)], axis=0)
    grads = pltpu.roll(grads, lax.rem(span - offset, span), 1)[:, :columns]
    mod_bias_grad[...] = jnp.sum(grads, axis=0, keepdims=True)
    total_images = images * PAIR

    def image_of(device):
        return device * share // kept

    source = lax.broadcasted_iota(jnp.int32, (everyone, groups * total_images), 0)
    target = lax.broadcasted_iota(jnp.int32, (everyone, groups * total_images), 1)
    row_image = source // devices * total_images + image_of(source % devices)
    chosen = jnp.where(row_image == target, 1.0, 0.0).astype(LOW)
    silu_rows = dot(
        chosen,
        jnp.concatenate([silu_all[member].astype(F32) for member in range(groups)], axis=0).astype(
            LOW
        ),
    ).astype(LOW)
    parts = split_low(grads)
    spread.take(1)
    fold.three()
    mod_weight_grad[...] = (
        dot_tn(parts[0], silu_rows) + dot_tn(parts[1], silu_rows) + dot_tn(parts[2], silu_rows)
    )
    source = lax.broadcasted_iota(jnp.int32, (total_images, everyone), 1)
    target = lax.broadcasted_iota(jnp.int32, (total_images, everyone), 0)
    chosen = jnp.where(
        (source // devices == group) & (image_of(source % devices) == target), 1.0, 0.0
    ).astype(LOW)
    mine = dot(chosen, parts[0]) + dot(chosen, parts[1]) + dot(chosen, parts[2])
    parts = split_low(mine)
    term = (
        dot(parts[0], mod_weight[...])
        + dot(parts[1], mod_weight[...])
        + dot(parts[2], mod_weight[...])
    )
    cond_land[me] = term

    def cond_copy(step):
        return remote(
            cond_land.at[me],
            cond_land.at[me],
            cond_send.at[step],
            cond_recv.at[step],
            (me + step) % devices,
        )

    for step in range(1, devices):
        cond_copy(step).start()
    for turn in range(2, depth - 1):
        spread.take(turn)
    fold.four()
    for step in range(1, PAIR * groups):
        crossed = step // groups
        source_group = (group + groups - step % groups) % groups
        source_side = jnp.where(crossed == 1, 1 - side, side)
        view = bias_land.at[source_side * groups + source_group]
        remote(view, view, bias_send.at[step], bias_recv.at[step], me).wait_recv()
    rows = biases.shape[0]
    result = jnp.zeros((rows, width), F32)
    for member in range(PAIR * groups):
        value = bias_land[member]
        turned = jnp.concatenate([value[3:6, :], value[0:3, :], value[6:, :]], axis=0)
        same = side == member // groups
        result = result + jnp.where(same, value, turned)
    bias_total[...] = result
    for step in range(1, devices):
        source = (me + devices - step) % devices
        view = cond_land.at[source]
        remote(view, view, cond_send.at[step], cond_recv.at[step], me).wait_recv()
    back = cond_land[0]
    for device in range(1, devices):
        back = back + cond_land[device]
    value = cond[...].astype(F32)
    gate = 1.0 / (1.0 + jnp.exp(-value))
    grad_cond[...] = (back * (gate + value * gate * (1.0 - gate))).astype(LOW)

    def place_image(image):
        rows = pl.ds(pl.multiple_of(image * kept, kept), kept)
        positions = lax.broadcasted_iota(jnp.int32, (grad_patches.shape[1], kept), 0)
        pick = jnp.where(positions == index[pl.ds(image, 1), :], 1.0, 0.0).astype(LOW)
        grad_patches[image] = dot(pick, whole[rows, :]).astype(LOW)

    both = PAIR * share // kept

    def put(where):
        spread.crossed(where)
        for image in range(both):
            place_image(where * both + image)

    def arrived(turn, carry):
        put(spread.line.arrival(turn)[2])
        return carry

    put(up)
    lax.fori_loop(1, depth - 1, arrived, 0)
    spread.take(depth - 1)
    fold.five()
    put(spread.line.arrival(depth - 1)[2])
    fold.six()
    spread.close()

    def done_sum(step, carry):
        sum_copy(step).wait_send()
        return carry

    lax.fori_loop(1, everyone, done_sum, 0)
    for step in range(1, PAIR * groups):
        bias_copy(step).wait_send()
    for step in range(1, devices):
        cond_copy(step).wait_send()


def close(sizes, groups, args):
    depth, images, kept, share, pieces = sizes
    index, grad_tokens = args[:2]
    heads_grad, silu_all, mod_weight, cond, local, spots = args[-6:]
    devices = depth * PAIR
    width = grad_tokens.shape[1]
    columns = mod_weight.shape[0]
    biases = (8, width)
    span = max(-(-((device * columns) % 128 + columns) // 128) * 128 for device in range(devices))
    long = max((device * columns) // 128 * 128 + span for device in range(devices))
    long = max(long, 6 * width + 128)
    shape = jax.ShapeDtypeStruct
    rows = PAIR * images * kept
    everyone = devices * groups
    return pl.pallas_call(
        functools.partial(close_kernel, sizes, groups),
        out_shape=(
            shape((PAIR * images, spots, width), LOW),
            shape((4 * local, width), F32),
            shape(biases, F32),
            shape(mod_weight.shape, F32),
            shape((1, columns), F32),
            shape(cond.shape, LOW),
        ),
        in_specs=[VM] * 12,
        out_specs=(VM,) * 6,
        scratch_shapes=[
            pltpu.VMEM((rows, width), LOW),
            pltpu.VMEM(biases, F32),
            pltpu.VMEM((1, long), F32),
            pltpu.VMEM((everyone, 1, span), F32),
            pltpu.VMEM((PAIR * groups,) + biases, F32),
            pltpu.VMEM((devices,) + cond.shape, F32),
            DMA,
            DMA((everyone,)),
            DMA((everyone,)),
            DMA((PAIR * groups,)),
            DMA((PAIR * groups,)),
            DMA((devices,)),
            DMA((devices,)),
        ]
        + Spread.scratch(depth, pieces)
        + Fold.scratch(heads_grad.shape, groups),
        compiler_params=pltpu.CompilerParams(
            collective_id=4, has_side_effects=True, vmem_limit_bytes=62 << 20
        ),
        name="close",
    )(*args[:-2])


def on_device(
    patches,
    conditioning,
    keep_count,
    keep_index,
    mod_weight,
    mod_bias,
    qkv_weight,
    qv_bias,
    out_weight,
    out_bias,
    up_weight,
    up_bias,
    down_weight,
    down_bias,
    out_cotangent,
):
    devices = lax.axis_size("tensor")
    depth = devices // PAIR
    all_images, kept = keep_index.shape
    width = patches.shape[2]
    images = all_images // PAIR
    share = images * kept // depth
    pieces = 4 if share % 64 == 0 else 2
    sizes = (depth, images, kept, share, pieces)
    groups = lax.axis_size("dp")
    local, units, mods = qkv_weight.shape[2], up_weight.shape[1], mod_weight.shape[1]
    up = up_weight.T
    mod_rows = mod_weight.T
    heads = jnp.concatenate(
        [jnp.swapaxes(qkv_weight, 1, 2).reshape(3 * local, width), out_weight], axis=0
    )

    def spaced(value):
        return jnp.pad(value.astype(F32), (0, lanes(value.shape[0]) - value.shape[0]))

    row = jnp.concatenate(
        [
            spaced(value)
            for value in (out_bias, down_bias, up_bias, qv_bias[0], qv_bias[1], mod_bias)
        ]
    )[None, :]
    (
        normed_one,
        proj,
        attended,
        tokens_own,
        mid,
        branch,
        normed_two,
        mod,
        silu_all,
        heads_other,
        up_other,
        down_other,
        row_other,
    ) = attend(
        sizes,
        groups,
        (keep_count, keep_index, patches, conditioning, mod_rows, heads, up, down_weight, row),
    )
    (
        up_grad,
        down_grad,
        up_bias_grad,
        down_bias_grad,
        block_own,
        grad_mid,
        grad_branch,
        sums_two,
    ) = feed(
        sizes,
        groups,
        (
            keep_count,
            normed_two,
            out_cotangent,
            mod,
            up,
            up_other,
            row,
            row_other,
            down_weight,
            down_other,
            mid,
            branch,
        ),
    )
    (
        heads_grad,
        qv_grad,
        out_bias_grad,
        grad_tokens,
        sums_one,
        block_out,
        up_total,
        down_total,
    ) = attend_back(
        sizes,
        groups,
        (
            keep_count,
            grad_branch,
            normed_one,
            proj,
            attended,
            heads,
            heads_other,
            mod,
            tokens_own,
            grad_mid,
            block_own,
            up_grad,
            down_grad,
            units,
        ),
    )
    (
        grad_patches,
        heads_total,
        bias_total,
        mod_rows_grad,
        mod_bias_grad,
        grad_conditioning,
    ) = close(
        sizes,
        groups,
        (
            keep_index,
            grad_tokens,
            sums_one,
            sums_two,
            up_bias_grad,
            qv_grad,
            down_bias_grad,
            out_bias_grad,
            heads_grad,
            silu_all,
            mod_rows,
            conditioning,
            local,
            patches.shape[1],
        ),
    )
    return (
        block_out.reshape(all_images, kept, width),
        grad_patches,
        grad_conditioning,
        mod_rows_grad.T,
        mod_bias_grad[0],
        jnp.swapaxes(heads_total[: 3 * local].reshape(3, local, width), 1, 2),
        bias_total[1:3, :local],
        heads_total[3 * local :],
        bias_total[7],
        up_total.T,
        bias_total[0, :units],
        down_total,
        bias_total[6],
    )


def solution(mesh):
    placed = (
        P("dp", None, None),
        P("dp", None),
        P("dp"),
        P("dp", None),
        P(None, "tensor"),
        P("tensor"),
        P(None, None, "tensor"),
        P(None, "tensor"),
        P("tensor", None),
        P(),
        P(None, "tensor"),
        P("tensor"),
        P("tensor", None),
        P(),
        P("dp", None, None),
    )
    return jax.shard_map(
        on_device,
        mesh=mesh,
        in_specs=placed,
        out_specs=(
            P("dp", None, None),
            P("dp", None, None),
            P("dp", None),
            P(None, "tensor"),
            P("tensor"),
            P(None, None, "tensor"),
            P(None, "tensor"),
            P("tensor", None),
            P(),
            P(None, "tensor"),
            P("tensor"),
            P("tensor", None),
            P(),
        ),
        check_vma=False,
    )
```

```python
import functools

import jax
import jax.numpy as jnp
from jax import lax
from jax.experimental import pallas as pl
from jax.experimental.pallas import tpu as pltpu
from jax.sharding import PartitionSpec as P

HD = 72
MESH = pl.DeviceIdType.MESH
F32 = jnp.float32
LOW = jnp.bfloat16
DMA = pltpu.SemaphoreType.DMA
VM = pl.BlockSpec(memory_space=pltpu.VMEM)
SM = pl.BlockSpec(memory_space=pltpu.SMEM)
HB = pl.BlockSpec(memory_space=pl.ANY)
PAIR = 2
GELU_ROOT = 0.7978845608028654
GELU_CUBE = 0.044715


def remote(source, target, send_sem, recv_sem, device, group=None):
    there = {"tensor": device} if group is None else {"dp": group, "tensor": device}
    return pltpu.make_async_remote_copy(
        src_ref=source,
        dst_ref=target,
        send_sem=send_sem,
        recv_sem=recv_sem,
        device_id=there,
        device_id_type=MESH,
    )


def place(depth):
    me = lax.axis_index("tensor")
    return me, me % depth, me // depth


def bits_of(depth):
    return depth.bit_length() - 1


def toward(spot, bit):
    return (1 - 2 * ((spot // (1 << bit)) % 2)) * (1 << bit)


def across(spot, offset, depth):
    result = spot
    for bit in range(bits_of(depth)):
        result = result + ((offset // (1 << bit)) % 2) * toward(spot, bit)
    return result


def offset_between(left, right, depth):
    result = 0
    for bit in range(bits_of(depth)):
        size = 1 << bit
        result = result + ((left // size + right // size) % 2) * size
    return result


def meet(peers):
    barrier = pltpu.get_barrier_semaphore()
    for group, peer in peers:
        pl.semaphore_signal(
            barrier, inc=1, device_id={"dp": group, "tensor": peer}, device_id_type=MESH
        )
    pl.semaphore_wait(barrier, len(peers))


def column_peers(depth):
    me, spot, side = place(depth)
    group = lax.axis_index("dp")
    return [(group, me + toward(spot, bit)) for bit in range(bits_of(depth))]


def cube_peers(depth, groups):
    me, spot, side = place(depth)
    group = lax.axis_index("dp")
    other = me + depth * (1 - 2 * side)
    peers = [((group + step) % groups, me) for step in range(1, groups)]
    return peers + [((group + step) % groups, other) for step in range(groups)]


def padded(rows, groups):
    return -(-rows // (16 * groups)) * 16 * groups


def lanes(columns):
    return -(-columns // 128) * 128


def row_spots(width, units, local, mods):
    spots = {}
    start = 0
    for name, size in (
        ("out", width),
        ("down", width),
        ("up", units),
        ("query", local),
        ("value", local),
        ("mod", mods),
    ):
        spots[name] = start
        start += lanes(size)
    return spots, start


def tile_of(width):
    return 384 if width % 384 == 0 else 128


def dot(left, right):
    return jnp.dot(left, right, preferred_element_type=F32)


def dot_nt(left, right):
    return lax.dot_general(left, right, (((1,), (1,)), ((), ())), preferred_element_type=F32)


def dot_tn(left, right):
    return lax.dot_general(left, right, (((0,), (0,)), ((), ())), preferred_element_type=F32)


def norm_parts(rows):
    width = rows.shape[-1]
    centred = rows - jnp.sum(rows, axis=-1, keepdims=True) * (1.0 / width)
    spread = lax.rsqrt(jnp.sum(centred * centred, axis=-1, keepdims=True) * (1.0 / width) + 1e-06)
    return centred * spread, spread


def norm_back(norm, spread, grad):
    width = norm.shape[-1]
    mean_grad = jnp.sum(grad, axis=-1, keepdims=True) * (1.0 / width)
    mean_both = jnp.sum(grad * norm, axis=-1, keepdims=True) * (1.0 / width)
    return (grad - mean_grad - norm * mean_both) * spread


class Line:
    def __init__(self, buffer, share, depth, pieces, send, recv):
        self.buffer, self.share, self.depth, self.pieces = buffer, share, depth, pieces
        self.send, self.recv = send, recv
        self.me = lax.axis_index("tensor")
        self.up, self.side = self.me // PAIR, self.me % PAIR

    def piece(self, index, part):
        rows = self.share // self.pieces
        start = (index * PAIR + self.side) * self.share + part * rows
        return self.buffer.at[pl.ds(pl.multiple_of(start, rows), rows), :]

    def copy(self, way, step, part):
        source = self.up - (step - 1) * (1 - 2 * way)
        target = self.up + 1 - 2 * way
        view = self.piece(source, part)
        return remote(
            view,
            view,
            self.send.at[way, step, part],
            self.recv.at[way, step, part],
            target * PAIR + self.side,
        )

    def may_send(self, way, step):
        if way == 0:
            return (self.up + 1 < self.depth) & (self.up >= step - 1)
        return (self.up >= 1) & (self.up + step - 1 < self.depth)

    def open(self):
        for part in range(self.pieces):
            for way in range(2):

                @pl.when(self.may_send(way, 1))
                def _():
                    self.copy(way, 1, part).start()

    def arrival(self, turn):
        below = self.up
        above = self.depth - 1 - self.up
        both = jnp.minimum(below, above)
        mixed = turn <= 2 * both
        way = jnp.where(mixed, (turn + 1) % 2, jnp.where(below > above, 0, 1))
        step = jnp.where(mixed, (turn + 1) // 2, turn - both)
        return way, step, self.up - step * (1 - 2 * way)

    def take(self, turn, then):
        way, step, source = self.arrival(turn)
        ahead = jnp.where(way == 0, self.up + 1 < self.depth, self.up >= 1)
        for part in range(self.pieces):
            view = self.piece(source, part)
            remote(
                view, view, self.send.at[way, step, part], self.recv.at[way, step, part], self.me
            ).wait_recv()

            @pl.when(ahead)
            def _():
                self.copy(way, step + 1, part).start()

            then(source, part)

    def close(self):
        for way in range(2):
            for step in range(1, self.depth):

                @pl.when(self.may_send(way, step))
                def _():
                    for part in range(self.pieces):
                        self.copy(way, step, part).wait_send()


class Cube:
    def __init__(self, share, depth, pieces):
        self.share, self.depth, self.pieces = share, depth, pieces
        self.me, self.spot, self.side = place(depth)
        self.bits = bits_of(depth)
        self.rows = share // pieces

    def order(self, part):
        ways = list(range(self.bits))
        return ways if part % 2 else ways[::-1]

    def span(self, index, part):
        return pl.ds(pl.multiple_of(index * self.share + part * self.rows, self.rows), self.rows)

    def neighbour(self, bit):
        return self.me + toward(self.spot, bit)


class Gather(Cube):
    def __init__(self, buffer, share, depth, pieces, send, recv):
        super().__init__(share, depth, pieces)
        self.buffer, self.send, self.recv = buffer, send, recv

    def last(self, offset, part):
        order = self.order(part)
        return max(
            (stage for stage in range(self.bits) if offset >> order[stage] & 1), default=-1
        )

    def copy(self, offset, stage, part):
        bit = self.order(part)[stage]
        view = self.buffer.at[self.span(across(self.spot, offset, self.depth), part), :]
        return remote(
            view,
            view,
            self.send.at[offset, stage, part],
            self.recv.at[offset ^ (1 << bit), part],
            self.neighbour(bit),
        )

    def landed(self, offset, part):
        view = self.buffer.at[self.span(across(self.spot, offset, self.depth), part), :]
        remote(
            view, view, self.send.at[0, 0, part], self.recv.at[offset, part], self.me
        ).wait_recv()

    def sends(self, offset):
        return [
            (stage, part)
            for part in range(self.pieces)
            for stage in range(self.last(offset, part) + 1, self.bits)
        ]

    def open(self):
        for stage, part in self.sends(0):
            self.copy(0, stage, part).start()

    def relay(self):
        for offset in sorted(range(1, self.depth), key=lambda value: bin(value).count("1")):
            for part in range(self.pieces):
                first = self.last(offset, part) + 1
                if first < self.bits:
                    self.landed(offset, part)
                    for stage in range(first, self.bits):
                        self.copy(offset, stage, part).start()

    def take(self, offset):
        for member in range(1, self.depth):

            @pl.when(offset == member)
            def _():
                for part in range(self.pieces):
                    if self.last(member, part) + 1 == self.bits:
                        self.landed(member, part)

    def close(self):
        for offset in range(self.depth):
            for stage, part in self.sends(offset):
                self.copy(offset, stage, part).wait_send()

    @staticmethod
    def scratch(depth, pieces):
        return [DMA((depth, bits_of(depth), pieces)), DMA((depth, pieces))]


class Reduce(Cube):
    def __init__(self, terms, landing, share, depth, pieces, send, recv):
        super().__init__(share, depth, pieces)
        self.terms, self.landing, self.send, self.recv = terms, landing, send, recv

    def slot(self, stage, offset, part):
        order = self.order(part)
        found = [
            (level, member)
            for level in range(self.bits)
            for member in range(self.depth)
            if not any(member >> order[below] & 1 for below in range(level + 1))
        ]
        return found.index((stage, offset))

    def first(self, offset, part):
        order = self.order(part)
        return min(stage for stage in range(self.bits) if offset >> order[stage] & 1)

    def copy(self, offset, part):
        stage = self.first(offset, part)
        bit = self.order(part)[stage]
        slot = self.slot(stage, offset ^ (1 << bit), part)
        return remote(
            self.terms.at[self.span(across(self.spot, offset, self.depth), part), :],
            self.landing.at[self.span(slot, part), :],
            self.send.at[offset, part],
            self.recv.at[slot, part],
            self.neighbour(bit),
        )

    def landed(self, slot, part):
        view = self.landing.at[self.span(slot, part), :]
        remote(view, view, self.send.at[0, part], self.recv.at[slot, part], self.me).wait_recv()

    def ready(self, offset):
        for member in range(1, self.depth):

            @pl.when(offset == member)
            def _():
                for part in range(self.pieces):
                    if self.first(member, part) == 0:
                        self.copy(member, part).start()

    def ready_share(self, index):
        self.ready(offset_between(index, self.spot, self.depth))

    def add(self, target, target_start, term_start, slots, part):
        def body(index, carry):
            offset = index * 16
            value = self.terms[pl.ds(pl.multiple_of(term_start + offset, 16), 16), :].astype(F32)
            for slot in slots:
                start = slot * self.share + part * self.rows
                value = value + self.landing[
                    pl.ds(pl.multiple_of(start + offset, 16), 16), :
                ].astype(F32)
            target[pl.ds(pl.multiple_of(target_start + offset, 16), 16), :] = value.astype(
                target.dtype
            )
            return carry

        lax.fori_loop(0, self.rows // 16, body, 0)

    def relay(self):
        for level in range(1, self.bits):
            for part in range(self.pieces):
                for offset in range(1, self.depth):
                    if self.first(offset, part) == level:
                        slots = [self.slot(below, offset, part) for below in range(level)]
                        for slot in slots:
                            self.landed(slot, part)
                        start = (
                            across(self.spot, offset, self.depth) * self.share + part * self.rows
                        )
                        self.add(self.terms, start, start, slots, part)
                        self.copy(offset, part).start()

    def finish(self, total):
        for part in range(self.pieces):
            slots = [self.slot(stage, 0, part) for stage in range(self.bits)]
            for slot in slots:
                self.landed(slot, part)
            skip = part * self.rows
            self.add(total, skip, self.spot * self.share + skip, slots, part)

    def close(self):
        for offset in range(1, self.depth):
            for part in range(self.pieces):
                self.copy(offset, part).wait_send()

    @staticmethod
    def scratch(depth, pieces):
        return [DMA((depth, pieces)), DMA((depth - 1, pieces))]


class Fold:
    def __init__(self, source, scratch, out, depth, groups):
        self.source, self.out = source, out
        (
            self.stage,
            self.near,
            self.land,
            self.part,
            self.side_land,
            self.low,
            self.send,
            self.recv,
        ) = scratch
        self.me = lax.axis_index("tensor")
        self.group = lax.axis_index("dp")
        self.lines = groups // PAIR
        self.core = self.group % PAIR
        self.line = self.group // PAIR
        self.mate = self.group + 1 - 2 * self.core
        self.partner = self.me + depth * (1 - 2 * (self.me // depth))
        self.rows = self.part.shape[1]
        self.half = self.rows * self.lines

    @staticmethod
    def scratch(shape, groups):
        _, rows, width = shape
        lines = groups // PAIR
        part = rows // groups
        return [
            pltpu.VMEM((PAIR, part * lines, width), LOW),
            pltpu.VMEM((PAIR, part * lines, width), LOW),
            pltpu.VMEM((lines, PAIR, part, width), LOW),
            pltpu.VMEM((PAIR, part, width), LOW),
            pltpu.VMEM((part, width), LOW),
            pltpu.VMEM((rows, width), LOW),
            DMA((2 + 3 * lines,)),
            DMA((2 + 3 * lines,)),
        ]

    def each(self, rows, body):
        step = 48 if rows % 48 == 0 else 16 if rows % 16 == 0 else rows

        def run(index, carry):
            body(pl.multiple_of(index * step, step), step)
            return carry

        lax.fori_loop(0, rows // step, run, 0)

    def window(self, start, size):
        return pl.ds(pl.multiple_of(start, 16), size)

    def behind(self, step):
        return (self.line + self.lines - step) % self.lines

    def block(self, core, line):
        return self.low.at[self.window(core * self.half + line * self.rows, self.rows), :]

    def near_copy(self):
        return remote(
            self.source.at[:, self.window((1 - self.core) * self.half, self.half), :],
            self.near,
            self.send.at[0],
            self.recv.at[0],
            self.me,
            self.mate,
        )

    def cross_copy(self, step):
        line = (self.line + step) % self.lines
        return remote(
            self.stage.at[:, self.window(line * self.rows, self.rows), :],
            self.land.at[self.line],
            self.send.at[2 + step],
            self.recv.at[2 + step],
            self.me,
            line * PAIR + self.core,
        )

    def side_copy(self):
        return remote(
            self.part.at[1],
            self.side_land,
            self.send.at[1],
            self.recv.at[1],
            self.partner,
            self.group,
        )

    def line_copy(self, step):
        line = (self.line + step) % self.lines
        view = self.block(self.core, self.line)
        slot = 2 + self.lines + step
        return remote(
            view,
            view,
            self.send.at[slot],
            self.recv.at[slot],
            self.me,
            line * PAIR + self.core,
        )

    def mate_copy(self, core, line):
        view = self.block(core, line)
        slot = 2 + 2 * self.lines + line
        return remote(view, view, self.send.at[slot], self.recv.at[slot], self.me, self.mate)

    def one(self):
        self.near_copy().start()

    def two(self):
        self.near_copy().wait_recv()

        def add(at, size):
            rows = self.window(at, size)
            for shard in range(PAIR):
                mine = self.source[shard, self.window(self.core * self.half + at, size), :]
                self.stage[shard, rows, :] = (
                    mine.astype(F32) + self.near[shard, rows, :].astype(F32)
                ).astype(LOW)

        self.each(self.half, add)
        for step in range(1, self.lines):
            self.cross_copy(step).start()

    def three(self):
        for step in range(1, self.lines):
            view = self.land.at[self.behind(step)]
            remote(
                view, view, self.send.at[2 + step], self.recv.at[2 + step], self.me, self.mate
            ).wait_recv()

        def add(at, size):
            rows = self.window(at, size)
            for shard in range(PAIR):
                value = self.stage[
                    shard, self.window(self.line * self.rows + at, size), :
                ].astype(F32)
                for step in range(1, self.lines):
                    value = value + self.land[self.behind(step), shard, rows, :].astype(F32)
                self.part[shard, rows, :] = value.astype(LOW)

        self.each(self.rows, add)
        self.side_copy().start()

    def four(self):
        self.side_copy().wait_recv()

        def add(at, size):
            rows = self.window(at, size)
            value = self.part[0, rows, :].astype(F32) + self.side_land[rows, :].astype(F32)
            spot = self.window(self.core * self.half + self.line * self.rows + at, size)
            self.low[spot, :] = value.astype(LOW)

        self.each(self.rows, add)
        for step in range(1, self.lines):
            self.line_copy(step).start()
        self.mate_copy(self.core, self.line).start()

    def five(self):
        for step in range(1, self.lines):
            line = self.behind(step)
            view = self.block(self.core, line)
            slot = 2 + self.lines + step
            remote(
                view, view, self.send.at[slot], self.recv.at[slot], self.me, self.mate
            ).wait_recv()
            self.mate_copy(self.core, line).start()

    def six(self):
        for line in range(self.lines):
            self.mate_copy(1 - self.core, line).wait_recv()

        def put(at, size):
            rows = pl.ds(at, size)
            self.out[rows, :] = self.low[rows, :].astype(F32)

        self.each(self.out.shape[0], put)
        self.near_copy().wait_send()
        self.side_copy().wait_send()
        for step in range(1, self.lines):
            self.cross_copy(step).wait_send()
            self.line_copy(step).wait_send()
        for line in range(self.lines):
            self.mate_copy(self.core, line).wait_send()


class Spread:
    def __init__(self, whole, share, depth, pieces, scratch):
        self.whole, self.share, self.depth, self.pieces = whole, share, depth, pieces
        send, recv, self.side_send, self.side_recv = scratch
        self.line = Line(whole, share, depth, pieces, send, recv)
        self.me, self.up, self.side = self.line.me, self.line.up, self.line.side

    @staticmethod
    def scratch(depth, pieces):
        return [
            DMA((2, depth, pieces)),
            DMA((2, depth, pieces)),
            DMA((depth, pieces)),
            DMA((depth, pieces)),
        ]

    def peers(self):
        group = lax.axis_index("dp")
        line = [
            (group, (self.up + step) % self.depth * PAIR + self.side)
            for step in range(1, self.depth)
        ]
        return line + [(group, self.me + 1 - 2 * self.side)]

    def peers_beyond(self, depth):
        me, spot, side = place(depth)
        group = lax.axis_index("dp")
        return [
            (group, (self.up + step) % self.depth * PAIR + self.side)
            for step in range(1, self.depth)
        ]

    def view(self, side, index, part):
        rows = self.share // self.pieces
        start = (index * PAIR + side) * self.share + part * rows
        return self.whole.at[pl.ds(pl.multiple_of(start, rows), rows), :]

    def own(self):
        return self.whole.at[pl.ds(pl.multiple_of(self.me * self.share, self.share), self.share), :]

    def across(self, index, part):
        view = self.view(self.side, index, part)
        return remote(
            view,
            view,
            self.side_send.at[index, part],
            self.side_recv.at[index, part],
            self.me + 1 - 2 * self.side,
        )

    def open(self):
        self.line.open()
        for part in range(self.pieces):
            self.across(self.up, part).start()

    def take(self, turn):
        self.line.take(turn, lambda source, part: self.across(source, part).start())

    def crossed(self, index):
        for part in range(self.pieces):
            view = self.view(1 - self.side, index, part)
            remote(
                view, view, self.side_send.at[index, part], self.side_recv.at[index, part], self.me
            ).wait_recv()

    def close(self):
        self.line.close()
        for index in range(self.depth):
            for part in range(self.pieces):
                self.across(index, part).wait_send()


class Share:
    def __init__(self, source, target, send, recv, which, depth, groups):
        self.source, self.target = source, target
        self.send, self.recv, self.which = send, recv, which
        self.me, _, side = place(depth)
        self.group = lax.axis_index("dp")
        self.partner = self.me + depth * (1 - 2 * side)
        rows = source.shape[0]
        self.all_lines = groups // PAIR
        self.cores = PAIR if rows % (PAIR * 16) == 0 else 1
        self.lines = self.all_lines if rows % (groups * 16) == 0 else 1
        self.rows = rows // (self.cores * self.lines)
        self.core = self.group % PAIR
        self.line = self.group // PAIR
        self.my_core = self.core if self.cores > 1 else 0
        self.my_line = self.line if self.lines > 1 else 0

    @staticmethod
    def scratch(members, groups):
        lines = groups // PAIR
        return [DMA((members, 1 + 2 * lines)), DMA((members, 1 + 2 * lines))]

    def view(self, array, core, line):
        if self.cores == 1:
            return array
        start = (core * self.lines + line) * self.rows
        return array.at[pl.ds(pl.multiple_of(start, 16), self.rows), :]

    def behind(self, step):
        return (self.line + self.lines - step) % self.lines

    def copy(self):
        return remote(
            self.view(self.source, self.my_core, self.my_line),
            self.view(self.target, self.my_core, self.my_line),
            self.send.at[self.which, 0],
            self.recv.at[self.which, 0],
            self.partner,
        )

    def hand(self, step):
        view = self.view(self.target, self.my_core, self.my_line)
        return remote(
            view,
            view,
            self.send.at[self.which, step],
            self.recv.at[self.which, step],
            self.me,
            (self.line + step) % self.lines * PAIR + self.core,
        )

    def mate(self, core, line):
        view = self.view(self.target, core, line)
        slot = self.all_lines + line
        return remote(
            view,
            view,
            self.send.at[self.which, slot],
            self.recv.at[self.which, slot],
            self.me,
            self.group + 1 - 2 * self.core,
        )

    def start(self):
        self.copy().start()

    def pass_on(self):
        self.copy().wait_recv()
        for step in range(1, self.lines):
            self.hand(step).start()
        if self.cores > 1:
            self.mate(self.core, self.my_line).start()

    def relay(self):
        for step in range(1, self.lines):
            line = self.behind(step)
            view = self.view(self.target, self.core, line)
            remote(
                view,
                view,
                self.send.at[self.which, step],
                self.recv.at[self.which, step],
                self.me,
                self.group,
            ).wait_recv()
            self.mate(self.core, line).start()

    def wait(self):
        if self.cores > 1:
            for line in range(self.lines):
                self.mate(1 - self.core, line).wait_recv()

    def close(self):
        self.copy().wait_send()
        for step in range(1, self.lines):
            self.hand(step).wait_send()
        if self.cores > 1:
            for line in range(self.lines):
                self.mate(self.core, line).wait_send()


def head_mask(head, width):
    lane = lax.broadcasted_iota(jnp.int32, (1, width), 1)
    return (lane >= head * HD) & (lane < (head + 1) * HD)


def softmax_rows(queries, keys, key_live, scale):
    scores = dot_nt(queries, keys) * scale
    scores = jnp.where(key_live, scores, -1e30)
    top = jnp.max(scores, axis=-1, keepdims=True)
    raised = jnp.exp(scores - top)
    return raised / jnp.sum(raised, axis=-1, keepdims=True)


def attend_shard(normed, heads, row, spots, proj_out, shard, rows, key_live, scale):
    local = heads.shape[0] // 4
    query_bias = row[:, spots["query"] : spots["query"] + local]
    value_bias = row[:, spots["value"] : spots["value"] + local]
    queries = (dot_nt(normed, heads[0:local, :]) + query_bias).astype(LOW)
    keys = dot_nt(normed, heads[local : 2 * local, :]).astype(LOW)
    values = (dot_nt(normed, heads[2 * local : 3 * local, :]) + value_bias).astype(LOW)
    proj_out[shard, 0, rows, :] = queries
    proj_out[shard, 1, rows, :] = keys
    proj_out[shard, 2, rows, :] = values
    attended = jnp.zeros((normed.shape[0], local), F32)
    for head in range(local // HD):
        mask = head_mask(head, local)
        weights = softmax_rows(jnp.where(mask, queries, 0.0).astype(LOW), keys, key_live, scale)
        attended = attended + dot(weights.astype(LOW), jnp.where(mask, values, 0.0).astype(LOW))
    return attended.astype(LOW)


def ahead_kernel(
    sizes,
    groups,
    count,
    index,
    patches,
    cotangent,
    cond,
    mod_weight,
    heads_own,
    up_own,
    down_own,
    row_own,
    normed_out,
    proj_out,
    attended_out,
    tokens_own,
    mod,
    silu_all,
    heads_other,
    up_grad,
    down_grad,
    up_bias_grad,
    down_bias_grad,
    block_own,
    grad_mid_out,
    grad_branch_out,
    sums_out,
    up_other,
    down_other,
    row_other,
    mid_out,
    branch_out,
    patch_rows,
    tokens,
    terms,
    landing,
    total,
    mod_mine,
    mod_gathered,
    patch_sem,
    send,
    recv,
    mod_send,
    mod_recv,
    silu_send,
    silu_recv,
    weight_send,
    weight_recv,
    *rest,
):
    depth, images, kept, share, pieces = sizes
    devices = depth * PAIR
    me, up, side = place(depth)
    group = lax.axis_index("dp")
    width = patches.shape[2]
    local = heads_own.shape[0] // 4
    mods = mod_weight.shape[0]
    spots, _ = row_spots(width, up_own.shape[0], local, mods)
    scale = HD ** (-0.5)
    fold = depth // images
    first = side * images

    def fetch(image):
        return pltpu.make_async_copy(
            patches.at[first + image], patch_rows.at[image], patch_sem.at[image]
        )

    def image_at(turn):
        return across(up // fold, images - 1 - turn, images)

    (
        normed_two,
        cot,
        hidden,
        grad_pre,
        grad_mlp,
        back_terms,
        back_landing,
        mlp_terms,
        mlp_landing,
        back_part,
        mlp_part,
        back_total,
        mlp_total,
        up_sums,
        down_sums,
        cot_sem,
        gather_send,
        gather_recv,
        back_send,
        back_recv,
        mlp_send,
        mlp_recv,
    ) = rest
    units = up_own.shape[0]

    def fetch_cotangent(image):
        return pltpu.make_async_copy(
            cotangent.at[first + image],
            cot.at[pl.ds(pl.multiple_of(image * kept, kept), kept), :],
            cot_sem.at[image],
        )

    for turn in range(images):
        fetch(image_at(turn)).start()
    meet(
        [(group, (me + step) % devices) for step in range(1, devices)]
        + [((group + step) % groups, me) for step in range(1, groups)]
    )
    value = cond[...].astype(F32)
    silu = (value / (1.0 + jnp.exp(-value))).astype(LOW)
    silu_all[group] = silu
    local_mod = (
        dot_nt(silu, mod_weight[...]) + row_own[:, spots["mod"] : spots["mod"] + mods]
    ).astype(LOW)
    mod_mine[...] = local_mod
    mod_gathered[me] = local_mod
    mod_copies = [
        remote(
            mod_mine,
            mod_gathered.at[me],
            mod_send.at[step],
            mod_recv.at[step],
            (me + step) % devices,
        )
        for step in range(1, devices)
    ]
    silu_copies = [
        remote(
            silu_all.at[group],
            silu_all.at[group],
            silu_send.at[step],
            silu_recv.at[step],
            me,
            (group + step) % groups,
        )
        for step in range(1, groups)
    ]
    for copy in mod_copies + silu_copies:
        copy.start()

    shares = [
        Share(source, target, weight_send, weight_recv, which, depth, groups)
        for which, (source, target) in enumerate(
            (
                (row_own, row_other),
                (heads_own, heads_other),
                (up_own, up_other),
                (down_own, down_other),
            )
        )
    ]
    outer = up // (depth // PAIR) == side
    shares[0].start()
    shares[1].start()

    @pl.when(jnp.logical_not(outer))
    def _():
        shares[2].start()
        shares[3].start()

    for image in range(images):
        fetch_cotangent(image).start()
    reduce = Reduce(terms, landing, share, depth, pieces, send, recv)
    gather = Gather(normed_two, share, depth, pieces, gather_send, gather_recv)
    back_reduce = Reduce(back_terms, back_landing, share, depth, pieces, back_send, back_recv)
    mlp_reduce = Reduce(mlp_terms, mlp_landing, share, depth, pieces, mlp_send, mlp_recv)

    def pick_rows(turn, carry):
        image = image_at(turn)
        fetch(image).wait()
        rows = pl.ds(pl.multiple_of(image * kept, kept), kept)
        positions = lax.broadcasted_iota(jnp.int32, (patches.shape[1], kept), 0)
        slots = lax.broadcasted_iota(jnp.int32, (patches.shape[1], kept), 1)
        listed = index[pl.ds(first + image, 1), :]
        pick = jnp.where((positions == listed) & (slots < count[first + image]), 1.0, 0.0)
        tokens[rows, :] = dot_tn(pick.astype(LOW), patch_rows[image]).astype(LOW)
        return carry

    lax.fori_loop(0, images, pick_rows, 0)
    for step in range(1, devices):
        source = (me + devices - step) % devices
        remote(
            mod_mine, mod_gathered.at[source], mod_send.at[step], mod_recv.at[step], me
        ).wait_recv()
    mod[...] = jnp.concatenate(
        [mod_gathered[device].astype(F32) for device in range(devices)], axis=-1
    )

    def block(image, member):
        return mod[pl.ds(first + image, 1), member * width : (member + 1) * width]

    def one(turn, carry):
        image = image_at(turn)
        rows = pl.ds(pl.multiple_of(image * kept, kept), kept)

        @pl.when(turn == images - 1)
        def _():
            shares[0].pass_on()
            shares[1].pass_on()

        norm, _ = norm_parts(tokens[rows, :].astype(F32))
        normed = (norm * (1.0 + block(image, 1)) + block(image, 0)).astype(LOW)
        normed_out[rows, :] = normed
        key_live = lax.broadcasted_iota(jnp.int32, (1, kept), 1) < count[first + image]
        attended_out[0, rows, :] = attend_shard(
            normed, heads_own, row_own, spots, proj_out, 0, rows, key_live, scale
        )
        return carry

    def two(turn, carry):
        image = image_at(turn)
        rows = pl.ds(pl.multiple_of(image * kept, kept), kept)
        key_live = lax.broadcasted_iota(jnp.int32, (1, kept), 1) < count[first + image]
        attended = attend_shard(
            normed_out[rows, :], heads_other, row_other, spots, proj_out, 1, rows, key_live, scale
        )
        attended_out[1, rows, :] = attended
        branch = dot(attended_out[0, rows, :], heads_own[3 * local :, :]) + dot(
            attended, heads_other[3 * local :, :]
        )
        terms[rows, :] = branch.astype(LOW)
        for part in range(fold):
            reduce.ready_share(image * fold + part)
        return carry

    lax.fori_loop(0, images, one, 0)
    shares[1].relay()
    shares[1].wait()
    lax.fori_loop(0, images, two, 0)

    @pl.when(outer)
    def _():
        shares[2].start()
        shares[3].start()

    reduce.relay()
    shares[2].pass_on()
    reduce.finish(total)
    image = (up * share) // kept
    own_rows = pl.ds(pl.multiple_of(up * share, share), share)
    own = tokens[own_rows, :]
    tokens_own[...] = own
    branch = total[...] + row_own[:, spots["out"] : spots["out"] + width]
    branch_out[...] = branch
    mid = own.astype(F32) + block(image, 2) * branch
    mid_out[...] = mid
    norm, _ = norm_parts(mid)
    normed_two[own_rows, :] = (norm * (1.0 + block(image, 4)) + block(image, 3)).astype(LOW)
    shares[2].relay()
    gather.open()

    def half_pass(rows, shard, weight_up, row, weight_down):
        source = normed_two[rows, :]
        grad = grad_mlp[rows, :]
        bias = row[:, spots["up"] : spots["up"] + units]
        pre = dot_nt(source, weight_up[...]) + bias
        square = pre * pre
        bent = jnp.tanh(GELU_ROOT * pre * (1.0 + GELU_CUBE * square))
        half = 0.5 * (1.0 + bent)
        low_hidden = (pre * half).astype(LOW)
        hidden[shard, rows, :] = low_hidden
        slope = half + 0.5 * pre * (1.0 - bent * bent) * (
            GELU_ROOT * (1.0 + 3.0 * GELU_CUBE * square)
        )
        low_grad = (slope * dot_nt(grad, weight_down[...])).astype(LOW)
        grad_pre[shard, rows, :] = low_grad
        sums = jnp.sum(low_grad.astype(F32), axis=0, keepdims=True)
        return dot(low_hidden, weight_down[...]), dot(low_grad, weight_up[...]), sums

    def own_pass(image):
        fetch_cotangent(image).wait()
        rows = pl.ds(pl.multiple_of(image * kept, kept), kept)
        live = lax.broadcasted_iota(jnp.int32, (kept, 1), 0) < count[first + image]
        grad = jnp.where(live, cot[rows, :].astype(F32), 0.0)
        grad = (block(image, 5) * grad).astype(LOW)
        grad_mlp[rows, :] = grad
        down_sums[image] = jnp.sum(grad.astype(F32), axis=0, keepdims=True)
        mlp, back, sums = half_pass(rows, 0, up_own, row_own, down_own)
        up_sums[0, image] = sums
        mlp_part[rows, :] = mlp
        back_part[rows, :] = back

    def other_pass(image):
        rows = pl.ds(pl.multiple_of(image * kept, kept), kept)
        mlp, back, sums = half_pass(rows, 1, up_other, row_other, down_other)
        up_sums[1, image] = sums
        back_terms[rows, :] = (back_part[rows, :] + back).astype(LOW)
        mlp_terms[rows, :] = (mlp_part[rows, :] + mlp).astype(LOW)
        for part in range(fold):
            back_reduce.ready_share(image * fold + part)
            mlp_reduce.ready_share(image * fold + part)

    if fold == 1:

        def own_turn(turn, carry):
            @pl.when(turn == 1)
            def _():
                gather.relay()

            offset = turn + (turn // 2) * (1 - 2 * (turn % 2))
            gather.take(offset)
            own_pass(across(up, offset, depth))

            @pl.when(turn == 1)
            def _():
                shares[3].pass_on()

            return carry

        lax.fori_loop(0, depth, own_turn, 0)
    else:

        def own_image(image, carry):
            own_pass(image)
            return carry

        gather.relay()
        for offset in range(1, depth):
            gather.take(offset)
        shares[3].pass_on()
        lax.fori_loop(0, images, own_image, 0)
    shares[3].relay()
    for member in shares[2:]:
        member.wait()

    def other_turn(turn, carry):
        other_pass(image_at(turn))
        return carry

    lax.fori_loop(0, images, other_turn, 0)
    back_reduce.relay()
    mlp_reduce.relay()
    wide = tile_of(width)
    for shard in range(PAIR):

        def tile(step, carry):
            columns = pl.ds(pl.multiple_of(step * wide, 128), wide)
            up_grad[shard, 0:units, columns] = dot_tn(
                grad_pre[shard], normed_two[:, columns]
            ).astype(LOW)
            down_grad[shard, 0:units, columns] = dot_tn(
                hidden[shard], grad_mlp[:, columns]
            ).astype(LOW)
            return carry

        lax.fori_loop(0, width // wide, tile, 0)
        if units < up_grad.shape[1]:
            rest_rows = jnp.zeros((up_grad.shape[1] - units, width), LOW)
            up_grad[shard, units:, :] = rest_rows
            down_grad[shard, units:, :] = rest_rows
    back_reduce.finish(back_total)
    for shard in range(PAIR):
        up_bias_grad[shard : shard + 1, :] = sum(up_sums[shard, member] for member in range(images))
    down_bias_grad[...] = sum(down_sums[member] for member in range(images))
    live = (
        lax.broadcasted_iota(jnp.int32, (share, 1), 0) + (up * share) % kept
        < count[first + image]
    )
    grad_out = jnp.where(live, cot[own_rows, :].astype(F32), 0.0)
    norm, spread = norm_parts(mid_out[...])
    back = back_total[...]
    grad_mid = grad_out + norm_back(norm, spread, back * (1.0 + block(image, 4)))
    grad_mid_out[...] = grad_mid
    grad_branch_out[...] = (block(image, 2) * grad_mid).astype(LOW)
    sums_out[0:1, :] = jnp.sum(grad_mid * branch_out[...], axis=0, keepdims=True)
    sums_out[1:2, :] = jnp.sum(back, axis=0, keepdims=True)
    sums_out[2:3, :] = jnp.sum(back * norm, axis=0, keepdims=True)
    mlp_reduce.finish(mlp_total)
    mlp = mlp_total[...] + row_own[:, spots["down"] : spots["down"] + width]
    sums_out[3:4, :] = jnp.sum(grad_out * mlp, axis=0, keepdims=True)
    block_own[...] = jnp.where(live, mid_out[...] + block(image, 5) * mlp, 0.0).astype(LOW)
    for step in range(1, groups):
        source = (group + groups - step) % groups
        view = silu_all.at[source]
        remote(
            view, view, silu_send.at[step], silu_recv.at[step], me, group
        ).wait_recv()
    for member in shares:
        member.close()
    for copy in mod_copies + silu_copies:
        copy.wait_send()
    reduce.close()
    gather.close()
    back_reduce.close()
    mlp_reduce.close()


def ahead(sizes, groups, args):
    depth, images, kept, share, pieces = sizes
    count, index, patches, cotangent, cond, mod_weight, heads, up, down, row = args
    spots, width = patches.shape[1:]
    local = heads.shape[0] // 4
    mods = mod_weight.shape[0]
    units = up.shape[0]
    rows = images * kept
    shape = jax.ShapeDtypeStruct
    devices = depth * PAIR
    return pl.pallas_call(
        functools.partial(ahead_kernel, sizes, groups),
        out_shape=(
            shape((rows, width), LOW),
            shape((PAIR, 3, rows, local), LOW),
            shape((PAIR, rows, local), LOW),
            shape((share, width), LOW),
            shape((cond.shape[0], devices * mods), F32),
            shape((groups,) + cond.shape, LOW),
            shape(heads.shape, LOW),
            shape((PAIR, padded(units, groups), width), LOW),
            shape((PAIR, padded(units, groups), width), LOW),
            shape((PAIR, units), F32),
            shape((1, width), F32),
            shape((share, width), LOW),
            shape((share, width), F32),
            shape((share, width), LOW),
            shape((4, width), F32),
        ),
        in_specs=[SM, VM, HB, HB] + [VM] * 6,
        out_specs=(VM,) * 15,
        scratch_shapes=[
            pltpu.VMEM(up.shape, LOW),
            pltpu.VMEM(down.shape, LOW),
            pltpu.VMEM(row.shape, F32),
            pltpu.VMEM((share, width), F32),
            pltpu.VMEM((share, width), F32),
            pltpu.VMEM((images, spots, width), LOW),
            pltpu.VMEM((rows, width), LOW),
            pltpu.VMEM((rows, width), LOW),
            pltpu.VMEM((rows - share, width), LOW),
            pltpu.VMEM((share, width), F32),
            pltpu.VMEM((cond.shape[0], mods), LOW),
            pltpu.VMEM((devices, cond.shape[0], mods), LOW),
            DMA((images,)),
        ]
        + Reduce.scratch(depth, pieces)
        + [
            DMA((devices,)),
            DMA((devices,)),
            DMA((groups,)),
            DMA((groups,)),
        ]
        + Share.scratch(4, groups)
        + [
            pltpu.VMEM((rows, width), LOW),
            pltpu.VMEM((rows, width), LOW),
            pltpu.VMEM((PAIR, rows, units), LOW),
            pltpu.VMEM((PAIR, rows, units), LOW),
            pltpu.VMEM((rows, width), LOW),
            pltpu.VMEM((rows, width), LOW),
            pltpu.VMEM((rows - share, width), LOW),
            pltpu.VMEM((rows, width), LOW),
            pltpu.VMEM((rows - share, width), LOW),
            pltpu.VMEM((rows, width), F32),
            pltpu.VMEM((rows, width), F32),
            pltpu.VMEM((share, width), F32),
            pltpu.VMEM((share, width), F32),
            pltpu.VMEM((PAIR, images, 1, units), F32),
            pltpu.VMEM((images, 1, width), F32),
            DMA((images,)),
        ]
        + Gather.scratch(depth, pieces)
        + Reduce.scratch(depth, pieces)
        + Reduce.scratch(depth, pieces),
        compiler_params=pltpu.CompilerParams(
            collective_id=1, has_side_effects=True, vmem_limit_bytes=62 << 20
        ),
        name="ahead",
    )(*args)


def attend_back_kernel(
    sizes,
    groups,
    count,
    grad_own,
    normed,
    proj,
    attended,
    heads_own,
    heads_other,
    mod,
    tokens_own,
    grad_mid,
    block_own,
    up_grad,
    down_grad,
    heads_grad,
    qv_grad,
    out_bias_grad,
    grad_tokens,
    sums_out,
    block_out,
    up_total,
    down_total,
    grads,
    grad_proj,
    terms,
    landing,
    total,
    qv_sums,
    out_sums,
    own_sem,
    gather_send,
    gather_recv,
    send,
    recv,
    *rest,
):
    depth, images, kept, share, pieces = sizes
    me, up, side = place(depth)
    width = grad_own.shape[1]
    local = heads_own.shape[0] // 4
    scale = HD ** (-0.5)
    fold = depth // images
    first = side * images
    up_fold = Fold(up_grad, rest[:8], up_total, depth, groups)
    down_fold = Fold(down_grad, rest[8:16], down_total, depth, groups)
    spread = Spread(block_out, share, depth, pieces, rest[16:20])
    own_rows = pl.ds(pl.multiple_of(up * share, share), share)
    own_copy = pltpu.make_async_copy(grad_own, grads.at[own_rows, :], own_sem.at[0])
    own_copy.start()
    block_copy = pltpu.make_async_copy(block_own, spread.own(), own_sem.at[1])
    block_copy.start()
    meet(column_peers(depth) + cube_peers(depth, groups) + spread.peers_beyond(depth))
    own_copy.wait()
    gather = Gather(grads, share, depth, pieces, gather_send, gather_recv)
    reduce = Reduce(terms, landing, share, depth, pieces, send, recv)
    gather.open()
    up_fold.one()
    down_fold.one()
    block_copy.wait()

    def one(image):
        rows = pl.ds(pl.multiple_of(image * kept, kept), kept)
        key_live = lax.broadcasted_iota(jnp.int32, (1, kept), 1) < count[first + image]
        grad = grads[rows, :]
        out_sums[image] = jnp.sum(grad.astype(F32), axis=0, keepdims=True)
        back = None
        for shard, heads in enumerate((heads_own, heads_other)):
            grad_att = dot_nt(grad, heads[3 * local :, :]).astype(LOW)
            queries = proj[shard, 0, rows, :]
            keys = proj[shard, 1, rows, :]
            values = proj[shard, 2, rows, :]
            grad_q = jnp.zeros((kept, local), F32)
            grad_k = jnp.zeros((kept, local), F32)
            grad_v = jnp.zeros((kept, local), F32)
            for head in range(local // HD):
                mask = head_mask(head, local)
                head_q = jnp.where(mask, queries, 0.0).astype(LOW)
                head_grad = jnp.where(mask, grad_att, 0.0).astype(LOW)
                weights = softmax_rows(head_q, keys, key_live, scale)
                grad_weights = dot_nt(head_grad, values)
                inner = jnp.sum(weights * grad_weights, axis=-1, keepdims=True)
                grad_scores = (weights * (grad_weights - inner)).astype(LOW)
                grad_v = grad_v + dot_tn(weights.astype(LOW), head_grad)
                grad_q = grad_q + dot(grad_scores, jnp.where(mask, keys, 0.0).astype(LOW))
                grad_k = grad_k + dot_tn(grad_scores, head_q)
            for member, value in enumerate((grad_q * scale, grad_k * scale, grad_v)):
                low = value.astype(LOW)
                grad_proj[shard, member, rows, :] = low
                part = dot(low, heads[member * local : (member + 1) * local, :])
                back = part if back is None else back + part
                if member != 1:
                    row = 2 * shard + member // 2
                    qv_sums[row, image] = jnp.sum(low.astype(F32), axis=0, keepdims=True)
        terms[rows, :] = back.astype(LOW)
        for part in range(fold):
            reduce.ready_share(image * fold + part)

    if fold == 1:

        def turn_of(turn, carry):
            @pl.when(turn == 1)
            def _():
                gather.relay()

            offset = turn + (turn // 2) * (1 - 2 * (turn % 2))
            gather.take(offset)
            one(across(up, offset, depth))

            @pl.when(turn == 0)
            def _():
                up_fold.two()
                down_fold.two()

            @pl.when(turn == 1)
            def _():
                spread.open()

            @pl.when(turn == 2)
            def _():
                up_fold.three()

            @pl.when(turn == 3)
            def _():
                down_fold.three()

            return carry

        lax.fori_loop(0, depth, turn_of, 0)
    else:

        def image_of(image, carry):
            one(image)
            return carry

        gather.relay()
        for offset in range(1, depth):
            gather.take(offset)
        up_fold.two()
        down_fold.two()
        spread.open()
        lax.fori_loop(0, images, image_of, 0)
        up_fold.three()
        down_fold.three()

    def spread_of(turn, carry):
        spread.take(turn)
        return carry

    reduce.relay()
    lax.fori_loop(1, depth - 1, spread_of, 0)
    up_fold.four()
    down_fold.four()
    wide = tile_of(width)
    for shard in range(PAIR):

        def tile(step, carry):
            columns = pl.ds(pl.multiple_of(step * wide, 128), wide)
            source = normed[:, columns]
            for member in range(3):
                heads_grad[shard, member * local : (member + 1) * local, columns] = dot_tn(
                    grad_proj[shard, member], source
                ).astype(LOW)
            heads_grad[shard, 3 * local : 4 * local, columns] = dot_tn(
                attended[shard], grads[:, columns]
            ).astype(LOW)
            return carry

        lax.fori_loop(0, width // wide, tile, 0)
        if 4 * local < heads_grad.shape[1]:
            heads_grad[shard, 4 * local :, :] = jnp.zeros(
                (heads_grad.shape[1] - 4 * local, width), LOW
            )
    up_fold.five()
    spread.take(depth - 1)
    down_fold.five()
    reduce.finish(total)
    for row in range(2 * PAIR):
        qv_grad[row : row + 1, :] = sum(qv_sums[row, image] for image in range(images))
    out_bias_grad[...] = sum(out_sums[image] for image in range(images))
    image = first + (up * share) // kept
    live = (
        lax.broadcasted_iota(jnp.int32, (share, 1), 0) + (up * share) % kept < count[image]
    )
    norm, spread_rows = norm_parts(tokens_own[...].astype(F32))
    back = total[...]
    scale_one = mod[pl.ds(image, 1), width : 2 * width]
    grad = grad_mid[...] + norm_back(norm, spread_rows, back * (1.0 + scale_one))
    grad_tokens[...] = jnp.where(live, grad, 0.0).astype(LOW)
    sums_out[0:1, :] = jnp.sum(back, axis=0, keepdims=True)
    sums_out[1:2, :] = jnp.sum(back * norm, axis=0, keepdims=True)
    up_fold.six()
    down_fold.six()
    for index in range(depth):
        spread.crossed(index)
    spread.close()
    gather.close()
    reduce.close()


def attend_back(sizes, groups, args):
    depth, images, kept, share, pieces = sizes
    width = args[1].shape[1]
    local = args[5].shape[0] // 4
    up_grad, down_grad, units = args[-3:]
    rows = images * kept
    shape = jax.ShapeDtypeStruct
    return pl.pallas_call(
        functools.partial(attend_back_kernel, sizes, groups),
        out_shape=(
            shape((PAIR, padded(4 * local, groups), width), LOW),
            shape((2 * PAIR, local), F32),
            shape((1, width), F32),
            shape((share, width), LOW),
            shape((2, width), F32),
            shape((PAIR * rows, width), LOW),
            shape((units, width), F32),
            shape((units, width), F32),
        ),
        in_specs=[SM] + [VM] * 12,
        out_specs=(VM,) * 8,
        scratch_shapes=[
            pltpu.VMEM((rows, width), LOW),
            pltpu.VMEM((PAIR, 3, rows, local), LOW),
            pltpu.VMEM((rows, width), LOW),
            pltpu.VMEM((rows - share, width), LOW),
            pltpu.VMEM((share, width), F32),
            pltpu.VMEM((2 * PAIR, images, 1, local), F32),
            pltpu.VMEM((images, 1, width), F32),
            DMA((2,)),
        ]
        + Gather.scratch(depth, pieces)
        + Reduce.scratch(depth, pieces)
        + Fold.scratch(up_grad.shape, groups)
        + Fold.scratch(down_grad.shape, groups)
        + Spread.scratch(depth, pieces),
        compiler_params=pltpu.CompilerParams(
            collective_id=3, has_side_effects=True, vmem_limit_bytes=62 << 20
        ),
        name="attend_back",
    )(*args[:-1])


def split_low(value):
    high = value.astype(LOW)
    rest = value - high.astype(F32)
    low = rest.astype(LOW)
    return high, low, (rest - low.astype(F32)).astype(LOW)


def close_kernel(
    sizes,
    groups,
    index,
    grad_tokens,
    sums_one,
    sums_two,
    up_bias_grad,
    qv_grad,
    down_bias_grad,
    out_bias_grad,
    heads_grad,
    silu_all,
    mod_weight,
    cond,
    grad_patches,
    heads_total,
    bias_total,
    mod_weight_grad,
    mod_bias_grad,
    grad_cond,
    whole,
    biases,
    sum_row,
    sum_land,
    bias_land,
    cond_land,
    own_sem,
    sum_send,
    sum_recv,
    bias_send,
    bias_recv,
    cond_send,
    cond_recv,
    *rest,
):
    depth, images, kept, share, pieces = sizes
    devices = depth * PAIR
    everyone = devices * groups
    me, _, side = place(depth)
    up = me // PAIR
    group = lax.axis_index("dp")
    flat = group * devices + me
    width = grad_tokens.shape[1]
    columns = mod_weight.shape[0]
    span = sum_land.shape[2]
    spread = Spread(whole, share, depth, pieces, rest[:4])
    fold = Fold(heads_grad, rest[4:12], heads_total, depth, groups)
    own_copy = pltpu.make_async_copy(grad_tokens, spread.own(), own_sem)
    own_copy.start()
    barrier = pltpu.get_barrier_semaphore()

    def greet(step, carry):
        there = (flat + step) % everyone
        pl.semaphore_signal(
            barrier,
            inc=1,
            device_id={"dp": there // devices, "tensor": there % devices},
            device_id_type=MESH,
        )
        return carry

    lax.fori_loop(1, everyone, greet, 0)
    pl.semaphore_wait(barrier, everyone - 1)
    own_copy.wait()
    fold.one()
    spread.open()

    def aligned(device):
        return pl.multiple_of((device * columns) // 128 * 128, 128)

    for member in range(6):
        part = sums_one[member : member + 1, :] if member < 2 else sums_two[member - 2 : member - 1, :]
        sum_row[:, member * width : (member + 1) * width] = part
    sum_row[:, 6 * width :] = jnp.zeros((1, sum_row.shape[1] - 6 * width), F32)

    def sum_copy(step):
        there = (flat + step) % everyone
        device = there % devices
        return remote(
            sum_row.at[:, pl.ds(aligned(device), span)],
            sum_land.at[flat],
            sum_send.at[step],
            sum_recv.at[step],
            device,
            there // devices,
        )

    def send_sum(step, carry):
        sum_copy(step).start()
        return carry

    lax.fori_loop(1, everyone, send_sum, 0)
    sum_land[flat] = sum_row[:, pl.ds(aligned(me), span)]
    units, local = up_bias_grad.shape[1], qv_grad.shape[1]
    biases[...] = jnp.zeros(biases.shape, F32)
    for shard in range(PAIR):
        biases[3 * shard : 3 * shard + 1, 0:units] = up_bias_grad[shard : shard + 1, :]
        biases[3 * shard + 1 : 3 * shard + 3, 0:local] = qv_grad[2 * shard : 2 * shard + 2, :]
    biases[6:7, :] = down_bias_grad[...]
    biases[7:8, :] = out_bias_grad[...]
    slot = side * groups + group
    bias_land[slot] = biases[...]
    partner = me + depth * (1 - 2 * side)

    def bias_copy(step):
        crossed = step // groups
        there = (group + step) % groups
        device = jnp.where(crossed == 1, partner, me)
        return remote(
            biases, bias_land.at[slot], bias_send.at[step], bias_recv.at[step], device, there
        )

    for step in range(1, PAIR * groups):
        bias_copy(step).start()
    fold.two()

    def wait_sum(step, carry):
        source = (flat + everyone - step) % everyone
        view = sum_land.at[source]
        remote(view, view, sum_send.at[step], sum_recv.at[step], me).wait_recv()
        return carry

    lax.fori_loop(1, everyone, wait_sum, 0)
    offset = (me * columns) % 128
    grads = jnp.concatenate([sum_land[device] for device in range(everyone)], axis=0)
    grads = pltpu.roll(grads, lax.rem(span - offset, span), 1)[:, :columns]
    mod_bias_grad[...] = jnp.sum(grads, axis=0, keepdims=True)
    total_images = images * PAIR

    def image_of(device):
        return device * share // kept

    source = lax.broadcasted_iota(jnp.int32, (everyone, groups * total_images), 0)
    target = lax.broadcasted_iota(jnp.int32, (everyone, groups * total_images), 1)
    row_image = source // devices * total_images + image_of(source % devices)
    chosen = jnp.where(row_image == target, 1.0, 0.0).astype(LOW)
    silu_rows = dot(
        chosen,
        jnp.concatenate([silu_all[member].astype(F32) for member in range(groups)], axis=0).astype(
            LOW
        ),
    ).astype(LOW)
    parts = split_low(grads)
    spread.take(1)
    fold.three()
    mod_weight_grad[...] = (
        dot_tn(parts[0], silu_rows) + dot_tn(parts[1], silu_rows) + dot_tn(parts[2], silu_rows)
    )
    source = lax.broadcasted_iota(jnp.int32, (total_images, everyone), 1)
    target = lax.broadcasted_iota(jnp.int32, (total_images, everyone), 0)
    chosen = jnp.where(
        (source // devices == group) & (image_of(source % devices) == target), 1.0, 0.0
    ).astype(LOW)
    mine = dot(chosen, parts[0]) + dot(chosen, parts[1]) + dot(chosen, parts[2])
    parts = split_low(mine)
    term = (
        dot(parts[0], mod_weight[...])
        + dot(parts[1], mod_weight[...])
        + dot(parts[2], mod_weight[...])
    )
    cond_land[me] = term

    def cond_copy(step):
        return remote(
            cond_land.at[me],
            cond_land.at[me],
            cond_send.at[step],
            cond_recv.at[step],
            (me + step) % devices,
        )

    for step in range(1, devices):
        cond_copy(step).start()
    for turn in range(2, depth - 1):
        spread.take(turn)
    fold.four()
    for step in range(1, PAIR * groups):
        crossed = step // groups
        source_group = (group + groups - step % groups) % groups
        source_side = jnp.where(crossed == 1, 1 - side, side)
        view = bias_land.at[source_side * groups + source_group]
        remote(view, view, bias_send.at[step], bias_recv.at[step], me).wait_recv()
    rows = biases.shape[0]
    result = jnp.zeros((rows, width), F32)
    for member in range(PAIR * groups):
        value = bias_land[member]
        turned = jnp.concatenate([value[3:6, :], value[0:3, :], value[6:, :]], axis=0)
        same = side == member // groups
        result = result + jnp.where(same, value, turned)
    bias_total[...] = result
    for step in range(1, devices):
        source = (me + devices - step) % devices
        view = cond_land.at[source]
        remote(view, view, cond_send.at[step], cond_recv.at[step], me).wait_recv()
    back = cond_land[0]
    for device in range(1, devices):
        back = back + cond_land[device]
    value = cond[...].astype(F32)
    gate = 1.0 / (1.0 + jnp.exp(-value))
    grad_cond[...] = (back * (gate + value * gate * (1.0 - gate))).astype(LOW)

    def place_image(image):
        rows = pl.ds(pl.multiple_of(image * kept, kept), kept)
        positions = lax.broadcasted_iota(jnp.int32, (grad_patches.shape[1], kept), 0)
        pick = jnp.where(positions == index[pl.ds(image, 1), :], 1.0, 0.0).astype(LOW)
        grad_patches[image] = dot(pick, whole[rows, :]).astype(LOW)

    both = PAIR * share // kept

    def put(where):
        spread.crossed(where)
        for image in range(both):
            place_image(where * both + image)

    def arrived(turn, carry):
        put(spread.line.arrival(turn)[2])
        return carry

    put(up)
    lax.fori_loop(1, depth - 1, arrived, 0)
    spread.take(depth - 1)
    fold.five()
    put(spread.line.arrival(depth - 1)[2])
    fold.six()
    spread.close()

    def done_sum(step, carry):
        sum_copy(step).wait_send()
        return carry

    lax.fori_loop(1, everyone, done_sum, 0)
    for step in range(1, PAIR * groups):
        bias_copy(step).wait_send()
    for step in range(1, devices):
        cond_copy(step).wait_send()


def close(sizes, groups, args):
    depth, images, kept, share, pieces = sizes
    index, grad_tokens = args[:2]
    heads_grad, silu_all, mod_weight, cond, local, spots = args[-6:]
    devices = depth * PAIR
    width = grad_tokens.shape[1]
    columns = mod_weight.shape[0]
    biases = (8, width)
    span = max(-(-((device * columns) % 128 + columns) // 128) * 128 for device in range(devices))
    long = max((device * columns) // 128 * 128 + span for device in range(devices))
    long = max(long, 6 * width + 128)
    shape = jax.ShapeDtypeStruct
    rows = PAIR * images * kept
    everyone = devices * groups
    return pl.pallas_call(
        functools.partial(close_kernel, sizes, groups),
        out_shape=(
            shape((PAIR * images, spots, width), LOW),
            shape((4 * local, width), F32),
            shape(biases, F32),
            shape(mod_weight.shape, F32),
            shape((1, columns), F32),
            shape(cond.shape, LOW),
        ),
        in_specs=[VM] * 12,
        out_specs=(VM,) * 6,
        scratch_shapes=[
            pltpu.VMEM((rows, width), LOW),
            pltpu.VMEM(biases, F32),
            pltpu.VMEM((1, long), F32),
            pltpu.VMEM((everyone, 1, span), F32),
            pltpu.VMEM((PAIR * groups,) + biases, F32),
            pltpu.VMEM((devices,) + cond.shape, F32),
            DMA,
            DMA((everyone,)),
            DMA((everyone,)),
            DMA((PAIR * groups,)),
            DMA((PAIR * groups,)),
            DMA((devices,)),
            DMA((devices,)),
        ]
        + Spread.scratch(depth, pieces)
        + Fold.scratch(heads_grad.shape, groups),
        compiler_params=pltpu.CompilerParams(
            collective_id=4, has_side_effects=True, vmem_limit_bytes=62 << 20
        ),
        name="close",
    )(*args[:-2])


def on_device(
    patches,
    conditioning,
    keep_count,
    keep_index,
    mod_weight,
    mod_bias,
    qkv_weight,
    qv_bias,
    out_weight,
    out_bias,
    up_weight,
    up_bias,
    down_weight,
    down_bias,
    out_cotangent,
):
    devices = lax.axis_size("tensor")
    depth = devices // PAIR
    all_images, kept = keep_index.shape
    width = patches.shape[2]
    images = all_images // PAIR
    share = images * kept // depth
    pieces = 4 if share % 64 == 0 else 2
    sizes = (depth, images, kept, share, pieces)
    groups = lax.axis_size("dp")
    local, units, mods = qkv_weight.shape[2], up_weight.shape[1], mod_weight.shape[1]
    up = up_weight.T
    mod_rows = mod_weight.T
    heads = jnp.concatenate(
        [jnp.swapaxes(qkv_weight, 1, 2).reshape(3 * local, width), out_weight], axis=0
    )

    def spaced(value):
        return jnp.pad(value.astype(F32), (0, lanes(value.shape[0]) - value.shape[0]))

    row = jnp.concatenate(
        [
            spaced(value)
            for value in (out_bias, down_bias, up_bias, qv_bias[0], qv_bias[1], mod_bias)
        ]
    )[None, :]
    (
        normed_one,
        proj,
        attended,
        tokens_own,
        mod,
        silu_all,
        heads_other,
        up_grad,
        down_grad,
        up_bias_grad,
        down_bias_grad,
        block_own,
        grad_mid,
        grad_branch,
        sums_two,
    ) = ahead(
        sizes,
        groups,
        (
            keep_count,
            keep_index,
            patches,
            out_cotangent,
            conditioning,
            mod_rows,
            heads,
            up,
            down_weight,
            row,
        ),
    )
    (
        heads_grad,
        qv_grad,
        out_bias_grad,
        grad_tokens,
        sums_one,
        block_out,
        up_total,
        down_total,
    ) = attend_back(
        sizes,
        groups,
        (
            keep_count,
            grad_branch,
            normed_one,
            proj,
            attended,
            heads,
            heads_other,
            mod,
            tokens_own,
            grad_mid,
            block_own,
            up_grad,
            down_grad,
            units,
        ),
    )
    (
        grad_patches,
        heads_total,
        bias_total,
        mod_rows_grad,
        mod_bias_grad,
        grad_conditioning,
    ) = close(
        sizes,
        groups,
        (
            keep_index,
            grad_tokens,
            sums_one,
            sums_two,
            up_bias_grad,
            qv_grad,
            down_bias_grad,
            out_bias_grad,
            heads_grad,
            silu_all,
            mod_rows,
            conditioning,
            local,
            patches.shape[1],
        ),
    )
    return (
        block_out.reshape(all_images, kept, width),
        grad_patches,
        grad_conditioning,
        mod_rows_grad.T,
        mod_bias_grad[0],
        jnp.swapaxes(heads_total[: 3 * local].reshape(3, local, width), 1, 2),
        bias_total[1:3, :local],
        heads_total[3 * local :],
        bias_total[7],
        up_total.T,
        bias_total[0, :units],
        down_total,
        bias_total[6],
    )


def solution(mesh):
    placed = (
        P("dp", None, None),
        P("dp", None),
        P("dp"),
        P("dp", None),
        P(None, "tensor"),
        P("tensor"),
        P(None, None, "tensor"),
        P(None, "tensor"),
        P("tensor", None),
        P(),
        P(None, "tensor"),
        P("tensor"),
        P("tensor", None),
        P(),
        P("dp", None, None),
    )
    return jax.shard_map(
        on_device,
        mesh=mesh,
        in_specs=placed,
        out_specs=(
            P("dp", None, None),
            P("dp", None, None),
            P("dp", None),
            P(None, "tensor"),
            P("tensor"),
            P(None, None, "tensor"),
            P(None, "tensor"),
            P("tensor", None),
            P(),
            P(None, "tensor"),
            P("tensor"),
            P("tensor", None),
            P(),
        ),
        check_vma=False,
    )
```

```python
import functools

import jax
import jax.numpy as jnp
from jax import lax
from jax.experimental import pallas as pl
from jax.experimental.pallas import tpu as pltpu
from jax.sharding import PartitionSpec as P

HD = 72
MESH = pl.DeviceIdType.MESH
F32 = jnp.float32
LOW = jnp.bfloat16
DMA = pltpu.SemaphoreType.DMA
VM = pl.BlockSpec(memory_space=pltpu.VMEM)
SM = pl.BlockSpec(memory_space=pltpu.SMEM)
HB = pl.BlockSpec(memory_space=pl.ANY)
PAIR = 2
GELU_ROOT = 0.7978845608028654
GELU_CUBE = 0.044715


def remote(source, target, send_sem, recv_sem, device, group=None):
    there = {"tensor": device} if group is None else {"dp": group, "tensor": device}
    return pltpu.make_async_remote_copy(
        src_ref=source,
        dst_ref=target,
        send_sem=send_sem,
        recv_sem=recv_sem,
        device_id=there,
        device_id_type=MESH,
    )


def place(depth):
    me = lax.axis_index("tensor")
    return me, me % depth, me // depth


def bits_of(depth):
    return depth.bit_length() - 1


def toward(spot, bit):
    return (1 - 2 * ((spot // (1 << bit)) % 2)) * (1 << bit)


def across(spot, offset, depth):
    result = spot
    for bit in range(bits_of(depth)):
        result = result + ((offset // (1 << bit)) % 2) * toward(spot, bit)
    return result


def offset_between(left, right, depth):
    result = 0
    for bit in range(bits_of(depth)):
        size = 1 << bit
        result = result + ((left // size + right // size) % 2) * size
    return result


def meet(peers):
    barrier = pltpu.get_barrier_semaphore()
    for group, peer in peers:
        pl.semaphore_signal(
            barrier, inc=1, device_id={"dp": group, "tensor": peer}, device_id_type=MESH
        )
    pl.semaphore_wait(barrier, len(peers))


def column_peers(depth):
    me, spot, side = place(depth)
    group = lax.axis_index("dp")
    return [(group, me + toward(spot, bit)) for bit in range(bits_of(depth))]


def cube_peers(depth, groups):
    me, spot, side = place(depth)
    group = lax.axis_index("dp")
    other = me + depth * (1 - 2 * side)
    peers = [((group + step) % groups, me) for step in range(1, groups)]
    return peers + [((group + step) % groups, other) for step in range(groups)]


def padded(rows, groups):
    return -(-rows // (16 * groups)) * 16 * groups


def lanes(columns):
    return -(-columns // 128) * 128


def row_spots(width, units, local, mods):
    spots = {}
    start = 0
    for name, size in (
        ("out", width),
        ("down", width),
        ("up", units),
        ("query", local),
        ("value", local),
        ("mod", mods),
    ):
        spots[name] = start
        start += lanes(size)
    return spots, start


def tile_of(width):
    return 384 if width % 384 == 0 else 128


def dot(left, right):
    return jnp.dot(left, right, preferred_element_type=F32)


def dot_nt(left, right):
    return lax.dot_general(left, right, (((1,), (1,)), ((), ())), preferred_element_type=F32)


def dot_tn(left, right):
    return lax.dot_general(left, right, (((0,), (0,)), ((), ())), preferred_element_type=F32)


def norm_parts(rows):
    width = rows.shape[-1]
    centred = rows - jnp.sum(rows, axis=-1, keepdims=True) * (1.0 / width)
    spread = lax.rsqrt(jnp.sum(centred * centred, axis=-1, keepdims=True) * (1.0 / width) + 1e-06)
    return centred * spread, spread


def norm_back(norm, spread, grad):
    width = norm.shape[-1]
    mean_grad = jnp.sum(grad, axis=-1, keepdims=True) * (1.0 / width)
    mean_both = jnp.sum(grad * norm, axis=-1, keepdims=True) * (1.0 / width)
    return (grad - mean_grad - norm * mean_both) * spread


class Line:
    def __init__(self, buffer, share, depth, pieces, send, recv):
        self.buffer, self.share, self.depth, self.pieces = buffer, share, depth, pieces
        self.send, self.recv = send, recv
        self.me = lax.axis_index("tensor")
        self.up, self.side = self.me // PAIR, self.me % PAIR

    def piece(self, index, part):
        rows = self.share // self.pieces
        start = (index * PAIR + self.side) * self.share + part * rows
        return self.buffer.at[pl.ds(pl.multiple_of(start, rows), rows), :]

    def copy(self, way, step, part):
        source = self.up - (step - 1) * (1 - 2 * way)
        target = self.up + 1 - 2 * way
        view = self.piece(source, part)
        return remote(
            view,
            view,
            self.send.at[way, step, part],
            self.recv.at[way, step, part],
            target * PAIR + self.side,
        )

    def may_send(self, way, step):
        if way == 0:
            return (self.up + 1 < self.depth) & (self.up >= step - 1)
        return (self.up >= 1) & (self.up + step - 1 < self.depth)

    def open(self):
        for part in range(self.pieces):
            for way in range(2):

                @pl.when(self.may_send(way, 1))
                def _():
                    self.copy(way, 1, part).start()

    def arrival(self, turn):
        below = self.up
        above = self.depth - 1 - self.up
        both = jnp.minimum(below, above)
        mixed = turn <= 2 * both
        way = jnp.where(mixed, (turn + 1) % 2, jnp.where(below > above, 0, 1))
        step = jnp.where(mixed, (turn + 1) // 2, turn - both)
        return way, step, self.up - step * (1 - 2 * way)

    def take(self, turn, then):
        way, step, source = self.arrival(turn)
        ahead = jnp.where(way == 0, self.up + 1 < self.depth, self.up >= 1)
        for part in range(self.pieces):
            view = self.piece(source, part)
            remote(
                view, view, self.send.at[way, step, part], self.recv.at[way, step, part], self.me
            ).wait_recv()

            @pl.when(ahead)
            def _():
                self.copy(way, step + 1, part).start()

            then(source, part)

    def close(self):
        for way in range(2):
            for step in range(1, self.depth):

                @pl.when(self.may_send(way, step))
                def _():
                    for part in range(self.pieces):
                        self.copy(way, step, part).wait_send()


class Cube:
    def __init__(self, share, depth, pieces):
        self.share, self.depth, self.pieces = share, depth, pieces
        self.me, self.spot, self.side = place(depth)
        self.bits = bits_of(depth)
        self.rows = share // pieces

    def order(self, part):
        ways = list(range(self.bits))
        return ways if part % 2 else ways[::-1]

    def span(self, index, part):
        return pl.ds(pl.multiple_of(index * self.share + part * self.rows, self.rows), self.rows)

    def neighbour(self, bit):
        return self.me + toward(self.spot, bit)


class Gather(Cube):
    def __init__(self, buffer, share, depth, pieces, send, recv):
        super().__init__(share, depth, pieces)
        self.buffer, self.send, self.recv = buffer, send, recv

    def last(self, offset, part):
        order = self.order(part)
        return max(
            (stage for stage in range(self.bits) if offset >> order[stage] & 1), default=-1
        )

    def copy(self, offset, stage, part):
        bit = self.order(part)[stage]
        view = self.buffer.at[self.span(across(self.spot, offset, self.depth), part), :]
        return remote(
            view,
            view,
            self.send.at[offset, stage, part],
            self.recv.at[offset ^ (1 << bit), part],
            self.neighbour(bit),
        )

    def landed(self, offset, part):
        view = self.buffer.at[self.span(across(self.spot, offset, self.depth), part), :]
        remote(
            view, view, self.send.at[0, 0, part], self.recv.at[offset, part], self.me
        ).wait_recv()

    def sends(self, offset):
        return [
            (stage, part)
            for part in range(self.pieces)
            for stage in range(self.last(offset, part) + 1, self.bits)
        ]

    def open(self):
        for stage, part in self.sends(0):
            self.copy(0, stage, part).start()

    def relay(self):
        for offset in sorted(range(1, self.depth), key=lambda value: bin(value).count("1")):
            for part in range(self.pieces):
                first = self.last(offset, part) + 1
                if first < self.bits:
                    self.landed(offset, part)
                    for stage in range(first, self.bits):
                        self.copy(offset, stage, part).start()

    def take(self, offset):
        for member in range(1, self.depth):

            @pl.when(offset == member)
            def _():
                for part in range(self.pieces):
                    if self.last(member, part) + 1 == self.bits:
                        self.landed(member, part)

    def close(self):
        for offset in range(self.depth):
            for stage, part in self.sends(offset):
                self.copy(offset, stage, part).wait_send()

    @staticmethod
    def scratch(depth, pieces):
        return [DMA((depth, bits_of(depth), pieces)), DMA((depth, pieces))]


class Reduce(Cube):
    def __init__(self, terms, landing, share, depth, pieces, send, recv):
        super().__init__(share, depth, pieces)
        self.terms, self.landing, self.send, self.recv = terms, landing, send, recv

    def slot(self, stage, offset, part):
        order = self.order(part)
        found = [
            (level, member)
            for level in range(self.bits)
            for member in range(self.depth)
            if not any(member >> order[below] & 1 for below in range(level + 1))
        ]
        return found.index((stage, offset))

    def first(self, offset, part):
        order = self.order(part)
        return min(stage for stage in range(self.bits) if offset >> order[stage] & 1)

    def copy(self, offset, part):
        stage = self.first(offset, part)
        bit = self.order(part)[stage]
        slot = self.slot(stage, offset ^ (1 << bit), part)
        return remote(
            self.terms.at[self.span(across(self.spot, offset, self.depth), part), :],
            self.landing.at[self.span(slot, part), :],
            self.send.at[offset, part],
            self.recv.at[slot, part],
            self.neighbour(bit),
        )

    def landed(self, slot, part):
        view = self.landing.at[self.span(slot, part), :]
        remote(view, view, self.send.at[0, part], self.recv.at[slot, part], self.me).wait_recv()

    def ready(self, offset):
        for member in range(1, self.depth):

            @pl.when(offset == member)
            def _():
                for part in range(self.pieces):
                    if self.first(member, part) == 0:
                        self.copy(member, part).start()

    def ready_share(self, index):
        self.ready(offset_between(index, self.spot, self.depth))

    def add(self, target, target_start, term_start, slots, part):
        def body(index, carry):
            offset = index * 16
            value = self.terms[pl.ds(pl.multiple_of(term_start + offset, 16), 16), :].astype(F32)
            for slot in slots:
                start = slot * self.share + part * self.rows
                value = value + self.landing[
                    pl.ds(pl.multiple_of(start + offset, 16), 16), :
                ].astype(F32)
            target[pl.ds(pl.multiple_of(target_start + offset, 16), 16), :] = value.astype(
                target.dtype
            )
            return carry

        lax.fori_loop(0, self.rows // 16, body, 0)

    def relay(self):
        for level in range(1, self.bits):
            for part in range(self.pieces):
                for offset in range(1, self.depth):
                    if self.first(offset, part) == level:
                        slots = [self.slot(below, offset, part) for below in range(level)]
                        for slot in slots:
                            self.landed(slot, part)
                        start = (
                            across(self.spot, offset, self.depth) * self.share + part * self.rows
                        )
                        self.add(self.terms, start, start, slots, part)
                        self.copy(offset, part).start()

    def finish(self, total):
        for part in range(self.pieces):
            slots = [self.slot(stage, 0, part) for stage in range(self.bits)]
            for slot in slots:
                self.landed(slot, part)
            skip = part * self.rows
            self.add(total, skip, self.spot * self.share + skip, slots, part)

    def close(self):
        for offset in range(1, self.depth):
            for part in range(self.pieces):
                self.copy(offset, part).wait_send()

    @staticmethod
    def scratch(depth, pieces):
        return [DMA((depth, pieces)), DMA((depth - 1, pieces))]


class Fold:
    def __init__(self, source, scratch, low, depth, groups):
        self.source, self.low = source, low
        (
            self.stage,
            self.near,
            self.land,
            self.part,
            self.side_land,
            self.send,
            self.recv,
        ) = scratch
        self.me = lax.axis_index("tensor")
        self.group = lax.axis_index("dp")
        self.lines = groups // PAIR
        self.core = self.group % PAIR
        self.line = self.group // PAIR
        self.mate = self.group + 1 - 2 * self.core
        self.partner = self.me + depth * (1 - 2 * (self.me // depth))
        self.rows = self.part.shape[1]
        self.half = self.rows * self.lines

    @staticmethod
    def scratch(shape, groups):
        _, rows, width = shape
        lines = groups // PAIR
        part = rows // groups
        return [
            pltpu.VMEM((PAIR, part * lines, width), LOW),
            pltpu.VMEM((PAIR, part * lines, width), LOW),
            pltpu.VMEM((lines, PAIR, part, width), LOW),
            pltpu.VMEM((PAIR, part, width), LOW),
            pltpu.VMEM((part, width), LOW),
            DMA((2 + 3 * lines,)),
            DMA((2 + 3 * lines,)),
        ]

    def each(self, rows, body):
        step = 48 if rows % 48 == 0 else 16 if rows % 16 == 0 else rows

        def run(index, carry):
            body(pl.multiple_of(index * step, step), step)
            return carry

        lax.fori_loop(0, rows // step, run, 0)

    def window(self, start, size):
        return pl.ds(pl.multiple_of(start, 16), size)

    def behind(self, step):
        return (self.line + self.lines - step) % self.lines

    def block(self, core, line):
        return self.low.at[self.window(core * self.half + line * self.rows, self.rows), :]

    def near_copy(self):
        return remote(
            self.source.at[:, self.window((1 - self.core) * self.half, self.half), :],
            self.near,
            self.send.at[0],
            self.recv.at[0],
            self.me,
            self.mate,
        )

    def cross_copy(self, step):
        line = (self.line + step) % self.lines
        return remote(
            self.stage.at[:, self.window(line * self.rows, self.rows), :],
            self.land.at[self.line],
            self.send.at[2 + step],
            self.recv.at[2 + step],
            self.me,
            line * PAIR + self.core,
        )

    def side_copy(self):
        return remote(
            self.part.at[1],
            self.side_land,
            self.send.at[1],
            self.recv.at[1],
            self.partner,
            self.group,
        )

    def line_copy(self, step):
        line = (self.line + step) % self.lines
        view = self.block(self.core, self.line)
        slot = 2 + self.lines + step
        return remote(
            view,
            view,
            self.send.at[slot],
            self.recv.at[slot],
            self.me,
            line * PAIR + self.core,
        )

    def mate_copy(self, core, line):
        view = self.block(core, line)
        slot = 2 + 2 * self.lines + line
        return remote(view, view, self.send.at[slot], self.recv.at[slot], self.me, self.mate)

    def one(self):
        self.near_copy().start()

    def two(self):
        self.near_copy().wait_recv()

        def add(at, size):
            rows = self.window(at, size)
            for shard in range(PAIR):
                mine = self.source[shard, self.window(self.core * self.half + at, size), :]
                self.stage[shard, rows, :] = (
                    mine.astype(F32) + self.near[shard, rows, :].astype(F32)
                ).astype(LOW)

        self.each(self.half, add)
        for step in range(1, self.lines):
            self.cross_copy(step).start()

    def three(self):
        for step in range(1, self.lines):
            view = self.land.at[self.behind(step)]
            remote(
                view, view, self.send.at[2 + step], self.recv.at[2 + step], self.me, self.mate
            ).wait_recv()

        def add(at, size):
            rows = self.window(at, size)
            for shard in range(PAIR):
                value = self.stage[
                    shard, self.window(self.line * self.rows + at, size), :
                ].astype(F32)
                for step in range(1, self.lines):
                    value = value + self.land[self.behind(step), shard, rows, :].astype(F32)
                self.part[shard, rows, :] = value.astype(LOW)

        self.each(self.rows, add)
        self.side_copy().start()

    def four(self):
        self.side_copy().wait_recv()

        def add(at, size):
            rows = self.window(at, size)
            value = self.part[0, rows, :].astype(F32) + self.side_land[rows, :].astype(F32)
            spot = self.window(self.core * self.half + self.line * self.rows + at, size)
            self.low[spot, :] = value.astype(LOW)

        self.each(self.rows, add)
        for step in range(1, self.lines):
            self.line_copy(step).start()
        self.mate_copy(self.core, self.line).start()

    def five(self):
        for step in range(1, self.lines):
            line = self.behind(step)
            view = self.block(self.core, line)
            slot = 2 + self.lines + step
            remote(
                view, view, self.send.at[slot], self.recv.at[slot], self.me, self.mate
            ).wait_recv()
            self.mate_copy(self.core, line).start()

    def six(self):
        for line in range(self.lines):
            self.mate_copy(1 - self.core, line).wait_recv()
        self.near_copy().wait_send()
        self.side_copy().wait_send()
        for step in range(1, self.lines):
            self.cross_copy(step).wait_send()
            self.line_copy(step).wait_send()
        for line in range(self.lines):
            self.mate_copy(self.core, line).wait_send()


class Spread:
    def __init__(self, whole, share, depth, pieces, scratch):
        self.whole, self.share, self.depth, self.pieces = whole, share, depth, pieces
        send, recv, self.side_send, self.side_recv = scratch
        self.line = Line(whole, share, depth, pieces, send, recv)
        self.me, self.up, self.side = self.line.me, self.line.up, self.line.side

    @staticmethod
    def scratch(depth, pieces):
        return [
            DMA((2, depth, pieces)),
            DMA((2, depth, pieces)),
            DMA((depth, pieces)),
            DMA((depth, pieces)),
        ]

    def peers(self):
        group = lax.axis_index("dp")
        line = [
            (group, (self.up + step) % self.depth * PAIR + self.side)
            for step in range(1, self.depth)
        ]
        return line + [(group, self.me + 1 - 2 * self.side)]

    def peers_beyond(self, depth):
        me, spot, side = place(depth)
        group = lax.axis_index("dp")
        return [
            (group, (self.up + step) % self.depth * PAIR + self.side)
            for step in range(1, self.depth)
        ]

    def view(self, side, index, part):
        rows = self.share // self.pieces
        start = (index * PAIR + side) * self.share + part * rows
        return self.whole.at[pl.ds(pl.multiple_of(start, rows), rows), :]

    def own(self):
        return self.whole.at[pl.ds(pl.multiple_of(self.me * self.share, self.share), self.share), :]

    def across(self, index, part):
        view = self.view(self.side, index, part)
        return remote(
            view,
            view,
            self.side_send.at[index, part],
            self.side_recv.at[index, part],
            self.me + 1 - 2 * self.side,
        )

    def open(self):
        self.line.open()
        for part in range(self.pieces):
            self.across(self.up, part).start()

    def take(self, turn):
        self.line.take(turn, lambda source, part: self.across(source, part).start())

    def crossed(self, index):
        for part in range(self.pieces):
            view = self.view(1 - self.side, index, part)
            remote(
                view, view, self.side_send.at[index, part], self.side_recv.at[index, part], self.me
            ).wait_recv()

    def close(self):
        self.line.close()
        for index in range(self.depth):
            for part in range(self.pieces):
                self.across(index, part).wait_send()


class Share:
    def __init__(self, source, target, send, recv, which, depth, groups):
        self.source, self.target = source, target
        self.send, self.recv, self.which = send, recv, which
        self.me, _, side = place(depth)
        self.group = lax.axis_index("dp")
        self.partner = self.me + depth * (1 - 2 * side)
        rows = source.shape[0]
        self.all_lines = groups // PAIR
        self.cores = PAIR if rows % (PAIR * 16) == 0 else 1
        self.lines = self.all_lines if rows % (groups * 16) == 0 else 1
        self.rows = rows // (self.cores * self.lines)
        self.core = self.group % PAIR
        self.line = self.group // PAIR
        self.my_core = self.core if self.cores > 1 else 0
        self.my_line = self.line if self.lines > 1 else 0

    @staticmethod
    def scratch(members, groups):
        lines = groups // PAIR
        return [DMA((members, 1 + 2 * lines)), DMA((members, 1 + 2 * lines))]

    def view(self, array, core, line):
        if self.cores == 1:
            return array
        start = (core * self.lines + line) * self.rows
        return array.at[pl.ds(pl.multiple_of(start, 16), self.rows), :]

    def behind(self, step):
        return (self.line + self.lines - step) % self.lines

    def copy(self):
        return remote(
            self.view(self.source, self.my_core, self.my_line),
            self.view(self.target, self.my_core, self.my_line),
            self.send.at[self.which, 0],
            self.recv.at[self.which, 0],
            self.partner,
        )

    def hand(self, step):
        view = self.view(self.target, self.my_core, self.my_line)
        return remote(
            view,
            view,
            self.send.at[self.which, step],
            self.recv.at[self.which, step],
            self.me,
            (self.line + step) % self.lines * PAIR + self.core,
        )

    def mate(self, core, line):
        view = self.view(self.target, core, line)
        slot = self.all_lines + line
        return remote(
            view,
            view,
            self.send.at[self.which, slot],
            self.recv.at[self.which, slot],
            self.me,
            self.group + 1 - 2 * self.core,
        )

    def start(self):
        self.copy().start()

    def pass_on(self):
        self.copy().wait_recv()
        for step in range(1, self.lines):
            self.hand(step).start()
        if self.cores > 1:
            self.mate(self.core, self.my_line).start()

    def relay(self):
        for step in range(1, self.lines):
            line = self.behind(step)
            view = self.view(self.target, self.core, line)
            remote(
                view,
                view,
                self.send.at[self.which, step],
                self.recv.at[self.which, step],
                self.me,
                self.group,
            ).wait_recv()
            self.mate(self.core, line).start()

    def wait(self):
        if self.cores > 1:
            for line in range(self.lines):
                self.mate(1 - self.core, line).wait_recv()

    def close(self):
        self.copy().wait_send()
        for step in range(1, self.lines):
            self.hand(step).wait_send()
        if self.cores > 1:
            for line in range(self.lines):
                self.mate(self.core, line).wait_send()


def head_mask(head, width):
    lane = lax.broadcasted_iota(jnp.int32, (1, width), 1)
    return (lane >= head * HD) & (lane < (head + 1) * HD)


def softmax_rows(queries, keys, key_live, scale):
    scores = dot_nt(queries, keys) * scale
    scores = jnp.where(key_live, scores, -1e30)
    top = jnp.max(scores, axis=-1, keepdims=True)
    raised = jnp.exp(scores - top)
    return raised / jnp.sum(raised, axis=-1, keepdims=True)


def attend_shard(normed, heads, row, spots, proj_out, shard, rows, key_live, scale):
    local = heads.shape[0] // 4
    query_bias = row[:, spots["query"] : spots["query"] + local]
    value_bias = row[:, spots["value"] : spots["value"] + local]
    queries = (dot_nt(normed, heads[0:local, :]) + query_bias).astype(LOW)
    keys = dot_nt(normed, heads[local : 2 * local, :]).astype(LOW)
    values = (dot_nt(normed, heads[2 * local : 3 * local, :]) + value_bias).astype(LOW)
    proj_out[shard, 0, rows, :] = queries
    proj_out[shard, 1, rows, :] = keys
    proj_out[shard, 2, rows, :] = values
    attended = jnp.zeros((normed.shape[0], local), F32)
    for head in range(local // HD):
        mask = head_mask(head, local)
        weights = softmax_rows(jnp.where(mask, queries, 0.0).astype(LOW), keys, key_live, scale)
        attended = attended + dot(weights.astype(LOW), jnp.where(mask, values, 0.0).astype(LOW))
    return attended.astype(LOW)


def ahead_kernel(
    sizes,
    groups,
    count,
    index,
    patches,
    cotangent,
    cond,
    mod_weight,
    heads_own,
    up_own,
    down_own,
    row_own,
    normed_out,
    proj_out,
    attended_out,
    tokens_own,
    mod,
    silu_all,
    heads_other,
    up_grad,
    down_grad,
    up_bias_grad,
    down_bias_grad,
    block_own,
    grad_mid_out,
    grad_branch_out,
    sums_out,
    up_other,
    down_other,
    row_other,
    mid_out,
    branch_out,
    patch_rows,
    tokens,
    terms,
    landing,
    total,
    mod_mine,
    mod_gathered,
    patch_sem,
    send,
    recv,
    mod_send,
    mod_recv,
    silu_send,
    silu_recv,
    weight_send,
    weight_recv,
    *rest,
):
    depth, images, kept, share, pieces = sizes
    devices = depth * PAIR
    me, up, side = place(depth)
    group = lax.axis_index("dp")
    width = patches.shape[2]
    local = heads_own.shape[0] // 4
    mods = mod_weight.shape[0]
    spots, _ = row_spots(width, up_own.shape[0], local, mods)
    scale = HD ** (-0.5)
    fold = depth // images
    first = side * images

    def fetch(image):
        return pltpu.make_async_copy(
            patches.at[first + image], patch_rows.at[image], patch_sem.at[image]
        )

    def image_at(turn):
        return across(up // fold, images - 1 - turn, images)

    (
        normed_two,
        cot,
        hidden,
        grad_pre,
        grad_mlp,
        back_terms,
        back_landing,
        mlp_terms,
        mlp_landing,
        back_part,
        mlp_part,
        back_total,
        mlp_total,
        up_sums,
        down_sums,
        cot_sem,
        gather_send,
        gather_recv,
        back_send,
        back_recv,
        mlp_send,
        mlp_recv,
    ) = rest
    units = up_own.shape[0]

    def fetch_cotangent(image):
        return pltpu.make_async_copy(
            cotangent.at[first + image],
            cot.at[pl.ds(pl.multiple_of(image * kept, kept), kept), :],
            cot_sem.at[image],
        )

    for turn in range(images):
        fetch(image_at(turn)).start()
    meet(
        [(group, (me + step) % devices) for step in range(1, devices)]
        + [((group + step) % groups, me) for step in range(1, groups)]
    )
    value = cond[...].astype(F32)
    silu = (value / (1.0 + jnp.exp(-value))).astype(LOW)
    silu_all[group] = silu
    local_mod = (
        dot_nt(silu, mod_weight[...]) + row_own[:, spots["mod"] : spots["mod"] + mods]
    ).astype(LOW)
    mod_mine[...] = local_mod
    mod_gathered[me] = local_mod
    mod_copies = [
        remote(
            mod_mine,
            mod_gathered.at[me],
            mod_send.at[step],
            mod_recv.at[step],
            (me + step) % devices,
        )
        for step in range(1, devices)
    ]
    silu_copies = [
        remote(
            silu_all.at[group],
            silu_all.at[group],
            silu_send.at[step],
            silu_recv.at[step],
            me,
            (group + step) % groups,
        )
        for step in range(1, groups)
    ]
    for copy in mod_copies + silu_copies:
        copy.start()

    shares = [
        Share(source, target, weight_send, weight_recv, which, depth, groups)
        for which, (source, target) in enumerate(
            (
                (row_own, row_other),
                (heads_own, heads_other),
                (up_own, up_other),
                (down_own, down_other),
            )
        )
    ]
    outer = up // (depth // PAIR) == side
    shares[0].start()
    shares[1].start()

    @pl.when(jnp.logical_not(outer))
    def _():
        shares[2].start()
        shares[3].start()

    for image in range(images):
        fetch_cotangent(image).start()
    reduce = Reduce(terms, landing, share, depth, pieces, send, recv)
    gather = Gather(normed_two, share, depth, pieces, gather_send, gather_recv)
    back_reduce = Reduce(back_terms, back_landing, share, depth, pieces, back_send, back_recv)
    mlp_reduce = Reduce(mlp_terms, mlp_landing, share, depth, pieces, mlp_send, mlp_recv)

    def pick_rows(turn, carry):
        image = image_at(turn)
        fetch(image).wait()
        rows = pl.ds(pl.multiple_of(image * kept, kept), kept)
        positions = lax.broadcasted_iota(jnp.int32, (patches.shape[1], kept), 0)
        slots = lax.broadcasted_iota(jnp.int32, (patches.shape[1], kept), 1)
        listed = index[pl.ds(first + image, 1), :]
        pick = jnp.where((positions == listed) & (slots < count[first + image]), 1.0, 0.0)
        tokens[rows, :] = dot_tn(pick.astype(LOW), patch_rows[image]).astype(LOW)
        return carry

    lax.fori_loop(0, images, pick_rows, 0)
    for step in range(1, devices):
        source = (me + devices - step) % devices
        remote(
            mod_mine, mod_gathered.at[source], mod_send.at[step], mod_recv.at[step], me
        ).wait_recv()
    mod[...] = jnp.concatenate(
        [mod_gathered[device].astype(F32) for device in range(devices)], axis=-1
    )

    def block(image, member):
        return mod[pl.ds(first + image, 1), member * width : (member + 1) * width]

    def one(turn, carry):
        image = image_at(turn)
        rows = pl.ds(pl.multiple_of(image * kept, kept), kept)

        @pl.when(turn == images - 1)
        def _():
            shares[0].pass_on()
            shares[1].pass_on()

        norm, _ = norm_parts(tokens[rows, :].astype(F32))
        normed = (norm * (1.0 + block(image, 1)) + block(image, 0)).astype(LOW)
        normed_out[rows, :] = normed
        key_live = lax.broadcasted_iota(jnp.int32, (1, kept), 1) < count[first + image]
        attended_out[0, rows, :] = attend_shard(
            normed, heads_own, row_own, spots, proj_out, 0, rows, key_live, scale
        )
        return carry

    def two(turn, carry):
        image = image_at(turn)
        rows = pl.ds(pl.multiple_of(image * kept, kept), kept)
        key_live = lax.broadcasted_iota(jnp.int32, (1, kept), 1) < count[first + image]
        attended = attend_shard(
            normed_out[rows, :], heads_other, row_other, spots, proj_out, 1, rows, key_live, scale
        )
        attended_out[1, rows, :] = attended
        branch = dot(attended_out[0, rows, :], heads_own[3 * local :, :]) + dot(
            attended, heads_other[3 * local :, :]
        )
        terms[rows, :] = branch.astype(LOW)
        for part in range(fold):
            reduce.ready_share(image * fold + part)
        return carry

    lax.fori_loop(0, images, one, 0)
    shares[1].relay()
    shares[1].wait()
    lax.fori_loop(0, images, two, 0)

    @pl.when(outer)
    def _():
        shares[2].start()
        shares[3].start()

    reduce.relay()
    shares[2].pass_on()
    reduce.finish(total)
    image = (up * share) // kept
    own_rows = pl.ds(pl.multiple_of(up * share, share), share)
    own = tokens[own_rows, :]
    tokens_own[...] = own
    branch = total[...] + row_own[:, spots["out"] : spots["out"] + width]
    branch_out[...] = branch
    mid = own.astype(F32) + block(image, 2) * branch
    mid_out[...] = mid
    norm, _ = norm_parts(mid)
    normed_two[own_rows, :] = (norm * (1.0 + block(image, 4)) + block(image, 3)).astype(LOW)
    shares[2].relay()
    gather.open()

    def half_pass(rows, shard, weight_up, row, weight_down):
        source = normed_two[rows, :]
        grad = grad_mlp[rows, :]
        bias = row[:, spots["up"] : spots["up"] + units]
        pre = dot_nt(source, weight_up[...]) + bias
        square = pre * pre
        bent = jnp.tanh(GELU_ROOT * pre * (1.0 + GELU_CUBE * square))
        half = 0.5 * (1.0 + bent)
        low_hidden = (pre * half).astype(LOW)
        hidden[shard, rows, :] = low_hidden
        slope = half + 0.5 * pre * (1.0 - bent * bent) * (
            GELU_ROOT * (1.0 + 3.0 * GELU_CUBE * square)
        )
        low_grad = (slope * dot_nt(grad, weight_down[...])).astype(LOW)
        grad_pre[shard, rows, :] = low_grad
        sums = jnp.sum(low_grad.astype(F32), axis=0, keepdims=True)
        return dot(low_hidden, weight_down[...]), dot(low_grad, weight_up[...]), sums

    def own_pass(image):
        fetch_cotangent(image).wait()
        rows = pl.ds(pl.multiple_of(image * kept, kept), kept)
        live = lax.broadcasted_iota(jnp.int32, (kept, 1), 0) < count[first + image]
        grad = jnp.where(live, cot[rows, :].astype(F32), 0.0)
        grad = (block(image, 5) * grad).astype(LOW)
        grad_mlp[rows, :] = grad
        down_sums[image] = jnp.sum(grad.astype(F32), axis=0, keepdims=True)
        mlp, back, sums = half_pass(rows, 0, up_own, row_own, down_own)
        up_sums[0, image] = sums
        mlp_part[rows, :] = mlp
        back_part[rows, :] = back

    def other_pass(image):
        rows = pl.ds(pl.multiple_of(image * kept, kept), kept)
        mlp, back, sums = half_pass(rows, 1, up_other, row_other, down_other)
        up_sums[1, image] = sums
        back_terms[rows, :] = (back_part[rows, :] + back).astype(LOW)
        mlp_terms[rows, :] = (mlp_part[rows, :] + mlp).astype(LOW)
        for part in range(fold):
            back_reduce.ready_share(image * fold + part)
            mlp_reduce.ready_share(image * fold + part)

    if fold == 1:

        def own_turn(turn, carry):
            @pl.when(turn == 1)
            def _():
                gather.relay()

            offset = turn + (turn // 2) * (1 - 2 * (turn % 2))
            gather.take(offset)
            own_pass(across(up, offset, depth))

            @pl.when(turn == 1)
            def _():
                shares[3].pass_on()

            return carry

        lax.fori_loop(0, depth, own_turn, 0)
    else:

        def own_image(image, carry):
            own_pass(image)
            return carry

        gather.relay()
        for offset in range(1, depth):
            gather.take(offset)
        shares[3].pass_on()
        lax.fori_loop(0, images, own_image, 0)
    shares[3].relay()
    for member in shares[2:]:
        member.wait()

    def other_turn(turn, carry):
        other_pass(image_at(turn))
        return carry

    lax.fori_loop(0, images, other_turn, 0)
    back_reduce.relay()
    mlp_reduce.relay()
    wide = tile_of(width)
    for shard in range(PAIR):

        def tile(step, carry):
            columns = pl.ds(pl.multiple_of(step * wide, 128), wide)
            up_grad[shard, 0:units, columns] = dot_tn(
                grad_pre[shard], normed_two[:, columns]
            ).astype(LOW)
            down_grad[shard, 0:units, columns] = dot_tn(
                hidden[shard], grad_mlp[:, columns]
            ).astype(LOW)
            return carry

        lax.fori_loop(0, width // wide, tile, 0)
        if units < up_grad.shape[1]:
            rest_rows = jnp.zeros((up_grad.shape[1] - units, width), LOW)
            up_grad[shard, units:, :] = rest_rows
            down_grad[shard, units:, :] = rest_rows
    back_reduce.finish(back_total)
    for shard in range(PAIR):
        up_bias_grad[shard : shard + 1, :] = sum(up_sums[shard, member] for member in range(images))
    down_bias_grad[...] = sum(down_sums[member] for member in range(images))
    live = (
        lax.broadcasted_iota(jnp.int32, (share, 1), 0) + (up * share) % kept
        < count[first + image]
    )
    grad_out = jnp.where(live, cot[own_rows, :].astype(F32), 0.0)
    norm, spread = norm_parts(mid_out[...])
    back = back_total[...]
    grad_mid = grad_out + norm_back(norm, spread, back * (1.0 + block(image, 4)))
    grad_mid_out[...] = grad_mid
    grad_branch_out[...] = (block(image, 2) * grad_mid).astype(LOW)
    sums_out[0:1, :] = jnp.sum(grad_mid * branch_out[...], axis=0, keepdims=True)
    sums_out[1:2, :] = jnp.sum(back, axis=0, keepdims=True)
    sums_out[2:3, :] = jnp.sum(back * norm, axis=0, keepdims=True)
    mlp_reduce.finish(mlp_total)
    mlp = mlp_total[...] + row_own[:, spots["down"] : spots["down"] + width]
    sums_out[3:4, :] = jnp.sum(grad_out * mlp, axis=0, keepdims=True)
    block_own[...] = jnp.where(live, mid_out[...] + block(image, 5) * mlp, 0.0).astype(LOW)
    for step in range(1, groups):
        source = (group + groups - step) % groups
        view = silu_all.at[source]
        remote(
            view, view, silu_send.at[step], silu_recv.at[step], me, group
        ).wait_recv()
    for member in shares:
        member.close()
    for copy in mod_copies + silu_copies:
        copy.wait_send()
    reduce.close()
    gather.close()
    back_reduce.close()
    mlp_reduce.close()


def ahead(sizes, groups, args):
    depth, images, kept, share, pieces = sizes
    count, index, patches, cotangent, cond, mod_weight, heads, up, down, row = args
    spots, width = patches.shape[1:]
    local = heads.shape[0] // 4
    mods = mod_weight.shape[0]
    units = up.shape[0]
    rows = images * kept
    shape = jax.ShapeDtypeStruct
    devices = depth * PAIR
    return pl.pallas_call(
        functools.partial(ahead_kernel, sizes, groups),
        out_shape=(
            shape((rows, width), LOW),
            shape((PAIR, 3, rows, local), LOW),
            shape((PAIR, rows, local), LOW),
            shape((share, width), LOW),
            shape((cond.shape[0], devices * mods), F32),
            shape((groups,) + cond.shape, LOW),
            shape(heads.shape, LOW),
            shape((PAIR, padded(units, groups), width), LOW),
            shape((PAIR, padded(units, groups), width), LOW),
            shape((PAIR, units), F32),
            shape((1, width), F32),
            shape((share, width), LOW),
            shape((share, width), F32),
            shape((share, width), LOW),
            shape((4, width), F32),
        ),
        in_specs=[SM, VM, HB, HB] + [VM] * 6,
        out_specs=(VM,) * 15,
        scratch_shapes=[
            pltpu.VMEM(up.shape, LOW),
            pltpu.VMEM(down.shape, LOW),
            pltpu.VMEM(row.shape, F32),
            pltpu.VMEM((share, width), F32),
            pltpu.VMEM((share, width), F32),
            pltpu.VMEM((images, spots, width), LOW),
            pltpu.VMEM((rows, width), LOW),
            pltpu.VMEM((rows, width), LOW),
            pltpu.VMEM((rows - share, width), LOW),
            pltpu.VMEM((share, width), F32),
            pltpu.VMEM((cond.shape[0], mods), LOW),
            pltpu.VMEM((devices, cond.shape[0], mods), LOW),
            DMA((images,)),
        ]
        + Reduce.scratch(depth, pieces)
        + [
            DMA((devices,)),
            DMA((devices,)),
            DMA((groups,)),
            DMA((groups,)),
        ]
        + Share.scratch(4, groups)
        + [
            pltpu.VMEM((rows, width), LOW),
            pltpu.VMEM((rows, width), LOW),
            pltpu.VMEM((PAIR, rows, units), LOW),
            pltpu.VMEM((PAIR, rows, units), LOW),
            pltpu.VMEM((rows, width), LOW),
            pltpu.VMEM((rows, width), LOW),
            pltpu.VMEM((rows - share, width), LOW),
            pltpu.VMEM((rows, width), LOW),
            pltpu.VMEM((rows - share, width), LOW),
            pltpu.VMEM((rows, width), F32),
            pltpu.VMEM((rows, width), F32),
            pltpu.VMEM((share, width), F32),
            pltpu.VMEM((share, width), F32),
            pltpu.VMEM((PAIR, images, 1, units), F32),
            pltpu.VMEM((images, 1, width), F32),
            DMA((images,)),
        ]
        + Gather.scratch(depth, pieces)
        + Reduce.scratch(depth, pieces)
        + Reduce.scratch(depth, pieces),
        compiler_params=pltpu.CompilerParams(
            collective_id=1, has_side_effects=True, vmem_limit_bytes=62 << 20
        ),
        name="ahead",
    )(*args)


def attend_back_kernel(
    sizes,
    groups,
    count,
    grad_own,
    normed,
    proj,
    attended,
    heads_own,
    heads_other,
    mod,
    tokens_own,
    grad_mid,
    block_own,
    up_grad,
    down_grad,
    heads_grad,
    qv_grad,
    out_bias_grad,
    grad_tokens,
    sums_out,
    block_out,
    up_total,
    down_total,
    grads,
    grad_proj,
    terms,
    landing,
    total,
    qv_sums,
    out_sums,
    own_sem,
    gather_send,
    gather_recv,
    send,
    recv,
    *rest,
):
    depth, images, kept, share, pieces = sizes
    me, up, side = place(depth)
    width = grad_own.shape[1]
    local = heads_own.shape[0] // 4
    scale = HD ** (-0.5)
    fold = depth // images
    first = side * images
    up_fold = Fold(up_grad, rest[:7], up_total, depth, groups)
    down_fold = Fold(down_grad, rest[7:14], down_total, depth, groups)
    spread = Spread(block_out, share, depth, pieces, rest[14:18])
    own_rows = pl.ds(pl.multiple_of(up * share, share), share)
    own_copy = pltpu.make_async_copy(grad_own, grads.at[own_rows, :], own_sem.at[0])
    own_copy.start()
    block_copy = pltpu.make_async_copy(block_own, spread.own(), own_sem.at[1])
    block_copy.start()
    meet(column_peers(depth) + cube_peers(depth, groups) + spread.peers_beyond(depth))
    own_copy.wait()
    gather = Gather(grads, share, depth, pieces, gather_send, gather_recv)
    reduce = Reduce(terms, landing, share, depth, pieces, send, recv)
    gather.open()
    up_fold.one()
    down_fold.one()
    block_copy.wait()

    def one(image):
        rows = pl.ds(pl.multiple_of(image * kept, kept), kept)
        key_live = lax.broadcasted_iota(jnp.int32, (1, kept), 1) < count[first + image]
        grad = grads[rows, :]
        out_sums[image] = jnp.sum(grad.astype(F32), axis=0, keepdims=True)
        back = None
        for shard, heads in enumerate((heads_own, heads_other)):
            grad_att = dot_nt(grad, heads[3 * local :, :]).astype(LOW)
            queries = proj[shard, 0, rows, :]
            keys = proj[shard, 1, rows, :]
            values = proj[shard, 2, rows, :]
            grad_q = jnp.zeros((kept, local), F32)
            grad_k = jnp.zeros((kept, local), F32)
            grad_v = jnp.zeros((kept, local), F32)
            for head in range(local // HD):
                mask = head_mask(head, local)
                head_q = jnp.where(mask, queries, 0.0).astype(LOW)
                head_grad = jnp.where(mask, grad_att, 0.0).astype(LOW)
                weights = softmax_rows(head_q, keys, key_live, scale)
                grad_weights = dot_nt(head_grad, values)
                inner = jnp.sum(weights * grad_weights, axis=-1, keepdims=True)
                grad_scores = (weights * (grad_weights - inner)).astype(LOW)
                grad_v = grad_v + dot_tn(weights.astype(LOW), head_grad)
                grad_q = grad_q + dot(grad_scores, jnp.where(mask, keys, 0.0).astype(LOW))
                grad_k = grad_k + dot_tn(grad_scores, head_q)
            for member, value in enumerate((grad_q * scale, grad_k * scale, grad_v)):
                low = value.astype(LOW)
                grad_proj[shard, member, rows, :] = low
                part = dot(low, heads[member * local : (member + 1) * local, :])
                back = part if back is None else back + part
                if member != 1:
                    row = 2 * shard + member // 2
                    qv_sums[row, image] = jnp.sum(low.astype(F32), axis=0, keepdims=True)
        terms[rows, :] = back.astype(LOW)
        for part in range(fold):
            reduce.ready_share(image * fold + part)

    if fold == 1:

        def turn_of(turn, carry):
            @pl.when(turn == 1)
            def _():
                gather.relay()

            offset = turn + (turn // 2) * (1 - 2 * (turn % 2))
            gather.take(offset)
            one(across(up, offset, depth))

            @pl.when(turn == 0)
            def _():
                up_fold.two()
                down_fold.two()

            @pl.when(turn == 1)
            def _():
                spread.open()

            @pl.when(turn == 2)
            def _():
                up_fold.three()

            @pl.when(turn == 3)
            def _():
                down_fold.three()

            return carry

        lax.fori_loop(0, depth, turn_of, 0)
    else:

        def image_of(image, carry):
            one(image)
            return carry

        gather.relay()
        for offset in range(1, depth):
            gather.take(offset)
        up_fold.two()
        down_fold.two()
        spread.open()
        lax.fori_loop(0, images, image_of, 0)
        up_fold.three()
        down_fold.three()

    def spread_of(turn, carry):
        spread.take(turn)
        return carry

    reduce.relay()
    lax.fori_loop(1, depth - 1, spread_of, 0)
    up_fold.four()
    down_fold.four()
    wide = tile_of(width)
    for shard in range(PAIR):

        def tile(step, carry):
            columns = pl.ds(pl.multiple_of(step * wide, 128), wide)
            source = normed[:, columns]
            for member in range(3):
                heads_grad[shard, member * local : (member + 1) * local, columns] = dot_tn(
                    grad_proj[shard, member], source
                ).astype(LOW)
            heads_grad[shard, 3 * local : 4 * local, columns] = dot_tn(
                attended[shard], grads[:, columns]
            ).astype(LOW)
            return carry

        lax.fori_loop(0, width // wide, tile, 0)
        if 4 * local < heads_grad.shape[1]:
            heads_grad[shard, 4 * local :, :] = jnp.zeros(
                (heads_grad.shape[1] - 4 * local, width), LOW
            )
    up_fold.five()
    spread.take(depth - 1)
    down_fold.five()
    reduce.finish(total)
    for row in range(2 * PAIR):
        qv_grad[row : row + 1, :] = sum(qv_sums[row, image] for image in range(images))
    out_bias_grad[...] = sum(out_sums[image] for image in range(images))
    image = first + (up * share) // kept
    live = (
        lax.broadcasted_iota(jnp.int32, (share, 1), 0) + (up * share) % kept < count[image]
    )
    norm, spread_rows = norm_parts(tokens_own[...].astype(F32))
    back = total[...]
    scale_one = mod[pl.ds(image, 1), width : 2 * width]
    grad = grad_mid[...] + norm_back(norm, spread_rows, back * (1.0 + scale_one))
    grad_tokens[...] = jnp.where(live, grad, 0.0).astype(LOW)
    sums_out[0:1, :] = jnp.sum(back, axis=0, keepdims=True)
    sums_out[1:2, :] = jnp.sum(back * norm, axis=0, keepdims=True)
    up_fold.six()
    down_fold.six()
    for index in range(depth):
        spread.crossed(index)
    spread.close()
    gather.close()
    reduce.close()


def attend_back(sizes, groups, args):
    depth, images, kept, share, pieces = sizes
    width = args[1].shape[1]
    local = args[5].shape[0] // 4
    up_grad, down_grad = args[-2:]
    rows = images * kept
    shape = jax.ShapeDtypeStruct
    return pl.pallas_call(
        functools.partial(attend_back_kernel, sizes, groups),
        out_shape=(
            shape((PAIR, padded(4 * local, groups), width), LOW),
            shape((2 * PAIR, local), F32),
            shape((1, width), F32),
            shape((share, width), LOW),
            shape((2, width), F32),
            shape((PAIR * rows, width), LOW),
            shape(up_grad.shape[1:], LOW),
            shape(down_grad.shape[1:], LOW),
        ),
        in_specs=[SM] + [VM] * 12,
        out_specs=(VM,) * 8,
        scratch_shapes=[
            pltpu.VMEM((rows, width), LOW),
            pltpu.VMEM((PAIR, 3, rows, local), LOW),
            pltpu.VMEM((rows, width), LOW),
            pltpu.VMEM((rows - share, width), LOW),
            pltpu.VMEM((share, width), F32),
            pltpu.VMEM((2 * PAIR, images, 1, local), F32),
            pltpu.VMEM((images, 1, width), F32),
            DMA((2,)),
        ]
        + Gather.scratch(depth, pieces)
        + Reduce.scratch(depth, pieces)
        + Fold.scratch(up_grad.shape, groups)
        + Fold.scratch(down_grad.shape, groups)
        + Spread.scratch(depth, pieces),
        compiler_params=pltpu.CompilerParams(
            collective_id=3, has_side_effects=True, vmem_limit_bytes=62 << 20
        ),
        name="attend_back",
    )(*args)


def split_low(value):
    high = value.astype(LOW)
    rest = value - high.astype(F32)
    low = rest.astype(LOW)
    return high, low, (rest - low.astype(F32)).astype(LOW)


def close_kernel(
    sizes,
    groups,
    grad_tokens,
    sums_one,
    sums_two,
    up_bias_grad,
    qv_grad,
    down_bias_grad,
    out_bias_grad,
    heads_grad,
    silu_all,
    mod_weight,
    cond,
    whole,
    heads_total,
    bias_total,
    grads_out,
    silu_out,
    mod_bias_grad,
    grad_cond,
    biases,
    sum_row,
    sum_land,
    bias_land,
    cond_land,
    own_sem,
    sum_send,
    sum_recv,
    bias_send,
    bias_recv,
    cond_send,
    cond_recv,
    *rest,
):
    depth, images, kept, share, pieces = sizes
    devices = depth * PAIR
    everyone = devices * groups
    me, _, side = place(depth)
    group = lax.axis_index("dp")
    flat = group * devices + me
    width = grad_tokens.shape[1]
    columns = mod_weight.shape[0]
    span = sum_land.shape[2]
    spread = Spread(whole, share, depth, pieces, rest[:4])
    fold = Fold(heads_grad, rest[4:11], heads_total, depth, groups)
    own_copy = pltpu.make_async_copy(grad_tokens, spread.own(), own_sem)
    own_copy.start()
    barrier = pltpu.get_barrier_semaphore()

    def greet(step, carry):
        there = (flat + step) % everyone
        pl.semaphore_signal(
            barrier,
            inc=1,
            device_id={"dp": there // devices, "tensor": there % devices},
            device_id_type=MESH,
        )
        return carry

    lax.fori_loop(1, everyone, greet, 0)
    pl.semaphore_wait(barrier, everyone - 1)
    own_copy.wait()
    fold.one()
    spread.open()

    def aligned(device):
        return pl.multiple_of((device * columns) // 128 * 128, 128)

    for member in range(6):
        part = sums_one[member : member + 1, :] if member < 2 else sums_two[member - 2 : member - 1, :]
        sum_row[:, member * width : (member + 1) * width] = part
    sum_row[:, 6 * width :] = jnp.zeros((1, sum_row.shape[1] - 6 * width), F32)

    def sum_copy(step):
        there = (flat + step) % everyone
        device = there % devices
        return remote(
            sum_row.at[:, pl.ds(aligned(device), span)],
            sum_land.at[flat],
            sum_send.at[step],
            sum_recv.at[step],
            device,
            there // devices,
        )

    def send_sum(step, carry):
        sum_copy(step).start()
        return carry

    lax.fori_loop(1, everyone, send_sum, 0)
    sum_land[flat] = sum_row[:, pl.ds(aligned(me), span)]
    units, local = up_bias_grad.shape[1], qv_grad.shape[1]
    biases[...] = jnp.zeros(biases.shape, F32)
    for shard in range(PAIR):
        biases[3 * shard : 3 * shard + 1, 0:units] = up_bias_grad[shard : shard + 1, :]
        biases[3 * shard + 1 : 3 * shard + 3, 0:local] = qv_grad[2 * shard : 2 * shard + 2, :]
    biases[6:7, :] = down_bias_grad[...]
    biases[7:8, :] = out_bias_grad[...]
    slot = side * groups + group
    bias_land[slot] = biases[...]
    partner = me + depth * (1 - 2 * side)

    def bias_copy(step):
        crossed = step // groups
        there = (group + step) % groups
        device = jnp.where(crossed == 1, partner, me)
        return remote(
            biases, bias_land.at[slot], bias_send.at[step], bias_recv.at[step], device, there
        )

    for step in range(1, PAIR * groups):
        bias_copy(step).start()
    fold.two()

    def wait_sum(step, carry):
        source = (flat + everyone - step) % everyone
        view = sum_land.at[source]
        remote(view, view, sum_send.at[step], sum_recv.at[step], me).wait_recv()
        return carry

    lax.fori_loop(1, everyone, wait_sum, 0)
    offset = (me * columns) % 128
    grads = jnp.concatenate([sum_land[device] for device in range(everyone)], axis=0)
    grads = pltpu.roll(grads, lax.rem(span - offset, span), 1)[:, :columns]
    mod_bias_grad[...] = jnp.sum(grads, axis=0, keepdims=True)
    total_images = images * PAIR

    def image_of(device):
        return device * share // kept

    source = lax.broadcasted_iota(jnp.int32, (everyone, groups * total_images), 0)
    target = lax.broadcasted_iota(jnp.int32, (everyone, groups * total_images), 1)
    row_image = source // devices * total_images + image_of(source % devices)
    chosen = jnp.where(row_image == target, 1.0, 0.0).astype(LOW)
    silu_out[...] = dot(
        chosen,
        jnp.concatenate([silu_all[member].astype(F32) for member in range(groups)], axis=0).astype(
            LOW
        ),
    ).astype(LOW)
    parts = split_low(grads)
    spread.take(1)
    fold.three()
    grads_out[...] = grads.T
    source = lax.broadcasted_iota(jnp.int32, (total_images, everyone), 1)
    target = lax.broadcasted_iota(jnp.int32, (total_images, everyone), 0)
    chosen = jnp.where(
        (source // devices == group) & (image_of(source % devices) == target), 1.0, 0.0
    ).astype(LOW)
    mine = dot(chosen, parts[0]) + dot(chosen, parts[1]) + dot(chosen, parts[2])
    parts = split_low(mine)
    term = (
        dot(parts[0], mod_weight[...])
        + dot(parts[1], mod_weight[...])
        + dot(parts[2], mod_weight[...])
    )
    cond_land[me] = term

    def cond_copy(step):
        return remote(
            cond_land.at[me],
            cond_land.at[me],
            cond_send.at[step],
            cond_recv.at[step],
            (me + step) % devices,
        )

    for step in range(1, devices):
        cond_copy(step).start()
    for turn in range(2, depth - 1):
        spread.take(turn)
    fold.four()
    for step in range(1, PAIR * groups):
        crossed = step // groups
        source_group = (group + groups - step % groups) % groups
        source_side = jnp.where(crossed == 1, 1 - side, side)
        view = bias_land.at[source_side * groups + source_group]
        remote(view, view, bias_send.at[step], bias_recv.at[step], me).wait_recv()
    rows = biases.shape[0]
    result = jnp.zeros((rows, width), F32)
    for member in range(PAIR * groups):
        value = bias_land[member]
        turned = jnp.concatenate([value[3:6, :], value[0:3, :], value[6:, :]], axis=0)
        same = side == member // groups
        result = result + jnp.where(same, value, turned)
    bias_total[...] = result
    for step in range(1, devices):
        source = (me + devices - step) % devices
        view = cond_land.at[source]
        remote(view, view, cond_send.at[step], cond_recv.at[step], me).wait_recv()
    back = cond_land[0]
    for device in range(1, devices):
        back = back + cond_land[device]
    value = cond[...].astype(F32)
    gate = 1.0 / (1.0 + jnp.exp(-value))
    grad_cond[...] = (back * (gate + value * gate * (1.0 - gate))).astype(LOW)
    spread.take(depth - 1)
    fold.five()
    for where in range(depth):
        spread.crossed(where)
    fold.six()
    spread.close()

    def done_sum(step, carry):
        sum_copy(step).wait_send()
        return carry

    lax.fori_loop(1, everyone, done_sum, 0)
    for step in range(1, PAIR * groups):
        bias_copy(step).wait_send()
    for step in range(1, devices):
        cond_copy(step).wait_send()


def close(sizes, groups, args):
    depth, images, kept, share, pieces = sizes
    grad_tokens = args[0]
    heads_grad, silu_all, mod_weight, cond = args[-4:]
    devices = depth * PAIR
    width = grad_tokens.shape[1]
    columns = mod_weight.shape[0]
    biases = (8, width)
    span = max(-(-((device * columns) % 128 + columns) // 128) * 128 for device in range(devices))
    long = max((device * columns) // 128 * 128 + span for device in range(devices))
    long = max(long, 6 * width + 128)
    shape = jax.ShapeDtypeStruct
    rows = PAIR * images * kept
    everyone = devices * groups
    return pl.pallas_call(
        functools.partial(close_kernel, sizes, groups),
        out_shape=(
            shape((rows, width), LOW),
            shape(heads_grad.shape[1:], LOW),
            shape(biases, F32),
            shape((columns, everyone), F32),
            shape((everyone, width), LOW),
            shape((1, columns), F32),
            shape(cond.shape, LOW),
        ),
        in_specs=[VM] * 11,
        out_specs=(VM,) * 7,
        scratch_shapes=[
            pltpu.VMEM(biases, F32),
            pltpu.VMEM((1, long), F32),
            pltpu.VMEM((everyone, 1, span), F32),
            pltpu.VMEM((PAIR * groups,) + biases, F32),
            pltpu.VMEM((devices,) + cond.shape, F32),
            DMA,
            DMA((everyone,)),
            DMA((everyone,)),
            DMA((PAIR * groups,)),
            DMA((PAIR * groups,)),
            DMA((devices,)),
            DMA((devices,)),
        ]
        + Spread.scratch(depth, pieces)
        + Fold.scratch(heads_grad.shape, groups),
        compiler_params=pltpu.CompilerParams(
            collective_id=4, has_side_effects=True, vmem_limit_bytes=62 << 20
        ),
        name="close",
    )(*args)


def settle_kernel(
    index,
    whole,
    block,
    up_low,
    down_low,
    heads_low,
    mod_grads,
    silu_rows,
    biases,
    mod_bias,
    cond,
    block_out,
    grad_patches,
    grad_cond,
    mod_rows_grad,
    mod_bias_grad,
    qkv_grad,
    qv_grad,
    out_grad,
    out_bias_grad,
    up_grad,
    up_bias_grad,
    down_grad,
    down_bias_grad,
):
    members, kept, _ = block_out.shape
    step = pl.program_id(0)
    local, units = out_grad.shape[0], up_bias_grad.shape[1]
    for member in range(members):
        rows = slice(member * kept, (member + 1) * kept)
        block_out[member] = block[rows, :]
        positions = lax.broadcasted_iota(jnp.int32, (grad_patches.shape[1], kept), 0)
        listed = index[pl.ds(step * members + member, 1), :]
        pick = jnp.where(positions == listed, 1.0, 0.0).astype(LOW)
        grad_patches[member] = dot(pick, whole[rows, :]).astype(LOW)
    parts = split_low(mod_grads[...])
    silu = silu_rows[...]
    mod_rows_grad[...] = dot(parts[0], silu) + dot(parts[1], silu) + dot(parts[2], silu)
    up_grad[...] = up_low[...].astype(F32)
    down_grad[...] = down_low[...].astype(F32)

    @pl.when(step == 0)
    def _():
        for member in range(3):
            qkv_grad[member] = heads_low[member * local : (member + 1) * local, :].astype(F32)
        out_grad[...] = heads_low[3 * local : 4 * local, :].astype(F32)
        grad_cond[...] = cond[...]
        mod_bias_grad[...] = mod_bias[...]
        qv_grad[...] = biases[1:3, 0:local]
        up_bias_grad[...] = biases[0:1, 0:units]
        down_bias_grad[...] = biases[6:7, :]
        out_bias_grad[...] = biases[7:8, :]


def settle(local, units, spots, args):
    index, whole, block, up_low, down_low, heads_low, mod_grads, silu_rows, biases, mod_bias, cond = args
    images, kept = index.shape
    width = whole.shape[1]
    mods = mod_bias.shape[1]
    steps = 4 if units % 64 == 0 and mods % 32 == 0 else 2
    members = images // steps
    shape = jax.ShapeDtypeStruct

    def full(array):
        return pl.BlockSpec(array.shape, lambda step: (0,) * len(array.shape))

    def part(array, rows):
        rest = array.shape[1:]
        return pl.BlockSpec((rows,) + rest, lambda step: (step,) + (0,) * len(rest))

    outs = (
        shape((images, kept, width), LOW),
        shape((images, spots, width), LOW),
        shape(cond.shape, LOW),
        shape((mods, width), F32),
        shape((1, mods), F32),
        shape((3, local, width), F32),
        shape((2, local), F32),
        shape((local, width), F32),
        shape((1, width), F32),
        shape((units, width), F32),
        shape((1, units), F32),
        shape((units, width), F32),
        shape((1, width), F32),
    )
    return pl.pallas_call(
        settle_kernel,
        grid=(steps,),
        out_shape=outs,
        in_specs=[
            full(index),
            part(whole, members * kept),
            part(block, members * kept),
            part(up_low, units // steps),
            part(down_low, units // steps),
            full(heads_low),
            part(mod_grads, mods // steps),
            full(silu_rows),
            full(biases),
            full(mod_bias),
            full(cond),
        ],
        out_specs=(
            part(outs[0], members),
            part(outs[1], members),
            full(outs[2]),
            part(outs[3], mods // steps),
            full(outs[4]),
            full(outs[5]),
            full(outs[6]),
            full(outs[7]),
            full(outs[8]),
            part(outs[9], units // steps),
            full(outs[10]),
            part(outs[11], units // steps),
            full(outs[12]),
        ),
        compiler_params=pltpu.CompilerParams(vmem_limit_bytes=60 << 20),
        name="settle",
    )(*args)


def on_device(
    patches,
    conditioning,
    keep_count,
    keep_index,
    mod_weight,
    mod_bias,
    qkv_weight,
    qv_bias,
    out_weight,
    out_bias,
    up_weight,
    up_bias,
    down_weight,
    down_bias,
    out_cotangent,
):
    devices = lax.axis_size("tensor")
    depth = devices // PAIR
    all_images, kept = keep_index.shape
    width = patches.shape[2]
    images = all_images // PAIR
    share = images * kept // depth
    pieces = 4 if share % 64 == 0 else 2
    sizes = (depth, images, kept, share, pieces)
    groups = lax.axis_size("dp")
    local, units, mods = qkv_weight.shape[2], up_weight.shape[1], mod_weight.shape[1]
    up = up_weight.T
    mod_rows = mod_weight.T
    heads = jnp.concatenate(
        [jnp.swapaxes(qkv_weight, 1, 2).reshape(3 * local, width), out_weight], axis=0
    )

    def spaced(value):
        return jnp.pad(value.astype(F32), (0, lanes(value.shape[0]) - value.shape[0]))

    row = jnp.concatenate(
        [
            spaced(value)
            for value in (out_bias, down_bias, up_bias, qv_bias[0], qv_bias[1], mod_bias)
        ]
    )[None, :]
    (
        normed_one,
        proj,
        attended,
        tokens_own,
        mod,
        silu_all,
        heads_other,
        up_grad,
        down_grad,
        up_bias_grad,
        down_bias_grad,
        block_own,
        grad_mid,
        grad_branch,
        sums_two,
    ) = ahead(
        sizes,
        groups,
        (
            keep_count,
            keep_index,
            patches,
            out_cotangent,
            conditioning,
            mod_rows,
            heads,
            up,
            down_weight,
            row,
        ),
    )
    (
        heads_grad,
        qv_grad,
        out_bias_grad,
        grad_tokens,
        sums_one,
        block_out,
        up_total,
        down_total,
    ) = attend_back(
        sizes,
        groups,
        (
            keep_count,
            grad_branch,
            normed_one,
            proj,
            attended,
            heads,
            heads_other,
            mod,
            tokens_own,
            grad_mid,
            block_own,
            up_grad,
            down_grad,
        ),
    )
    (
        grad_whole,
        heads_total,
        bias_total,
        mod_grads,
        silu_rows,
        mod_bias_total,
        cond_total,
    ) = close(
        sizes,
        groups,
        (
            grad_tokens,
            sums_one,
            sums_two,
            up_bias_grad,
            qv_grad,
            down_bias_grad,
            out_bias_grad,
            heads_grad,
            silu_all,
            mod_rows,
            conditioning,
        ),
    )
    (
        block_out,
        grad_patches,
        grad_conditioning,
        mod_rows_grad,
        mod_bias_grad,
        qkv_grad,
        qv_bias_grad,
        out_weight_grad,
        out_bias_grad,
        up_rows_grad,
        up_bias_grad,
        down_weight_grad,
        down_bias_grad,
    ) = settle(
        local,
        units,
        patches.shape[1],
        (
            keep_index,
            grad_whole,
            block_out,
            up_total,
            down_total,
            heads_total,
            mod_grads,
            silu_rows,
            bias_total,
            mod_bias_total,
            cond_total,
        ),
    )
    return (
        block_out,
        grad_patches,
        grad_conditioning,
        mod_rows_grad.T,
        mod_bias_grad[0],
        jnp.swapaxes(qkv_grad, 1, 2),
        qv_bias_grad,
        out_weight_grad,
        out_bias_grad[0],
        up_rows_grad.T,
        up_bias_grad[0],
        down_weight_grad,
        down_bias_grad[0],
    )


def solution(mesh):
    placed = (
        P("dp", None, None),
        P("dp", None),
        P("dp"),
        P("dp", None),
        P(None, "tensor"),
        P("tensor"),
        P(None, None, "tensor"),
        P(None, "tensor"),
        P("tensor", None),
        P(),
        P(None, "tensor"),
        P("tensor"),
        P("tensor", None),
        P(),
        P("dp", None, None),
    )
    return jax.shard_map(
        on_device,
        mesh=mesh,
        in_specs=placed,
        out_specs=(
            P("dp", None, None),
            P("dp", None, None),
            P("dp", None),
            P(None, "tensor"),
            P("tensor"),
            P(None, None, "tensor"),
            P(None, "tensor"),
            P("tensor", None),
            P(),
            P(None, "tensor"),
            P("tensor"),
            P("tensor", None),
            P(),
        ),
        check_vma=False,
    )
```

```python
import functools

import jax
import jax.numpy as jnp
from jax import lax
from jax.experimental import pallas as pl
from jax.experimental.pallas import tpu as pltpu
from jax.sharding import PartitionSpec as P

HD = 72
MESH = pl.DeviceIdType.MESH
F32 = jnp.float32
LOW = jnp.bfloat16
DMA = pltpu.SemaphoreType.DMA
VM = pl.BlockSpec(memory_space=pltpu.VMEM)
SM = pl.BlockSpec(memory_space=pltpu.SMEM)
HB = pl.BlockSpec(memory_space=pl.ANY)
PAIR = 2
GELU_ROOT = 0.7978845608028654
GELU_CUBE = 0.044715


def remote(source, target, send_sem, recv_sem, device, group=None):
    there = {"tensor": device} if group is None else {"dp": group, "tensor": device}
    return pltpu.make_async_remote_copy(
        src_ref=source,
        dst_ref=target,
        send_sem=send_sem,
        recv_sem=recv_sem,
        device_id=there,
        device_id_type=MESH,
    )


def place(depth):
    me = lax.axis_index("tensor")
    return me, me % depth, me // depth


def bits_of(depth):
    return depth.bit_length() - 1


def toward(spot, bit):
    return (1 - 2 * ((spot // (1 << bit)) % 2)) * (1 << bit)


def across(spot, offset, depth):
    result = spot
    for bit in range(bits_of(depth)):
        result = result + ((offset // (1 << bit)) % 2) * toward(spot, bit)
    return result


def offset_between(left, right, depth):
    result = 0
    for bit in range(bits_of(depth)):
        size = 1 << bit
        result = result + ((left // size + right // size) % 2) * size
    return result


def meet(peers):
    barrier = pltpu.get_barrier_semaphore()
    for group, peer in peers:
        pl.semaphore_signal(
            barrier, inc=1, device_id={"dp": group, "tensor": peer}, device_id_type=MESH
        )
    pl.semaphore_wait(barrier, len(peers))


def column_peers(depth):
    me, spot, side = place(depth)
    group = lax.axis_index("dp")
    return [(group, me + toward(spot, bit)) for bit in range(bits_of(depth))]


def cube_peers(depth, groups):
    me, spot, side = place(depth)
    group = lax.axis_index("dp")
    other = me + depth * (1 - 2 * side)
    peers = [((group + step) % groups, me) for step in range(1, groups)]
    return peers + [((group + step) % groups, other) for step in range(groups)]


def padded(rows, groups):
    return -(-rows // (16 * groups)) * 16 * groups


def lanes(columns):
    return -(-columns // 128) * 128


def row_spots(width, units, local, mods):
    spots = {}
    start = 0
    for name, size in (
        ("out", width),
        ("down", width),
        ("up", units),
        ("query", local),
        ("value", local),
        ("mod", mods),
    ):
        spots[name] = start
        start += lanes(size)
    return spots, start


def tile_of(width):
    return 384 if width % 384 == 0 else 128


def dot(left, right):
    return jnp.dot(left, right, preferred_element_type=F32)


def dot_nt(left, right):
    return lax.dot_general(left, right, (((1,), (1,)), ((), ())), preferred_element_type=F32)


def dot_tn(left, right):
    return lax.dot_general(left, right, (((0,), (0,)), ((), ())), preferred_element_type=F32)


def norm_parts(rows):
    width = rows.shape[-1]
    centred = rows - jnp.sum(rows, axis=-1, keepdims=True) * (1.0 / width)
    spread = lax.rsqrt(jnp.sum(centred * centred, axis=-1, keepdims=True) * (1.0 / width) + 1e-06)
    return centred * spread, spread


def norm_back(norm, spread, grad):
    width = norm.shape[-1]
    mean_grad = jnp.sum(grad, axis=-1, keepdims=True) * (1.0 / width)
    mean_both = jnp.sum(grad * norm, axis=-1, keepdims=True) * (1.0 / width)
    return (grad - mean_grad - norm * mean_both) * spread


class Line:
    def __init__(self, buffer, share, depth, pieces, send, recv):
        self.buffer, self.share, self.depth, self.pieces = buffer, share, depth, pieces
        self.send, self.recv = send, recv
        self.me = lax.axis_index("tensor")
        self.up, self.side = self.me // PAIR, self.me % PAIR

    def piece(self, index, part):
        rows = self.share // self.pieces
        start = (index * PAIR + self.side) * self.share + part * rows
        return self.buffer.at[pl.ds(pl.multiple_of(start, rows), rows), :]

    def copy(self, way, step, part):
        source = self.up - (step - 1) * (1 - 2 * way)
        target = self.up + 1 - 2 * way
        view = self.piece(source, part)
        return remote(
            view,
            view,
            self.send.at[way, step, part],
            self.recv.at[way, step, part],
            target * PAIR + self.side,
        )

    def may_send(self, way, step):
        if way == 0:
            return (self.up + 1 < self.depth) & (self.up >= step - 1)
        return (self.up >= 1) & (self.up + step - 1 < self.depth)

    def open(self):
        for part in range(self.pieces):
            for way in range(2):

                @pl.when(self.may_send(way, 1))
                def _():
                    self.copy(way, 1, part).start()

    def arrival(self, turn):
        below = self.up
        above = self.depth - 1 - self.up
        both = jnp.minimum(below, above)
        mixed = turn <= 2 * both
        way = jnp.where(mixed, (turn + 1) % 2, jnp.where(below > above, 0, 1))
        step = jnp.where(mixed, (turn + 1) // 2, turn - both)
        return way, step, self.up - step * (1 - 2 * way)

    def take(self, turn, then):
        way, step, source = self.arrival(turn)
        ahead = jnp.where(way == 0, self.up + 1 < self.depth, self.up >= 1)
        for part in range(self.pieces):
            view = self.piece(source, part)
            remote(
                view, view, self.send.at[way, step, part], self.recv.at[way, step, part], self.me
            ).wait_recv()

            @pl.when(ahead)
            def _():
                self.copy(way, step + 1, part).start()

            then(source, part)

    def close(self):
        for way in range(2):
            for step in range(1, self.depth):

                @pl.when(self.may_send(way, step))
                def _():
                    for part in range(self.pieces):
                        self.copy(way, step, part).wait_send()


class Cube:
    def __init__(self, share, depth, pieces):
        self.share, self.depth, self.pieces = share, depth, pieces
        self.me, self.spot, self.side = place(depth)
        self.bits = bits_of(depth)
        self.rows = share // pieces

    def order(self, part):
        ways = list(range(self.bits))
        return ways if part % 2 else ways[::-1]

    def span(self, index, part):
        return pl.ds(pl.multiple_of(index * self.share + part * self.rows, self.rows), self.rows)

    def neighbour(self, bit):
        return self.me + toward(self.spot, bit)


class Gather(Cube):
    def __init__(self, buffer, share, depth, pieces, send, recv):
        super().__init__(share, depth, pieces)
        self.buffer, self.send, self.recv = buffer, send, recv

    def last(self, offset, part):
        order = self.order(part)
        return max(
            (stage for stage in range(self.bits) if offset >> order[stage] & 1), default=-1
        )

    def copy(self, offset, stage, part):
        bit = self.order(part)[stage]
        view = self.buffer.at[self.span(across(self.spot, offset, self.depth), part), :]
        return remote(
            view,
            view,
            self.send.at[offset, stage, part],
            self.recv.at[offset ^ (1 << bit), part],
            self.neighbour(bit),
        )

    def landed(self, offset, part):
        view = self.buffer.at[self.span(across(self.spot, offset, self.depth), part), :]
        remote(
            view, view, self.send.at[0, 0, part], self.recv.at[offset, part], self.me
        ).wait_recv()

    def sends(self, offset):
        return [
            (stage, part)
            for part in range(self.pieces)
            for stage in range(self.last(offset, part) + 1, self.bits)
        ]

    def open(self):
        for stage, part in self.sends(0):
            self.copy(0, stage, part).start()

    def relay(self):
        for offset in sorted(range(1, self.depth), key=lambda value: bin(value).count("1")):
            for part in range(self.pieces):
                first = self.last(offset, part) + 1
                if first < self.bits:
                    self.landed(offset, part)
                    for stage in range(first, self.bits):
                        self.copy(offset, stage, part).start()

    def take(self, offset):
        for member in range(1, self.depth):

            @pl.when(offset == member)
            def _():
                for part in range(self.pieces):
                    if self.last(member, part) + 1 == self.bits:
                        self.landed(member, part)

    def close(self):
        for offset in range(self.depth):
            for stage, part in self.sends(offset):
                self.copy(offset, stage, part).wait_send()

    @staticmethod
    def scratch(depth, pieces):
        return [DMA((depth, bits_of(depth), pieces)), DMA((depth, pieces))]


class Reduce(Cube):
    def __init__(self, terms, landing, share, depth, pieces, send, recv):
        super().__init__(share, depth, pieces)
        self.terms, self.landing, self.send, self.recv = terms, landing, send, recv

    def slot(self, stage, offset, part):
        order = self.order(part)
        found = [
            (level, member)
            for level in range(self.bits)
            for member in range(self.depth)
            if not any(member >> order[below] & 1 for below in range(level + 1))
        ]
        return found.index((stage, offset))

    def first(self, offset, part):
        order = self.order(part)
        return min(stage for stage in range(self.bits) if offset >> order[stage] & 1)

    def copy(self, offset, part):
        stage = self.first(offset, part)
        bit = self.order(part)[stage]
        slot = self.slot(stage, offset ^ (1 << bit), part)
        return remote(
            self.terms.at[self.span(across(self.spot, offset, self.depth), part), :],
            self.landing.at[self.span(slot, part), :],
            self.send.at[offset, part],
            self.recv.at[slot, part],
            self.neighbour(bit),
        )

    def landed(self, slot, part):
        view = self.landing.at[self.span(slot, part), :]
        remote(view, view, self.send.at[0, part], self.recv.at[slot, part], self.me).wait_recv()

    def ready(self, offset):
        for member in range(1, self.depth):

            @pl.when(offset == member)
            def _():
                for part in range(self.pieces):
                    if self.first(member, part) == 0:
                        self.copy(member, part).start()

    def ready_share(self, index):
        self.ready(offset_between(index, self.spot, self.depth))

    def add(self, target, target_start, term_start, slots, part):
        def body(index, carry):
            offset = index * 16
            value = self.terms[pl.ds(pl.multiple_of(term_start + offset, 16), 16), :].astype(F32)
            for slot in slots:
                start = slot * self.share + part * self.rows
                value = value + self.landing[
                    pl.ds(pl.multiple_of(start + offset, 16), 16), :
                ].astype(F32)
            target[pl.ds(pl.multiple_of(target_start + offset, 16), 16), :] = value.astype(
                target.dtype
            )
            return carry

        lax.fori_loop(0, self.rows // 16, body, 0)

    def relay(self):
        for level in range(1, self.bits):
            for part in range(self.pieces):
                for offset in range(1, self.depth):
                    if self.first(offset, part) == level:
                        slots = [self.slot(below, offset, part) for below in range(level)]
                        for slot in slots:
                            self.landed(slot, part)
                        start = (
                            across(self.spot, offset, self.depth) * self.share + part * self.rows
                        )
                        self.add(self.terms, start, start, slots, part)
                        self.copy(offset, part).start()

    def finish(self, total):
        for part in range(self.pieces):
            slots = [self.slot(stage, 0, part) for stage in range(self.bits)]
            for slot in slots:
                self.landed(slot, part)
            skip = part * self.rows
            self.add(total, skip, self.spot * self.share + skip, slots, part)

    def close(self):
        for offset in range(1, self.depth):
            for part in range(self.pieces):
                self.copy(offset, part).wait_send()

    @staticmethod
    def scratch(depth, pieces):
        return [DMA((depth, pieces)), DMA((depth - 1, pieces))]


class Fold:
    def __init__(self, source, scratch, low, depth, groups):
        self.source, self.low = source, low
        (
            self.stage,
            self.near,
            self.land,
            self.part,
            self.side_land,
            self.send,
            self.recv,
        ) = scratch
        self.me = lax.axis_index("tensor")
        self.group = lax.axis_index("dp")
        self.lines = groups // PAIR
        self.core = self.group % PAIR
        self.line = self.group // PAIR
        self.mate = self.group + 1 - 2 * self.core
        self.partner = self.me + depth * (1 - 2 * (self.me // depth))
        self.rows = self.part.shape[1]
        self.half = self.rows * self.lines

    @staticmethod
    def scratch(shape, groups):
        _, rows, width = shape
        lines = groups // PAIR
        part = rows // groups
        return [
            pltpu.VMEM((PAIR, part * lines, width), LOW),
            pltpu.VMEM((PAIR, part * lines, width), LOW),
            pltpu.VMEM((lines, PAIR, part, width), LOW),
            pltpu.VMEM((PAIR, part, width), LOW),
            pltpu.VMEM((part, width), LOW),
            DMA((2 + 3 * lines,)),
            DMA((2 + 3 * lines,)),
        ]

    def each(self, rows, body):
        step = 48 if rows % 48 == 0 else 16 if rows % 16 == 0 else rows

        def run(index, carry):
            body(pl.multiple_of(index * step, step), step)
            return carry

        lax.fori_loop(0, rows // step, run, 0)

    def window(self, start, size):
        return pl.ds(pl.multiple_of(start, 16), size)

    def behind(self, step):
        return (self.line + self.lines - step) % self.lines

    def block(self, core, line):
        return self.low.at[self.window(core * self.half + line * self.rows, self.rows), :]

    def near_copy(self):
        return remote(
            self.source.at[:, self.window((1 - self.core) * self.half, self.half), :],
            self.near,
            self.send.at[0],
            self.recv.at[0],
            self.me,
            self.mate,
        )

    def cross_copy(self, step):
        line = (self.line + step) % self.lines
        return remote(
            self.stage.at[:, self.window(line * self.rows, self.rows), :],
            self.land.at[self.line],
            self.send.at[2 + step],
            self.recv.at[2 + step],
            self.me,
            line * PAIR + self.core,
        )

    def side_copy(self):
        return remote(
            self.part.at[1],
            self.side_land,
            self.send.at[1],
            self.recv.at[1],
            self.partner,
            self.group,
        )

    def line_copy(self, step):
        line = (self.line + step) % self.lines
        view = self.block(self.core, self.line)
        slot = 2 + self.lines + step
        return remote(
            view,
            view,
            self.send.at[slot],
            self.recv.at[slot],
            self.me,
            line * PAIR + self.core,
        )

    def mate_copy(self, core, line):
        view = self.block(core, line)
        slot = 2 + 2 * self.lines + line
        return remote(view, view, self.send.at[slot], self.recv.at[slot], self.me, self.mate)

    def one(self):
        self.near_copy().start()

    def two(self):
        self.near_copy().wait_recv()

        def add(at, size):
            rows = self.window(at, size)
            for shard in range(PAIR):
                mine = self.source[shard, self.window(self.core * self.half + at, size), :]
                self.stage[shard, rows, :] = (
                    mine.astype(F32) + self.near[shard, rows, :].astype(F32)
                ).astype(LOW)

        self.each(self.half, add)
        for step in range(1, self.lines):
            self.cross_copy(step).start()

    def three(self):
        for step in range(1, self.lines):
            view = self.land.at[self.behind(step)]
            remote(
                view, view, self.send.at[2 + step], self.recv.at[2 + step], self.me, self.mate
            ).wait_recv()

        def add(at, size):
            rows = self.window(at, size)
            for shard in range(PAIR):
                value = self.stage[
                    shard, self.window(self.line * self.rows + at, size), :
                ].astype(F32)
                for step in range(1, self.lines):
                    value = value + self.land[self.behind(step), shard, rows, :].astype(F32)
                self.part[shard, rows, :] = value.astype(LOW)

        self.each(self.rows, add)
        self.side_copy().start()

    def four(self):
        self.side_copy().wait_recv()

        def add(at, size):
            rows = self.window(at, size)
            value = self.part[0, rows, :].astype(F32) + self.side_land[rows, :].astype(F32)
            spot = self.window(self.core * self.half + self.line * self.rows + at, size)
            self.low[spot, :] = value.astype(LOW)

        self.each(self.rows, add)
        for step in range(1, self.lines):
            self.line_copy(step).start()
        self.mate_copy(self.core, self.line).start()

    def five(self):
        for step in range(1, self.lines):
            line = self.behind(step)
            view = self.block(self.core, line)
            slot = 2 + self.lines + step
            remote(
                view, view, self.send.at[slot], self.recv.at[slot], self.me, self.mate
            ).wait_recv()
            self.mate_copy(self.core, line).start()

    def six(self):
        for line in range(self.lines):
            self.mate_copy(1 - self.core, line).wait_recv()
        self.near_copy().wait_send()
        self.side_copy().wait_send()
        for step in range(1, self.lines):
            self.cross_copy(step).wait_send()
            self.line_copy(step).wait_send()
        for line in range(self.lines):
            self.mate_copy(self.core, line).wait_send()


class Spread:
    def __init__(self, whole, share, depth, pieces, scratch):
        self.whole, self.share, self.depth, self.pieces = whole, share, depth, pieces
        send, recv, self.side_send, self.side_recv = scratch
        self.line = Line(whole, share, depth, pieces, send, recv)
        self.me, self.up, self.side = self.line.me, self.line.up, self.line.side

    @staticmethod
    def scratch(depth, pieces):
        return [
            DMA((2, depth, pieces)),
            DMA((2, depth, pieces)),
            DMA((depth, pieces)),
            DMA((depth, pieces)),
        ]

    def peers(self):
        group = lax.axis_index("dp")
        line = [
            (group, (self.up + step) % self.depth * PAIR + self.side)
            for step in range(1, self.depth)
        ]
        return line + [(group, self.me + 1 - 2 * self.side)]

    def peers_beyond(self, depth):
        me, spot, side = place(depth)
        group = lax.axis_index("dp")
        return [
            (group, (self.up + step) % self.depth * PAIR + self.side)
            for step in range(1, self.depth)
        ]

    def view(self, side, index, part):
        rows = self.share // self.pieces
        start = (index * PAIR + side) * self.share + part * rows
        return self.whole.at[pl.ds(pl.multiple_of(start, rows), rows), :]

    def own(self):
        return self.whole.at[pl.ds(pl.multiple_of(self.me * self.share, self.share), self.share), :]

    def across(self, index, part):
        view = self.view(self.side, index, part)
        return remote(
            view,
            view,
            self.side_send.at[index, part],
            self.side_recv.at[index, part],
            self.me + 1 - 2 * self.side,
        )

    def open(self):
        self.line.open()
        for part in range(self.pieces):
            self.across(self.up, part).start()

    def take(self, turn):
        self.line.take(turn, lambda source, part: self.across(source, part).start())

    def crossed(self, index):
        for part in range(self.pieces):
            view = self.view(1 - self.side, index, part)
            remote(
                view, view, self.side_send.at[index, part], self.side_recv.at[index, part], self.me
            ).wait_recv()

    def close(self):
        self.line.close()
        for index in range(self.depth):
            for part in range(self.pieces):
                self.across(index, part).wait_send()


class Share:
    def __init__(self, source, target, send, recv, which, depth, groups):
        self.source, self.target = source, target
        self.send, self.recv, self.which = send, recv, which
        self.me, _, side = place(depth)
        self.group = lax.axis_index("dp")
        self.partner = self.me + depth * (1 - 2 * side)
        rows = source.shape[0]
        self.all_lines = groups // PAIR
        self.cores = PAIR if rows % (PAIR * 16) == 0 else 1
        self.lines = self.all_lines if rows % (groups * 16) == 0 else 1
        self.rows = rows // (self.cores * self.lines)
        self.core = self.group % PAIR
        self.line = self.group // PAIR
        self.my_core = self.core if self.cores > 1 else 0
        self.my_line = self.line if self.lines > 1 else 0

    @staticmethod
    def scratch(members, groups):
        lines = groups // PAIR
        return [DMA((members, 1 + 2 * lines)), DMA((members, 1 + 2 * lines))]

    def view(self, array, core, line):
        if self.cores == 1:
            return array
        start = (core * self.lines + line) * self.rows
        return array.at[pl.ds(pl.multiple_of(start, 16), self.rows), :]

    def behind(self, step):
        return (self.line + self.lines - step) % self.lines

    def copy(self):
        return remote(
            self.view(self.source, self.my_core, self.my_line),
            self.view(self.target, self.my_core, self.my_line),
            self.send.at[self.which, 0],
            self.recv.at[self.which, 0],
            self.partner,
        )

    def hand(self, step):
        view = self.view(self.target, self.my_core, self.my_line)
        return remote(
            view,
            view,
            self.send.at[self.which, step],
            self.recv.at[self.which, step],
            self.me,
            (self.line + step) % self.lines * PAIR + self.core,
        )

    def mate(self, core, line):
        view = self.view(self.target, core, line)
        slot = self.all_lines + line
        return remote(
            view,
            view,
            self.send.at[self.which, slot],
            self.recv.at[self.which, slot],
            self.me,
            self.group + 1 - 2 * self.core,
        )

    def start(self):
        self.copy().start()

    def pass_on(self):
        self.copy().wait_recv()
        for step in range(1, self.lines):
            self.hand(step).start()
        if self.cores > 1:
            self.mate(self.core, self.my_line).start()

    def relay(self):
        for step in range(1, self.lines):
            line = self.behind(step)
            view = self.view(self.target, self.core, line)
            remote(
                view,
                view,
                self.send.at[self.which, step],
                self.recv.at[self.which, step],
                self.me,
                self.group,
            ).wait_recv()
            self.mate(self.core, line).start()

    def wait(self):
        if self.cores > 1:
            for line in range(self.lines):
                self.mate(1 - self.core, line).wait_recv()

    def close(self):
        self.copy().wait_send()
        for step in range(1, self.lines):
            self.hand(step).wait_send()
        if self.cores > 1:
            for line in range(self.lines):
                self.mate(self.core, line).wait_send()


def head_mask(head, width):
    lane = lax.broadcasted_iota(jnp.int32, (1, width), 1)
    return (lane >= head * HD) & (lane < (head + 1) * HD)


def softmax_rows(queries, keys, key_live, scale):
    scores = dot_nt(queries, keys) * scale
    scores = jnp.where(key_live, scores, -1e30)
    top = jnp.max(scores, axis=-1, keepdims=True)
    raised = jnp.exp(scores - top)
    return raised / jnp.sum(raised, axis=-1, keepdims=True)


def attend_shard(normed, heads, row, spots, proj_out, shard, rows, key_live, scale):
    local = heads.shape[0] // 4
    query_bias = row[:, spots["query"] : spots["query"] + local]
    value_bias = row[:, spots["value"] : spots["value"] + local]
    queries = (dot_nt(normed, heads[0:local, :]) + query_bias).astype(LOW)
    keys = dot_nt(normed, heads[local : 2 * local, :]).astype(LOW)
    values = (dot_nt(normed, heads[2 * local : 3 * local, :]) + value_bias).astype(LOW)
    proj_out[shard, 0, rows, :] = queries
    proj_out[shard, 1, rows, :] = keys
    proj_out[shard, 2, rows, :] = values
    attended = jnp.zeros((normed.shape[0], local), F32)
    for head in range(local // HD):
        mask = head_mask(head, local)
        weights = softmax_rows(jnp.where(mask, queries, 0.0).astype(LOW), keys, key_live, scale)
        attended = attended + dot(weights.astype(LOW), jnp.where(mask, values, 0.0).astype(LOW))
    return attended.astype(LOW)


def ahead_kernel(
    sizes,
    groups,
    count,
    index,
    patches,
    cotangent,
    qkv,
    out_weight,
    cond,
    mod_weight,
    up_own,
    down_own,
    mod_bias,
    qv_bias,
    out_bias,
    up_bias,
    down_bias,
    normed_out,
    proj_out,
    attended_out,
    tokens_own,
    mod,
    silu_all,
    heads_other,
    up_grad,
    down_grad,
    up_bias_grad,
    down_bias_grad,
    block_own,
    grad_mid_out,
    grad_branch_out,
    sums_out,
    heads_own,
    row_own,
    heads_sem,
    up_other,
    down_other,
    row_other,
    mid_out,
    branch_out,
    patch_rows,
    tokens,
    terms,
    landing,
    total,
    mod_mine,
    mod_gathered,
    patch_sem,
    send,
    recv,
    mod_send,
    mod_recv,
    silu_send,
    silu_recv,
    weight_send,
    weight_recv,
    *rest,
):
    depth, images, kept, share, pieces = sizes
    devices = depth * PAIR
    me, up, side = place(depth)
    group = lax.axis_index("dp")
    width = patches.shape[2]
    local = heads_own.shape[0] // 4
    mods = mod_weight.shape[0]
    spots, _ = row_spots(width, up_own.shape[0], local, mods)
    scale = HD ** (-0.5)
    fold = depth // images
    first = side * images

    def fetch(image):
        return pltpu.make_async_copy(
            patches.at[first + image], patch_rows.at[image], patch_sem.at[image]
        )

    def image_at(turn):
        return across(up // fold, images - 1 - turn, images)

    (
        normed_two,
        cot,
        hidden,
        grad_pre,
        grad_mlp,
        back_terms,
        back_landing,
        mlp_terms,
        mlp_landing,
        back_part,
        mlp_part,
        back_total,
        mlp_total,
        up_sums,
        down_sums,
        cot_sem,
        gather_send,
        gather_recv,
        back_send,
        back_recv,
        mlp_send,
        mlp_recv,
    ) = rest
    units = up_own.shape[0]

    def fetch_cotangent(image):
        return pltpu.make_async_copy(
            cotangent.at[first + image],
            cot.at[pl.ds(pl.multiple_of(image * kept, kept), kept), :],
            cot_sem.at[image],
        )

    def fetch_heads(member):
        return pltpu.make_async_copy(
            qkv.at[member] if member < 3 else out_weight,
            heads_own.at[pl.ds(member * local, local), :],
            heads_sem.at[member],
        )

    for member in range(4):
        fetch_heads(member).start()
    row_own[...] = jnp.zeros(row_own.shape, F32)
    for name, bias in (
        ("out", out_bias[...]),
        ("down", down_bias[...]),
        ("up", up_bias[...]),
        ("query", qv_bias[0:1, :]),
        ("value", qv_bias[1:2, :]),
        ("mod", mod_bias[...]),
    ):
        size = bias.shape[-1]
        row_own[:, spots[name] : spots[name] + size] = bias.astype(F32).reshape(1, size)
    for turn in range(images):
        fetch(image_at(turn)).start()
    meet(
        [(group, (me + step) % devices) for step in range(1, devices)]
        + [((group + step) % groups, me) for step in range(1, groups)]
    )
    value = cond[...].astype(F32)
    silu = (value / (1.0 + jnp.exp(-value))).astype(LOW)
    silu_all[group] = silu
    local_mod = (
        dot_nt(silu, mod_weight[...]) + row_own[:, spots["mod"] : spots["mod"] + mods]
    ).astype(LOW)
    mod_mine[...] = local_mod
    mod_gathered[me] = local_mod
    mod_copies = [
        remote(
            mod_mine,
            mod_gathered.at[me],
            mod_send.at[step],
            mod_recv.at[step],
            (me + step) % devices,
        )
        for step in range(1, devices)
    ]
    silu_copies = [
        remote(
            silu_all.at[group],
            silu_all.at[group],
            silu_send.at[step],
            silu_recv.at[step],
            me,
            (group + step) % groups,
        )
        for step in range(1, groups)
    ]
    for copy in mod_copies + silu_copies:
        copy.start()

    shares = [
        Share(source, target, weight_send, weight_recv, which, depth, groups)
        for which, (source, target) in enumerate(
            (
                (row_own, row_other),
                (heads_own, heads_other),
                (up_own, up_other),
                (down_own, down_other),
            )
        )
    ]
    for member in range(4):
        fetch_heads(member).wait()
    outer = up // (depth // PAIR) == side
    shares[0].start()
    shares[1].start()

    @pl.when(jnp.logical_not(outer))
    def _():
        shares[2].start()
        shares[3].start()

    for image in range(images):
        fetch_cotangent(image).start()
    reduce = Reduce(terms, landing, share, depth, pieces, send, recv)
    gather = Gather(normed_two, share, depth, pieces, gather_send, gather_recv)
    back_reduce = Reduce(back_terms, back_landing, share, depth, pieces, back_send, back_recv)
    mlp_reduce = Reduce(mlp_terms, mlp_landing, share, depth, pieces, mlp_send, mlp_recv)

    def pick_rows(turn, carry):
        image = image_at(turn)
        fetch(image).wait()
        rows = pl.ds(pl.multiple_of(image * kept, kept), kept)
        positions = lax.broadcasted_iota(jnp.int32, (patches.shape[1], kept), 0)
        slots = lax.broadcasted_iota(jnp.int32, (patches.shape[1], kept), 1)
        listed = index[pl.ds(first + image, 1), :]
        pick = jnp.where((positions == listed) & (slots < count[first + image]), 1.0, 0.0)
        tokens[rows, :] = dot_tn(pick.astype(LOW), patch_rows[image]).astype(LOW)
        return carry

    lax.fori_loop(0, images, pick_rows, 0)
    for step in range(1, devices):
        source = (me + devices - step) % devices
        remote(
            mod_mine, mod_gathered.at[source], mod_send.at[step], mod_recv.at[step], me
        ).wait_recv()
    mod[...] = jnp.concatenate(
        [mod_gathered[device].astype(F32) for device in range(devices)], axis=-1
    )

    def block(image, member):
        return mod[pl.ds(first + image, 1), member * width : (member + 1) * width]

    def one(turn, carry):
        image = image_at(turn)
        rows = pl.ds(pl.multiple_of(image * kept, kept), kept)

        @pl.when(turn == images - 1)
        def _():
            shares[0].pass_on()
            shares[1].pass_on()

        norm, _ = norm_parts(tokens[rows, :].astype(F32))
        normed = (norm * (1.0 + block(image, 1)) + block(image, 0)).astype(LOW)
        normed_out[rows, :] = normed
        key_live = lax.broadcasted_iota(jnp.int32, (1, kept), 1) < count[first + image]
        attended_out[0, rows, :] = attend_shard(
            normed, heads_own, row_own, spots, proj_out, 0, rows, key_live, scale
        )
        return carry

    def two(turn, carry):
        image = image_at(turn)
        rows = pl.ds(pl.multiple_of(image * kept, kept), kept)
        key_live = lax.broadcasted_iota(jnp.int32, (1, kept), 1) < count[first + image]
        attended = attend_shard(
            normed_out[rows, :], heads_other, row_other, spots, proj_out, 1, rows, key_live, scale
        )
        attended_out[1, rows, :] = attended
        branch = dot(attended_out[0, rows, :], heads_own[3 * local :, :]) + dot(
            attended, heads_other[3 * local :, :]
        )
        terms[rows, :] = branch.astype(LOW)
        for part in range(fold):
            reduce.ready_share(image * fold + part)
        return carry

    lax.fori_loop(0, images, one, 0)
    shares[1].relay()
    shares[1].wait()
    lax.fori_loop(0, images, two, 0)

    @pl.when(outer)
    def _():
        shares[2].start()
        shares[3].start()

    reduce.relay()
    shares[2].pass_on()
    reduce.finish(total)
    image = (up * share) // kept
    own_rows = pl.ds(pl.multiple_of(up * share, share), share)
    own = tokens[own_rows, :]
    tokens_own[...] = own
    branch = total[...] + row_own[:, spots["out"] : spots["out"] + width]
    branch_out[...] = branch
    mid = own.astype(F32) + block(image, 2) * branch
    mid_out[...] = mid
    norm, _ = norm_parts(mid)
    normed_two[own_rows, :] = (norm * (1.0 + block(image, 4)) + block(image, 3)).astype(LOW)
    shares[2].relay()
    gather.open()

    def half_pass(rows, shard, weight_up, row, weight_down):
        source = normed_two[rows, :]
        grad = grad_mlp[rows, :]
        bias = row[:, spots["up"] : spots["up"] + units]
        pre = dot_nt(source, weight_up[...]) + bias
        square = pre * pre
        bent = jnp.tanh(GELU_ROOT * pre * (1.0 + GELU_CUBE * square))
        half = 0.5 * (1.0 + bent)
        low_hidden = (pre * half).astype(LOW)
        hidden[shard, rows, :] = low_hidden
        slope = half + 0.5 * pre * (1.0 - bent * bent) * (
            GELU_ROOT * (1.0 + 3.0 * GELU_CUBE * square)
        )
        low_grad = (slope * dot_nt(grad, weight_down[...])).astype(LOW)
        grad_pre[shard, rows, :] = low_grad
        sums = jnp.sum(low_grad.astype(F32), axis=0, keepdims=True)
        return dot(low_hidden, weight_down[...]), dot(low_grad, weight_up[...]), sums

    def own_pass(image):
        fetch_cotangent(image).wait()
        rows = pl.ds(pl.multiple_of(image * kept, kept), kept)
        live = lax.broadcasted_iota(jnp.int32, (kept, 1), 0) < count[first + image]
        grad = jnp.where(live, cot[rows, :].astype(F32), 0.0)
        grad = (block(image, 5) * grad).astype(LOW)
        grad_mlp[rows, :] = grad
        down_sums[image] = jnp.sum(grad.astype(F32), axis=0, keepdims=True)
        mlp, back, sums = half_pass(rows, 0, up_own, row_own, down_own)
        up_sums[0, image] = sums
        mlp_part[rows, :] = mlp
        back_part[rows, :] = back

    def other_pass(image):
        rows = pl.ds(pl.multiple_of(image * kept, kept), kept)
        mlp, back, sums = half_pass(rows, 1, up_other, row_other, down_other)
        up_sums[1, image] = sums
        back_terms[rows, :] = (back_part[rows, :] + back).astype(LOW)
        mlp_terms[rows, :] = (mlp_part[rows, :] + mlp).astype(LOW)
        for part in range(fold):
            back_reduce.ready_share(image * fold + part)
            mlp_reduce.ready_share(image * fold + part)

    if fold == 1:

        def own_turn(turn, carry):
            @pl.when(turn == 1)
            def _():
                gather.relay()

            offset = turn + (turn // 2) * (1 - 2 * (turn % 2))
            gather.take(offset)
            own_pass(across(up, offset, depth))

            @pl.when(turn == 1)
            def _():
                shares[3].pass_on()

            return carry

        lax.fori_loop(0, depth, own_turn, 0)
    else:

        def own_image(image, carry):
            own_pass(image)
            return carry

        gather.relay()
        for offset in range(1, depth):
            gather.take(offset)
        shares[3].pass_on()
        lax.fori_loop(0, images, own_image, 0)
    shares[3].relay()
    for member in shares[2:]:
        member.wait()

    def other_turn(turn, carry):
        other_pass(image_at(turn))
        return carry

    lax.fori_loop(0, images, other_turn, 0)
    back_reduce.relay()
    mlp_reduce.relay()
    wide = tile_of(width)
    for shard in range(PAIR):

        def tile(step, carry):
            columns = pl.ds(pl.multiple_of(step * wide, 128), wide)
            up_grad[shard, 0:units, columns] = dot_tn(
                grad_pre[shard], normed_two[:, columns]
            ).astype(LOW)
            down_grad[shard, 0:units, columns] = dot_tn(
                hidden[shard], grad_mlp[:, columns]
            ).astype(LOW)
            return carry

        lax.fori_loop(0, width // wide, tile, 0)
        if units < up_grad.shape[1]:
            rest_rows = jnp.zeros((up_grad.shape[1] - units, width), LOW)
            up_grad[shard, units:, :] = rest_rows
            down_grad[shard, units:, :] = rest_rows
    back_reduce.finish(back_total)
    for shard in range(PAIR):
        up_bias_grad[shard : shard + 1, :] = sum(up_sums[shard, member] for member in range(images))
    down_bias_grad[...] = sum(down_sums[member] for member in range(images))
    live = (
        lax.broadcasted_iota(jnp.int32, (share, 1), 0) + (up * share) % kept
        < count[first + image]
    )
    grad_out = jnp.where(live, cot[own_rows, :].astype(F32), 0.0)
    norm, spread = norm_parts(mid_out[...])
    back = back_total[...]
    grad_mid = grad_out + norm_back(norm, spread, back * (1.0 + block(image, 4)))
    grad_mid_out[...] = grad_mid
    grad_branch_out[...] = (block(image, 2) * grad_mid).astype(LOW)
    sums_out[0:1, :] = jnp.sum(grad_mid * branch_out[...], axis=0, keepdims=True)
    sums_out[1:2, :] = jnp.sum(back, axis=0, keepdims=True)
    sums_out[2:3, :] = jnp.sum(back * norm, axis=0, keepdims=True)
    mlp_reduce.finish(mlp_total)
    mlp = mlp_total[...] + row_own[:, spots["down"] : spots["down"] + width]
    sums_out[3:4, :] = jnp.sum(grad_out * mlp, axis=0, keepdims=True)
    block_own[...] = jnp.where(live, mid_out[...] + block(image, 5) * mlp, 0.0).astype(LOW)
    for step in range(1, groups):
        source = (group + groups - step) % groups
        view = silu_all.at[source]
        remote(
            view, view, silu_send.at[step], silu_recv.at[step], me, group
        ).wait_recv()
    for member in shares:
        member.close()
    for copy in mod_copies + silu_copies:
        copy.wait_send()
    reduce.close()
    gather.close()
    back_reduce.close()
    mlp_reduce.close()


def ahead(sizes, groups, args):
    depth, images, kept, share, pieces = sizes
    patches, cotangent, qkv, out_weight, cond, mod_weight, up, down = args[2:10]
    spots, width = patches.shape[1:]
    local = out_weight.shape[0]
    mods = mod_weight.shape[0]
    units = up.shape[0]
    rows = images * kept
    heads = (4 * local, width)
    row = (1, row_spots(width, units, local, mods)[1])
    shape = jax.ShapeDtypeStruct
    devices = depth * PAIR
    return pl.pallas_call(
        functools.partial(ahead_kernel, sizes, groups),
        out_shape=(
            shape((rows, width), LOW),
            shape((PAIR, 3, rows, local), LOW),
            shape((PAIR, rows, local), LOW),
            shape((share, width), LOW),
            shape((cond.shape[0], devices * mods), F32),
            shape((groups,) + cond.shape, LOW),
            shape(heads, LOW),
            shape((PAIR, padded(units, groups), width), LOW),
            shape((PAIR, padded(units, groups), width), LOW),
            shape((PAIR, units), F32),
            shape((1, width), F32),
            shape((share, width), LOW),
            shape((share, width), F32),
            shape((share, width), LOW),
            shape((4, width), F32),
        ),
        in_specs=[SM, VM] + [HB] * 4 + [VM] * 9,
        out_specs=(VM,) * 15,
        scratch_shapes=[
            pltpu.VMEM(heads, LOW),
            pltpu.VMEM(row, F32),
            DMA((4,)),
            pltpu.VMEM(up.shape, LOW),
            pltpu.VMEM(down.shape, LOW),
            pltpu.VMEM(row, F32),
            pltpu.VMEM((share, width), F32),
            pltpu.VMEM((share, width), F32),
            pltpu.VMEM((images, spots, width), LOW),
            pltpu.VMEM((rows, width), LOW),
            pltpu.VMEM((rows, width), LOW),
            pltpu.VMEM((rows - share, width), LOW),
            pltpu.VMEM((share, width), F32),
            pltpu.VMEM((cond.shape[0], mods), LOW),
            pltpu.VMEM((devices, cond.shape[0], mods), LOW),
            DMA((images,)),
        ]
        + Reduce.scratch(depth, pieces)
        + [
            DMA((devices,)),
            DMA((devices,)),
            DMA((groups,)),
            DMA((groups,)),
        ]
        + Share.scratch(4, groups)
        + [
            pltpu.VMEM((rows, width), LOW),
            pltpu.VMEM((rows, width), LOW),
            pltpu.VMEM((PAIR, rows, units), LOW),
            pltpu.VMEM((PAIR, rows, units), LOW),
            pltpu.VMEM((rows, width), LOW),
            pltpu.VMEM((rows, width), LOW),
            pltpu.VMEM((rows - share, width), LOW),
            pltpu.VMEM((rows, width), LOW),
            pltpu.VMEM((rows - share, width), LOW),
            pltpu.VMEM((rows, width), F32),
            pltpu.VMEM((rows, width), F32),
            pltpu.VMEM((share, width), F32),
            pltpu.VMEM((share, width), F32),
            pltpu.VMEM((PAIR, images, 1, units), F32),
            pltpu.VMEM((images, 1, width), F32),
            DMA((images,)),
        ]
        + Gather.scratch(depth, pieces)
        + Reduce.scratch(depth, pieces)
        + Reduce.scratch(depth, pieces),
        compiler_params=pltpu.CompilerParams(
            collective_id=1, has_side_effects=True, vmem_limit_bytes=62 << 20
        ),
        name="ahead",
    )(*args)


def attend_back_kernel(
    sizes,
    groups,
    count,
    grad_own,
    normed,
    proj,
    attended,
    qkv_own,
    out_own,
    heads_other,
    mod,
    tokens_own,
    grad_mid,
    block_own,
    up_grad,
    down_grad,
    heads_grad,
    qv_grad,
    out_bias_grad,
    grad_tokens,
    sums_out,
    block_out,
    up_total,
    down_total,
    grads,
    grad_proj,
    terms,
    landing,
    total,
    qv_sums,
    out_sums,
    own_sem,
    gather_send,
    gather_recv,
    send,
    recv,
    *rest,
):
    depth, images, kept, share, pieces = sizes
    me, up, side = place(depth)
    width = grad_own.shape[1]
    local = out_own.shape[0]
    scale = HD ** (-0.5)
    fold = depth // images
    first = side * images
    up_fold = Fold(up_grad, rest[:7], up_total, depth, groups)
    down_fold = Fold(down_grad, rest[7:14], down_total, depth, groups)
    spread = Spread(block_out, share, depth, pieces, rest[14:18])
    own_rows = pl.ds(pl.multiple_of(up * share, share), share)
    own_copy = pltpu.make_async_copy(grad_own, grads.at[own_rows, :], own_sem.at[0])
    own_copy.start()
    block_copy = pltpu.make_async_copy(block_own, spread.own(), own_sem.at[1])
    block_copy.start()
    meet(column_peers(depth) + cube_peers(depth, groups) + spread.peers_beyond(depth))
    own_copy.wait()
    gather = Gather(grads, share, depth, pieces, gather_send, gather_recv)
    reduce = Reduce(terms, landing, share, depth, pieces, send, recv)
    gather.open()
    up_fold.one()
    down_fold.one()
    block_copy.wait()

    def one(image):
        rows = pl.ds(pl.multiple_of(image * kept, kept), kept)
        key_live = lax.broadcasted_iota(jnp.int32, (1, kept), 1) < count[first + image]
        grad = grads[rows, :]
        out_sums[image] = jnp.sum(grad.astype(F32), axis=0, keepdims=True)
        back = None
        for shard in range(PAIR):
            weights_in = [
                heads_other[member * local : (member + 1) * local, :] if shard else qkv_own[member]
                for member in range(3)
            ]
            weights_out = heads_other[3 * local :, :] if shard else out_own[...]
            grad_att = dot_nt(grad, weights_out).astype(LOW)
            queries = proj[shard, 0, rows, :]
            keys = proj[shard, 1, rows, :]
            values = proj[shard, 2, rows, :]
            grad_q = jnp.zeros((kept, local), F32)
            grad_k = jnp.zeros((kept, local), F32)
            grad_v = jnp.zeros((kept, local), F32)
            for head in range(local // HD):
                mask = head_mask(head, local)
                head_q = jnp.where(mask, queries, 0.0).astype(LOW)
                head_grad = jnp.where(mask, grad_att, 0.0).astype(LOW)
                weights = softmax_rows(head_q, keys, key_live, scale)
                grad_weights = dot_nt(head_grad, values)
                inner = jnp.sum(weights * grad_weights, axis=-1, keepdims=True)
                grad_scores = (weights * (grad_weights - inner)).astype(LOW)
                grad_v = grad_v + dot_tn(weights.astype(LOW), head_grad)
                grad_q = grad_q + dot(grad_scores, jnp.where(mask, keys, 0.0).astype(LOW))
                grad_k = grad_k + dot_tn(grad_scores, head_q)
            for member, value in enumerate((grad_q * scale, grad_k * scale, grad_v)):
                low = value.astype(LOW)
                grad_proj[shard, member, rows, :] = low
                part = dot(low, weights_in[member])
                back = part if back is None else back + part
                if member != 1:
                    row = 2 * shard + member // 2
                    qv_sums[row, image] = jnp.sum(low.astype(F32), axis=0, keepdims=True)
        terms[rows, :] = back.astype(LOW)
        for part in range(fold):
            reduce.ready_share(image * fold + part)

    if fold == 1:

        def turn_of(turn, carry):
            @pl.when(turn == 1)
            def _():
                gather.relay()

            offset = turn + (turn // 2) * (1 - 2 * (turn % 2))
            gather.take(offset)
            one(across(up, offset, depth))

            @pl.when(turn == 0)
            def _():
                up_fold.two()
                down_fold.two()

            @pl.when(turn == 1)
            def _():
                spread.open()

            @pl.when(turn == 2)
            def _():
                up_fold.three()

            @pl.when(turn == 3)
            def _():
                down_fold.three()

            return carry

        lax.fori_loop(0, depth, turn_of, 0)
    else:

        def image_of(image, carry):
            one(image)
            return carry

        gather.relay()
        for offset in range(1, depth):
            gather.take(offset)
        up_fold.two()
        down_fold.two()
        spread.open()
        lax.fori_loop(0, images, image_of, 0)
        up_fold.three()
        down_fold.three()

    def spread_of(turn, carry):
        spread.take(turn)
        return carry

    reduce.relay()
    lax.fori_loop(1, depth - 1, spread_of, 0)
    up_fold.four()
    down_fold.four()
    wide = tile_of(width)
    for shard in range(PAIR):

        def tile(step, carry):
            columns = pl.ds(pl.multiple_of(step * wide, 128), wide)
            source = normed[:, columns]
            for member in range(3):
                heads_grad[shard, member * local : (member + 1) * local, columns] = dot_tn(
                    grad_proj[shard, member], source
                ).astype(LOW)
            heads_grad[shard, 3 * local : 4 * local, columns] = dot_tn(
                attended[shard], grads[:, columns]
            ).astype(LOW)
            return carry

        lax.fori_loop(0, width // wide, tile, 0)
        if 4 * local < heads_grad.shape[1]:
            heads_grad[shard, 4 * local :, :] = jnp.zeros(
                (heads_grad.shape[1] - 4 * local, width), LOW
            )
    up_fold.five()
    spread.take(depth - 1)
    down_fold.five()
    reduce.finish(total)
    for row in range(2 * PAIR):
        qv_grad[row : row + 1, :] = sum(qv_sums[row, image] for image in range(images))
    out_bias_grad[...] = sum(out_sums[image] for image in range(images))
    image = first + (up * share) // kept
    live = (
        lax.broadcasted_iota(jnp.int32, (share, 1), 0) + (up * share) % kept < count[image]
    )
    norm, spread_rows = norm_parts(tokens_own[...].astype(F32))
    back = total[...]
    scale_one = mod[pl.ds(image, 1), width : 2 * width]
    grad = grad_mid[...] + norm_back(norm, spread_rows, back * (1.0 + scale_one))
    grad_tokens[...] = jnp.where(live, grad, 0.0).astype(LOW)
    sums_out[0:1, :] = jnp.sum(back, axis=0, keepdims=True)
    sums_out[1:2, :] = jnp.sum(back * norm, axis=0, keepdims=True)
    up_fold.six()
    down_fold.six()
    for index in range(depth):
        spread.crossed(index)
    spread.close()
    gather.close()
    reduce.close()


def attend_back(sizes, groups, args):
    depth, images, kept, share, pieces = sizes
    width = args[1].shape[1]
    local = args[6].shape[0]
    up_grad, down_grad = args[-2:]
    rows = images * kept
    shape = jax.ShapeDtypeStruct
    return pl.pallas_call(
        functools.partial(attend_back_kernel, sizes, groups),
        out_shape=(
            shape((PAIR, padded(4 * local, groups), width), LOW),
            shape((2 * PAIR, local), F32),
            shape((1, width), F32),
            shape((share, width), LOW),
            shape((2, width), F32),
            shape((PAIR * rows, width), LOW),
            shape(up_grad.shape[1:], LOW),
            shape(down_grad.shape[1:], LOW),
        ),
        in_specs=[SM] + [VM] * 13,
        out_specs=(VM,) * 8,
        scratch_shapes=[
            pltpu.VMEM((rows, width), LOW),
            pltpu.VMEM((PAIR, 3, rows, local), LOW),
            pltpu.VMEM((rows, width), LOW),
            pltpu.VMEM((rows - share, width), LOW),
            pltpu.VMEM((share, width), F32),
            pltpu.VMEM((2 * PAIR, images, 1, local), F32),
            pltpu.VMEM((images, 1, width), F32),
            DMA((2,)),
        ]
        + Gather.scratch(depth, pieces)
        + Reduce.scratch(depth, pieces)
        + Fold.scratch(up_grad.shape, groups)
        + Fold.scratch(down_grad.shape, groups)
        + Spread.scratch(depth, pieces),
        compiler_params=pltpu.CompilerParams(
            collective_id=3, has_side_effects=True, vmem_limit_bytes=62 << 20
        ),
        name="attend_back",
    )(*args)


def split_low(value):
    high = value.astype(LOW)
    rest = value - high.astype(F32)
    low = rest.astype(LOW)
    return high, low, (rest - low.astype(F32)).astype(LOW)


def close_kernel(
    sizes,
    groups,
    grad_tokens,
    sums_one,
    sums_two,
    up_bias_grad,
    qv_grad,
    down_bias_grad,
    out_bias_grad,
    heads_grad,
    silu_all,
    mod_weight,
    cond,
    whole,
    heads_total,
    bias_total,
    grads_out,
    silu_out,
    mod_bias_grad,
    grad_cond,
    biases,
    sum_row,
    sum_land,
    bias_land,
    cond_land,
    own_sem,
    sum_send,
    sum_recv,
    bias_send,
    bias_recv,
    cond_send,
    cond_recv,
    *rest,
):
    depth, images, kept, share, pieces = sizes
    devices = depth * PAIR
    everyone = devices * groups
    me, _, side = place(depth)
    group = lax.axis_index("dp")
    flat = group * devices + me
    width = grad_tokens.shape[1]
    columns = mod_weight.shape[0]
    span = sum_land.shape[2]
    spread = Spread(whole, share, depth, pieces, rest[:4])
    fold = Fold(heads_grad, rest[4:11], heads_total, depth, groups)
    own_copy = pltpu.make_async_copy(grad_tokens, spread.own(), own_sem)
    own_copy.start()
    barrier = pltpu.get_barrier_semaphore()

    def greet(step, carry):
        there = (flat + step) % everyone
        pl.semaphore_signal(
            barrier,
            inc=1,
            device_id={"dp": there // devices, "tensor": there % devices},
            device_id_type=MESH,
        )
        return carry

    lax.fori_loop(1, everyone, greet, 0)
    pl.semaphore_wait(barrier, everyone - 1)
    own_copy.wait()
    fold.one()
    spread.open()

    def aligned(device):
        return pl.multiple_of((device * columns) // 128 * 128, 128)

    for member in range(6):
        part = sums_one[member : member + 1, :] if member < 2 else sums_two[member - 2 : member - 1, :]
        sum_row[:, member * width : (member + 1) * width] = part
    sum_row[:, 6 * width :] = jnp.zeros((1, sum_row.shape[1] - 6 * width), F32)

    def sum_copy(step):
        there = (flat + step) % everyone
        device = there % devices
        return remote(
            sum_row.at[:, pl.ds(aligned(device), span)],
            sum_land.at[flat],
            sum_send.at[step],
            sum_recv.at[step],
            device,
            there // devices,
        )

    def send_sum(step, carry):
        sum_copy(step).start()
        return carry

    lax.fori_loop(1, everyone, send_sum, 0)
    sum_land[flat] = sum_row[:, pl.ds(aligned(me), span)]
    units, local = up_bias_grad.shape[1], qv_grad.shape[1]
    biases[...] = jnp.zeros(biases.shape, F32)
    for shard in range(PAIR):
        biases[3 * shard : 3 * shard + 1, 0:units] = up_bias_grad[shard : shard + 1, :]
        biases[3 * shard + 1 : 3 * shard + 3, 0:local] = qv_grad[2 * shard : 2 * shard + 2, :]
    biases[6:7, :] = down_bias_grad[...]
    biases[7:8, :] = out_bias_grad[...]
    slot = side * groups + group
    bias_land[slot] = biases[...]
    partner = me + depth * (1 - 2 * side)

    def bias_copy(step):
        crossed = step // groups
        there = (group + step) % groups
        device = jnp.where(crossed == 1, partner, me)
        return remote(
            biases, bias_land.at[slot], bias_send.at[step], bias_recv.at[step], device, there
        )

    for step in range(1, PAIR * groups):
        bias_copy(step).start()
    fold.two()

    def wait_sum(step, carry):
        source = (flat + everyone - step) % everyone
        view = sum_land.at[source]
        remote(view, view, sum_send.at[step], sum_recv.at[step], me).wait_recv()
        return carry

    lax.fori_loop(1, everyone, wait_sum, 0)
    offset = (me * columns) % 128
    grads = jnp.concatenate([sum_land[device] for device in range(everyone)], axis=0)
    grads = pltpu.roll(grads, lax.rem(span - offset, span), 1)[:, :columns]
    mod_bias_grad[...] = jnp.sum(grads, axis=0, keepdims=True)
    total_images = images * PAIR

    def image_of(device):
        return device * share // kept

    source = lax.broadcasted_iota(jnp.int32, (everyone, groups * total_images), 0)
    target = lax.broadcasted_iota(jnp.int32, (everyone, groups * total_images), 1)
    row_image = source // devices * total_images + image_of(source % devices)
    chosen = jnp.where(row_image == target, 1.0, 0.0).astype(LOW)
    silu_out[...] = dot(
        chosen,
        jnp.concatenate([silu_all[member].astype(F32) for member in range(groups)], axis=0).astype(
            LOW
        ),
    ).astype(LOW)
    parts = split_low(grads)
    spread.take(1)
    fold.three()
    grads_out[...] = grads.T
    source = lax.broadcasted_iota(jnp.int32, (total_images, everyone), 1)
    target = lax.broadcasted_iota(jnp.int32, (total_images, everyone), 0)
    chosen = jnp.where(
        (source // devices == group) & (image_of(source % devices) == target), 1.0, 0.0
    ).astype(LOW)
    mine = dot(chosen, parts[0]) + dot(chosen, parts[1]) + dot(chosen, parts[2])
    parts = split_low(mine)
    term = (
        dot(parts[0], mod_weight[...])
        + dot(parts[1], mod_weight[...])
        + dot(parts[2], mod_weight[...])
    )
    cond_land[me] = term

    def cond_copy(step):
        return remote(
            cond_land.at[me],
            cond_land.at[me],
            cond_send.at[step],
            cond_recv.at[step],
            (me + step) % devices,
        )

    for step in range(1, devices):
        cond_copy(step).start()
    for turn in range(2, depth - 1):
        spread.take(turn)
    fold.four()
    for step in range(1, PAIR * groups):
        crossed = step // groups
        source_group = (group + groups - step % groups) % groups
        source_side = jnp.where(crossed == 1, 1 - side, side)
        view = bias_land.at[source_side * groups + source_group]
        remote(view, view, bias_send.at[step], bias_recv.at[step], me).wait_recv()
    rows = biases.shape[0]
    result = jnp.zeros((rows, width), F32)
    for member in range(PAIR * groups):
        value = bias_land[member]
        turned = jnp.concatenate([value[3:6, :], value[0:3, :], value[6:, :]], axis=0)
        same = side == member // groups
        result = result + jnp.where(same, value, turned)
    bias_total[...] = result
    for step in range(1, devices):
        source = (me + devices - step) % devices
        view = cond_land.at[source]
        remote(view, view, cond_send.at[step], cond_recv.at[step], me).wait_recv()
    back = cond_land[0]
    for device in range(1, devices):
        back = back + cond_land[device]
    value = cond[...].astype(F32)
    gate = 1.0 / (1.0 + jnp.exp(-value))
    grad_cond[...] = (back * (gate + value * gate * (1.0 - gate))).astype(LOW)
    spread.take(depth - 1)
    fold.five()
    for where in range(depth):
        spread.crossed(where)
    fold.six()
    spread.close()

    def done_sum(step, carry):
        sum_copy(step).wait_send()
        return carry

    lax.fori_loop(1, everyone, done_sum, 0)
    for step in range(1, PAIR * groups):
        bias_copy(step).wait_send()
    for step in range(1, devices):
        cond_copy(step).wait_send()


def close(sizes, groups, args):
    depth, images, kept, share, pieces = sizes
    grad_tokens = args[0]
    heads_grad, silu_all, mod_weight, cond = args[-4:]
    devices = depth * PAIR
    width = grad_tokens.shape[1]
    columns = mod_weight.shape[0]
    biases = (8, width)
    span = max(-(-((device * columns) % 128 + columns) // 128) * 128 for device in range(devices))
    long = max((device * columns) // 128 * 128 + span for device in range(devices))
    long = max(long, 6 * width + 128)
    shape = jax.ShapeDtypeStruct
    rows = PAIR * images * kept
    everyone = devices * groups
    return pl.pallas_call(
        functools.partial(close_kernel, sizes, groups),
        out_shape=(
            shape((rows, width), LOW),
            shape(heads_grad.shape[1:], LOW),
            shape(biases, F32),
            shape((columns, everyone), F32),
            shape((everyone, width), LOW),
            shape((1, columns), F32),
            shape(cond.shape, LOW),
        ),
        in_specs=[VM] * 11,
        out_specs=(VM,) * 7,
        scratch_shapes=[
            pltpu.VMEM(biases, F32),
            pltpu.VMEM((1, long), F32),
            pltpu.VMEM((everyone, 1, span), F32),
            pltpu.VMEM((PAIR * groups,) + biases, F32),
            pltpu.VMEM((devices,) + cond.shape, F32),
            DMA,
            DMA((everyone,)),
            DMA((everyone,)),
            DMA((PAIR * groups,)),
            DMA((PAIR * groups,)),
            DMA((devices,)),
            DMA((devices,)),
        ]
        + Spread.scratch(depth, pieces)
        + Fold.scratch(heads_grad.shape, groups),
        compiler_params=pltpu.CompilerParams(
            collective_id=4, has_side_effects=True, vmem_limit_bytes=62 << 20
        ),
        name="close",
    )(*args)


def settle_kernel(
    index,
    whole,
    block,
    up_low,
    down_low,
    heads_low,
    mod_grads,
    silu_rows,
    biases,
    mod_bias,
    cond,
    block_out,
    grad_patches,
    grad_cond,
    mod_rows_grad,
    mod_bias_grad,
    qkv_grad,
    qv_grad,
    out_grad,
    out_bias_grad,
    up_grad,
    up_bias_grad,
    down_grad,
    down_bias_grad,
):
    members, kept, _ = block_out.shape
    step = pl.program_id(0)
    local, units = out_grad.shape[0], up_bias_grad.shape[0]
    for member in range(members):
        rows = slice(member * kept, (member + 1) * kept)
        block_out[member] = block[rows, :]
        positions = lax.broadcasted_iota(jnp.int32, (grad_patches.shape[1], kept), 0)
        listed = index[pl.ds(step * members + member, 1), :]
        pick = jnp.where(positions == listed, 1.0, 0.0).astype(LOW)
        grad_patches[member] = dot(pick, whole[rows, :]).astype(LOW)
    parts = split_low(mod_grads[...])
    silu = silu_rows[...]
    mod_rows_grad[...] = dot(parts[0], silu) + dot(parts[1], silu) + dot(parts[2], silu)
    up_grad[...] = up_low[...].astype(F32)
    down_grad[...] = down_low[...].astype(F32)

    @pl.when(step == 0)
    def _():
        for member in range(3):
            qkv_grad[member] = heads_low[member * local : (member + 1) * local, :].astype(F32)
        out_grad[...] = heads_low[3 * local : 4 * local, :].astype(F32)
        grad_cond[...] = cond[...]
        mod_bias_grad[...] = mod_bias[...].reshape(mod_bias_grad.shape)
        qv_grad[...] = biases[1:3, 0:local]
        up_bias_grad[...] = biases[0:1, 0:units].reshape(up_bias_grad.shape)
        down_bias_grad[...] = biases[6:7, :].reshape(down_bias_grad.shape)
        out_bias_grad[...] = biases[7:8, :].reshape(out_bias_grad.shape)


def settle(local, units, spots, args):
    index, whole, block, up_low, down_low, heads_low, mod_grads, silu_rows, biases, mod_bias, cond = args
    images, kept = index.shape
    width = whole.shape[1]
    mods = mod_bias.shape[1]
    steps = 4 if units % 64 == 0 and mods % 32 == 0 else 2
    members = images // steps
    shape = jax.ShapeDtypeStruct

    def full(array):
        return pl.BlockSpec(array.shape, lambda step: (0,) * len(array.shape))

    def part(array, rows):
        rest = array.shape[1:]
        return pl.BlockSpec((rows,) + rest, lambda step: (step,) + (0,) * len(rest))

    outs = (
        shape((images, kept, width), LOW),
        shape((images, spots, width), LOW),
        shape(cond.shape, LOW),
        shape((mods, width), F32),
        shape((mods,), F32),
        shape((3, local, width), F32),
        shape((2, local), F32),
        shape((local, width), F32),
        shape((width,), F32),
        shape((units, width), F32),
        shape((units,), F32),
        shape((units, width), F32),
        shape((width,), F32),
    )
    return pl.pallas_call(
        settle_kernel,
        grid=(steps,),
        out_shape=outs,
        in_specs=[
            full(index),
            part(whole, members * kept),
            part(block, members * kept),
            part(up_low, units // steps),
            part(down_low, units // steps),
            full(heads_low),
            part(mod_grads, mods // steps),
            full(silu_rows),
            full(biases),
            full(mod_bias),
            full(cond),
        ],
        out_specs=(
            part(outs[0], members),
            part(outs[1], members),
            full(outs[2]),
            part(outs[3], mods // steps),
            full(outs[4]),
            full(outs[5]),
            full(outs[6]),
            full(outs[7]),
            full(outs[8]),
            part(outs[9], units // steps),
            full(outs[10]),
            part(outs[11], units // steps),
            full(outs[12]),
        ),
        compiler_params=pltpu.CompilerParams(vmem_limit_bytes=60 << 20),
        name="settle",
    )(*args)


def on_device(
    patches,
    conditioning,
    keep_count,
    keep_index,
    mod_weight,
    mod_bias,
    qkv_weight,
    qv_bias,
    out_weight,
    out_bias,
    up_weight,
    up_bias,
    down_weight,
    down_bias,
    out_cotangent,
):
    devices = lax.axis_size("tensor")
    depth = devices // PAIR
    all_images, kept = keep_index.shape
    width = patches.shape[2]
    images = all_images // PAIR
    share = images * kept // depth
    pieces = 4 if share % 64 == 0 else 2
    sizes = (depth, images, kept, share, pieces)
    groups = lax.axis_size("dp")
    local, units = qkv_weight.shape[2], up_weight.shape[1]
    up = up_weight.T
    mod_rows = mod_weight.T
    qkv = jnp.swapaxes(qkv_weight, 1, 2)
    (
        normed_one,
        proj,
        attended,
        tokens_own,
        mod,
        silu_all,
        heads_other,
        up_grad,
        down_grad,
        up_bias_grad,
        down_bias_grad,
        block_own,
        grad_mid,
        grad_branch,
        sums_two,
    ) = ahead(
        sizes,
        groups,
        (
            keep_count,
            keep_index,
            patches,
            out_cotangent,
            qkv,
            out_weight,
            conditioning,
            mod_rows,
            up,
            down_weight,
            mod_bias,
            qv_bias,
            out_bias,
            up_bias,
            down_bias,
        ),
    )
    (
        heads_grad,
        qv_grad,
        out_bias_grad,
        grad_tokens,
        sums_one,
        block_out,
        up_total,
        down_total,
    ) = attend_back(
        sizes,
        groups,
        (
            keep_count,
            grad_branch,
            normed_one,
            proj,
            attended,
            qkv,
            out_weight,
            heads_other,
            mod,
            tokens_own,
            grad_mid,
            block_own,
            up_grad,
            down_grad,
        ),
    )
    (
        grad_whole,
        heads_total,
        bias_total,
        mod_grads,
        silu_rows,
        mod_bias_total,
        cond_total,
    ) = close(
        sizes,
        groups,
        (
            grad_tokens,
            sums_one,
            sums_two,
            up_bias_grad,
            qv_grad,
            down_bias_grad,
            out_bias_grad,
            heads_grad,
            silu_all,
            mod_rows,
            conditioning,
        ),
    )
    (
        block_out,
        grad_patches,
        grad_conditioning,
        mod_rows_grad,
        mod_bias_grad,
        qkv_grad,
        qv_bias_grad,
        out_weight_grad,
        out_bias_grad,
        up_rows_grad,
        up_bias_grad,
        down_weight_grad,
        down_bias_grad,
    ) = settle(
        local,
        units,
        patches.shape[1],
        (
            keep_index,
            grad_whole,
            block_out,
            up_total,
            down_total,
            heads_total,
            mod_grads,
            silu_rows,
            bias_total,
            mod_bias_total,
            cond_total,
        ),
    )
    return (
        block_out,
        grad_patches,
        grad_conditioning,
        mod_rows_grad.T,
        mod_bias_grad,
        jnp.swapaxes(qkv_grad, 1, 2),
        qv_bias_grad,
        out_weight_grad,
        out_bias_grad,
        up_rows_grad.T,
        up_bias_grad,
        down_weight_grad,
        down_bias_grad,
    )


def solution(mesh):
    placed = (
        P("dp", None, None),
        P("dp", None),
        P("dp"),
        P("dp", None),
        P(None, "tensor"),
        P("tensor"),
        P(None, None, "tensor"),
        P(None, "tensor"),
        P("tensor", None),
        P(),
        P(None, "tensor"),
        P("tensor"),
        P("tensor", None),
        P(),
        P("dp", None, None),
    )
    return jax.shard_map(
        on_device,
        mesh=mesh,
        in_specs=placed,
        out_specs=(
            P("dp", None, None),
            P("dp", None, None),
            P("dp", None),
            P(None, "tensor"),
            P("tensor"),
            P(None, None, "tensor"),
            P(None, "tensor"),
            P("tensor", None),
            P(),
            P(None, "tensor"),
            P("tensor"),
            P("tensor", None),
            P(),
        ),
        check_vma=False,
    )
```

```python
import functools

import jax
import jax.numpy as jnp
from jax import lax
from jax.experimental import pallas as pl
from jax.experimental.pallas import tpu as pltpu
from jax.sharding import PartitionSpec as P

HD = 72
MESH = pl.DeviceIdType.MESH
F32 = jnp.float32
LOW = jnp.bfloat16
DMA = pltpu.SemaphoreType.DMA
VM = pl.BlockSpec(memory_space=pltpu.VMEM)
SM = pl.BlockSpec(memory_space=pltpu.SMEM)
HB = pl.BlockSpec(memory_space=pl.ANY)
PAIR = 2
GELU_ROOT = 0.7978845608028654
GELU_CUBE = 0.044715


def remote(source, target, send_sem, recv_sem, device, group=None):
    there = {"tensor": device} if group is None else {"dp": group, "tensor": device}
    return pltpu.make_async_remote_copy(
        src_ref=source,
        dst_ref=target,
        send_sem=send_sem,
        recv_sem=recv_sem,
        device_id=there,
        device_id_type=MESH,
    )


def place(depth):
    me = lax.axis_index("tensor")
    return me, me % depth, me // depth


def bits_of(depth):
    return depth.bit_length() - 1


def toward(spot, bit):
    return (1 - 2 * ((spot // (1 << bit)) % 2)) * (1 << bit)


def across(spot, offset, depth):
    result = spot
    for bit in range(bits_of(depth)):
        result = result + ((offset // (1 << bit)) % 2) * toward(spot, bit)
    return result


def offset_between(left, right, depth):
    result = 0
    for bit in range(bits_of(depth)):
        size = 1 << bit
        result = result + ((left // size + right // size) % 2) * size
    return result


def meet(peers):
    barrier = pltpu.get_barrier_semaphore()
    for group, peer in peers:
        pl.semaphore_signal(
            barrier, inc=1, device_id={"dp": group, "tensor": peer}, device_id_type=MESH
        )
    pl.semaphore_wait(barrier, len(peers))


def column_peers(depth):
    me, spot, side = place(depth)
    group = lax.axis_index("dp")
    return [(group, me + toward(spot, bit)) for bit in range(bits_of(depth))]


def cube_peers(depth, groups):
    me, spot, side = place(depth)
    group = lax.axis_index("dp")
    other = me + depth * (1 - 2 * side)
    peers = [((group + step) % groups, me) for step in range(1, groups)]
    return peers + [((group + step) % groups, other) for step in range(groups)]


def padded(rows, groups):
    return -(-rows // (16 * groups)) * 16 * groups


def lanes(columns):
    return -(-columns // 128) * 128


def row_spots(width, units, local, mods):
    spots = {}
    start = 0
    for name, size in (
        ("out", width),
        ("down", width),
        ("up", units),
        ("query", local),
        ("value", local),
        ("mod", mods),
    ):
        spots[name] = start
        start += lanes(size)
    return spots, start


def tile_of(width):
    return 384 if width % 384 == 0 else 128


def dot(left, right):
    return jnp.dot(left, right, preferred_element_type=F32)


def dot_nt(left, right):
    return lax.dot_general(left, right, (((1,), (1,)), ((), ())), preferred_element_type=F32)


def dot_tn(left, right):
    return lax.dot_general(left, right, (((0,), (0,)), ((), ())), preferred_element_type=F32)


def norm_parts(rows):
    width = rows.shape[-1]
    centred = rows - jnp.sum(rows, axis=-1, keepdims=True) * (1.0 / width)
    spread = lax.rsqrt(jnp.sum(centred * centred, axis=-1, keepdims=True) * (1.0 / width) + 1e-06)
    return centred * spread, spread


def norm_back(norm, spread, grad):
    width = norm.shape[-1]
    mean_grad = jnp.sum(grad, axis=-1, keepdims=True) * (1.0 / width)
    mean_both = jnp.sum(grad * norm, axis=-1, keepdims=True) * (1.0 / width)
    return (grad - mean_grad - norm * mean_both) * spread


class Line:
    def __init__(self, buffer, share, depth, pieces, send, recv):
        self.buffer, self.share, self.depth, self.pieces = buffer, share, depth, pieces
        self.send, self.recv = send, recv
        self.me = lax.axis_index("tensor")
        self.up, self.side = self.me // PAIR, self.me % PAIR

    def piece(self, index, part):
        rows = self.share // self.pieces
        start = (index * PAIR + self.side) * self.share + part * rows
        return self.buffer.at[pl.ds(pl.multiple_of(start, rows), rows), :]

    def copy(self, way, step, part):
        source = self.up - (step - 1) * (1 - 2 * way)
        target = self.up + 1 - 2 * way
        view = self.piece(source, part)
        return remote(
            view,
            view,
            self.send.at[way, step, part],
            self.recv.at[way, step, part],
            target * PAIR + self.side,
        )

    def may_send(self, way, step):
        if way == 0:
            return (self.up + 1 < self.depth) & (self.up >= step - 1)
        return (self.up >= 1) & (self.up + step - 1 < self.depth)

    def open(self):
        for part in range(self.pieces):
            for way in range(2):

                @pl.when(self.may_send(way, 1))
                def _():
                    self.copy(way, 1, part).start()

    def arrival(self, turn):
        below = self.up
        above = self.depth - 1 - self.up
        both = jnp.minimum(below, above)
        mixed = turn <= 2 * both
        way = jnp.where(mixed, (turn + 1) % 2, jnp.where(below > above, 0, 1))
        step = jnp.where(mixed, (turn + 1) // 2, turn - both)
        return way, step, self.up - step * (1 - 2 * way)

    def take(self, turn, then):
        way, step, source = self.arrival(turn)
        ahead = jnp.where(way == 0, self.up + 1 < self.depth, self.up >= 1)
        for part in range(self.pieces):
            view = self.piece(source, part)
            remote(
                view, view, self.send.at[way, step, part], self.recv.at[way, step, part], self.me
            ).wait_recv()

            @pl.when(ahead)
            def _():
                self.copy(way, step + 1, part).start()

            then(source, part)

    def close(self):
        for way in range(2):
            for step in range(1, self.depth):

                @pl.when(self.may_send(way, step))
                def _():
                    for part in range(self.pieces):
                        self.copy(way, step, part).wait_send()


class Cube:
    def __init__(self, share, depth, pieces):
        self.share, self.depth, self.pieces = share, depth, pieces
        self.me, self.spot, self.side = place(depth)
        self.bits = bits_of(depth)
        self.rows = share // pieces

    def order(self, part):
        ways = list(range(self.bits))
        return ways if part % 2 else ways[::-1]

    def span(self, index, part):
        return pl.ds(pl.multiple_of(index * self.share + part * self.rows, self.rows), self.rows)

    def neighbour(self, bit):
        return self.me + toward(self.spot, bit)


class Gather(Cube):
    def __init__(self, buffer, share, depth, pieces, send, recv):
        super().__init__(share, depth, pieces)
        self.buffer, self.send, self.recv = buffer, send, recv

    def last(self, offset, part):
        order = self.order(part)
        return max(
            (stage for stage in range(self.bits) if offset >> order[stage] & 1), default=-1
        )

    def copy(self, offset, stage, part):
        bit = self.order(part)[stage]
        view = self.buffer.at[self.span(across(self.spot, offset, self.depth), part), :]
        return remote(
            view,
            view,
            self.send.at[offset, stage, part],
            self.recv.at[offset ^ (1 << bit), part],
            self.neighbour(bit),
        )

    def landed(self, offset, part):
        view = self.buffer.at[self.span(across(self.spot, offset, self.depth), part), :]
        remote(
            view, view, self.send.at[0, 0, part], self.recv.at[offset, part], self.me
        ).wait_recv()

    def sends(self, offset):
        return [
            (stage, part)
            for part in range(self.pieces)
            for stage in range(self.last(offset, part) + 1, self.bits)
        ]

    def open(self):
        for stage, part in self.sends(0):
            self.copy(0, stage, part).start()

    def relay(self):
        for offset in sorted(range(1, self.depth), key=lambda value: bin(value).count("1")):
            for part in range(self.pieces):
                first = self.last(offset, part) + 1
                if first < self.bits:
                    self.landed(offset, part)
                    for stage in range(first, self.bits):
                        self.copy(offset, stage, part).start()

    def take(self, offset):
        for member in range(1, self.depth):

            @pl.when(offset == member)
            def _():
                for part in range(self.pieces):
                    if self.last(member, part) + 1 == self.bits:
                        self.landed(member, part)

    def close(self):
        for offset in range(self.depth):
            for stage, part in self.sends(offset):
                self.copy(offset, stage, part).wait_send()

    @staticmethod
    def scratch(depth, pieces):
        return [DMA((depth, bits_of(depth), pieces)), DMA((depth, pieces))]


class Reduce(Cube):
    def __init__(self, terms, landing, share, depth, pieces, send, recv):
        super().__init__(share, depth, pieces)
        self.terms, self.landing, self.send, self.recv = terms, landing, send, recv

    def slot(self, stage, offset, part):
        order = self.order(part)
        found = [
            (level, member)
            for level in range(self.bits)
            for member in range(self.depth)
            if not any(member >> order[below] & 1 for below in range(level + 1))
        ]
        return found.index((stage, offset))

    def first(self, offset, part):
        order = self.order(part)
        return min(stage for stage in range(self.bits) if offset >> order[stage] & 1)

    def copy(self, offset, part):
        stage = self.first(offset, part)
        bit = self.order(part)[stage]
        slot = self.slot(stage, offset ^ (1 << bit), part)
        return remote(
            self.terms.at[self.span(across(self.spot, offset, self.depth), part), :],
            self.landing.at[self.span(slot, part), :],
            self.send.at[offset, part],
            self.recv.at[slot, part],
            self.neighbour(bit),
        )

    def landed(self, slot, part):
        view = self.landing.at[self.span(slot, part), :]
        remote(view, view, self.send.at[0, part], self.recv.at[slot, part], self.me).wait_recv()

    def ready(self, offset):
        for member in range(1, self.depth):

            @pl.when(offset == member)
            def _():
                for part in range(self.pieces):
                    if self.first(member, part) == 0:
                        self.copy(member, part).start()

    def ready_share(self, index):
        self.ready(offset_between(index, self.spot, self.depth))

    def add(self, target, target_start, term_start, slots, part):
        def body(index, carry):
            offset = index * 16
            value = self.terms[pl.ds(pl.multiple_of(term_start + offset, 16), 16), :].astype(F32)
            for slot in slots:
                start = slot * self.share + part * self.rows
                value = value + self.landing[
                    pl.ds(pl.multiple_of(start + offset, 16), 16), :
                ].astype(F32)
            target[pl.ds(pl.multiple_of(target_start + offset, 16), 16), :] = value.astype(
                target.dtype
            )
            return carry

        lax.fori_loop(0, self.rows // 16, body, 0)

    def relay(self):
        for level in range(1, self.bits):
            for part in range(self.pieces):
                for offset in range(1, self.depth):
                    if self.first(offset, part) == level:
                        slots = [self.slot(below, offset, part) for below in range(level)]
                        for slot in slots:
                            self.landed(slot, part)
                        start = (
                            across(self.spot, offset, self.depth) * self.share + part * self.rows
                        )
                        self.add(self.terms, start, start, slots, part)
                        self.copy(offset, part).start()

    def finish(self, total):
        for part in range(self.pieces):
            slots = [self.slot(stage, 0, part) for stage in range(self.bits)]
            for slot in slots:
                self.landed(slot, part)
            skip = part * self.rows
            self.add(total, skip, self.spot * self.share + skip, slots, part)

    def close(self):
        for offset in range(1, self.depth):
            for part in range(self.pieces):
                self.copy(offset, part).wait_send()

    @staticmethod
    def scratch(depth, pieces):
        return [DMA((depth, pieces)), DMA((depth - 1, pieces))]


class Fold:
    def __init__(self, source, scratch, low, depth, groups):
        self.source, self.low = source, low
        (
            self.stage,
            self.near,
            self.land,
            self.part,
            self.side_land,
            self.send,
            self.recv,
        ) = scratch
        self.me = lax.axis_index("tensor")
        self.group = lax.axis_index("dp")
        self.lines = groups // PAIR
        self.core = self.group % PAIR
        self.line = self.group // PAIR
        self.mate = self.group + 1 - 2 * self.core
        self.partner = self.me + depth * (1 - 2 * (self.me // depth))
        self.rows = self.part.shape[1]
        self.half = self.rows * self.lines

    @staticmethod
    def scratch(shape, groups):
        _, rows, width = shape
        lines = groups // PAIR
        part = rows // groups
        return [
            pltpu.VMEM((PAIR, part * lines, width), LOW),
            pltpu.VMEM((PAIR, part * lines, width), LOW),
            pltpu.VMEM((lines, PAIR, part, width), LOW),
            pltpu.VMEM((PAIR, part, width), LOW),
            pltpu.VMEM((part, width), LOW),
            DMA((2 + 3 * lines,)),
            DMA((2 + 3 * lines,)),
        ]

    def each(self, rows, body):
        step = 48 if rows % 48 == 0 else 16 if rows % 16 == 0 else rows

        def run(index, carry):
            body(pl.multiple_of(index * step, step), step)
            return carry

        lax.fori_loop(0, rows // step, run, 0)

    def window(self, start, size):
        return pl.ds(pl.multiple_of(start, 16), size)

    def behind(self, step):
        return (self.line + self.lines - step) % self.lines

    def block(self, core, line):
        return self.low.at[self.window(core * self.half + line * self.rows, self.rows), :]

    def near_copy(self):
        return remote(
            self.source.at[:, self.window((1 - self.core) * self.half, self.half), :],
            self.near,
            self.send.at[0],
            self.recv.at[0],
            self.me,
            self.mate,
        )

    def cross_copy(self, step):
        line = (self.line + step) % self.lines
        return remote(
            self.stage.at[:, self.window(line * self.rows, self.rows), :],
            self.land.at[self.line],
            self.send.at[2 + step],
            self.recv.at[2 + step],
            self.me,
            line * PAIR + self.core,
        )

    def side_copy(self):
        return remote(
            self.part.at[1],
            self.side_land,
            self.send.at[1],
            self.recv.at[1],
            self.partner,
            self.group,
        )

    def line_copy(self, step):
        line = (self.line + step) % self.lines
        view = self.block(self.core, self.line)
        slot = 2 + self.lines + step
        return remote(
            view,
            view,
            self.send.at[slot],
            self.recv.at[slot],
            self.me,
            line * PAIR + self.core,
        )

    def mate_copy(self, core, line):
        view = self.block(core, line)
        slot = 2 + 2 * self.lines + line
        return remote(view, view, self.send.at[slot], self.recv.at[slot], self.me, self.mate)

    def one(self):
        self.near_copy().start()

    def two(self):
        self.near_copy().wait_recv()

        def add(at, size):
            rows = self.window(at, size)
            for shard in range(PAIR):
                mine = self.source[shard, self.window(self.core * self.half + at, size), :]
                self.stage[shard, rows, :] = (
                    mine.astype(F32) + self.near[shard, rows, :].astype(F32)
                ).astype(LOW)

        self.each(self.half, add)
        for step in range(1, self.lines):
            self.cross_copy(step).start()

    def three(self):
        for step in range(1, self.lines):
            view = self.land.at[self.behind(step)]
            remote(
                view, view, self.send.at[2 + step], self.recv.at[2 + step], self.me, self.mate
            ).wait_recv()

        def add(at, size):
            rows = self.window(at, size)
            for shard in range(PAIR):
                value = self.stage[
                    shard, self.window(self.line * self.rows + at, size), :
                ].astype(F32)
                for step in range(1, self.lines):
                    value = value + self.land[self.behind(step), shard, rows, :].astype(F32)
                self.part[shard, rows, :] = value.astype(LOW)

        self.each(self.rows, add)
        self.side_copy().start()

    def four(self):
        self.side_copy().wait_recv()

        def add(at, size):
            rows = self.window(at, size)
            value = self.part[0, rows, :].astype(F32) + self.side_land[rows, :].astype(F32)
            spot = self.window(self.core * self.half + self.line * self.rows + at, size)
            self.low[spot, :] = value.astype(LOW)

        self.each(self.rows, add)
        for step in range(1, self.lines):
            self.line_copy(step).start()
        self.mate_copy(self.core, self.line).start()

    def five(self):
        for step in range(1, self.lines):
            line = self.behind(step)
            view = self.block(self.core, line)
            slot = 2 + self.lines + step
            remote(
                view, view, self.send.at[slot], self.recv.at[slot], self.me, self.mate
            ).wait_recv()
            self.mate_copy(self.core, line).start()

    def six(self):
        for line in range(self.lines):
            self.mate_copy(1 - self.core, line).wait_recv()
        self.near_copy().wait_send()
        self.side_copy().wait_send()
        for step in range(1, self.lines):
            self.cross_copy(step).wait_send()
            self.line_copy(step).wait_send()
        for line in range(self.lines):
            self.mate_copy(self.core, line).wait_send()


class Spread:
    def __init__(self, whole, share, depth, pieces, scratch):
        self.whole, self.share, self.depth, self.pieces = whole, share, depth, pieces
        send, recv, self.side_send, self.side_recv = scratch
        self.line = Line(whole, share, depth, pieces, send, recv)
        self.me, self.up, self.side = self.line.me, self.line.up, self.line.side

    @staticmethod
    def scratch(depth, pieces):
        return [
            DMA((2, depth, pieces)),
            DMA((2, depth, pieces)),
            DMA((depth, pieces)),
            DMA((depth, pieces)),
        ]

    def peers(self):
        group = lax.axis_index("dp")
        line = [
            (group, (self.up + step) % self.depth * PAIR + self.side)
            for step in range(1, self.depth)
        ]
        return line + [(group, self.me + 1 - 2 * self.side)]

    def peers_beyond(self, depth):
        me, spot, side = place(depth)
        group = lax.axis_index("dp")
        return [
            (group, (self.up + step) % self.depth * PAIR + self.side)
            for step in range(1, self.depth)
        ]

    def view(self, side, index, part):
        rows = self.share // self.pieces
        start = (index * PAIR + side) * self.share + part * rows
        return self.whole.at[pl.ds(pl.multiple_of(start, rows), rows), :]

    def own(self):
        return self.whole.at[pl.ds(pl.multiple_of(self.me * self.share, self.share), self.share), :]

    def across(self, index, part):
        view = self.view(self.side, index, part)
        return remote(
            view,
            view,
            self.side_send.at[index, part],
            self.side_recv.at[index, part],
            self.me + 1 - 2 * self.side,
        )

    def open(self):
        self.line.open()
        for part in range(self.pieces):
            self.across(self.up, part).start()

    def take(self, turn):
        self.line.take(turn, lambda source, part: self.across(source, part).start())

    def crossed(self, index):
        for part in range(self.pieces):
            view = self.view(1 - self.side, index, part)
            remote(
                view, view, self.side_send.at[index, part], self.side_recv.at[index, part], self.me
            ).wait_recv()

    def close(self):
        self.line.close()
        for index in range(self.depth):
            for part in range(self.pieces):
                self.across(index, part).wait_send()


class Share:
    def __init__(self, source, target, send, recv, which, depth, groups):
        self.source, self.target = source, target
        self.send, self.recv, self.which = send, recv, which
        self.me, _, side = place(depth)
        self.group = lax.axis_index("dp")
        self.partner = self.me + depth * (1 - 2 * side)
        rows = source.shape[0]
        self.all_lines = groups // PAIR
        self.cores = PAIR if rows % (PAIR * 16) == 0 else 1
        self.lines = self.all_lines if rows % (groups * 16) == 0 else 1
        self.rows = rows // (self.cores * self.lines)
        self.core = self.group % PAIR
        self.line = self.group // PAIR
        self.my_core = self.core if self.cores > 1 else 0
        self.my_line = self.line if self.lines > 1 else 0

    @staticmethod
    def scratch(members, groups):
        lines = groups // PAIR
        return [DMA((members, 1 + 2 * lines)), DMA((members, 1 + 2 * lines))]

    def view(self, array, core, line):
        if self.cores == 1:
            return array
        start = (core * self.lines + line) * self.rows
        return array.at[pl.ds(pl.multiple_of(start, 16), self.rows), :]

    def behind(self, step):
        return (self.line + self.lines - step) % self.lines

    def copy(self):
        return remote(
            self.view(self.source, self.my_core, self.my_line),
            self.view(self.target, self.my_core, self.my_line),
            self.send.at[self.which, 0],
            self.recv.at[self.which, 0],
            self.partner,
        )

    def hand(self, step):
        view = self.view(self.target, self.my_core, self.my_line)
        return remote(
            view,
            view,
            self.send.at[self.which, step],
            self.recv.at[self.which, step],
            self.me,
            (self.line + step) % self.lines * PAIR + self.core,
        )

    def mate(self, core, line):
        view = self.view(self.target, core, line)
        slot = self.all_lines + line
        return remote(
            view,
            view,
            self.send.at[self.which, slot],
            self.recv.at[self.which, slot],
            self.me,
            self.group + 1 - 2 * self.core,
        )

    def start(self):
        self.copy().start()

    def pass_on(self):
        self.copy().wait_recv()
        for step in range(1, self.lines):
            self.hand(step).start()
        if self.cores > 1:
            self.mate(self.core, self.my_line).start()

    def relay(self):
        for step in range(1, self.lines):
            line = self.behind(step)
            view = self.view(self.target, self.core, line)
            remote(
                view,
                view,
                self.send.at[self.which, step],
                self.recv.at[self.which, step],
                self.me,
                self.group,
            ).wait_recv()
            self.mate(self.core, line).start()

    def wait(self):
        if self.cores > 1:
            for line in range(self.lines):
                self.mate(1 - self.core, line).wait_recv()

    def close(self):
        self.copy().wait_send()
        for step in range(1, self.lines):
            self.hand(step).wait_send()
        if self.cores > 1:
            for line in range(self.lines):
                self.mate(self.core, line).wait_send()


def head_mask(head, width):
    lane = lax.broadcasted_iota(jnp.int32, (1, width), 1)
    return (lane >= head * HD) & (lane < (head + 1) * HD)


def softmax_rows(queries, keys, key_live, scale):
    scores = dot_nt(queries, keys) * scale
    scores = jnp.where(key_live, scores, -1e30)
    top = jnp.max(scores, axis=-1, keepdims=True)
    raised = jnp.exp(scores - top)
    return raised / jnp.sum(raised, axis=-1, keepdims=True)


def attend_shard(normed, heads, row, spots, proj_out, shard, rows, key_live, scale):
    local = heads.shape[0] // 4
    query_bias = row[:, spots["query"] : spots["query"] + local]
    value_bias = row[:, spots["value"] : spots["value"] + local]
    queries = (dot_nt(normed, heads[0:local, :]) + query_bias).astype(LOW)
    keys = dot_nt(normed, heads[local : 2 * local, :]).astype(LOW)
    values = (dot_nt(normed, heads[2 * local : 3 * local, :]) + value_bias).astype(LOW)
    proj_out[shard, 0, rows, :] = queries
    proj_out[shard, 1, rows, :] = keys
    proj_out[shard, 2, rows, :] = values
    attended = jnp.zeros((normed.shape[0], local), F32)
    for head in range(local // HD):
        mask = head_mask(head, local)
        weights = softmax_rows(jnp.where(mask, queries, 0.0).astype(LOW), keys, key_live, scale)
        attended = attended + dot(weights.astype(LOW), jnp.where(mask, values, 0.0).astype(LOW))
    return attended.astype(LOW)


def ahead_kernel(
    sizes,
    groups,
    count,
    index,
    patches,
    cotangent,
    qkv,
    out_weight,
    cond,
    mod_weight,
    up_own,
    down_own,
    mod_bias,
    qv_bias,
    out_bias,
    up_bias,
    down_bias,
    normed_kept,
    proj_kept,
    attended_kept,
    tokens_own,
    mod,
    silu_all,
    heads_other,
    up_grad,
    down_grad,
    up_bias_grad,
    down_bias_grad,
    block_own,
    grad_mid_out,
    grad_branch_out,
    sums_out,
    normed_out,
    proj_out,
    attended_out,
    keep_sem,
    heads_own,
    row_own,
    heads_sem,
    up_other,
    down_other,
    row_other,
    mid_out,
    branch_out,
    patch_rows,
    tokens,
    terms,
    landing,
    total,
    mod_mine,
    mod_gathered,
    patch_sem,
    send,
    recv,
    mod_send,
    mod_recv,
    silu_send,
    silu_recv,
    weight_send,
    weight_recv,
    *rest,
):
    depth, images, kept, share, pieces = sizes
    devices = depth * PAIR
    me, up, side = place(depth)
    group = lax.axis_index("dp")
    width = patches.shape[2]
    local = heads_own.shape[0] // 4
    mods = mod_weight.shape[0]
    spots, _ = row_spots(width, up_own.shape[0], local, mods)
    scale = HD ** (-0.5)
    fold = depth // images
    first = side * images

    def fetch(image):
        return pltpu.make_async_copy(
            patches.at[first + image], patch_rows.at[image], patch_sem.at[image]
        )

    def image_at(turn):
        return across(up // fold, images - 1 - turn, images)

    (
        normed_two,
        cot,
        hidden,
        grad_pre,
        grad_mlp,
        back_terms,
        back_landing,
        mlp_terms,
        mlp_landing,
        back_part,
        mlp_part,
        back_total,
        mlp_total,
        up_sums,
        down_sums,
        cot_sem,
        gather_send,
        gather_recv,
        back_send,
        back_recv,
        mlp_send,
        mlp_recv,
    ) = rest
    units = up_own.shape[0]

    def fetch_cotangent(image):
        return pltpu.make_async_copy(
            cotangent.at[first + image],
            cot.at[pl.ds(pl.multiple_of(image * kept, kept), kept), :],
            cot_sem.at[image],
        )

    def fetch_heads(member):
        return pltpu.make_async_copy(
            qkv.at[member] if member < 3 else out_weight,
            heads_own.at[pl.ds(member * local, local), :],
            heads_sem.at[member],
        )

    for member in range(4):
        fetch_heads(member).start()
    row_own[...] = jnp.zeros(row_own.shape, F32)
    for name, bias in (
        ("out", out_bias[...]),
        ("down", down_bias[...]),
        ("up", up_bias[...]),
        ("query", qv_bias[0:1, :]),
        ("value", qv_bias[1:2, :]),
        ("mod", mod_bias[...]),
    ):
        size = bias.shape[-1]
        row_own[:, spots[name] : spots[name] + size] = bias.astype(F32).reshape(1, size)
    for turn in range(images):
        fetch(image_at(turn)).start()
    meet(
        [(group, (me + step) % devices) for step in range(1, devices)]
        + [((group + step) % groups, me) for step in range(1, groups)]
    )
    value = cond[...].astype(F32)
    silu = (value / (1.0 + jnp.exp(-value))).astype(LOW)
    silu_all[group] = silu
    local_mod = (
        dot_nt(silu, mod_weight[...]) + row_own[:, spots["mod"] : spots["mod"] + mods]
    ).astype(LOW)
    mod_mine[...] = local_mod
    mod_gathered[me] = local_mod
    mod_copies = [
        remote(
            mod_mine,
            mod_gathered.at[me],
            mod_send.at[step],
            mod_recv.at[step],
            (me + step) % devices,
        )
        for step in range(1, devices)
    ]
    silu_copies = [
        remote(
            silu_all.at[group],
            silu_all.at[group],
            silu_send.at[step],
            silu_recv.at[step],
            me,
            (group + step) % groups,
        )
        for step in range(1, groups)
    ]
    for copy in mod_copies + silu_copies:
        copy.start()

    shares = [
        Share(source, target, weight_send, weight_recv, which, depth, groups)
        for which, (source, target) in enumerate(
            (
                (row_own, row_other),
                (heads_own, heads_other),
                (up_own, up_other),
                (down_own, down_other),
            )
        )
    ]
    for member in range(4):
        fetch_heads(member).wait()
    outer = up // (depth // PAIR) == side
    shares[0].start()
    shares[1].start()

    @pl.when(jnp.logical_not(outer))
    def _():
        shares[2].start()
        shares[3].start()

    for image in range(images):
        fetch_cotangent(image).start()
    reduce = Reduce(terms, landing, share, depth, pieces, send, recv)
    gather = Gather(normed_two, share, depth, pieces, gather_send, gather_recv)
    back_reduce = Reduce(back_terms, back_landing, share, depth, pieces, back_send, back_recv)
    mlp_reduce = Reduce(mlp_terms, mlp_landing, share, depth, pieces, mlp_send, mlp_recv)

    def pick_rows(turn, carry):
        image = image_at(turn)
        fetch(image).wait()
        rows = pl.ds(pl.multiple_of(image * kept, kept), kept)
        positions = lax.broadcasted_iota(jnp.int32, (patches.shape[1], kept), 0)
        slots = lax.broadcasted_iota(jnp.int32, (patches.shape[1], kept), 1)
        listed = index[pl.ds(first + image, 1), :]
        pick = jnp.where((positions == listed) & (slots < count[first + image]), 1.0, 0.0)
        tokens[rows, :] = dot_tn(pick.astype(LOW), patch_rows[image]).astype(LOW)
        return carry

    lax.fori_loop(0, images, pick_rows, 0)
    for step in range(1, devices):
        source = (me + devices - step) % devices
        remote(
            mod_mine, mod_gathered.at[source], mod_send.at[step], mod_recv.at[step], me
        ).wait_recv()
    mod[...] = jnp.concatenate(
        [mod_gathered[device].astype(F32) for device in range(devices)], axis=-1
    )

    def block(image, member):
        return mod[pl.ds(first + image, 1), member * width : (member + 1) * width]

    def one(turn, carry):
        image = image_at(turn)
        rows = pl.ds(pl.multiple_of(image * kept, kept), kept)

        @pl.when(turn == images - 1)
        def _():
            shares[0].pass_on()
            shares[1].pass_on()

        norm, _ = norm_parts(tokens[rows, :].astype(F32))
        normed = (norm * (1.0 + block(image, 1)) + block(image, 0)).astype(LOW)
        normed_out[rows, :] = normed
        key_live = lax.broadcasted_iota(jnp.int32, (1, kept), 1) < count[first + image]
        attended_out[0, rows, :] = attend_shard(
            normed, heads_own, row_own, spots, proj_out, 0, rows, key_live, scale
        )
        return carry

    def two(turn, carry):
        image = image_at(turn)
        rows = pl.ds(pl.multiple_of(image * kept, kept), kept)
        key_live = lax.broadcasted_iota(jnp.int32, (1, kept), 1) < count[first + image]
        attended = attend_shard(
            normed_out[rows, :], heads_other, row_other, spots, proj_out, 1, rows, key_live, scale
        )
        attended_out[1, rows, :] = attended
        branch = dot(attended_out[0, rows, :], heads_own[3 * local :, :]) + dot(
            attended, heads_other[3 * local :, :]
        )
        terms[rows, :] = branch.astype(LOW)
        for part in range(fold):
            reduce.ready_share(image * fold + part)
        return carry

    lax.fori_loop(0, images, one, 0)
    shares[1].relay()
    shares[1].wait()
    lax.fori_loop(0, images, two, 0)
    keeps = [
        pltpu.make_async_copy(source, target, keep_sem.at[member])
        for member, (source, target) in enumerate(
            (
                (normed_out, normed_kept),
                (proj_out, proj_kept),
                (attended_out, attended_kept),
            )
        )
    ]
    for copy in keeps:
        copy.start()

    @pl.when(outer)
    def _():
        shares[2].start()
        shares[3].start()

    reduce.relay()
    shares[2].pass_on()
    reduce.finish(total)
    image = (up * share) // kept
    own_rows = pl.ds(pl.multiple_of(up * share, share), share)
    own = tokens[own_rows, :]
    tokens_own[...] = own
    branch = total[...] + row_own[:, spots["out"] : spots["out"] + width]
    branch_out[...] = branch
    mid = own.astype(F32) + block(image, 2) * branch
    mid_out[...] = mid
    norm, _ = norm_parts(mid)
    normed_two[own_rows, :] = (norm * (1.0 + block(image, 4)) + block(image, 3)).astype(LOW)
    shares[2].relay()
    gather.open()

    def half_pass(rows, shard, weight_up, row, weight_down):
        source = normed_two[rows, :]
        grad = grad_mlp[rows, :]
        bias = row[:, spots["up"] : spots["up"] + units]
        pre = dot_nt(source, weight_up[...]) + bias
        square = pre * pre
        bent = jnp.tanh(GELU_ROOT * pre * (1.0 + GELU_CUBE * square))
        half = 0.5 * (1.0 + bent)
        low_hidden = (pre * half).astype(LOW)
        hidden[shard, rows, :] = low_hidden
        slope = half + 0.5 * pre * (1.0 - bent * bent) * (
            GELU_ROOT * (1.0 + 3.0 * GELU_CUBE * square)
        )
        low_grad = (slope * dot_nt(grad, weight_down[...])).astype(LOW)
        grad_pre[shard, rows, :] = low_grad
        sums = jnp.sum(low_grad.astype(F32), axis=0, keepdims=True)
        return dot(low_hidden, weight_down[...]), dot(low_grad, weight_up[...]), sums

    def own_pass(image):
        fetch_cotangent(image).wait()
        rows = pl.ds(pl.multiple_of(image * kept, kept), kept)
        live = lax.broadcasted_iota(jnp.int32, (kept, 1), 0) < count[first + image]
        grad = jnp.where(live, cot[rows, :].astype(F32), 0.0)
        grad = (block(image, 5) * grad).astype(LOW)
        grad_mlp[rows, :] = grad
        down_sums[image] = jnp.sum(grad.astype(F32), axis=0, keepdims=True)
        mlp, back, sums = half_pass(rows, 0, up_own, row_own, down_own)
        up_sums[0, image] = sums
        mlp_part[rows, :] = mlp
        back_part[rows, :] = back

    def other_pass(image):
        rows = pl.ds(pl.multiple_of(image * kept, kept), kept)
        mlp, back, sums = half_pass(rows, 1, up_other, row_other, down_other)
        up_sums[1, image] = sums
        back_terms[rows, :] = (back_part[rows, :] + back).astype(LOW)
        mlp_terms[rows, :] = (mlp_part[rows, :] + mlp).astype(LOW)
        for part in range(fold):
            back_reduce.ready_share(image * fold + part)
            mlp_reduce.ready_share(image * fold + part)

    if fold == 1:

        def own_turn(turn, carry):
            @pl.when(turn == 1)
            def _():
                gather.relay()

            offset = turn + (turn // 2) * (1 - 2 * (turn % 2))
            gather.take(offset)
            own_pass(across(up, offset, depth))

            @pl.when(turn == 1)
            def _():
                shares[3].pass_on()

            return carry

        lax.fori_loop(0, depth, own_turn, 0)
    else:

        def own_image(image, carry):
            own_pass(image)
            return carry

        gather.relay()
        for offset in range(1, depth):
            gather.take(offset)
        shares[3].pass_on()
        lax.fori_loop(0, images, own_image, 0)
    shares[3].relay()
    for member in shares[2:]:
        member.wait()

    def other_turn(turn, carry):
        other_pass(image_at(turn))
        return carry

    lax.fori_loop(0, images, other_turn, 0)
    back_reduce.relay()
    mlp_reduce.relay()
    wide = tile_of(width)
    for shard in range(PAIR):

        def tile(step, carry):
            columns = pl.ds(pl.multiple_of(step * wide, 128), wide)
            up_grad[shard, 0:units, columns] = dot_tn(
                grad_pre[shard], normed_two[:, columns]
            ).astype(LOW)
            down_grad[shard, 0:units, columns] = dot_tn(
                hidden[shard], grad_mlp[:, columns]
            ).astype(LOW)
            return carry

        lax.fori_loop(0, width // wide, tile, 0)
        if units < up_grad.shape[1]:
            rest_rows = jnp.zeros((up_grad.shape[1] - units, width), LOW)
            up_grad[shard, units:, :] = rest_rows
            down_grad[shard, units:, :] = rest_rows
    back_reduce.finish(back_total)
    for shard in range(PAIR):
        up_bias_grad[shard : shard + 1, :] = sum(up_sums[shard, member] for member in range(images))
    down_bias_grad[...] = sum(down_sums[member] for member in range(images))
    live = (
        lax.broadcasted_iota(jnp.int32, (share, 1), 0) + (up * share) % kept
        < count[first + image]
    )
    grad_out = jnp.where(live, cot[own_rows, :].astype(F32), 0.0)
    norm, spread = norm_parts(mid_out[...])
    back = back_total[...]
    grad_mid = grad_out + norm_back(norm, spread, back * (1.0 + block(image, 4)))
    grad_mid_out[...] = grad_mid
    grad_branch_out[...] = (block(image, 2) * grad_mid).astype(LOW)
    sums_out[0:1, :] = jnp.sum(grad_mid * branch_out[...], axis=0, keepdims=True)
    sums_out[1:2, :] = jnp.sum(back, axis=0, keepdims=True)
    sums_out[2:3, :] = jnp.sum(back * norm, axis=0, keepdims=True)
    mlp_reduce.finish(mlp_total)
    mlp = mlp_total[...] + row_own[:, spots["down"] : spots["down"] + width]
    sums_out[3:4, :] = jnp.sum(grad_out * mlp, axis=0, keepdims=True)
    block_own[...] = jnp.where(live, mid_out[...] + block(image, 5) * mlp, 0.0).astype(LOW)
    for step in range(1, groups):
        source = (group + groups - step) % groups
        view = silu_all.at[source]
        remote(
            view, view, silu_send.at[step], silu_recv.at[step], me, group
        ).wait_recv()
    for copy in keeps:
        copy.wait()
    for member in shares:
        member.close()
    for copy in mod_copies + silu_copies:
        copy.wait_send()
    reduce.close()
    gather.close()
    back_reduce.close()
    mlp_reduce.close()


def ahead(sizes, groups, args):
    depth, images, kept, share, pieces = sizes
    patches, cotangent, qkv, out_weight, cond, mod_weight, up, down = args[2:10]
    spots, width = patches.shape[1:]
    local = out_weight.shape[0]
    mods = mod_weight.shape[0]
    units = up.shape[0]
    rows = images * kept
    heads = (4 * local, width)
    row = (1, row_spots(width, units, local, mods)[1])
    shape = jax.ShapeDtypeStruct
    devices = depth * PAIR
    return pl.pallas_call(
        functools.partial(ahead_kernel, sizes, groups),
        out_shape=(
            shape((rows, width), LOW),
            shape((PAIR, 3, rows, local), LOW),
            shape((PAIR, rows, local), LOW),
            shape((share, width), LOW),
            shape((cond.shape[0], devices * mods), F32),
            shape((groups,) + cond.shape, LOW),
            shape(heads, LOW),
            shape((PAIR, padded(units, groups), width), LOW),
            shape((PAIR, padded(units, groups), width), LOW),
            shape((PAIR, units), F32),
            shape((1, width), F32),
            shape((share, width), LOW),
            shape((share, width), F32),
            shape((share, width), LOW),
            shape((4, width), F32),
        ),
        in_specs=[SM, VM] + [HB] * 4 + [VM] * 9,
        out_specs=(HB,) * 3 + (VM,) * 12,
        scratch_shapes=[
            pltpu.VMEM((rows, width), LOW),
            pltpu.VMEM((PAIR, 3, rows, local), LOW),
            pltpu.VMEM((PAIR, rows, local), LOW),
            DMA((3,)),
            pltpu.VMEM(heads, LOW),
            pltpu.VMEM(row, F32),
            DMA((4,)),
            pltpu.VMEM(up.shape, LOW),
            pltpu.VMEM(down.shape, LOW),
            pltpu.VMEM(row, F32),
            pltpu.VMEM((share, width), F32),
            pltpu.VMEM((share, width), F32),
            pltpu.VMEM((images, spots, width), LOW),
            pltpu.VMEM((rows, width), LOW),
            pltpu.VMEM((rows, width), LOW),
            pltpu.VMEM((rows - share, width), LOW),
            pltpu.VMEM((share, width), F32),
            pltpu.VMEM((cond.shape[0], mods), LOW),
            pltpu.VMEM((devices, cond.shape[0], mods), LOW),
            DMA((images,)),
        ]
        + Reduce.scratch(depth, pieces)
        + [
            DMA((devices,)),
            DMA((devices,)),
            DMA((groups,)),
            DMA((groups,)),
        ]
        + Share.scratch(4, groups)
        + [
            pltpu.VMEM((rows, width), LOW),
            pltpu.VMEM((rows, width), LOW),
            pltpu.VMEM((PAIR, rows, units), LOW),
            pltpu.VMEM((PAIR, rows, units), LOW),
            pltpu.VMEM((rows, width), LOW),
            pltpu.VMEM((rows, width), LOW),
            pltpu.VMEM((rows - share, width), LOW),
            pltpu.VMEM((rows, width), LOW),
            pltpu.VMEM((rows - share, width), LOW),
            pltpu.VMEM((rows, width), F32),
            pltpu.VMEM((rows, width), F32),
            pltpu.VMEM((share, width), F32),
            pltpu.VMEM((share, width), F32),
            pltpu.VMEM((PAIR, images, 1, units), F32),
            pltpu.VMEM((images, 1, width), F32),
            DMA((images,)),
        ]
        + Gather.scratch(depth, pieces)
        + Reduce.scratch(depth, pieces)
        + Reduce.scratch(depth, pieces),
        compiler_params=pltpu.CompilerParams(
            collective_id=1, has_side_effects=True, vmem_limit_bytes=62 << 20
        ),
        name="ahead",
    )(*args)


def attend_back_kernel(
    sizes,
    groups,
    count,
    grad_own,
    normed_kept,
    proj,
    attended_kept,
    qkv_own,
    out_own,
    heads_other,
    mod,
    tokens_own,
    grad_mid,
    block_own,
    up_grad,
    down_grad,
    heads_grad,
    qv_grad,
    out_bias_grad,
    grad_tokens,
    sums_out,
    block_out,
    up_total,
    down_total,
    normed,
    attended,
    kept_sem,
    grads,
    grad_proj,
    terms,
    landing,
    total,
    qv_sums,
    out_sums,
    own_sem,
    gather_send,
    gather_recv,
    send,
    recv,
    *rest,
):
    depth, images, kept, share, pieces = sizes
    me, up, side = place(depth)
    width = grad_own.shape[1]
    local = out_own.shape[0]
    scale = HD ** (-0.5)
    fold = depth // images
    first = side * images
    up_fold = Fold(up_grad, rest[:7], up_total, depth, groups)
    down_fold = Fold(down_grad, rest[7:14], down_total, depth, groups)
    spread = Spread(block_out, share, depth, pieces, rest[14:18])
    own_rows = pl.ds(pl.multiple_of(up * share, share), share)
    own_copy = pltpu.make_async_copy(grad_own, grads.at[own_rows, :], own_sem.at[0])
    own_copy.start()
    block_copy = pltpu.make_async_copy(block_own, spread.own(), own_sem.at[1])
    block_copy.start()
    keeps = [
        pltpu.make_async_copy(normed_kept, normed, kept_sem.at[0]),
        pltpu.make_async_copy(attended_kept, attended, kept_sem.at[1]),
    ]
    for copy in keeps:
        copy.start()
    meet(column_peers(depth) + cube_peers(depth, groups) + spread.peers_beyond(depth))
    own_copy.wait()
    gather = Gather(grads, share, depth, pieces, gather_send, gather_recv)
    reduce = Reduce(terms, landing, share, depth, pieces, send, recv)
    gather.open()
    up_fold.one()
    down_fold.one()
    block_copy.wait()

    def one(image):
        rows = pl.ds(pl.multiple_of(image * kept, kept), kept)
        key_live = lax.broadcasted_iota(jnp.int32, (1, kept), 1) < count[first + image]
        grad = grads[rows, :]
        out_sums[image] = jnp.sum(grad.astype(F32), axis=0, keepdims=True)
        back = None
        for shard in range(PAIR):
            weights_in = [
                heads_other[member * local : (member + 1) * local, :] if shard else qkv_own[member]
                for member in range(3)
            ]
            weights_out = heads_other[3 * local :, :] if shard else out_own[...]
            grad_att = dot_nt(grad, weights_out).astype(LOW)
            queries = proj[shard, 0, rows, :]
            keys = proj[shard, 1, rows, :]
            values = proj[shard, 2, rows, :]
            grad_q = jnp.zeros((kept, local), F32)
            grad_k = jnp.zeros((kept, local), F32)
            grad_v = jnp.zeros((kept, local), F32)
            for head in range(local // HD):
                mask = head_mask(head, local)
                head_q = jnp.where(mask, queries, 0.0).astype(LOW)
                head_grad = jnp.where(mask, grad_att, 0.0).astype(LOW)
                weights = softmax_rows(head_q, keys, key_live, scale)
                grad_weights = dot_nt(head_grad, values)
                inner = jnp.sum(weights * grad_weights, axis=-1, keepdims=True)
                grad_scores = (weights * (grad_weights - inner)).astype(LOW)
                grad_v = grad_v + dot_tn(weights.astype(LOW), head_grad)
                grad_q = grad_q + dot(grad_scores, jnp.where(mask, keys, 0.0).astype(LOW))
                grad_k = grad_k + dot_tn(grad_scores, head_q)
            for member, value in enumerate((grad_q * scale, grad_k * scale, grad_v)):
                low = value.astype(LOW)
                grad_proj[shard, member, rows, :] = low
                part = dot(low, weights_in[member])
                back = part if back is None else back + part
                if member != 1:
                    row = 2 * shard + member // 2
                    qv_sums[row, image] = jnp.sum(low.astype(F32), axis=0, keepdims=True)
        terms[rows, :] = back.astype(LOW)
        for part in range(fold):
            reduce.ready_share(image * fold + part)

    if fold == 1:

        def turn_of(turn, carry):
            @pl.when(turn == 1)
            def _():
                gather.relay()

            offset = turn + (turn // 2) * (1 - 2 * (turn % 2))
            gather.take(offset)
            one(across(up, offset, depth))

            @pl.when(turn == 0)
            def _():
                up_fold.two()
                down_fold.two()

            @pl.when(turn == 1)
            def _():
                spread.open()

            @pl.when(turn == 2)
            def _():
                up_fold.three()

            @pl.when(turn == 3)
            def _():
                down_fold.three()

            return carry

        lax.fori_loop(0, depth, turn_of, 0)
    else:

        def image_of(image, carry):
            one(image)
            return carry

        gather.relay()
        for offset in range(1, depth):
            gather.take(offset)
        up_fold.two()
        down_fold.two()
        spread.open()
        lax.fori_loop(0, images, image_of, 0)
        up_fold.three()
        down_fold.three()

    def spread_of(turn, carry):
        spread.take(turn)
        return carry

    reduce.relay()
    lax.fori_loop(1, depth - 1, spread_of, 0)
    up_fold.four()
    down_fold.four()
    for copy in keeps:
        copy.wait()
    wide = tile_of(width)
    for shard in range(PAIR):

        def tile(step, carry):
            columns = pl.ds(pl.multiple_of(step * wide, 128), wide)
            source = normed[:, columns]
            for member in range(3):
                heads_grad[shard, member * local : (member + 1) * local, columns] = dot_tn(
                    grad_proj[shard, member], source
                ).astype(LOW)
            heads_grad[shard, 3 * local : 4 * local, columns] = dot_tn(
                attended[shard], grads[:, columns]
            ).astype(LOW)
            return carry

        lax.fori_loop(0, width // wide, tile, 0)
        if 4 * local < heads_grad.shape[1]:
            heads_grad[shard, 4 * local :, :] = jnp.zeros(
                (heads_grad.shape[1] - 4 * local, width), LOW
            )
    up_fold.five()
    spread.take(depth - 1)
    down_fold.five()
    reduce.finish(total)
    for row in range(2 * PAIR):
        qv_grad[row : row + 1, :] = sum(qv_sums[row, image] for image in range(images))
    out_bias_grad[...] = sum(out_sums[image] for image in range(images))
    image = first + (up * share) // kept
    live = (
        lax.broadcasted_iota(jnp.int32, (share, 1), 0) + (up * share) % kept < count[image]
    )
    norm, spread_rows = norm_parts(tokens_own[...].astype(F32))
    back = total[...]
    scale_one = mod[pl.ds(image, 1), width : 2 * width]
    grad = grad_mid[...] + norm_back(norm, spread_rows, back * (1.0 + scale_one))
    grad_tokens[...] = jnp.where(live, grad, 0.0).astype(LOW)
    sums_out[0:1, :] = jnp.sum(back, axis=0, keepdims=True)
    sums_out[1:2, :] = jnp.sum(back * norm, axis=0, keepdims=True)
    up_fold.six()
    down_fold.six()
    for index in range(depth):
        spread.crossed(index)
    spread.close()
    gather.close()
    reduce.close()


def attend_back(sizes, groups, args):
    depth, images, kept, share, pieces = sizes
    width = args[1].shape[1]
    local = args[6].shape[0]
    up_grad, down_grad = args[-2:]
    rows = images * kept
    shape = jax.ShapeDtypeStruct
    return pl.pallas_call(
        functools.partial(attend_back_kernel, sizes, groups),
        out_shape=(
            shape((PAIR, padded(4 * local, groups), width), LOW),
            shape((2 * PAIR, local), F32),
            shape((1, width), F32),
            shape((share, width), LOW),
            shape((2, width), F32),
            shape((PAIR * rows, width), LOW),
            shape(up_grad.shape[1:], LOW),
            shape(down_grad.shape[1:], LOW),
        ),
        in_specs=[SM, VM, HB, VM, HB] + [VM] * 9,
        out_specs=(VM,) * 8,
        scratch_shapes=[
            pltpu.VMEM((rows, width), LOW),
            pltpu.VMEM((PAIR, rows, local), LOW),
            DMA((2,)),
            pltpu.VMEM((rows, width), LOW),
            pltpu.VMEM((PAIR, 3, rows, local), LOW),
            pltpu.VMEM((rows, width), LOW),
            pltpu.VMEM((rows - share, width), LOW),
            pltpu.VMEM((share, width), F32),
            pltpu.VMEM((2 * PAIR, images, 1, local), F32),
            pltpu.VMEM((images, 1, width), F32),
            DMA((2,)),
        ]
        + Gather.scratch(depth, pieces)
        + Reduce.scratch(depth, pieces)
        + Fold.scratch(up_grad.shape, groups)
        + Fold.scratch(down_grad.shape, groups)
        + Spread.scratch(depth, pieces),
        compiler_params=pltpu.CompilerParams(
            collective_id=3, has_side_effects=True, vmem_limit_bytes=62 << 20
        ),
        name="attend_back",
    )(*args)


def split_low(value):
    high = value.astype(LOW)
    rest = value - high.astype(F32)
    low = rest.astype(LOW)
    return high, low, (rest - low.astype(F32)).astype(LOW)


def close_kernel(
    sizes,
    groups,
    grad_tokens,
    sums_one,
    sums_two,
    up_bias_grad,
    qv_grad,
    down_bias_grad,
    out_bias_grad,
    heads_grad,
    silu_all,
    mod_weight,
    cond,
    whole,
    heads_total,
    bias_total,
    grads_out,
    silu_out,
    mod_bias_grad,
    grad_cond,
    biases,
    sum_row,
    sum_land,
    bias_land,
    cond_land,
    own_sem,
    sum_send,
    sum_recv,
    bias_send,
    bias_recv,
    cond_send,
    cond_recv,
    *rest,
):
    depth, images, kept, share, pieces = sizes
    devices = depth * PAIR
    everyone = devices * groups
    me, _, side = place(depth)
    group = lax.axis_index("dp")
    flat = group * devices + me
    width = grad_tokens.shape[1]
    columns = mod_weight.shape[0]
    span = sum_land.shape[2]
    spread = Spread(whole, share, depth, pieces, rest[:4])
    fold = Fold(heads_grad, rest[4:11], heads_total, depth, groups)
    own_copy = pltpu.make_async_copy(grad_tokens, spread.own(), own_sem)
    own_copy.start()
    barrier = pltpu.get_barrier_semaphore()

    def greet(step, carry):
        there = (flat + step) % everyone
        pl.semaphore_signal(
            barrier,
            inc=1,
            device_id={"dp": there // devices, "tensor": there % devices},
            device_id_type=MESH,
        )
        return carry

    lax.fori_loop(1, everyone, greet, 0)
    pl.semaphore_wait(barrier, everyone - 1)
    own_copy.wait()
    fold.one()
    spread.open()

    def aligned(device):
        return pl.multiple_of((device * columns) // 128 * 128, 128)

    for member in range(6):
        part = sums_one[member : member + 1, :] if member < 2 else sums_two[member - 2 : member - 1, :]
        sum_row[:, member * width : (member + 1) * width] = part
    sum_row[:, 6 * width :] = jnp.zeros((1, sum_row.shape[1] - 6 * width), F32)

    def sum_copy(step):
        there = (flat + step) % everyone
        device = there % devices
        return remote(
            sum_row.at[:, pl.ds(aligned(device), span)],
            sum_land.at[flat],
            sum_send.at[step],
            sum_recv.at[step],
            device,
            there // devices,
        )

    def send_sum(step, carry):
        sum_copy(step).start()
        return carry

    lax.fori_loop(1, everyone, send_sum, 0)
    sum_land[flat] = sum_row[:, pl.ds(aligned(me), span)]
    units, local = up_bias_grad.shape[1], qv_grad.shape[1]
    biases[...] = jnp.zeros(biases.shape, F32)
    for shard in range(PAIR):
        biases[3 * shard : 3 * shard + 1, 0:units] = up_bias_grad[shard : shard + 1, :]
        biases[3 * shard + 1 : 3 * shard + 3, 0:local] = qv_grad[2 * shard : 2 * shard + 2, :]
    biases[6:7, :] = down_bias_grad[...]
    biases[7:8, :] = out_bias_grad[...]
    slot = side * groups + group
    bias_land[slot] = biases[...]
    partner = me + depth * (1 - 2 * side)

    def bias_copy(step):
        crossed = step // groups
        there = (group + step) % groups
        device = jnp.where(crossed == 1, partner, me)
        return remote(
            biases, bias_land.at[slot], bias_send.at[step], bias_recv.at[step], device, there
        )

    for step in range(1, PAIR * groups):
        bias_copy(step).start()
    fold.two()

    def wait_sum(step, carry):
        source = (flat + everyone - step) % everyone
        view = sum_land.at[source]
        remote(view, view, sum_send.at[step], sum_recv.at[step], me).wait_recv()
        return carry

    lax.fori_loop(1, everyone, wait_sum, 0)
    offset = (me * columns) % 128
    grads = jnp.concatenate([sum_land[device] for device in range(everyone)], axis=0)
    grads = pltpu.roll(grads, lax.rem(span - offset, span), 1)[:, :columns]
    mod_bias_grad[...] = jnp.sum(grads, axis=0, keepdims=True)
    total_images = images * PAIR

    def image_of(device):
        return device * share // kept

    source = lax.broadcasted_iota(jnp.int32, (everyone, groups * total_images), 0)
    target = lax.broadcasted_iota(jnp.int32, (everyone, groups * total_images), 1)
    row_image = source // devices * total_images + image_of(source % devices)
    chosen = jnp.where(row_image == target, 1.0, 0.0).astype(LOW)
    silu_out[...] = dot(
        chosen,
        jnp.concatenate([silu_all[member].astype(F32) for member in range(groups)], axis=0).astype(
            LOW
        ),
    ).astype(LOW)
    parts = split_low(grads)
    spread.take(1)
    fold.three()
    grads_out[...] = grads.T
    source = lax.broadcasted_iota(jnp.int32, (total_images, everyone), 1)
    target = lax.broadcasted_iota(jnp.int32, (total_images, everyone), 0)
    chosen = jnp.where(
        (source // devices == group) & (image_of(source % devices) == target), 1.0, 0.0
    ).astype(LOW)
    mine = dot(chosen, parts[0]) + dot(chosen, parts[1]) + dot(chosen, parts[2])
    parts = split_low(mine)
    term = (
        dot(parts[0], mod_weight[...])
        + dot(parts[1], mod_weight[...])
        + dot(parts[2], mod_weight[...])
    )
    cond_land[me] = term

    def cond_copy(step):
        return remote(
            cond_land.at[me],
            cond_land.at[me],
            cond_send.at[step],
            cond_recv.at[step],
            (me + step) % devices,
        )

    for step in range(1, devices):
        cond_copy(step).start()
    for turn in range(2, depth - 1):
        spread.take(turn)
    fold.four()
    for step in range(1, PAIR * groups):
        crossed = step // groups
        source_group = (group + groups - step % groups) % groups
        source_side = jnp.where(crossed == 1, 1 - side, side)
        view = bias_land.at[source_side * groups + source_group]
        remote(view, view, bias_send.at[step], bias_recv.at[step], me).wait_recv()
    rows = biases.shape[0]
    result = jnp.zeros((rows, width), F32)
    for member in range(PAIR * groups):
        value = bias_land[member]
        turned = jnp.concatenate([value[3:6, :], value[0:3, :], value[6:, :]], axis=0)
        same = side == member // groups
        result = result + jnp.where(same, value, turned)
    bias_total[...] = result
    for step in range(1, devices):
        source = (me + devices - step) % devices
        view = cond_land.at[source]
        remote(view, view, cond_send.at[step], cond_recv.at[step], me).wait_recv()
    back = cond_land[0]
    for device in range(1, devices):
        back = back + cond_land[device]
    value = cond[...].astype(F32)
    gate = 1.0 / (1.0 + jnp.exp(-value))
    grad_cond[...] = (back * (gate + value * gate * (1.0 - gate))).astype(LOW)
    spread.take(depth - 1)
    fold.five()
    for where in range(depth):
        spread.crossed(where)
    fold.six()
    spread.close()

    def done_sum(step, carry):
        sum_copy(step).wait_send()
        return carry

    lax.fori_loop(1, everyone, done_sum, 0)
    for step in range(1, PAIR * groups):
        bias_copy(step).wait_send()
    for step in range(1, devices):
        cond_copy(step).wait_send()


def close(sizes, groups, args):
    depth, images, kept, share, pieces = sizes
    grad_tokens = args[0]
    heads_grad, silu_all, mod_weight, cond = args[-4:]
    devices = depth * PAIR
    width = grad_tokens.shape[1]
    columns = mod_weight.shape[0]
    biases = (8, width)
    span = max(-(-((device * columns) % 128 + columns) // 128) * 128 for device in range(devices))
    long = max((device * columns) // 128 * 128 + span for device in range(devices))
    long = max(long, 6 * width + 128)
    shape = jax.ShapeDtypeStruct
    rows = PAIR * images * kept
    everyone = devices * groups
    return pl.pallas_call(
        functools.partial(close_kernel, sizes, groups),
        out_shape=(
            shape((rows, width), LOW),
            shape(heads_grad.shape[1:], LOW),
            shape(biases, F32),
            shape((columns, everyone), F32),
            shape((everyone, width), LOW),
            shape((1, columns), F32),
            shape(cond.shape, LOW),
        ),
        in_specs=[VM] * 11,
        out_specs=(VM,) * 7,
        scratch_shapes=[
            pltpu.VMEM(biases, F32),
            pltpu.VMEM((1, long), F32),
            pltpu.VMEM((everyone, 1, span), F32),
            pltpu.VMEM((PAIR * groups,) + biases, F32),
            pltpu.VMEM((devices,) + cond.shape, F32),
            DMA,
            DMA((everyone,)),
            DMA((everyone,)),
            DMA((PAIR * groups,)),
            DMA((PAIR * groups,)),
            DMA((devices,)),
            DMA((devices,)),
        ]
        + Spread.scratch(depth, pieces)
        + Fold.scratch(heads_grad.shape, groups),
        compiler_params=pltpu.CompilerParams(
            collective_id=4, has_side_effects=True, vmem_limit_bytes=62 << 20
        ),
        name="close",
    )(*args)


def settle_kernel(
    index,
    whole,
    block,
    up_low,
    down_low,
    heads_low,
    mod_grads,
    silu_rows,
    biases,
    mod_bias,
    cond,
    block_out,
    grad_patches,
    grad_cond,
    mod_rows_grad,
    mod_bias_grad,
    qkv_grad,
    qv_grad,
    out_grad,
    out_bias_grad,
    up_grad,
    up_bias_grad,
    down_grad,
    down_bias_grad,
):
    members, kept, _ = block_out.shape
    step = pl.program_id(0)
    local, units = out_grad.shape[0], up_bias_grad.shape[0]
    for member in range(members):
        rows = slice(member * kept, (member + 1) * kept)
        block_out[member] = block[rows, :]
        positions = lax.broadcasted_iota(jnp.int32, (grad_patches.shape[1], kept), 0)
        listed = index[pl.ds(step * members + member, 1), :]
        pick = jnp.where(positions == listed, 1.0, 0.0).astype(LOW)
        grad_patches[member] = dot(pick, whole[rows, :]).astype(LOW)
    parts = split_low(mod_grads[...])
    silu = silu_rows[...]
    mod_rows_grad[...] = dot(parts[0], silu) + dot(parts[1], silu) + dot(parts[2], silu)
    up_grad[...] = up_low[...].astype(F32)
    down_grad[...] = down_low[...].astype(F32)

    @pl.when(step == 0)
    def _():
        for member in range(3):
            qkv_grad[member] = heads_low[member * local : (member + 1) * local, :].astype(F32)
        out_grad[...] = heads_low[3 * local : 4 * local, :].astype(F32)
        grad_cond[...] = cond[...]
        mod_bias_grad[...] = mod_bias[...].reshape(mod_bias_grad.shape)
        qv_grad[...] = biases[1:3, 0:local]
        up_bias_grad[...] = biases[0:1, 0:units].reshape(up_bias_grad.shape)
        down_bias_grad[...] = biases[6:7, :].reshape(down_bias_grad.shape)
        out_bias_grad[...] = biases[7:8, :].reshape(out_bias_grad.shape)


def settle(local, units, spots, args):
    index, whole, block, up_low, down_low, heads_low, mod_grads, silu_rows, biases, mod_bias, cond = args
    images, kept = index.shape
    width = whole.shape[1]
    mods = mod_bias.shape[1]
    steps = 4 if units % 64 == 0 and mods % 32 == 0 else 2
    members = images // steps
    shape = jax.ShapeDtypeStruct

    def full(array):
        return pl.BlockSpec(array.shape, lambda step: (0,) * len(array.shape))

    def part(array, rows):
        rest = array.shape[1:]
        return pl.BlockSpec((rows,) + rest, lambda step: (step,) + (0,) * len(rest))

    outs = (
        shape((images, kept, width), LOW),
        shape((images, spots, width), LOW),
        shape(cond.shape, LOW),
        shape((mods, width), F32),
        shape((mods,), F32),
        shape((3, local, width), F32),
        shape((2, local), F32),
        shape((local, width), F32),
        shape((width,), F32),
        shape((units, width), F32),
        shape((units,), F32),
        shape((units, width), F32),
        shape((width,), F32),
    )
    return pl.pallas_call(
        settle_kernel,
        grid=(steps,),
        out_shape=outs,
        in_specs=[
            full(index),
            part(whole, members * kept),
            part(block, members * kept),
            part(up_low, units // steps),
            part(down_low, units // steps),
            full(heads_low),
            part(mod_grads, mods // steps),
            full(silu_rows),
            full(biases),
            full(mod_bias),
            full(cond),
        ],
        out_specs=(
            part(outs[0], members),
            part(outs[1], members),
            full(outs[2]),
            part(outs[3], mods // steps),
            full(outs[4]),
            full(outs[5]),
            full(outs[6]),
            full(outs[7]),
            full(outs[8]),
            part(outs[9], units // steps),
            full(outs[10]),
            part(outs[11], units // steps),
            full(outs[12]),
        ),
        compiler_params=pltpu.CompilerParams(vmem_limit_bytes=60 << 20),
        name="settle",
    )(*args)


def on_device(
    patches,
    conditioning,
    keep_count,
    keep_index,
    mod_weight,
    mod_bias,
    qkv_weight,
    qv_bias,
    out_weight,
    out_bias,
    up_weight,
    up_bias,
    down_weight,
    down_bias,
    out_cotangent,
):
    devices = lax.axis_size("tensor")
    depth = devices // PAIR
    all_images, kept = keep_index.shape
    width = patches.shape[2]
    images = all_images // PAIR
    share = images * kept // depth
    pieces = 4 if share % 64 == 0 else 2
    sizes = (depth, images, kept, share, pieces)
    groups = lax.axis_size("dp")
    local, units = qkv_weight.shape[2], up_weight.shape[1]
    up = up_weight.T
    mod_rows = mod_weight.T
    qkv = jnp.swapaxes(qkv_weight, 1, 2)
    (
        normed_one,
        proj,
        attended,
        tokens_own,
        mod,
        silu_all,
        heads_other,
        up_grad,
        down_grad,
        up_bias_grad,
        down_bias_grad,
        block_own,
        grad_mid,
        grad_branch,
        sums_two,
    ) = ahead(
        sizes,
        groups,
        (
            keep_count,
            keep_index,
            patches,
            out_cotangent,
            qkv,
            out_weight,
            conditioning,
            mod_rows,
            up,
            down_weight,
            mod_bias,
            qv_bias,
            out_bias,
            up_bias,
            down_bias,
        ),
    )
    (
        heads_grad,
        qv_grad,
        out_bias_grad,
        grad_tokens,
        sums_one,
        block_out,
        up_total,
        down_total,
    ) = attend_back(
        sizes,
        groups,
        (
            keep_count,
            grad_branch,
            normed_one,
            proj,
            attended,
            qkv,
            out_weight,
            heads_other,
            mod,
            tokens_own,
            grad_mid,
            block_own,
            up_grad,
            down_grad,
        ),
    )
    (
        grad_whole,
        heads_total,
        bias_total,
        mod_grads,
        silu_rows,
        mod_bias_total,
        cond_total,
    ) = close(
        sizes,
        groups,
        (
            grad_tokens,
            sums_one,
            sums_two,
            up_bias_grad,
            qv_grad,
            down_bias_grad,
            out_bias_grad,
            heads_grad,
            silu_all,
            mod_rows,
            conditioning,
        ),
    )
    (
        block_out,
        grad_patches,
        grad_conditioning,
        mod_rows_grad,
        mod_bias_grad,
        qkv_grad,
        qv_bias_grad,
        out_weight_grad,
        out_bias_grad,
        up_rows_grad,
        up_bias_grad,
        down_weight_grad,
        down_bias_grad,
    ) = settle(
        local,
        units,
        patches.shape[1],
        (
            keep_index,
            grad_whole,
            block_out,
            up_total,
            down_total,
            heads_total,
            mod_grads,
            silu_rows,
            bias_total,
            mod_bias_total,
            cond_total,
        ),
    )
    return (
        block_out,
        grad_patches,
        grad_conditioning,
        mod_rows_grad.T,
        mod_bias_grad,
        jnp.swapaxes(qkv_grad, 1, 2),
        qv_bias_grad,
        out_weight_grad,
        out_bias_grad,
        up_rows_grad.T,
        up_bias_grad,
        down_weight_grad,
        down_bias_grad,
    )


def solution(mesh):
    placed = (
        P("dp", None, None),
        P("dp", None),
        P("dp"),
        P("dp", None),
        P(None, "tensor"),
        P("tensor"),
        P(None, None, "tensor"),
        P(None, "tensor"),
        P("tensor", None),
        P(),
        P(None, "tensor"),
        P("tensor"),
        P("tensor", None),
        P(),
        P("dp", None, None),
    )
    return jax.shard_map(
        on_device,
        mesh=mesh,
        in_specs=placed,
        out_specs=(
            P("dp", None, None),
            P("dp", None, None),
            P("dp", None),
            P(None, "tensor"),
            P("tensor"),
            P(None, None, "tensor"),
            P(None, "tensor"),
            P("tensor", None),
            P(),
            P(None, "tensor"),
            P("tensor"),
            P("tensor", None),
            P(),
        ),
        check_vma=False,
    )
```
